32 devices in a mesh: dp: 4 (over x, core), fsdp: 8 (over z, y).
Axes of the slice: x: 2, y: 2, z: 4, core: 2. Of those that a mesh axis runs over, the one named last changes fastest.
Arguments:
- features: bfloat16 [12288, 512], P(('dp', 'fsdp')), may hold values from -6 to 6
- cotangent: bfloat16 [12288, 512], P(('dp', 'fsdp')), may hold values from -6 to 6
- lengths: int32 [32, 4], P(('dp', 'fsdp')), may hold values from 0 to 384, as said below
- front_up: bfloat16 [512, 2048], P(('dp', 'fsdp')), may hold values from -0.25 to 0.25
- front_down: bfloat16 [2048, 512], P(('dp', 'fsdp')), may hold values from -0.125 to 0.125
- heads_input: bfloat16 [512, 1536], P(('dp', 'fsdp')), may hold values from -0.25 to 0.25
- heads_output: bfloat16 [512, 512], P(('dp', 'fsdp')), may hold values from -3 to 3
- gated_input: bfloat16 [512, 3072], P(('dp', 'fsdp')), may hold values from -0.25 to 0.25
- gated_output: bfloat16 [1536, 512], P(('dp', 'fsdp')), may hold values from -0.15625 to 0.15625
- merge_output: bfloat16 [1024, 512], P(('dp', 'fsdp')), may hold values from -0.1875 to 0.1875
- rear_up: bfloat16 [512, 2048], P(('dp', 'fsdp')), may hold values from -0.25 to 0.25
- rear_down: bfloat16 [2048, 512], P(('dp', 'fsdp')), may hold values from -0.125 to 0.125
- gate_kernel: bfloat16 [31, 1536], P(None, ('dp', 'fsdp')), may hold values from -1 to 1
- merge_kernel: bfloat16 [31, 1024], P(None, ('dp', 'fsdp')), may hold values from -1 to 1
- front_gain: bfloat16 [512], P(('dp', 'fsdp')), may hold values from 0.25 to 1.75
- heads_gain: bfloat16 [512], P(('dp', 'fsdp')), may hold values from 0.25 to 1.75
- gated_gain: bfloat16 [512], P(('dp', 'fsdp')), may hold values from 0.25 to 1.75
- gate_gain: bfloat16 [1536], P(('dp', 'fsdp')), may hold values from 0.25 to 1.75
- rear_gain: bfloat16 [512], P(('dp', 'fsdp')), may hold values from 0.25 to 1.75
- final_gain: bfloat16 [512], P(('dp', 'fsdp')), may hold values from 0.25 to 1.75
Outputs:
- encoded: bfloat16 [12288, 512], P(('dp', 'fsdp'))
- features_grad: bfloat16 [12288, 512], P(('dp', 'fsdp'))
- front_up_grad: float32 [512, 2048], P(('dp', 'fsdp'))
- front_down_grad: float32 [2048, 512], P(('dp', 'fsdp'))
- heads_input_grad: float32 [512, 1536], P(('dp', 'fsdp'))
- heads_output_grad: float32 [512, 512], P(('dp', 'fsdp'))
- gated_input_grad: float32 [512, 3072], P(('dp', 'fsdp'))
- gated_output_grad: float32 [1536, 512], P(('dp', 'fsdp'))
- merge_output_grad: float32 [1024, 512], P(('dp', 'fsdp'))
- rear_up_grad: float32 [512, 2048], P(('dp', 'fsdp'))
- rear_down_grad: float32 [2048, 512], P(('dp', 'fsdp'))
- gate_kernel_grad: float32 [31, 1536], P(None, ('dp', 'fsdp'))
- merge_kernel_grad: float32 [31, 1024], P(None, ('dp', 'fsdp'))
- front_gain_grad: float32 [512], P(('dp', 'fsdp'))
- heads_gain_grad: float32 [512], P(('dp', 'fsdp'))
- gated_gain_grad: float32 [512], P(('dp', 'fsdp'))
- gate_gain_grad: float32 [1536], P(('dp', 'fsdp'))
- rear_gain_grad: float32 [512], P(('dp', 'fsdp'))
- final_gain_grad: float32 [512], P(('dp', 'fsdp'))
- statistics: float32 [7], replicated
The draws below stay inside these ranges and needn't reach their ends.
Inputs may be any that keep to these rules, and one draw needn't show every extreme that they name: `lengths`: row r holds the frame counts of the utterances of the r-th block, in order from the block's start; zero counts are empty slots; a row sums to at most 384 and to at least 192; in every draw some row is one utterance of 384 frames followed by zeros.
All inputs are finite; a program needn't handle non-finite values.
Results may differ from the reference program's by a relative error of at most 0.018.
Values may be sent and summed in bfloat16 or wider, within the bound.
No kernel may reach another device: no remote copies, remote signals or barrier semaphores. Data moves between devices by JAX's collectives and lax.ppermute only.
A program may use at most 320 MiB of HBM per device.

```python
import jax
import jax.numpy as jnp
from jax import lax

D = 512
HEADS = 8
FF = 2048
CG = 3072
KW = 31
UTT_DEV = 4
TOK_DEV = 384
TOKENS = 12288
DEVICES = 32


def draw_features(key, part):
    position = jnp.arange(TOKENS, dtype=jnp.float32) / TOKENS
    row_scale = 0.5 + position
    base = jnp.clip(jax.random.normal(key, (TOKENS, D), jnp.float32), -4.0, 4.0)
    return (base * row_scale[:, None]).astype(jnp.bfloat16)


def draw_lengths(key, part):
    key_one, key_two, key_three = jax.random.split(key, 3)
    spoken = jax.random.randint(key_one, (DEVICES, UTT_DEV), TOK_DEV // 8, TOK_DEV // UTT_DEV + 1)
    reading = jax.random.randint(key_two, (DEVICES,), 0, 8) == 0
    chosen = jax.random.randint(key_three, (), 0, DEVICES)
    reading = jnp.logical_or(reading, jnp.arange(DEVICES) == chosen)
    single = jnp.where(jnp.arange(UTT_DEV) == 0, TOK_DEV, 0)
    return jnp.where(reading[:, None], single[None, :], spoken).astype(jnp.int32)


def steps_of(own_key, extent, pieces, low, high):
    gain = 1.0
    for dim, blocks in pieces:
        heights = jax.random.uniform(jax.random.fold_in(jax.random.fold_in(own_key, 6), dim), (blocks,), jnp.float32, low / len(pieces), high / len(pieces))
        gain = gain * jnp.repeat(jnp.exp(heights), extent[dim] // blocks).reshape((-1,) + (1,) * (len(extent) - 1 - dim))
    return gain


def bell_draw(key, shape, scale, reach, cuts=(), kind=jnp.bfloat16):
    entries = scale * jax.random.normal(key, shape, jnp.float32)
    if cuts:
        entries = entries * steps_of(key, shape, cuts, -0.22, 0.18)
    return jnp.clip(entries, -reach, reach).astype(kind)


def setup_inputs(seed: int = 0) -> dict:
    splits = jax.random.split(jax.random.key(seed), 21)
    features = draw_features(jax.random.fold_in(splits[20], 71), 0)
    cotangent = bell_draw(splits[1], (TOKENS, D), 1.0, 6.0, ((0, 32),))
    lengths = draw_lengths(jax.random.fold_in(splits[20], 71), 0)
    front_up = bell_draw(splits[3], (D, FF), D ** -0.5, 0.25, ((0, 32),))
    front_down = bell_draw(splits[4], (FF, D), FF ** -0.5, 0.125, ((0, 32),))
    heads_input = bell_draw(splits[5], (D, 3 * D), D ** -0.5, 0.25, ((0, 32),))
    heads_output = bell_draw(splits[6], (D, D), 4 ** -0.5, 3.0, ((0, 32),))
    gated_input = bell_draw(splits[7], (D, CG), D ** -0.5, 0.25, ((0, 32),))
    gated_output = bell_draw(splits[8], (CG // 2, D), (CG // 2) ** -0.5, 0.15625, ((0, 32),))
    merge_output = bell_draw(splits[9], (2 * D, D), (2 * D) ** -0.5, 0.1875, ((0, 32),))
    rear_up = bell_draw(splits[10], (D, FF), D ** -0.5, 0.25, ((0, 32),))
    rear_down = bell_draw(splits[11], (FF, D), FF ** -0.5, 0.125, ((0, 32),))
    gate_kernel = bell_draw(splits[12], (KW, CG // 2), KW ** -0.5, 1.0, ((1, 32),))
    merge_kernel = bell_draw(splits[13], (KW, 2 * D), KW ** -0.5, 1.0, ((1, 32),))
    front_gain = jnp.clip(1.0 + 0.15 * jax.random.normal(splits[14], (D,), jnp.float32), 0.25, 1.75).astype(jnp.bfloat16)
    heads_gain = jnp.clip(1.0 + 0.15 * jax.random.normal(splits[15], (D,), jnp.float32), 0.25, 1.75).astype(jnp.bfloat16)
    gated_gain = jnp.clip(1.0 + 0.15 * jax.random.normal(splits[16], (D,), jnp.float32), 0.25, 1.75).astype(jnp.bfloat16)
    gate_gain = jnp.clip(1.0 + 0.15 * jax.random.normal(splits[17], (CG // 2,), jnp.float32), 0.25, 1.75).astype(jnp.bfloat16)
    rear_gain = jnp.clip(1.0 + 0.15 * jax.random.normal(splits[18], (D,), jnp.float32), 0.25, 1.75).astype(jnp.bfloat16)
    final_gain = jnp.clip(1.0 + 0.15 * jax.random.normal(splits[19], (D,), jnp.float32), 0.25, 1.75).astype(jnp.bfloat16)
    return dict(features=features, cotangent=cotangent, lengths=lengths, front_up=front_up, front_down=front_down, heads_input=heads_input, heads_output=heads_output, gated_input=gated_input, gated_output=gated_output, merge_output=merge_output, rear_up=rear_up, rear_down=rear_down, gate_kernel=gate_kernel, merge_kernel=merge_kernel, front_gain=front_gain, heads_gain=heads_gain, gated_gain=gated_gain, gate_gain=gate_gain, rear_gain=rear_gain, final_gain=final_gain)


EPSILON = 1e-05
HIGHEST_PRECISION = lax.Precision.HIGHEST

@jax.custom_vjp
def low(v):
    return lax.optimization_barrier(v.astype(jnp.bfloat16)).astype(jnp.float32)

@jax.custom_vjp
def low_back(v):
    return v

def low_keep(v):
    return (low(v), None)

def low_pass(kept, grad):
    return (grad,)

def back_keep(v):
    return (v, None)

def back_low(kept, grad):
    return (low(grad),)
low.defvjp(low_keep, low_pass)
low_back.defvjp(back_keep, back_low)

def matmul(left_side, right_side):
    return jnp.dot(left_side, right_side, precision=HIGHEST_PRECISION, preferred_element_type=jnp.float32)

def layer_norm(values, norm_gain):
    centred = values - lax.optimization_barrier(jnp.mean(values, axis=-1, keepdims=True))
    variance = lax.optimization_barrier(jnp.mean(centred * centred, axis=-1, keepdims=True))
    return centred * lax.rsqrt(variance + EPSILON) * norm_gain

def segment_ids(length_row, row_count):
    utterance_ends = jnp.cumsum(length_row).astype(jnp.int32)
    position = jnp.arange(row_count, dtype=jnp.int32)
    return lax.optimization_barrier(jnp.sum((position[None, :] >= utterance_ends[:, None]).astype(jnp.int32), axis=0)).astype(jnp.int32)

def shifted(values, offset):
    if offset > 0:
        return jnp.concatenate([values[offset:], jnp.zeros((offset,) + values.shape[1:], values.dtype)], axis=0)
    if offset < 0:
        return jnp.concatenate([jnp.zeros((-offset,) + values.shape[1:], values.dtype), values[:offset]], axis=0)
    return values

def conv_masks(segments, taps):
    half_width = (taps - 1) // 2
    marked = segments + 1
    return [(shifted(marked, tap_index - half_width) == marked).astype(jnp.float32)[:, None] for tap_index in range(taps)]

def segment_conv(values, kernel, tap_masks):
    half_width = (kernel.shape[0] - 1) // 2
    summed = jnp.zeros_like(values)
    for tap_index in range(kernel.shape[0]):
        summed = summed + kernel[tap_index] * shifted(values, tap_index - half_width) * tap_masks[tap_index]
    return summed

def feed_forward(normed, up_weight, down_weight):
    before = low_back(matmul(low(normed), up_weight))
    hidden = low(jax.nn.silu(before))
    return 0.5 * low_back(matmul(hidden, down_weight))

def attention(normed, packed_weight, output_weight, segments):
    row_count, feature_width = normed.shape
    head_size = feature_width // HEADS
    packed = low(low_back(matmul(low(normed), packed_weight))).reshape(row_count, 3, HEADS, head_size)
    queries = packed[:, 0]
    keys_part = packed[:, 1]
    values = packed[:, 2]
    scores = low_back(jnp.einsum('qhd,khd->hqk', queries, keys_part, precision=HIGHEST_PRECISION) * head_size ** (-0.5))
    allowed = (segments[:, None] == segments[None, :])[None]
    scores = jnp.where(allowed, scores, -1000000000.0)
    weights = low(jax.nn.softmax(scores, axis=-1))
    mixed_heads = low(low_back(jnp.einsum('hqk,khd->qhd', weights, values, precision=HIGHEST_PRECISION)))
    return low_back(matmul(mixed_heads.reshape(row_count, feature_width), output_weight))

def gated_branch(normed, input_weight, output_weight, gate_gain, gate_kernel, tap_masks):
    before = low_back(matmul(low(normed), input_weight))
    activated = jax.nn.gelu(before)
    half_width = activated.shape[1] // 2
    gate_part = segment_conv(layer_norm(activated[:, half_width:], gate_gain), gate_kernel, tap_masks)
    product = low(activated[:, :half_width] * gate_part)
    return low_back(matmul(product, output_weight))

def forward(inputs, segments, valid_rows, tap_masks, params):
    front_up, front_down, heads_input, heads_output, gated_input, gated_output, merge_output, rear_up, rear_down, gate_kernel, merge_kernel, front_gain, heads_gain, gated_gain, gate_gain, rear_gain, final_gain = params
    front_part = feed_forward(layer_norm(inputs, front_gain), front_up, front_down)
    after_front = inputs + front_part
    attended = attention(layer_norm(after_front, heads_gain), heads_input, heads_output, segments)
    gated_out = gated_branch(layer_norm(after_front, gated_gain), gated_input, gated_output, gate_gain, gate_kernel, tap_masks)
    joined = jnp.concatenate([attended, gated_out], axis=1)
    merged = joined + segment_conv(joined, merge_kernel, tap_masks)
    merge_part = low_back(matmul(low(merged), merge_output))
    after_merge = after_front + merge_part
    rear_part = feed_forward(layer_norm(after_merge, rear_gain), rear_up, rear_down)
    after_rear = after_merge + rear_part
    encoded = layer_norm(after_rear, final_gain) * valid_rows
    tracked = [inputs, after_front, after_merge, after_rear, front_part, merge_part, rear_part]
    squares = jnp.stack([jnp.sum(element * element * valid_rows) for element in tracked])
    return (encoded, squares)

def reference(features, cotangent, lengths, front_up, front_down, heads_input, heads_output, gated_input, gated_output, merge_output, rear_up, rear_down, gate_kernel, merge_kernel, front_gain, heads_gain, gated_gain, gate_gain, rear_gain, final_gain):
    params = tuple((element.astype(jnp.float32) for element in (front_up, front_down, heads_input, heads_output, gated_input, gated_output, merge_output, rear_up, rear_down, gate_kernel, merge_kernel, front_gain, heads_gain, gated_gain, gate_gain, rear_gain, final_gain)))
    feature_width = features.shape[1]
    blocks = features.astype(jnp.float32).reshape(DEVICES, TOK_DEV, feature_width)
    cotangent_blocks = cotangent.astype(jnp.float32).reshape(DEVICES, TOK_DEV, feature_width)

    def one_block(carried, element):
        block_rows, block_cotangent, length_row = element
        segments = segment_ids(length_row, TOK_DEV)
        valid_rows = (segments < UTT_DEV).astype(jnp.float32)[:, None]
        tap_masks = conv_masks(segments, KW)

        def local_layer(inputs, *weight_list):
            return forward(inputs, segments, valid_rows, tap_masks, weight_list)
        encoded, pullback, squares = jax.vjp(local_layer, block_rows, *params, has_aux=True)
        gradients = pullback(block_cotangent)
        grad_sums, total_squares, frame_count = carried
        grad_sums = tuple((left_side + right_side for left_side, right_side in zip(grad_sums, gradients[1:])))
        carried = (grad_sums, total_squares + squares, frame_count + jnp.sum(valid_rows))
        return (carried, (encoded.astype(jnp.bfloat16), gradients[0].astype(jnp.bfloat16)))
    initial = (tuple((jnp.zeros_like(element) for element in params)), jnp.zeros((7,), jnp.float32), jnp.zeros((), jnp.float32))
    carried, outputs = lax.scan(one_block, initial, (blocks, cotangent_blocks, lengths))
    grad_sums, total_squares, frame_count = carried
    encoded = outputs[0].reshape(TOKENS, feature_width)
    features_grad = outputs[1].reshape(TOKENS, feature_width)
    statistics = jnp.sqrt(total_squares / (frame_count * feature_width))
    return (encoded, features_grad, grad_sums[0], grad_sums[1], grad_sums[2], grad_sums[3], grad_sums[4], grad_sums[5], grad_sums[6], grad_sums[7], grad_sums[8], grad_sums[9], grad_sums[10], grad_sums[11], grad_sums[12], grad_sums[13], grad_sums[14], grad_sums[15], grad_sums[16], statistics)
```

```python
import jax
import jax.numpy as jnp
from jax import lax
from jax.sharding import PartitionSpec as P

HEADS = 8


EPSILON = 1e-05
NEGATIVE = -1000000000.0
AXES = ("dp", "fsdp")
LANE = 512


def matmul(left_side, right_side):
    return jnp.dot(left_side, right_side, preferred_element_type=jnp.float32)


def matmul_left_t(left_side, right_side):
    return lax.dot_general(
        left_side, right_side, (((0,), (0,)), ((), ())), preferred_element_type=jnp.float32
    )


def matmul_right_t(left_side, right_side):
    return lax.dot_general(
        left_side, right_side, (((1,), (1,)), ((), ())), preferred_element_type=jnp.float32
    )


def to_low(values):
    return values.astype(jnp.bfloat16)


def pack_rows(shard):
    rows, columns = shard.shape
    if columns == LANE:
        return shard
    pieces = shard.reshape(rows, columns // LANE, LANE).transpose(1, 0, 2)
    return pieces.reshape(rows * columns // LANE, LANE)


def pack_small(parts):
    flat = jnp.concatenate([part.reshape(-1) for part in parts])
    rows = -(-flat.shape[0] // LANE)
    rows = -(-rows // 16) * 16
    return jnp.pad(flat, (0, rows * LANE - flat.shape[0])).reshape(rows, LANE)


def gather_weights(matrices, smaller, count):
    packed = [pack_rows(element) for element in matrices] + [pack_small(smaller)]
    gathered = lax.all_gather(jnp.concatenate(packed), AXES, axis=0)
    weights = []
    start = 0
    for element, piece in zip(matrices, packed):
        rows, columns = element.shape
        window = gathered[:, start : start + piece.shape[0]]
        start += piece.shape[0]
        window = window.reshape(count, columns // LANE, rows, LANE).transpose(0, 2, 1, 3)
        weights.append(window.reshape(count * rows, columns))
    flat = gathered[:, start:].reshape(count, -1)
    start = 0
    for element in smaller:
        size = element.size
        window = flat[:, start : start + size].astype(jnp.float32)
        start += size
        if element.ndim == 2:
            taps, columns = element.shape
            window = window.reshape(count, taps, columns).transpose(1, 0, 2)
            weights.append(window.reshape(taps, count * columns))
        else:
            weights.append(window.reshape(-1))
    return weights


def scatter_gradients(matrices, smaller, count):
    pieces = []
    for element in matrices:
        rows, columns = element.shape
        low = element.astype(jnp.bfloat16).reshape(count, rows // count, columns // LANE, LANE)
        pieces.append(low.transpose(0, 2, 1, 3).reshape(count, -1, LANE))
    flat = []
    for element in smaller:
        if element.ndim == 2:
            taps, columns = element.shape
            flat.append(
                element.reshape(taps, count, columns // count).transpose(1, 0, 2).reshape(count, -1)
            )
        else:
            flat.append(element.reshape(count, -1))
    flat = jnp.concatenate(flat, axis=1).astype(jnp.bfloat16)
    rows = -(-flat.shape[1] // LANE)
    rows = -(-rows // 16) * 16
    flat = jnp.pad(flat, ((0, 0), (0, rows * LANE - flat.shape[1])))
    pieces.append(flat.reshape(count, rows, LANE))
    summed = lax.psum_scatter(
        jnp.concatenate(pieces, axis=1), AXES, scatter_dimension=0, tiled=False
    )
    shards = []
    start = 0
    for element in matrices:
        rows, columns = element.shape
        rows = rows // count
        size = rows * columns // LANE
        window = summed[start : start + size].astype(jnp.float32)
        start += size
        window = window.reshape(columns // LANE, rows, LANE).transpose(1, 0, 2)
        shards.append(window.reshape(rows, columns))
    flat = summed[start:].reshape(-1).astype(jnp.float32)
    start = 0
    for element in smaller:
        size = element.size // count
        window = flat[start : start + size]
        start += size
        if element.ndim == 2:
            window = window.reshape(element.shape[0], -1)
        shards.append(window)
    return tuple(shards)


def norm_forward(values, norm_gain):
    centred = values - jnp.mean(values, axis=-1, keepdims=True)
    variance = jnp.mean(centred * centred, axis=-1, keepdims=True)
    inverse = lax.rsqrt(variance + EPSILON)
    normal = centred * inverse
    return (normal * norm_gain, (normal, inverse))


def norm_backward(upstream, norm_gain, saved_state):
    normal, inverse = saved_state
    gain_grad = jnp.sum(upstream * normal, axis=0)
    scaled = upstream * norm_gain
    mean_scaled = jnp.mean(scaled, axis=-1, keepdims=True)
    mean_cross = jnp.mean(scaled * normal, axis=-1, keepdims=True)
    return (inverse * (scaled - mean_scaled - normal * mean_cross), gain_grad)


def segment_ids(length_row, row_count):
    utterance_ends = jnp.cumsum(length_row)
    position = jnp.arange(row_count, dtype=jnp.int32)
    return jnp.sum((position[None, :] >= utterance_ends[:, None]).astype(jnp.int32), axis=0)


def shifted(values, offset):
    if offset > 0:
        return jnp.concatenate(
            [values[offset:], jnp.zeros((offset,) + values.shape[1:], values.dtype)], axis=0
        )
    if offset < 0:
        return jnp.concatenate(
            [jnp.zeros((-offset,) + values.shape[1:], values.dtype), values[:offset]], axis=0
        )
    return values


def conv_masks(segments, taps):
    half_width = (taps - 1) // 2
    marked = segments + 1
    return [
        (shifted(marked, tap_index - half_width) == marked).astype(jnp.float32)[:, None]
        for tap_index in range(taps)
    ]


def segment_conv(values, kernel, tap_masks):
    half_width = (kernel.shape[0] - 1) // 2
    summed = jnp.zeros_like(values)
    for tap_index in range(kernel.shape[0]):
        summed = (
            summed
            + kernel[tap_index] * shifted(values, tap_index - half_width) * tap_masks[tap_index]
        )
    return summed


def conv_backward(upstream, values, kernel, tap_masks):
    half_width = (kernel.shape[0] - 1) // 2
    summed = jnp.zeros_like(values)
    kernel_rows = []
    for tap_index in range(kernel.shape[0]):
        offset = tap_index - half_width
        masked = upstream * tap_masks[tap_index]
        summed = summed + kernel[tap_index] * shifted(masked, -offset)
        kernel_rows.append(jnp.sum(masked * shifted(values, offset), axis=0))
    return (summed, jnp.stack(kernel_rows))


def ffn_forward(stream, up_weight, down_weight, norm_gain):
    normed, norm_state = norm_forward(stream, norm_gain)
    normed_low = to_low(normed)
    before = matmul(normed_low, up_weight)
    hidden = to_low(jax.nn.silu(before))
    return (0.5 * matmul(hidden, down_weight), (norm_state, normed_low, before, hidden))


def ffn_backward(stream_grad, up_weight, down_weight, norm_gain, saved_state):
    norm_state, normed_low, before, hidden = saved_state
    part_grad = to_low(0.5 * stream_grad)
    down_grad = matmul_left_t(hidden, part_grad)
    hidden_grad = matmul_right_t(part_grad, down_weight)
    before_grad = to_low(jax.vjp(jax.nn.silu, before)[1](hidden_grad)[0])
    up_grad = matmul_left_t(normed_low, before_grad)
    normed_grad = matmul_right_t(before_grad, up_weight)
    input_grad, gain_grad = norm_backward(normed_grad, norm_gain, norm_state)
    return (stream_grad + input_grad, up_grad, down_grad, gain_grad)


def head_scores(packed, allowed, score_scale):
    raw_scores = (
        jnp.einsum("qhd,khd->hqk", packed[:, 0], packed[:, 1], preferred_element_type=jnp.float32)
        * score_scale
    )
    return jnp.where(allowed, raw_scores, NEGATIVE)


def attention_forward(normed_low, packed_weight, output_weight, allowed):
    row_count, feature_width = normed_low.shape
    head_size = feature_width // HEADS
    score_scale = head_size ** (-0.5)
    packed = to_low(matmul(normed_low, packed_weight)).reshape(row_count, 3, HEADS, head_size)
    scores = head_scores(packed, allowed, score_scale)
    largest = jnp.max(scores, axis=-1, keepdims=True)
    exponent = jnp.exp(scores - largest)
    summed = jnp.sum(exponent, axis=-1, keepdims=True)
    probs_low = to_low(exponent / summed)
    log_total = largest + jnp.log(summed)
    mixed_low = to_low(
        jnp.einsum("hqk,khd->qhd", probs_low, packed[:, 2], preferred_element_type=jnp.float32)
    )
    mixed_low = mixed_low.reshape(row_count, feature_width)
    return (matmul(mixed_low, output_weight), (packed, log_total, mixed_low))


def attention_backward(
    attended_grad, normed_low, packed_weight, output_weight, allowed, saved_state
):
    packed, log_total, mixed_low = saved_state
    row_count, feature_width = normed_low.shape
    head_size = feature_width // HEADS
    score_scale = head_size ** (-0.5)
    attended_low = to_low(attended_grad)
    output_grad = matmul_left_t(mixed_low, attended_low)
    mixed_grad = to_low(matmul_right_t(attended_low, output_weight)).reshape(
        row_count, HEADS, head_size
    )
    probs = jnp.exp(head_scores(packed, allowed, score_scale) - log_total)
    probs_low = to_low(probs)
    probs_grad = jnp.einsum(
        "qhd,khd->hqk", mixed_grad, packed[:, 2], preferred_element_type=jnp.float32
    )
    value_grad = jnp.einsum(
        "hqk,qhd->khd", probs_low, mixed_grad, preferred_element_type=jnp.float32
    )
    inner_sum = jnp.sum(probs_grad * probs, axis=-1, keepdims=True)
    score_grad = to_low(probs * (probs_grad - inner_sum))
    query_grad = (
        jnp.einsum("hqk,khd->qhd", score_grad, packed[:, 1], preferred_element_type=jnp.float32)
        * score_scale
    )
    key_grad = (
        jnp.einsum("hqk,qhd->khd", score_grad, packed[:, 0], preferred_element_type=jnp.float32)
        * score_scale
    )
    packed_grad = to_low(
        jnp.stack([query_grad, key_grad, value_grad], axis=1).reshape(row_count, 3 * feature_width)
    )
    packed_weight_grad = matmul_left_t(normed_low, packed_grad)
    normed_grad = matmul_right_t(packed_grad, packed_weight)
    return (normed_grad, packed_weight_grad, output_grad)


def gated_forward(normed_low, input_weight, output_weight, gate_gain, gate_kernel, tap_masks):
    before = matmul(normed_low, input_weight)
    activated = jax.nn.gelu(before)
    half_width = activated.shape[1] // 2
    gate_normed, gate_state = norm_forward(activated[:, half_width:], gate_gain)
    gate_part = segment_conv(gate_normed, gate_kernel, tap_masks)
    product_low = to_low(activated[:, :half_width] * gate_part)
    return (
        matmul(product_low, output_weight),
        (before, gate_normed, gate_state, gate_part, product_low),
    )


def gated_backward(
    gated_grad,
    normed_low,
    input_weight,
    output_weight,
    gate_gain,
    gate_kernel,
    tap_masks,
    saved_state,
):
    before, gate_normed, gate_state, gate_part, product_low = saved_state
    gated_low = to_low(gated_grad)
    output_grad = matmul_left_t(product_low, gated_low)
    product_grad = matmul_right_t(gated_low, output_weight)
    activated, gelu_pull = jax.vjp(jax.nn.gelu, before)
    half_width = activated.shape[1] // 2
    linear_grad = product_grad * gate_part
    part_grad = product_grad * activated[:, :half_width]
    normed_gate_grad, kernel_grad = conv_backward(part_grad, gate_normed, gate_kernel, tap_masks)
    gate_grad, gain_grad = norm_backward(normed_gate_grad, gate_gain, gate_state)
    before_grad = to_low(gelu_pull(jnp.concatenate([linear_grad, gate_grad], axis=1))[0])
    input_grad = matmul_left_t(normed_low, before_grad)
    normed_grad = matmul_right_t(before_grad, input_weight)
    return (normed_grad, input_grad, output_grad, gain_grad, kernel_grad)


def per_device(
    features,
    cotangent,
    lengths,
    front_up,
    front_down,
    heads_input,
    heads_output,
    gated_input,
    gated_output,
    merge_output,
    rear_up,
    rear_down,
    gate_kernel,
    merge_kernel,
    front_gain,
    heads_gain,
    gated_gain,
    gate_gain,
    rear_gain,
    final_gain,
):
    count = lax.axis_size(AXES)
    matrices = (front_up, front_down, heads_input, heads_output, gated_input, gated_output, merge_output, rear_up, rear_down)
    smaller = (gate_kernel, merge_kernel, front_gain, heads_gain, gated_gain, gate_gain, rear_gain, final_gain)
    (
        w_front_up,
        w_front_down,
        w_heads_input,
        w_heads_output,
        w_gated_input,
        w_gated_output,
        w_merge_output,
        w_rear_up,
        w_rear_down,
        w_gate_kernel,
        w_merge_kernel,
        w_front_gain,
        w_heads_gain,
        w_gated_gain,
        w_gate_gain,
        w_rear_gain,
        w_final_gain,
    ) = gather_weights(matrices, smaller, count)
    row_count, feature_width = features.shape
    segments = segment_ids(lengths[0], row_count)
    valid_rows = (segments < lengths.shape[1]).astype(jnp.float32)[:, None]
    tap_masks = conv_masks(segments, w_gate_kernel.shape[0])
    allowed = (segments[:, None] == segments[None, :])[None]
    inputs = features.astype(jnp.float32)
    front_part, front_state = ffn_forward(
        inputs, w_front_up, w_front_down, w_front_gain
    )
    after_front = inputs + front_part
    heads_normed, heads_norm_state = norm_forward(after_front, w_heads_gain)
    heads_low = to_low(heads_normed)
    attended, heads_state = attention_forward(
        heads_low, w_heads_input, w_heads_output, allowed
    )
    gated_normed, gated_norm_state = norm_forward(after_front, w_gated_gain)
    gated_low = to_low(gated_normed)
    gated_out, gated_state = gated_forward(
        gated_low,
        w_gated_input,
        w_gated_output,
        w_gate_gain,
        w_gate_kernel,
        tap_masks,
    )
    joined = jnp.concatenate([attended, gated_out], axis=1)
    merged_low = to_low(joined + segment_conv(joined, w_merge_kernel, tap_masks))
    merge_part = matmul(merged_low, w_merge_output)
    after_merge = after_front + merge_part
    rear_part, rear_state = ffn_forward(
        after_merge, w_rear_up, w_rear_down, w_rear_gain
    )
    after_rear = after_merge + rear_part
    final_normed, final_state = norm_forward(after_rear, w_final_gain)
    encoded = (final_normed * valid_rows).astype(jnp.bfloat16)
    tracked = [inputs, after_front, after_merge, after_rear, front_part, merge_part, rear_part]
    squares = jnp.stack([jnp.sum(element * element * valid_rows) for element in tracked])
    totals = lax.psum((squares, jnp.sum(valid_rows)), AXES)
    statistics = jnp.sqrt(totals[0] / (totals[1] * feature_width))
    upstream = cotangent.astype(jnp.float32) * valid_rows
    rear_stream_grad, final_gain_grad = norm_backward(
        upstream, w_final_gain, final_state
    )
    merge_stream_grad, rear_up_grad, rear_down_grad, rear_gain_grad = ffn_backward(
        rear_stream_grad,
        w_rear_up,
        w_rear_down,
        w_rear_gain,
        rear_state,
    )
    merge_low_grad = to_low(merge_stream_grad)
    merge_output_grad = matmul_left_t(merged_low, merge_low_grad)
    merged_grad = matmul_right_t(merge_low_grad, w_merge_output)
    conv_grad, merge_kernel_grad = conv_backward(
        merged_grad, joined, w_merge_kernel, tap_masks
    )
    joined_grad = merged_grad + conv_grad
    heads_normed_grad, heads_input_grad, heads_output_grad = attention_backward(
        joined_grad[:, :feature_width],
        heads_low,
        w_heads_input,
        w_heads_output,
        allowed,
        heads_state,
    )
    gated_normed_grad, gated_input_grad, gated_output_grad, gate_gain_grad, gate_kernel_grad = (
        gated_backward(
            joined_grad[:, feature_width:],
            gated_low,
            w_gated_input,
            w_gated_output,
            w_gate_gain,
            w_gate_kernel,
            tap_masks,
            gated_state,
        )
    )
    heads_stream, heads_gain_grad = norm_backward(
        heads_normed_grad, w_heads_gain, heads_norm_state
    )
    gated_stream, gated_gain_grad = norm_backward(
        gated_normed_grad, w_gated_gain, gated_norm_state
    )
    front_stream_grad = merge_stream_grad + heads_stream + gated_stream
    inputs_grad, front_up_grad, front_down_grad, front_gain_grad = ffn_backward(
        front_stream_grad,
        w_front_up,
        w_front_down,
        w_front_gain,
        front_state,
    )
    shards = scatter_gradients(
        (front_up_grad, front_down_grad, heads_input_grad, heads_output_grad, gated_input_grad, gated_output_grad, merge_output_grad, rear_up_grad, rear_down_grad),
        (gate_kernel_grad, merge_kernel_grad, front_gain_grad, heads_gain_grad, gated_gain_grad, gate_gain_grad, rear_gain_grad, final_gain_grad),
        count,
    )
    return (encoded, inputs_grad.astype(jnp.bfloat16)) + tuple(shards) + (statistics,)


def solution(mesh):
    rows = P(AXES, None)
    columns = P(None, AXES)
    vector = P(AXES)
    weights = (rows,) * 9 + (columns,) * 2 + (vector,) * 6
    return jax.shard_map(
        per_device,
        mesh=mesh,
        in_specs=(rows, rows, rows) + weights,
        out_specs=(rows, rows) + weights + (P(),),
        check_vma=False,
    )
```

```python
import functools

import jax
import jax.numpy as jnp
from jax import lax
from jax.experimental import pallas as pl
from jax.experimental.pallas import tpu as pltpu
from jax.sharding import Mesh, PartitionSpec as P

HEADS = 8
EPSILON = 1e-05
NEGATIVE = -1000000000.0
TILE = 8
GAP = 16
CHAN = 128
WIDTH = 512
BLOCKS = 32
F32 = jnp.float32
LOW = jnp.bfloat16


def dot(left, right):
    return jnp.dot(left, right, preferred_element_type=F32)


def dot_tn(left, right):
    return lax.dot_general(left, right, (((0,), (0,)), ((), ())), preferred_element_type=F32)


def dot_nt(left, right):
    return lax.dot_general(left, right, (((1,), (1,)), ((), ())), preferred_element_type=F32)


def normalize(values):
    centred = values - jnp.mean(values, axis=-1, keepdims=True)
    variance = jnp.mean(centred * centred, axis=-1, keepdims=True)
    inverse = lax.rsqrt(variance + EPSILON)
    return centred * inverse, inverse


def normalize_back(upstream, gain, normal, inverse):
    scaled = upstream * gain
    mean_scaled = jnp.mean(scaled, axis=-1, keepdims=True)
    mean_cross = jnp.mean(scaled * normal, axis=-1, keepdims=True)
    return inverse * (scaled - mean_scaled - normal * mean_cross)


def row_sum(values):
    return jnp.sum(values, axis=0, keepdims=True)


GELU_A = 0.7978845608028654
GELU_B = 0.044715


def gelu(v):
    return 0.5 * v * (1.0 + jnp.tanh(GELU_A * (v + GELU_B * v * v * v)))


def gelu_pair(v):
    square = v * v
    bend = jnp.tanh(GELU_A * (v + GELU_B * square * v))
    value = 0.5 * v * (1.0 + bend)
    slope = 0.5 * (1.0 + bend) + 0.5 * v * (1.0 - bend * bend) * (
        GELU_A * (1.0 + 3.0 * GELU_B * square)
    )
    return value, slope


def silu(v):
    return v * jax.nn.sigmoid(v)


def store_halves(value, send, keep, mine, rows, start):
    parts = value.astype(LOW).reshape(2, 2, 8, rows, WIDTH)

    @pl.when(mine == 0)
    def _():
        keep[:, :, pl.ds(start, rows), :] = parts[:, 0]
        send[:, :, pl.ds(start, rows), :] = parts[:, 1]

    @pl.when(mine == 1)
    def _():
        keep[:, :, pl.ds(start, rows), :] = parts[:, 1]
        send[:, :, pl.ds(start, rows), :] = parts[:, 0]


def join_rows(first, second, mine):
    low = jnp.where(mine == 0, first, second)
    high = jnp.where(mine == 0, second, first)
    return jnp.stack([low, high], axis=1).reshape(-1, WIDTH)


def pick_rows(first, second, flag):
    return jnp.where(flag, first, second).reshape(-1, WIDTH)


def visits(info, segments, body):
    for s in range(segments):
        begin, end = info[1 + s], info[1 + segments + s]

        def visit(i, _, s=s, begin=begin, end=end):
            row = i * TILE + lax.broadcasted_iota(jnp.int32, (TILE, CHAN), 0)
            inside = jnp.logical_and(row >= begin, row < end)
            body(s, pl.multiple_of(i * TILE, TILE), inside)
            return 0

        lax.fori_loop(begin // TILE, (end + TILE - 1) // TILE, visit, 0)


def spread(source, padded, info, segments, blocks):
    padded[...] = jnp.zeros_like(padded)

    def body(s, base, inside):
        for c in range(blocks):
            value = source[pl.ds(base, TILE), c * CHAN : (c + 1) * CHAN]
            padded[c, pl.ds(base + GAP * (s + 1), TILE), :] = jnp.where(inside, value, 0.0)

    visits(info, segments, body)


def unspread(padded, target, info, segments, blocks):
    def body(s, base, inside):
        for c in range(blocks):
            lanes = slice(c * CHAN, (c + 1) * CHAN)
            value = padded[c, pl.ds(base + GAP * (s + 1), TILE), :]
            target[pl.ds(base, TILE), lanes] = jnp.where(
                inside, value, target[pl.ds(base, TILE), lanes]
            )

    visits(info, segments, body)


def conv_rows(padded, kernel, out, blocks, row_block, taps, flip):
    half = (taps - 1) // 2
    steps = (padded.shape[1] - 2 * GAP) // row_block

    def body(step, _):
        c = step // steps
        base = (step % steps) * row_block + GAP
        lanes = pl.ds(pl.multiple_of(c * CHAN, CHAN), CHAN)
        total = jnp.zeros((row_block, CHAN), F32)
        for j in range(taps):
            shift = half - j if flip else j - half
            total += kernel[pl.ds(j, 1), lanes] * padded[c, pl.ds(base + shift, row_block), :]
        out[c, pl.ds(pl.multiple_of(base, TILE), row_block), :] = total
        return 0

    lax.fori_loop(0, blocks * steps, body, 0)


def conv_taps(padded_grad, padded, out, blocks, row_block, taps):
    half = (taps - 1) // 2
    steps = (padded.shape[1] - 2 * GAP) // row_block
    tiles = row_block // TILE

    def block(c, _):
        lanes = pl.ds(pl.multiple_of(c * CHAN, CHAN), CHAN)

        def body(step, sums):
            base = pl.multiple_of(step * row_block + GAP, TILE)
            grad = padded_grad[c, pl.ds(base, row_block), :]
            new = []
            for j in range(taps):
                term = grad * padded[c, pl.ds(base + j - half, row_block), :]
                new.append(sums[j] + jnp.sum(term.reshape(tiles, TILE, CHAN), axis=0))
            return tuple(new)

        zero = jnp.zeros((TILE, CHAN), F32)
        sums = lax.fori_loop(0, steps, body, (zero,) * taps)
        for j in range(taps):
            out[pl.ds(j, 1), lanes] = row_sum(sums[j])
        return 0

    lax.fori_loop(0, blocks, block, 0)


def front_forward_kernel(
    info, x_ref, gain, valid, up, up_two, down, down_two, out, before_out, stat, low, total
):
    h = pl.program_id(0)
    mine = info[0]
    up_value = join_rows(up[...], up_two[...], mine)
    down_value = pick_rows(down[...], down_two[...], h % 2 == mine)

    @pl.when(h == 0)
    def _():
        normal, _ = normalize(x_ref[...].astype(F32))
        low[...] = (normal * gain[...]).astype(LOW)
        total[...] = jnp.zeros_like(total)

    before = dot(low[...], up_value)
    before_out[...] = before
    total[...] += dot(silu(before).astype(LOW), down_value)

    @pl.when(h == pl.num_programs(0) - 1)
    def _():
        x = x_ref[...].astype(F32)
        part = 0.5 * total[...]
        after = x + part
        out[...] = after
        v = valid[...]
        stat[0:1, :] = row_sum(x * x * v)
        stat[1:2, :] = row_sum(after * after * v)
        stat[2:3, :] = row_sum(part * part * v)
        stat[3:, :] = jnp.zeros((5, WIDTH), F32)


def head_masks(segs_col, segs_row):
    allowed = segs_col == segs_row
    lane = lax.broadcasted_iota(jnp.int32, (1, CHAN), 1)
    return allowed, (lane < CHAN // 2, lane >= CHAN // 2)


def head_probs(query, key, allowed, scale):
    scores = jnp.where(allowed, dot_nt(query, key) * scale, NEGATIVE)
    exponent = jnp.exp(scores - jnp.max(scores, axis=-1, keepdims=True))
    return exponent / jnp.sum(exponent, axis=-1, keepdims=True)


def heads_forward_kernel(
    info, x_ref, gain, segs_col, segs_row, w_in, w_in_two, w_out, w_out_two,
    attended, packed, mixed,
):
    mine = info[0]
    scale = (WIDTH // HEADS) ** -0.5
    normal, _ = normalize(x_ref[...])
    low = (normal * gain[...]).astype(LOW)
    for q in range(3):
        rows = slice(16 * q, 16 * (q + 1))
        weight = join_rows(w_in[:, :, rows, :], w_in_two[:, :, rows, :], mine)
        packed[:, WIDTH * q : WIDTH * (q + 1)] = dot(low, weight).astype(LOW)
    allowed, halves = head_masks(segs_col[...], segs_row[...])

    def pair(p, _):
        lanes = [
            pl.ds(pl.multiple_of(WIDTH * q + CHAN * p, CHAN), CHAN) for q in range(3)
        ]
        query, key, value = (packed[:, lane] for lane in lanes)
        parts = []
        for half in halves:
            probs = head_probs(jnp.where(half, query, 0), key, allowed, scale)
            parts.append(dot(probs.astype(LOW), value))
        mixed[:, lanes[0]] = jnp.where(halves[0], parts[0], parts[1]).astype(LOW)
        return 0

    lax.fori_loop(0, HEADS // 2, pair, 0)
    attended[...] = dot(mixed[...], join_rows(w_out[...], w_out_two[...], mine))


def heads_backward_kernel(
    info, grad, x_ref, gain, segs_col, segs_row, packed, mixed, w_in, w_in_two, w_out, w_out_two,
    stream, gain_grad, in_send, in_keep, out_send, out_keep, mixed_grad, packed_grad, low,
):
    scale = (WIDTH // HEADS) ** -0.5
    mine = info[0]
    attended_low = grad[...].astype(LOW)
    store_halves(dot_tn(mixed[...], attended_low), out_send, out_keep, mine, 16, 0)
    mixed_grad[...] = dot_nt(attended_low, join_rows(w_out[...], w_out_two[...], mine)).astype(LOW)
    normal, inverse = normalize(x_ref[...])
    low[...] = (normal * gain[...]).astype(LOW)
    allowed, halves = head_masks(segs_col[...], segs_row[...])

    def pair(p, _):
        lanes = [
            pl.ds(pl.multiple_of(WIDTH * q + CHAN * p, CHAN), CHAN) for q in range(3)
        ]
        query, key, value = (packed[:, lane] for lane in lanes)
        upstream = mixed_grad[:, lanes[0]]
        parts = []
        for half in halves:
            probs = head_probs(jnp.where(half, query, 0), key, allowed, scale)
            probs_grad = dot_nt(jnp.where(half, upstream, 0), value)
            value_grad = dot_tn(probs.astype(LOW), upstream)
            inner = jnp.sum(probs_grad * probs, axis=-1, keepdims=True)
            score_grad = (probs * (probs_grad - inner)).astype(LOW)
            query_grad = dot(score_grad, key) * scale
            key_grad = dot_tn(score_grad, query) * scale
            parts.append((query_grad, key_grad, value_grad))
        for q in range(3):
            packed_grad[:, lanes[q]] = jnp.where(halves[0], parts[0][q], parts[1][q]).astype(LOW)
        return 0

    lax.fori_loop(0, HEADS // 2, pair, 0)
    total = jnp.zeros(x_ref.shape, F32)
    for q in range(3):
        rows = slice(16 * q, 16 * (q + 1))
        weight = join_rows(w_in[:, :, rows, :], w_in_two[:, :, rows, :], mine)
        piece = packed_grad[:, WIDTH * q : WIDTH * (q + 1)]
        store_halves(dot_tn(low[...], piece), in_send, in_keep, mine, 16, 16 * q)
        total += dot_nt(piece, weight)
    gain_grad[...] = row_sum(total * normal)
    stream[...] = normalize_back(total, gain[...], normal, inverse)


def gated_forward_kernel(
    info, x_ref, gain, gate_gain, taps_ref, w_in, w_in_two, w_out, w_out_two,
    gated, before_out, normal_out, inverse_out, part_out, product,
    low, act, padded, conv, *, segments, row_block, taps,
):
    j = pl.program_id(0)
    thirds = WIDTH * 3

    @pl.when(j == 0)
    def _():
        normal, _ = normalize(x_ref[...])
        low[...] = (normal * gain[...]).astype(LOW)

    before = dot(low[...], join_rows(w_in[...], w_in_two[...], info[0]))
    before_out[...] = before
    value = gelu(before)

    @pl.when(j < 3)
    def _():
        act[:, pl.ds(pl.multiple_of(j * WIDTH, WIDTH), WIDTH)] = value

    @pl.when(j == 2)
    def _():
        normal, inverse = normalize(act[...])
        normal_out[...] = normal
        inverse_out[...] = inverse
        act[...] = normal * gate_gain[...]
        blocks = thirds // CHAN
        spread(act, padded, info, segments, blocks)
        conv_rows(padded, taps_ref, conv, blocks, row_block, taps, False)
        unspread(conv, part_out, info, segments, blocks)

    @pl.when(j >= 3)
    def _():
        lanes = pl.ds(pl.multiple_of((j - 3) * WIDTH, WIDTH), WIDTH)
        product[:, lanes] = (value * part_out[:, lanes]).astype(LOW)

    @pl.when(j == 5)
    def _():
        gated[...] = dot(product[...], join_rows(w_out[...], w_out_two[...], info[0]))


def gated_backward_kernel(
    info, grad, x_ref, gain, gate_gain, taps_ref, before, normal_ref, inverse_ref, part, product,
    w_in, w_in_two, w_out, w_out_two,
    stream, gain_grad, gate_gain_grad, taps_grad, in_send, in_keep, out_send, out_keep,
    low, product_grad, padded, padded_grad, conv, total, *, segments, row_block, taps,
):
    j = pl.program_id(0)
    mine = info[0]
    thirds = WIDTH * 3
    blocks = thirds // CHAN

    @pl.when(j == 0)
    def _():
        normal, _ = normalize(x_ref[...])
        low[...] = (normal * gain[...]).astype(LOW)
        total[...] = jnp.zeros_like(total)
        gated_low = grad[...].astype(LOW)
        store_halves(dot_tn(product[...], gated_low), out_send, out_keep, mine, 48, 0)
        product_grad[...] = dot_nt(gated_low, join_rows(w_out[...], w_out_two[...], mine))

    value, slope = gelu_pair(before[...])
    weight = join_rows(w_in[...], w_in_two[...], mine)

    def finish(before_grad, column):
        store_halves(
            dot_tn(low[...], before_grad), in_send, in_keep, mine, 16,
            pl.multiple_of(column * 16, 16),
        )
        total[...] += dot_nt(before_grad, weight)

    @pl.when(j < 3)
    def _():
        lanes = pl.ds(pl.multiple_of(j * WIDTH, WIDTH), WIDTH)
        upstream = product_grad[:, lanes]
        product_grad[:, lanes] = upstream * value
        finish((upstream * part[:, lanes] * slope).astype(LOW), j)

    @pl.when(j == 2)
    def _():
        spread(product_grad, padded_grad, info, segments, blocks)
        product_grad[...] = normal_ref[...] * gate_gain[...]
        spread(product_grad, padded, info, segments, blocks)
        conv_taps(padded_grad, padded, taps_grad, blocks, row_block, taps)
        conv_rows(padded_grad, taps_ref, conv, blocks, row_block, taps, True)
        unspread(conv, product_grad, info, segments, blocks)
        upstream = product_grad[...]
        normal = normal_ref[...]
        gate_gain_grad[...] = row_sum(upstream * normal)
        product_grad[...] = normalize_back(upstream, gate_gain[...], normal, inverse_ref[...])

    @pl.when(j >= 3)
    def _():
        lanes = pl.ds(pl.multiple_of((j - 3) * WIDTH, WIDTH), WIDTH)
        finish((product_grad[:, lanes] * slope).astype(LOW), j)

    @pl.when(j == 5)
    def _():
        normal, inverse = normalize(x_ref[...])
        gain_grad[...] = row_sum(total[...] * normal)
        stream[...] = normalize_back(total[...], gain[...], normal, inverse)


def merge_forward_kernel(
    info, x_ref, attended, gated, taps_ref, valid, weight, weight_two,
    out, merged_low, stat, joined, padded, conv, *, segments, row_block, taps,
):
    blocks = 2 * WIDTH // CHAN
    joined[:, :WIDTH] = attended[...]
    joined[:, WIDTH:] = gated[...]
    spread(joined, padded, info, segments, blocks)
    conv_rows(padded, taps_ref, conv, blocks, row_block, taps, False)
    for c in range(blocks):
        conv[c] += padded[c]
    unspread(conv, joined, info, segments, blocks)
    merged_low[...] = joined[...].astype(LOW)
    part = dot(merged_low[...], join_rows(weight[...], weight_two[...], info[0]))
    after = x_ref[...] + part
    out[...] = after
    v = valid[...]
    stat[0:1, :] = row_sum(after * after * v)
    stat[1:2, :] = row_sum(part * part * v)
    stat[2:, :] = jnp.zeros((6, WIDTH), F32)


def merge_backward_kernel(
    info, grad, attended, gated, merged_low, taps_ref, weight, weight_two,
    attended_grad, gated_grad, taps_grad, send, keep,
    joined, padded, padded_grad, conv, *, segments, row_block, taps,
):
    blocks = 2 * WIDTH // CHAN
    low = grad[...].astype(LOW)
    store_halves(dot_tn(merged_low[...], low), send, keep, info[0], 32, 0)
    joined[:, :WIDTH] = attended[...]
    joined[:, WIDTH:] = gated[...]
    spread(joined, padded, info, segments, blocks)
    joined[...] = dot_nt(low, join_rows(weight[...], weight_two[...], info[0]))
    spread(joined, padded_grad, info, segments, blocks)
    conv_taps(padded_grad, padded, taps_grad, blocks, row_block, taps)
    conv_rows(padded_grad, taps_ref, conv, blocks, row_block, taps, True)
    for c in range(blocks):
        conv[c] += padded_grad[c]
    unspread(conv, joined, info, segments, blocks)
    attended_grad[...] = joined[:, :WIDTH]
    gated_grad[...] = joined[:, WIDTH:]


def ffn_backward_step(h, mine, low, before, part_grad, up, down, sends, total):
    up_send, up_keep, down_send, down_keep = sends
    gate = jax.nn.sigmoid(before)
    hidden = (before * gate).astype(LOW)
    part_low = part_grad[...]
    hidden_grad = dot_nt(part_low, down)
    before_grad = (hidden_grad * (gate * (1.0 + before * (1.0 - gate)))).astype(LOW)
    down_grad = dot_tn(hidden, part_low).astype(LOW).reshape(8, 64, WIDTH)

    @pl.when(h % 2 == mine)
    def _():
        down_keep[h // 2] = down_grad

    @pl.when(h % 2 != mine)
    def _():
        down_send[h // 2] = down_grad

    store_halves(
        dot_tn(low[...], before_grad), up_send, up_keep, mine, 16, pl.multiple_of(h * 16, 16)
    )
    total[...] += dot_nt(before_grad, up)


def rear_kernel(
    info, x_ref, gain, final_gain, valid, cotangent, up, up_two, down, down_two,
    encoded, stream, gain_grad, final_gain_grad, stat,
    up_send, up_keep, down_send, down_keep,
    low, before, part_grad, stream_grad, total,
):
    step = pl.program_id(0)
    h = jnp.where(step < 4, step, 7 - step)
    up_value = join_rows(up[...], up_two[...], info[0])
    down_value = pick_rows(down[...], down_two[...], h % 2 == info[0])

    @pl.when(step == 0)
    def _():
        normal, _ = normalize(x_ref[...])
        low[...] = (normal * gain[...]).astype(LOW)
        total[...] = jnp.zeros_like(total)

    @pl.when(step < 4)
    def _():
        value = dot(low[...], up_value)
        before[step] = value
        total[...] += dot(silu(value).astype(LOW), down_value)

    @pl.when(step == 3)
    def _():
        part = 0.5 * total[...]
        after = x_ref[...] + part
        v = valid[...]
        stat[0:1, :] = row_sum(after * after * v)
        stat[1:2, :] = row_sum(part * part * v)
        stat[2:, :] = jnp.zeros((6, WIDTH), F32)
        normal, inverse = normalize(after)
        encoded[...] = (normal * final_gain[...] * v).astype(LOW)
        upstream = cotangent[...].astype(F32) * v
        final_gain_grad[...] = row_sum(upstream * normal)
        grad = normalize_back(upstream, final_gain[...], normal, inverse)
        stream_grad[...] = grad
        part_grad[...] = (0.5 * grad).astype(LOW)
        total[...] = jnp.zeros_like(total)

    @pl.when(step >= 4)
    def _():
        ffn_backward_step(
            h, info[0], low, before[h], part_grad, up_value, down_value,
            (up_send, up_keep, down_send, down_keep), total,
        )

    @pl.when(step == 7)
    def _():
        normal, inverse = normalize(x_ref[...])
        gain_grad[...] = row_sum(total[...] * normal)
        stream[...] = stream_grad[...] + normalize_back(total[...], gain[...], normal, inverse)


def front_backward_kernel(
    info, grad, heads_stream, gated_stream, x_ref, gain, before, up, up_two, down, down_two,
    x_grad, gain_send, gain_keep, up_send, up_keep, down_send, down_keep,
    low, part_grad, stream_grad, total,
):
    h = pl.program_id(0)

    @pl.when(h == 0)
    def _():
        normal, _ = normalize(x_ref[...].astype(F32))
        low[...] = (normal * gain[...]).astype(LOW)
        stream_sum = grad[...] + heads_stream[...] + gated_stream[...]
        stream_grad[...] = stream_sum
        part_grad[...] = (0.5 * stream_sum).astype(LOW)
        total[...] = jnp.zeros_like(total)

    ffn_backward_step(
        h, info[0], low, before[...], part_grad,
        join_rows(up[...], up_two[...], info[0]),
        pick_rows(down[...], down_two[...], h % 2 == info[0]),
        (up_send, up_keep, down_send, down_keep), total,
    )

    @pl.when(h == 3)
    def _():
        normal, inverse = normalize(x_ref[...].astype(F32))
        gain_grad = row_sum(total[...] * normal).astype(LOW)
        gain_send[...] = jnp.broadcast_to(gain_grad.reshape(1, 1, 1, WIDTH), gain_send.shape)
        gain_keep[...] = gain_send[...]
        x_grad[...] = (
            stream_grad[...] + normalize_back(total[...], gain[...], normal, inverse)
        ).astype(LOW)


def whole(shape):
    return pl.BlockSpec(shape, lambda *_: (0,) * len(shape))


def call(kernel, grid, inputs, outputs, scratch, info, flops):
    in_specs = [
        whole(array.shape) if block is None else pl.BlockSpec(block, index)
        for array, block, index in inputs
    ]
    out_specs = [
        whole(shape) if block is None else pl.BlockSpec(block, index)
        for shape, _, block, index in outputs
    ]
    arrays = [array for array, _, _ in inputs]
    shapes = [jax.ShapeDtypeStruct(shape, kind) for shape, kind, _, _ in outputs]
    moved = sum(array.size * array.dtype.itemsize for array in arrays)
    moved = sum(shape.size * shape.dtype.itemsize for shape in shapes) + min(moved, 1 << 24)
    return pl.pallas_call(
        kernel,
        grid_spec=pltpu.PrefetchScalarGridSpec(
            num_scalar_prefetch=1,
            grid=grid,
            in_specs=in_specs,
            out_specs=out_specs,
            scratch_shapes=scratch,
        ),
        out_shape=shapes,
        compiler_params=pltpu.CompilerParams(vmem_limit_bytes=56 * 1024 * 1024),
        cost_estimate=pl.CostEstimate(flops=flops, bytes_accessed=moved, transcendentals=0),
    )(info, *arrays)


def segment_table(lengths, mine, row_count):
    ends = jnp.cumsum(lengths)
    position = jnp.arange(row_count, dtype=jnp.int32)
    segments = jnp.sum((position[None, :] >= ends[:, None]).astype(jnp.int32), axis=0)
    zero = jnp.zeros((1,), jnp.int32)
    last = jnp.full((1,), row_count, jnp.int32)
    info = jnp.concatenate([jnp.full((1,), mine, jnp.int32), zero, ends, ends, last])
    return segments, info.astype(jnp.int32)


def layer(features, cotangent, lengths, mine, front, middle, rear, smaller, taps):
    gate_taps, merge_taps, front_gain, heads_gain, gated_gain, gate_gain, rear_gain, final_gain = (
        element if element.ndim == 2 else element.reshape(1, -1) for element in smaller
    )
    tokens = features.shape[0]
    count = lengths.shape[0]
    segments = count + 1
    seg_ids, info = segment_table(lengths, mine, tokens)
    segs_col, segs_row = seg_ids[:, None], seg_ids[None, :]
    valid = (segs_col < count).astype(F32)
    stream = (tokens, WIDTH)
    thirds, double, hidden = 3 * WIDTH, 2 * WIDTH, 4 * WIDTH
    spread_rows = tokens + GAP * (segments + 1)
    row_block = (spread_rows - 2 * GAP) // 4
    tokens_low = pltpu.VMEM(stream, LOW)
    tokens_f32 = pltpu.VMEM(stream, F32)
    stat = ((8, WIDTH), F32, None, None)
    vector = ((1, WIDTH), F32, None, None)
    flop = 2 * tokens * WIDTH * WIDTH

    def all_of(*arrays):
        return [(array, None, None) for array in arrays]

    def halves(rows):
        return [((2, 8, rows, WIDTH), LOW, None, None)] * 2

    def columns(pair, rows, start, index):
        block = (2, 8, rows, WIDTH), lambda *i: (0, 0, start // rows + index(*i), 0)
        return [(array, *block) for array in pair]

    def lines(pair, index):
        block = (1, 8, 64, WIDTH), lambda *i: (index(*i) // 2, 0, 1, 0)
        return [(array, *block) for array in pair]

    def first(*_):
        return 0

    def step(h, _):
        return h

    front_blocks = columns(front, 16, 0, step) + lines(front, step)
    after_front, front_before, front_stat = call(
        front_forward_kernel,
        (4,),
        all_of(features, front_gain, valid) + front_blocks,
        [
            (stream, F32, None, None),
            ((tokens, hidden), F32, (tokens, WIDTH), lambda h, _: (0, h)),
            stat,
        ],
        [tokens_low, tokens_f32],
        info,
        8 * flop,
    )
    heads_blocks = columns(middle, 48, 144, first) + columns(middle, 16, 192, first)
    attended, packed, mixed = call(
        heads_forward_kernel,
        (1,),
        all_of(after_front, heads_gain, segs_col, segs_row)
        + heads_blocks,
        [
            (stream, F32, None, None),
            ((tokens, thirds), LOW, None, None),
            (stream, LOW, None, None),
        ],
        [],
        info,
        6 * flop,
    )
    gated_out = columns(middle, 48, 96, first)
    padded = pltpu.VMEM((thirds // CHAN, spread_rows, CHAN), F32)
    gated, gated_before, gate_normal, gate_inverse, gate_part, product = call(
        functools.partial(gated_forward_kernel, segments=segments, row_block=row_block, taps=taps),
        (6,),
        all_of(after_front, gated_gain, gate_gain, gate_taps)
        + columns(middle, 16, 0, lambda j, _: (j + 3) % 6)
        + gated_out,
        [
            (stream, F32, None, None),
            ((tokens, 6 * WIDTH), F32, (tokens, WIDTH), lambda j, _: (0, (j + 3) % 6)),
            ((tokens, thirds), F32, None, None),
            ((tokens, 1), F32, None, None),
            ((tokens, thirds), F32, None, None),
            ((tokens, thirds), LOW, None, None),
        ],
        [tokens_low, pltpu.VMEM((tokens, thirds), F32), padded, padded],
        info,
        18 * flop,
    )
    merge_block = columns(rear, 32, 128, first)
    joined = pltpu.VMEM((tokens, double), F32)
    padded_two = pltpu.VMEM((double // CHAN, spread_rows, CHAN), F32)
    after_merge, merged_low, merge_stat = call(
        functools.partial(merge_forward_kernel, segments=segments, row_block=row_block, taps=taps),
        (1,),
        all_of(after_front, attended, gated, merge_taps, valid) + merge_block,
        [(stream, F32, None, None), ((tokens, double), LOW, None, None), stat],
        [joined, padded_two, padded_two],
        info,
        8 * flop,
    )

    def bounce(i, _):
        return jnp.where(i < 4, i, 7 - i)

    encoded, merge_grad, rear_gain_grad, final_gain_grad, rear_stat, *rear_halves = call(
        rear_kernel,
        (8,),
        all_of(after_merge, rear_gain, final_gain, valid, cotangent)
        + columns(rear, 16, 0, bounce)
        + lines(rear, bounce),
        [(stream, LOW, None, None), (stream, F32, None, None), vector, vector, stat]
        + halves(64)
        + halves(64),
        [tokens_low, pltpu.VMEM((4, tokens, WIDTH), F32), tokens_low, tokens_f32, tokens_f32],
        info,
        26 * flop,
    )
    attended_grad, gated_grad, merge_taps_grad, *merge_halves = call(
        functools.partial(merge_backward_kernel, segments=segments, row_block=row_block, taps=taps),
        (1,),
        all_of(merge_grad, attended, gated, merged_low, merge_taps) + merge_block,
        [(stream, F32, None, None), (stream, F32, None, None), ((taps + 1, double), F32, None, None)]
        + halves(32),
        [joined, padded_two, padded_two, padded_two],
        info,
        16 * flop,
    )
    heads_stream, heads_gain_grad, *heads_halves = call(
        heads_backward_kernel,
        (1,),
        all_of(attended_grad, after_front, heads_gain, segs_col, segs_row, packed, mixed)
        + heads_blocks,
        [(stream, F32, None, None), vector] + halves(48) + halves(16),
        [tokens_low, pltpu.VMEM((tokens, thirds), LOW), tokens_low],
        info,
        16 * flop,
    )
    gated_stream, gated_gain_grad, gate_gain_grad, gate_taps_grad, *gated_halves = call(
        functools.partial(gated_backward_kernel, segments=segments, row_block=row_block, taps=taps),
        (6,),
        all_of(gated_grad, after_front, gated_gain, gate_gain, gate_taps)
        + [(gated_before, (tokens, WIDTH), lambda j, _: (0, j))]
        + all_of(gate_normal, gate_inverse, gate_part, product)
        + columns(middle, 16, 0, step)
        + gated_out,
        [
            (stream, F32, None, None),
            vector,
            ((1, thirds), F32, None, None),
            ((taps + 1, thirds), F32, None, None),
        ]
        + halves(96)
        + halves(48),
        [tokens_low, pltpu.VMEM((tokens, thirds), F32), padded, padded, padded, tokens_f32],
        info,
        36 * flop,
    )
    features_grad, *front_halves = call(
        front_backward_kernel,
        (4,),
        all_of(merge_grad, heads_stream, gated_stream, features, front_gain)
        + [(front_before, (tokens, WIDTH), lambda h, _: (0, h))]
        + front_blocks,
        [(stream, LOW, None, None)] + halves(16) + halves(64) + halves(64),
        [tokens_low, tokens_low, tokens_f32, tokens_f32],
        info,
        16 * flop,
    )
    small_grads = (
        gate_taps_grad, merge_taps_grad, heads_gain_grad, gated_gain_grad, rear_gain_grad,
        final_gain_grad, gate_gain_grad,
    )
    stats = (front_stat, merge_stat, rear_stat)
    weight_halves = (front_halves, heads_halves, gated_halves, merge_halves, rear_halves)
    return encoded, features_grad, info, stats, weight_halves, small_grads


SMALL = 16


def ring(size, shift):
    return [(i, (i + shift) % size) for i in range(size)]


def local_call(kernel, inputs, outputs, scratch, info, grid=(1,), specs=None):
    in_specs, out_specs = specs if specs else (None, None)
    whole_out = [whole(shape) for shape, _ in outputs]
    return pl.pallas_call(
        kernel,
        grid_spec=pltpu.PrefetchScalarGridSpec(
            num_scalar_prefetch=1,
            grid=grid,
            in_specs=in_specs if in_specs else [whole(array.shape) for array in inputs],
            out_specs=out_specs if out_specs else whole_out,
            scratch_shapes=scratch,
        ),
        out_shape=[jax.ShapeDtypeStruct(shape, kind) for shape, kind in outputs],
        compiler_params=pltpu.CompilerParams(vmem_limit_bytes=40 * 1024 * 1024),
        cost_estimate=pl.CostEstimate(
            flops=0,
            bytes_accessed=2 * sum(array.size * array.dtype.itemsize for array in inputs),
            transcendentals=0,
        ),
    )(info, *inputs)


def pack_kernel(
    info, front_up, front_down, heads_in, heads_out, gated_in, gated_out, merge_out, rear_up,
    rear_down, gate_taps, merge_taps, gains, front, middle, rear,
):
    def put(target, start, source):
        rows, width = source.shape
        for q in range(width // WIDTH):
            target[start + rows * q : start + rows * (q + 1), :] = source[
                :, WIDTH * q : WIDTH * (q + 1)
            ]

    put(front, 0, front_up)
    put(front, 64, front_down)
    put(middle, 0, gated_in)
    put(middle, 96, gated_out)
    put(middle, 144, heads_in)
    put(middle, 192, heads_out)
    put(rear, 0, rear_up)
    put(rear, 64, rear_down)
    put(rear, 128, merge_out)
    gate = gate_taps[...].astype(F32)
    merge = merge_taps[...].astype(F32)
    last = lax.broadcasted_iota(jnp.int32, (SMALL, CHAN), 0) == SMALL - 1
    quads = [
        gate[:SMALL],
        jnp.where(last, gains[...].astype(F32), gate[SMALL:]),
        merge[:SMALL],
        merge[SMALL:],
    ]
    for q in range(4):
        front[128 : 128 + SMALL, CHAN * q : CHAN * (q + 1)] = quads[q].astype(LOW)


def place_line_kernel(info, *refs):
    pieces, out, sem = refs[:4], refs[4], refs[5]
    copies = [
        pltpu.make_async_copy(piece, out.at[info[i]], sem.at[i])
        for i, piece in enumerate(pieces)
    ]
    for copy in copies:
        copy.start()
    for copy in copies:
        copy.wait()


def place_plane_kernel(info, *refs):
    pieces, out, sem = refs[:4], refs[4], refs[5]
    copies = [
        pltpu.make_async_copy(piece, out.at[info[4 + 2 * i], :, info[5 + 2 * i]], sem.at[i])
        for i, piece in enumerate(pieces)
    ]
    for copy in copies:
        copy.start()
    for copy in copies:
        copy.wait()


def anywhere(count):
    return [pl.BlockSpec(memory_space=pl.ANY)] * count


def gather_chunk(shard, spots):
    rows = shard.shape[0]
    line = [shard] + [lax.ppermute(shard, "z", ring(4, d)) for d in (1, 2, 3)]
    (line,) = local_call(
        place_line_kernel,
        line,
        [((4, rows, WIDTH), LOW)],
        [pltpu.SemaphoreType.DMA((4,))],
        spots,
        specs=(anywhere(4), anywhere(1)),
    )
    plane = [line] + [
        lax.ppermute(line, ("x", "y"), [(i, i ^ d) for i in range(4)]) for d in (1, 2, 3)
    ]
    (mine,) = local_call(
        place_plane_kernel,
        plane,
        [((2, 4, 2, rows, WIDTH), LOW)],
        [pltpu.SemaphoreType.DMA((4,))],
        spots,
        specs=(anywhere(4), anywhere(1)),
    )
    mine = mine.reshape(2, 8, rows, WIDTH)
    return mine, lax.ppermute(mine, "k", ring(2, 1))


def unpack_kernel(info, first, second, gate_taps, merge_taps, gains, gate_gain):
    mine = info[0]
    lane = lax.broadcasted_iota(jnp.int32, (SMALL, CHAN), 1)
    lane_row = lane[:1]
    gate_gain[...] = jnp.zeros_like(gate_gain)
    gains[...] = jnp.zeros_like(gains)

    def put(target, rows, value, start, size, lanes):
        block, offset = start // CHAN, start % CHAN
        inside = jnp.logical_and(lanes >= offset, lanes < offset + size)
        window = slice(CHAN * block, CHAN * (block + 1))
        target[rows, window] = jnp.where(inside, value, target[rows, window])
        spill = offset + size - CHAN
        if spill > 0:
            window = slice(CHAN * (block + 1), CHAN * (block + 2))
            target[rows, window] = jnp.where(lanes < spill, value, target[rows, window])

    for i in range(BLOCKS):
        x, core, rest = i // 16, (i // 8) % 2, i % 8
        value = jnp.where(mine == core, first[x, rest], second[x, rest]).astype(F32)
        quads = [value[:, CHAN * q : CHAN * (q + 1)] for q in range(4)]
        start = 48 * i
        for half in range(2):
            rows = slice(SMALL * half, SMALL * (half + 1))
            rolled = pltpu.roll(quads[half], start % CHAN, 1)
            put(gate_taps, rows, rolled, start, 48, lane)
            rolled = pltpu.roll(quads[2 + half], (32 * i) % CHAN, 1)
            put(merge_taps, rows, rolled, 32 * i, 32, lane)
        line = quads[1][SMALL - 1 :]
        for g in range(5):
            rolled = pltpu.roll(line, (16 * i - 16 * g) % CHAN, 1)
            put(gains, slice(g, g + 1), rolled, 16 * i, 16, lane_row)
        rolled = pltpu.roll(line, (48 * i - 80) % CHAN, 1)
        put(gate_gain, slice(0, 1), rolled, 48 * i, 48, lane_row)


def pack_small_kernel(
    info, gate_taps, merge_taps, heads_gain, gated_gain, rear_gain, final_gain, gate_gain,
    front_stat, merge_stat, rear_stat,
    send_high, keep_high, send_low, keep_low, *, count_at,
):
    mine = info[0]
    lane = lax.broadcasted_iota(jnp.int32, (SMALL, CHAN), 1)
    lane_row = lane[:1]
    last = lax.broadcasted_iota(jnp.int32, (SMALL, CHAN), 0) == SMALL - 1
    stats = [
        front_stat[0:1, :], front_stat[1:2, :], merge_stat[0:1, :], rear_stat[0:1, :],
        front_stat[2:3, :], merge_stat[1:2, :], rear_stat[1:2, :],
    ]
    stat_line = jnp.where(lane_row == 7, info[count_at].astype(F32), 0.0)
    for i, stat in enumerate(stats):
        stat_line = jnp.where(lane_row == i, jnp.sum(stat, axis=1, keepdims=True), stat_line)

    def take(source, rows, start, size, lanes):
        block, offset = start // CHAN, start % CHAN
        value = pltpu.roll(source[rows, CHAN * block : CHAN * (block + 1)], (-offset) % CHAN, 1)
        if offset + size > CHAN:
            other = source[rows, CHAN * (block + 1) : CHAN * (block + 2)]
            value = jnp.where(lanes < CHAN - offset, value, pltpu.roll(other, (-offset) % CHAN, 1))
        return value

    for i in range(BLOCKS):
        x, core, rest = i // 16, (i // 8) % 2, i % 8
        halves = [slice(0, SMALL), slice(SMALL, 2 * SMALL)]
        quads = [take(gate_taps, rows, 48 * i, 48, lane) for rows in halves]
        quads += [take(merge_taps, rows, 32 * i, 32, lane) for rows in halves]
        line = pltpu.roll(take(gate_gain, slice(0, 1), 48 * i, 48, lane_row), 80, 1)
        for g, gain in enumerate((heads_gain, gated_gain, rear_gain, final_gain)):
            start = 16 * (g + 1)
            value = pltpu.roll(take(gain, slice(0, 1), 16 * i, 16, lane_row), start, 1)
            inside = jnp.logical_and(lane_row >= start, lane_row < start + 16)
            line = jnp.where(inside, value, line)
        quads[1] = jnp.where(last, line, quads[1])
        quads[3] = jnp.where(last, stat_line, quads[3])
        for q in range(4):
            lanes = slice(CHAN * q, CHAN * (q + 1))
            high = quads[q].astype(LOW)
            rest_low = (quads[q] - high.astype(F32)).astype(LOW)

            @pl.when(mine == core)
            def _():
                keep_high[x, rest, :, lanes] = high
                keep_low[x, rest, :, lanes] = rest_low

            @pl.when(mine != core)
            def _():
                send_high[x, rest, :, lanes] = high
                send_low[x, rest, :, lanes] = rest_low


def split_store(target, index, start, rows, total, paired):
    high = total.astype(LOW)
    target[index, start : start + rows, :] = high
    if paired:
        target[index, start + rows : start + 2 * rows, :] = (total - high.astype(F32)).astype(LOW)


def core_sum_kernel(info, *refs, sizes):
    outs = refs[-4:]
    inputs = refs[:-4]
    half = len(inputs) // 2
    keeps, gots = inputs[:half], inputs[half:]
    x, y = info[4], info[5]
    for d in range(4):
        xi = lax.rem(x + d // 2, 2)
        yi = lax.rem(y + d % 2, 2)
        start = 0
        at = 0
        for rows, paired in sizes:
            total = keeps[at][xi, 0, yi].astype(F32) + gots[at][xi, 0, yi].astype(F32)
            at += 1
            if paired:
                total += keeps[at][xi, 0, yi].astype(F32) + gots[at][xi, 0, yi].astype(F32)
                at += 1
            split_store(outs[d], 0, start, rows, total, paired)
            start += rows * (2 if paired else 1)


def windows(sizes):
    start = 0
    for rows, paired in sizes:
        yield start, rows, paired
        start += rows * (2 if paired else 1)


def plane_sum_kernel(info, *refs, sizes):
    pieces, outs = refs[:4], refs[4:]
    z = info[0]
    for e in range(4):
        zi = lax.rem(z + e, 4)
        for start, rows, paired in windows(sizes):
            span = slice(start, start + rows)
            total = sum(piece[zi, span, :].astype(F32) for piece in pieces)
            if paired:
                span = slice(start + rows, start + 2 * rows)
                total += sum(piece[zi, span, :].astype(F32) for piece in pieces)
            if e == 0:
                outs[0][start : start + rows, :] = total
            else:
                high = total.astype(LOW)
                outs[e][start : start + rows, :] = high
                if paired:
                    rest = (total - high.astype(F32)).astype(LOW)
                    outs[e][start + rows : start + 2 * rows, :] = rest


def line_sum_kernel(info, keep, one, two, three, *outs, sizes, shapes):
    at = 0
    for (start, rows, paired), shape in zip(windows(sizes), shapes):
        span = slice(start, start + rows)
        total = keep[span, :]
        for piece in (one, two, three):
            total += piece[span, :].astype(F32)
            if paired:
                total += piece[start + rows : start + 2 * rows, :].astype(F32)
        if paired:
            quads = [total[:, CHAN * q : CHAN * (q + 1)] for q in range(4)]
            outs[at][0:SMALL, :] = quads[0][:, :48]
            outs[at][SMALL : 2 * SMALL - 1, :] = quads[1][: SMALL - 1, :48]
            outs[at + 1][0:SMALL, :] = quads[2][:, :32]
            outs[at + 1][SMALL : 2 * SMALL - 1, :] = quads[3][: SMALL - 1, :32]
            outs[at + 2][...] = quads[1][SMALL - 1 :, :]
            outs[at + 3][...] = quads[3][SMALL - 1 :, :]
            at += 4
        elif shape is None:
            owner = info[12]
            block = total[0:1, :]
            base = (owner // 8) * CHAN
            line = jnp.zeros((1, CHAN), F32)
            for b in range(WIDTH // CHAN):
                line = jnp.where(
                    base == b * CHAN, block[:, CHAN * b : CHAN * (b + 1)], line
                )
            lane = lax.broadcasted_iota(jnp.int32, (16, CHAN), 1)
            row = lax.broadcasted_iota(jnp.int32, (16, CHAN), 0)
            chosen = jnp.where(lane == row + 16 * lax.rem(owner, 8), line, 0.0)
            outs[at][...] = jnp.broadcast_to(
                jnp.sum(chosen, axis=1, keepdims=True), (16, CHAN)
            )
            at += 1
        else:
            height, width = shape
            for q in range(width // WIDTH):
                outs[at][:, WIDTH * q : WIDTH * (q + 1)] = total[height * q : height * (q + 1), :]
            at += 1


def scatter_chunk(pairs, sizes, shapes, spots):
    got = [lax.ppermute(send, "k", ring(2, 1)) for send, _ in pairs]
    keep = [own for _, own in pairs]
    inputs = [array.reshape(2, 4, 2, array.shape[2], WIDTH) for array in keep + got]
    total = sum(array.shape[3] for array in inputs) // 2
    in_specs = [
        pl.BlockSpec((2, 1, 2, array.shape[3], WIDTH), lambda i, _: (0, i, 0, 0, 0))
        for array in inputs
    ]
    out_specs = [pl.BlockSpec((1, total, WIDTH), lambda i, _: (i, 0, 0))] * 4
    own, *rest = local_call(
        functools.partial(core_sum_kernel, sizes=sizes),
        inputs,
        [((4, total, WIDTH), LOW)] * 4,
        [],
        spots,
        grid=(4,),
        specs=(in_specs, out_specs),
    )
    rest = [
        lax.ppermute(array, ("x", "y"), [(i, i ^ d) for i in range(4)])
        for d, array in zip((1, 2, 3), rest)
    ]
    own, *rest = local_call(
        functools.partial(plane_sum_kernel, sizes=sizes),
        [own] + rest,
        [((total, WIDTH), F32)] + [((total, WIDTH), LOW)] * 3,
        [],
        spots,
    )
    rest = [lax.ppermute(array, "z", ring(4, d)) for d, array in zip((1, 2, 3), rest)]
    outputs = []
    for (_, paired), shape in zip(sizes, shapes):
        if paired:
            outputs += [((31, 48), F32), ((31, 32), F32), ((1, CHAN), F32), ((1, CHAN), F32)]
        elif shape is None:
            outputs.append(((16, CHAN), F32))
        else:
            outputs.append((shape, F32))
    return local_call(
        functools.partial(line_sum_kernel, sizes=sizes, shapes=shapes),
        [own] + rest,
        outputs,
        [],
        spots,
    )


def grid_device(
    features, cotangent, lengths, front_up, front_down, heads_input, heads_output, gated_input,
    gated_output, merge_output, rear_up, rear_down, gate_kernel, merge_kernel, front_gain,
    heads_gain, gated_gain, gate_gain, rear_gain, final_gain,
):
    x, k, z, y = (lax.axis_index(name) for name in ("x", "k", "z", "y"))
    places = [z, z + 3, z + 2, z + 1]
    places = [lax.rem(place, 4) for place in places]
    for dx, dy in ((0, 0), (0, 1), (1, 0), (1, 1)):
        places += [lax.rem(x + dx, 2), lax.rem(y + dy, 2)]
    places.append(((x * 2 + k) * 4 + z) * 2 + y)
    spots = jnp.stack([place.astype(jnp.int32) for place in places])
    mine = k.astype(jnp.int32)
    taps = gate_kernel.shape[0]

    def tall(element):
        return jnp.pad(element, ((0, 1), (0, CHAN - element.shape[1])))

    gains = jnp.concatenate([front_gain, heads_gain, gated_gain, rear_gain, final_gain, gate_gain])
    front, middle, rear = local_call(
        pack_kernel,
        [
            front_up, front_down, heads_input, heads_output, gated_input, gated_output,
            merge_output, rear_up, rear_down, tall(gate_kernel), tall(merge_kernel),
            gains.reshape(1, -1),
        ],
        [((144, WIDTH), LOW), ((208, WIDTH), LOW), ((160, WIDTH), LOW)],
        [],
        spots,
    )
    front = gather_chunk(front, spots)
    middle = gather_chunk(middle, spots)
    rear = gather_chunk(rear, spots)
    small_specs = [pl.BlockSpec((2, 8, SMALL, WIDTH), lambda *_: (0, 0, 8, 0))] * 2
    small_shapes = [((32, 3 * WIDTH), F32), ((32, 2 * WIDTH), F32), ((8, WIDTH), F32), ((1, 3 * WIDTH), F32)]
    gate_taps, merge_taps, gains, gate_full = local_call(
        unpack_kernel,
        list(front),
        small_shapes,
        [],
        mine.reshape(1),
        specs=(small_specs, [whole(shape) for shape, _ in small_shapes]),
    )
    lines = [gains[g : g + 1] for g in range(5)]
    smaller = (gate_taps, merge_taps, lines[0], lines[1], lines[2], gate_full, lines[3], lines[4])
    encoded, features_grad, info, stats, weight_halves, small_grads = layer(
        features, cotangent, lengths[0], mine, front, middle, rear, smaller, taps
    )
    front_halves, heads_halves, gated_halves, merge_halves, rear_halves = weight_halves
    count_at = 1 + 2 * lengths.shape[1]
    small_high_low = local_call(
        functools.partial(pack_small_kernel, count_at=count_at),
        list(small_grads) + list(stats),
        [((2, 8, SMALL, WIDTH), LOW)] * 4,
        [],
        info,
    )

    def by_two(arrays):
        return [tuple(arrays[i : i + 2]) for i in range(0, len(arrays), 2)]

    rear_up_grad, rear_down_grad, merge_output_grad = scatter_chunk(
        by_two(rear_halves) + by_two(merge_halves),
        ((64, False), (64, False), (32, False)),
        (rear_up.shape, rear_down.shape, merge_output.shape),
        spots,
    )
    (
        heads_input_grad, heads_output_grad, gated_input_grad, gated_output_grad,
        gate_kernel_grad, merge_kernel_grad, gain_line, stat_line,
    ) = scatter_chunk(
        by_two(heads_halves) + by_two(gated_halves) + by_two(small_high_low),
        ((48, False), (16, False), (96, False), (48, False), (16, True)),
        (heads_input.shape, heads_output.shape, gated_input.shape, gated_output.shape, None),
        spots,
    )
    front_gain_grad, front_up_grad, front_down_grad = scatter_chunk(
        by_two(front_halves),
        ((16, False), (64, False), (64, False)),
        (None, front_up.shape, front_down.shape),
        spots,
    )
    line = gain_line[0]
    statistics = jnp.sqrt(stat_line[0, :7] / (stat_line[0, 7] * features.shape[1]))
    return (
        encoded, features_grad, front_up_grad, front_down_grad, heads_input_grad,
        heads_output_grad, gated_input_grad, gated_output_grad, merge_output_grad, rear_up_grad,
        rear_down_grad, gate_kernel_grad, merge_kernel_grad, front_gain_grad[:, 0], line[16:32],
        line[32:48], line[80:128], line[48:64], line[64:80], statistics,
    )


def pack_rows(shard):
    rows, columns = shard.shape
    pieces = shard.reshape(rows, columns // WIDTH, WIDTH).transpose(1, 0, 2)
    return pieces.reshape(rows * columns // WIDTH, WIDTH)


def pad_lines(flat):
    rows = -(-flat.shape[-1] // (WIDTH * 16)) * 16
    spare = [(0, 0)] * (flat.ndim - 1) + [(0, rows * WIDTH - flat.shape[-1])]
    return jnp.pad(flat, spare).reshape(flat.shape[:-1] + (rows, WIDTH))


def to_owners(weight):
    rows, columns = weight.shape
    pieces = weight.reshape(BLOCKS, rows // BLOCKS, columns // WIDTH, WIDTH)
    pieces = pieces.transpose(0, 2, 1, 3).reshape(2, 2, 8, -1, WIDTH)
    return pieces[:, 0], pieces[:, 1]


def from_owners(halves, rows, columns):
    send, keep = halves
    pieces = jnp.stack([keep, send], axis=1)
    pieces = pieces.reshape(BLOCKS, columns // WIDTH, rows // BLOCKS, WIDTH)
    return pieces.transpose(0, 2, 1, 3).reshape(rows, columns)


def any_device(features, cotangent, lengths, *shards, axes):
    count = lax.axis_size(axes)
    matrices, smaller = shards[:9], shards[9:]
    packed = [pack_rows(element) for element in matrices]
    packed.append(pad_lines(jnp.concatenate([element.reshape(-1) for element in smaller])))
    gathered = lax.all_gather(jnp.concatenate(packed), axes, axis=0)
    weights = []
    start = 0
    for element, piece in zip(matrices, packed):
        rows, columns = element.shape
        window = gathered[:, start : start + piece.shape[0]]
        start += piece.shape[0]
        window = window.reshape(count, columns // WIDTH, rows, WIDTH).transpose(0, 2, 1, 3)
        weights.append(to_owners(window.reshape(count * rows, columns)))
    flat = gathered[:, start:].reshape(count, -1).astype(F32)
    lines = []
    start = 0
    for element in smaller:
        window = flat[:, start : start + element.size]
        start += element.size
        if element.ndim == 2:
            window = window.reshape((count,) + element.shape).transpose(1, 0, 2)
            window = window.reshape(element.shape[0], -1)
            lines.append(jnp.pad(window, ((0, 1), (0, 0))))
        else:
            lines.append(window.reshape(1, -1))
    up, down, h_in, h_out, g_in, g_out, m_out, r_up, r_down = weights

    def chunk(*members):
        return tuple(jnp.concatenate([member[i] for member in members], axis=2) for i in (0, 1))

    encoded, features_grad, info, stats, halves, small_grads = layer(
        features, cotangent, lengths[0], jnp.int32(0), chunk(up, down),
        chunk(g_in, g_out, h_in, h_out), chunk(r_up, r_down, m_out), lines, smaller[0].shape[0],
    )
    front, heads, gated, merge, rear = halves
    front_gain = front[1][0, 0, 0].astype(F32)
    ordered = (front[2:4], front[4:6], heads[:2], heads[2:], gated[:2], gated[2:], merge, rear[:2], rear[2:])
    pieces = []
    for element, halves in zip(matrices, ordered):
        rows, columns = element.shape
        full = from_owners(halves, rows * count, columns)
        full = full.reshape(count, rows, columns // WIDTH, WIDTH).transpose(0, 2, 1, 3)
        pieces.append(full.reshape(count, -1, WIDTH))
    gate_taps, merge_taps, heads_gain, gated_gain, rear_gain, final_gain, gate_gain = small_grads
    small_full = (gate_taps, merge_taps, front_gain, heads_gain, gated_gain, gate_gain, rear_gain, final_gain)
    flat = []
    for element, full in zip(smaller, small_full):
        if element.ndim == 2:
            full = full[: element.shape[0]].reshape(element.shape[0], count, -1).transpose(1, 0, 2)
        flat.append(full.reshape(count, -1))
    pieces.append(pad_lines(jnp.concatenate(flat, axis=1).astype(LOW)))
    summed = lax.psum_scatter(jnp.concatenate(pieces, axis=1), axes, scatter_dimension=0)
    outputs = []
    start = 0
    for element, piece in zip(matrices, pieces):
        rows, columns = element.shape
        window = summed[start : start + piece.shape[1]].astype(F32)
        start += piece.shape[1]
        window = window.reshape(columns // WIDTH, rows, WIDTH).transpose(1, 0, 2)
        outputs.append(window.reshape(rows, columns))
    flat = summed[start:].reshape(-1).astype(F32)
    start = 0
    for element in smaller:
        outputs.append(flat[start : start + element.size].reshape(element.shape))
        start += element.size
    front_stat, merge_stat, rear_stat = stats
    squares = jnp.stack(
        [
            front_stat[0], front_stat[1], merge_stat[0], rear_stat[0], front_stat[2],
            merge_stat[1], rear_stat[1],
        ]
    )
    totals = lax.psum(
        jnp.append(jnp.sum(squares, axis=1), jnp.sum(lengths).astype(F32)), axes
    )
    statistics = jnp.sqrt(totals[:7] / (totals[7] * features.shape[1]))
    return (encoded, features_grad) + tuple(outputs) + (statistics,)


def solution(mesh):
    body = grid_device
    axes = ("x", "k", "z", "y")
    if mesh.devices.shape == (4, 8):
        mesh = Mesh(mesh.devices.reshape(2, 2, 4, 2), axes)
    else:
        axes = tuple(mesh.axis_names)
        body = functools.partial(any_device, axes=axes)
    rows, columns, vector = P(axes, None), P(None, axes), P(axes)
    weights = (rows,) * 9 + (columns,) * 2 + (vector,) * 6
    return jax.shard_map(
        body,
        mesh=mesh,
        in_specs=(rows, rows, rows) + weights,
        out_specs=(rows, rows) + weights + (P(),),
        check_vma=False,
    )
```

```python
import functools

import jax
import jax.numpy as jnp
from jax import lax
from jax.experimental import pallas as pl
from jax.experimental.pallas import tpu as pltpu
from jax.sharding import Mesh, PartitionSpec as P

HEADS = 8
EPSILON = 1e-05
NEGATIVE = -1000000000.0
TILE = 8
GAP = 16
CHAN = 128
WIDTH = 512
BLOCKS = 32
F32 = jnp.float32
LOW = jnp.bfloat16


def dot(left, right):
    return jnp.dot(left, right, preferred_element_type=F32)


def dot_tn(left, right):
    return lax.dot_general(left, right, (((0,), (0,)), ((), ())), preferred_element_type=F32)


def dot_nt(left, right):
    return lax.dot_general(left, right, (((1,), (1,)), ((), ())), preferred_element_type=F32)


def normalize(values):
    centred = values - jnp.mean(values, axis=-1, keepdims=True)
    variance = jnp.mean(centred * centred, axis=-1, keepdims=True)
    inverse = lax.rsqrt(variance + EPSILON)
    return centred * inverse, inverse


def normalize_back(upstream, gain, normal, inverse):
    scaled = upstream * gain
    mean_scaled = jnp.mean(scaled, axis=-1, keepdims=True)
    mean_cross = jnp.mean(scaled * normal, axis=-1, keepdims=True)
    return inverse * (scaled - mean_scaled - normal * mean_cross)


def row_sum(values):
    return jnp.sum(values, axis=0, keepdims=True)


GELU_A = 0.7978845608028654
GELU_B = 0.044715


def gelu(v):
    return 0.5 * v * (1.0 + jnp.tanh(GELU_A * (v + GELU_B * v * v * v)))


def gelu_pair(v):
    square = v * v
    bend = jnp.tanh(GELU_A * (v + GELU_B * square * v))
    value = 0.5 * v * (1.0 + bend)
    slope = 0.5 * (1.0 + bend) + 0.5 * v * (1.0 - bend * bend) * (
        GELU_A * (1.0 + 3.0 * GELU_B * square)
    )
    return value, slope


def silu(v):
    return v * jax.nn.sigmoid(v)


def store_halves(value, send, keep, mine, rows, start):
    parts = value.astype(LOW).reshape(2, 2, 8, rows, WIDTH)

    @pl.when(mine == 0)
    def _():
        keep[:, :, pl.ds(start, rows), :] = parts[:, 0]
        send[:, :, pl.ds(start, rows), :] = parts[:, 1]

    @pl.when(mine == 1)
    def _():
        keep[:, :, pl.ds(start, rows), :] = parts[:, 1]
        send[:, :, pl.ds(start, rows), :] = parts[:, 0]


def join_rows(first, second, mine):
    cores = jnp.where(mine == 0, first, second), jnp.where(mine == 0, second, first)
    return jnp.concatenate(
        [core[2 * x + y, z] for x in (0, 1) for core in cores for z in range(4) for y in (0, 1)]
    )


def pick_rows(first, second, flag):
    chosen = jnp.where(flag, first, second)
    return jnp.concatenate([chosen[y, z] for z in range(4) for y in (0, 1)])


def visits(info, segments, body):
    for s in range(segments):
        begin, end = info[1 + s], info[1 + segments + s]

        def visit(i, _, s=s, begin=begin, end=end):
            row = i * TILE + lax.broadcasted_iota(jnp.int32, (TILE, CHAN), 0)
            inside = jnp.logical_and(row >= begin, row < end)
            body(s, pl.multiple_of(i * TILE, TILE), inside)
            return 0

        lax.fori_loop(begin // TILE, (end + TILE - 1) // TILE, visit, 0)


def spread(source, padded, info, segments, blocks):
    padded[...] = jnp.zeros_like(padded)

    def body(s, base, inside):
        for c in range(blocks):
            value = source[pl.ds(base, TILE), c * CHAN : (c + 1) * CHAN]
            padded[c, pl.ds(base + GAP * (s + 1), TILE), :] = jnp.where(inside, value, 0.0)

    visits(info, segments, body)


def unspread(padded, target, info, segments, blocks):
    def body(s, base, inside):
        for c in range(blocks):
            lanes = slice(c * CHAN, (c + 1) * CHAN)
            value = padded[c, pl.ds(base + GAP * (s + 1), TILE), :]
            target[pl.ds(base, TILE), lanes] = jnp.where(
                inside, value, target[pl.ds(base, TILE), lanes]
            )

    visits(info, segments, body)


def conv_rows(padded, kernel, out, blocks, row_block, taps, flip):
    half = (taps - 1) // 2
    steps = (padded.shape[1] - 2 * GAP) // row_block

    def body(step, _):
        c = step // steps
        base = (step % steps) * row_block + GAP
        lanes = pl.ds(pl.multiple_of(c * CHAN, CHAN), CHAN)
        total = jnp.zeros((row_block, CHAN), F32)
        for j in range(taps):
            shift = half - j if flip else j - half
            total += kernel[pl.ds(j, 1), lanes] * padded[c, pl.ds(base + shift, row_block), :]
        out[c, pl.ds(pl.multiple_of(base, TILE), row_block), :] = total
        return 0

    lax.fori_loop(0, blocks * steps, body, 0)


def conv_taps(padded_grad, padded, out, blocks, row_block, taps):
    half = (taps - 1) // 2
    steps = (padded.shape[1] - 2 * GAP) // row_block
    tiles = row_block // TILE

    def block(c, _):
        lanes = pl.ds(pl.multiple_of(c * CHAN, CHAN), CHAN)

        def body(step, sums):
            base = pl.multiple_of(step * row_block + GAP, TILE)
            grad = padded_grad[c, pl.ds(base, row_block), :]
            new = []
            for j in range(taps):
                term = grad * padded[c, pl.ds(base + j - half, row_block), :]
                new.append(sums[j] + jnp.sum(term.reshape(tiles, TILE, CHAN), axis=0))
            return tuple(new)

        zero = jnp.zeros((TILE, CHAN), F32)
        sums = lax.fori_loop(0, steps, body, (zero,) * taps)
        for j in range(taps):
            out[pl.ds(j, 1), lanes] = row_sum(sums[j])
        return 0

    lax.fori_loop(0, blocks, block, 0)


def front_forward_kernel(
    info, x_ref, gain, valid, up, up_two, down, down_two, out, before_out, stat, low, total
):
    h = pl.program_id(0)
    mine = info[0]
    up_value = join_rows(up[...], up_two[...], mine)
    down_value = pick_rows(down[...], down_two[...], h % 2 == mine)

    @pl.when(h == 0)
    def _():
        normal, _ = normalize(x_ref[...].astype(F32))
        low[...] = (normal * gain[...]).astype(LOW)
        total[...] = jnp.zeros_like(total)

    before = dot(low[...], up_value)
    before_out[...] = before
    total[...] += dot(silu(before).astype(LOW), down_value)

    @pl.when(h == pl.num_programs(0) - 1)
    def _():
        x = x_ref[...].astype(F32)
        part = 0.5 * total[...]
        after = x + part
        out[...] = after
        v = valid[...]
        stat[0:1, :] = row_sum(x * x * v)
        stat[1:2, :] = row_sum(after * after * v)
        stat[2:3, :] = row_sum(part * part * v)
        stat[3:, :] = jnp.zeros((5, WIDTH), F32)


def head_masks(segs_col, segs_row):
    allowed = segs_col == segs_row
    lane = lax.broadcasted_iota(jnp.int32, (1, CHAN), 1)
    return allowed, (lane < CHAN // 2, lane >= CHAN // 2)


def head_probs(query, key, allowed, scale):
    scores = jnp.where(allowed, dot_nt(query, key) * scale, NEGATIVE)
    exponent = jnp.exp(scores - jnp.max(scores, axis=-1, keepdims=True))
    return exponent / jnp.sum(exponent, axis=-1, keepdims=True)


def heads_forward_kernel(
    info, x_ref, gain, segs_col, segs_row, w_in, w_in_two, w_out, w_out_two,
    attended, packed, mixed,
):
    mine = info[0]
    scale = (WIDTH // HEADS) ** -0.5
    normal, _ = normalize(x_ref[...])
    low = (normal * gain[...]).astype(LOW)
    for q in range(3):
        rows = slice(16 * q, 16 * (q + 1))
        weight = join_rows(w_in[:, :, rows, :], w_in_two[:, :, rows, :], mine)
        packed[:, WIDTH * q : WIDTH * (q + 1)] = dot(low, weight).astype(LOW)
    allowed, halves = head_masks(segs_col[...], segs_row[...])

    def pair(p, _):
        lanes = [
            pl.ds(pl.multiple_of(WIDTH * q + CHAN * p, CHAN), CHAN) for q in range(3)
        ]
        query, key, value = (packed[:, lane] for lane in lanes)
        parts = []
        for half in halves:
            probs = head_probs(jnp.where(half, query, 0), key, allowed, scale)
            parts.append(dot(probs.astype(LOW), value))
        mixed[:, lanes[0]] = jnp.where(halves[0], parts[0], parts[1]).astype(LOW)
        return 0

    lax.fori_loop(0, HEADS // 2, pair, 0)
    attended[...] = dot(mixed[...], join_rows(w_out[...], w_out_two[...], mine))


def heads_backward_kernel(
    info, grad, x_ref, gain, segs_col, segs_row, packed, mixed, w_in, w_in_two, w_out, w_out_two,
    stream, gain_grad, send, keep, mixed_grad, packed_grad, low,
):
    scale = (WIDTH // HEADS) ** -0.5
    mine = info[0]
    attended_low = grad[...].astype(LOW)
    store_halves(dot_tn(mixed[...], attended_low), send, keep, mine, 16, 48)
    mixed_grad[...] = dot_nt(attended_low, join_rows(w_out[...], w_out_two[...], mine)).astype(LOW)
    normal, inverse = normalize(x_ref[...])
    low[...] = (normal * gain[...]).astype(LOW)
    allowed, halves = head_masks(segs_col[...], segs_row[...])

    def pair(p, _):
        lanes = [
            pl.ds(pl.multiple_of(WIDTH * q + CHAN * p, CHAN), CHAN) for q in range(3)
        ]
        query, key, value = (packed[:, lane] for lane in lanes)
        upstream = mixed_grad[:, lanes[0]]
        parts = []
        for half in halves:
            probs = head_probs(jnp.where(half, query, 0), key, allowed, scale)
            probs_grad = dot_nt(jnp.where(half, upstream, 0), value)
            value_grad = dot_tn(probs.astype(LOW), upstream)
            inner = jnp.sum(probs_grad * probs, axis=-1, keepdims=True)
            score_grad = (probs * (probs_grad - inner)).astype(LOW)
            query_grad = dot(score_grad, key) * scale
            key_grad = dot_tn(score_grad, query) * scale
            parts.append((query_grad, key_grad, value_grad))
        for q in range(3):
            packed_grad[:, lanes[q]] = jnp.where(halves[0], parts[0][q], parts[1][q]).astype(LOW)
        return 0

    lax.fori_loop(0, HEADS // 2, pair, 0)
    total = jnp.zeros(x_ref.shape, F32)
    for q in range(3):
        rows = slice(16 * q, 16 * (q + 1))
        weight = join_rows(w_in[:, :, rows, :], w_in_two[:, :, rows, :], mine)
        piece = packed_grad[:, WIDTH * q : WIDTH * (q + 1)]
        store_halves(dot_tn(low[...], piece), send, keep, mine, 16, 16 * q)
        total += dot_nt(piece, weight)
    gain_grad[...] = row_sum(total * normal)
    stream[...] = normalize_back(total, gain[...], normal, inverse)


def gated_forward_kernel(
    info, x_ref, gain, gate_gain, taps_ref, w_in, w_in_two, w_out, w_out_two,
    gated, before_out, normal_out, inverse_out, part_out, product,
    low, act, padded, conv, *, segments, row_block, taps,
):
    j = pl.program_id(0)
    thirds = WIDTH * 3

    @pl.when(j == 0)
    def _():
        normal, _ = normalize(x_ref[...])
        low[...] = (normal * gain[...]).astype(LOW)

    before = dot(low[...], join_rows(w_in[...], w_in_two[...], info[0]))
    before_out[...] = before
    value = gelu(before)

    @pl.when(j < 3)
    def _():
        act[:, pl.ds(pl.multiple_of(j * WIDTH, WIDTH), WIDTH)] = value

    @pl.when(j == 2)
    def _():
        normal, inverse = normalize(act[...])
        normal_out[...] = normal
        inverse_out[...] = inverse
        act[...] = normal * gate_gain[...]
        blocks = thirds // CHAN
        spread(act, padded, info, segments, blocks)
        conv_rows(padded, taps_ref, conv, blocks, row_block, taps, False)
        unspread(conv, part_out, info, segments, blocks)

    @pl.when(j >= 3)
    def _():
        lanes = pl.ds(pl.multiple_of((j - 3) * WIDTH, WIDTH), WIDTH)
        product[:, lanes] = (value * part_out[:, lanes]).astype(LOW)

    @pl.when(j == 5)
    def _():
        gated[...] = dot(product[...], join_rows(w_out[...], w_out_two[...], info[0]))


def gated_linear_kernel(
    info, grad, x_ref, gain, before, part, product, w_in, w_in_two, w_out, w_out_two,
    part_grad, total_out, send, keep, low, product_grad, gated_low,
):
    j = pl.program_id(0)
    mine = info[0]

    @pl.when(j == 0)
    def _():
        normal, _ = normalize(x_ref[...])
        low[...] = (normal * gain[...]).astype(LOW)
        total_out[...] = jnp.zeros_like(total_out)
        gated_low[...] = grad[...].astype(LOW)
        store_halves(dot_tn(product[...], gated_low[...]), send, keep, mine, 48, 48)
        product_grad[...] = dot_nt(gated_low[...], join_rows(w_out[...], w_out_two[...], mine))

    value, slope = gelu_pair(before[...])
    lanes = pl.ds(pl.multiple_of(j * WIDTH, WIDTH), WIDTH)
    upstream = product_grad[:, lanes]
    part_grad[...] = upstream * value
    before_grad = (upstream * part[...] * slope).astype(LOW)
    store_halves(
        dot_tn(low[...], before_grad), send, keep, mine, 16, pl.multiple_of(j * 16, 16)
    )
    total_out[...] += dot_nt(before_grad, join_rows(w_in[...], w_in_two[...], mine))


def gated_conv_kernel(
    info, part_grad, normal_ref, inverse_ref, gate_gain, taps_ref,
    gate_grad, gate_gain_grad, taps_grad, padded, padded_grad, conv, work,
    *, segments, row_block, taps,
):
    blocks = 3 * WIDTH // CHAN
    spread(part_grad, padded_grad, info, segments, blocks)
    work[...] = normal_ref[...] * gate_gain[...]
    spread(work, padded, info, segments, blocks)
    conv_taps(padded_grad, padded, taps_grad, blocks, row_block, taps)
    conv_rows(padded_grad, taps_ref, conv, blocks, row_block, taps, True)
    unspread(conv, work, info, segments, blocks)
    upstream = work[...]
    normal = normal_ref[...]
    gate_gain_grad[...] = row_sum(upstream * normal)
    gate_grad[...] = normalize_back(upstream, gate_gain[...], normal, inverse_ref[...])


def gated_gate_kernel(
    info, gate_grad, x_ref, gain, before, total_in, w_in, w_in_two,
    stream, gain_grad, send, keep, low, total,
):
    j = pl.program_id(0)
    mine = info[0]

    @pl.when(j == 0)
    def _():
        normal, _ = normalize(x_ref[...])
        low[...] = (normal * gain[...]).astype(LOW)
        total[...] = total_in[...]

    _, slope = gelu_pair(before[...])
    before_grad = (gate_grad[...] * slope).astype(LOW)
    store_halves(
        dot_tn(low[...], before_grad), send, keep, mine, 16, pl.multiple_of(j * 16, 16)
    )
    total[...] += dot_nt(before_grad, join_rows(w_in[...], w_in_two[...], mine))

    @pl.when(j == 2)
    def _():
        normal, inverse = normalize(x_ref[...])
        gain_grad[...] = row_sum(total[...] * normal)
        stream[...] = normalize_back(total[...], gain[...], normal, inverse)


def merge_forward_kernel(
    info, x_ref, attended, gated, taps_ref, valid, weight, weight_two,
    out, merged_low, stat, joined, padded, conv, *, segments, row_block, taps,
):
    blocks = 2 * WIDTH // CHAN
    joined[:, :WIDTH] = attended[...]
    joined[:, WIDTH:] = gated[...]
    spread(joined, padded, info, segments, blocks)
    conv_rows(padded, taps_ref, conv, blocks, row_block, taps, False)
    for c in range(blocks):
        conv[c] += padded[c]
    unspread(conv, joined, info, segments, blocks)
    merged_low[...] = joined[...].astype(LOW)
    part = dot(merged_low[...], join_rows(weight[...], weight_two[...], info[0]))
    after = x_ref[...] + part
    out[...] = after
    v = valid[...]
    stat[0:1, :] = row_sum(after * after * v)
    stat[1:2, :] = row_sum(part * part * v)
    stat[2:, :] = jnp.zeros((6, WIDTH), F32)


def merge_backward_kernel(
    info, grad, attended, gated, merged_low, taps_ref, weight, weight_two,
    attended_grad, gated_grad, taps_grad, send, keep,
    joined, padded, padded_grad, conv, *, segments, row_block, taps,
):
    blocks = 2 * WIDTH // CHAN
    low = grad[...].astype(LOW)
    store_halves(dot_tn(merged_low[...], low), send, keep, info[0], 32, 0)
    joined[:, :WIDTH] = attended[...]
    joined[:, WIDTH:] = gated[...]
    spread(joined, padded, info, segments, blocks)
    joined[...] = dot_nt(low, join_rows(weight[...], weight_two[...], info[0]))
    spread(joined, padded_grad, info, segments, blocks)
    conv_taps(padded_grad, padded, taps_grad, blocks, row_block, taps)
    conv_rows(padded_grad, taps_ref, conv, blocks, row_block, taps, True)
    for c in range(blocks):
        conv[c] += padded_grad[c]
    unspread(conv, joined, info, segments, blocks)
    attended_grad[...] = joined[:, :WIDTH]
    gated_grad[...] = joined[:, WIDTH:]


def hidden_back(h, mine, before, part_low, down, send, keep, start):
    gate = jax.nn.sigmoid(before)
    hidden = (before * gate).astype(LOW)
    hidden_grad = dot_nt(part_low, down)
    before_grad = (hidden_grad * (gate * (1.0 + before * (1.0 - gate)))).astype(LOW)
    down_grad = dot_tn(hidden, part_low).astype(LOW).reshape(8, 64, WIDTH)

    @pl.when(h % 2 == mine)
    def _():
        keep[h // 2, :, start : start + 64, :] = down_grad

    @pl.when(h % 2 != mine)
    def _():
        send[h // 2, :, start : start + 64, :] = down_grad

    return before_grad


def rear_kernel(
    info, x_ref, gain, final_gain, valid, cotangent, up, up_two, down, down_two,
    encoded, stream, gain_grad, final_gain_grad, stat,
    send, keep, low, before, part_grad, stream_grad, total,
):
    step = pl.program_id(0)
    h = jnp.where(step < 4, step, 7 - step)
    up_value = join_rows(up[...], up_two[...], info[0])
    down_value = pick_rows(down[...], down_two[...], h % 2 == info[0])

    @pl.when(step == 0)
    def _():
        normal, _ = normalize(x_ref[...])
        low[...] = (normal * gain[...]).astype(LOW)
        total[...] = jnp.zeros_like(total)

    @pl.when(step < 4)
    def _():
        value = dot(low[...], up_value)
        before[step] = value
        total[...] += dot(silu(value).astype(LOW), down_value)

    @pl.when(step == 3)
    def _():
        part = 0.5 * total[...]
        after = x_ref[...] + part
        v = valid[...]
        stat[0:1, :] = row_sum(after * after * v)
        stat[1:2, :] = row_sum(part * part * v)
        stat[2:, :] = jnp.zeros((6, WIDTH), F32)
        normal, inverse = normalize(after)
        encoded[...] = (normal * final_gain[...] * v).astype(LOW)
        upstream = cotangent[...].astype(F32) * v
        final_gain_grad[...] = row_sum(upstream * normal)
        grad = normalize_back(upstream, final_gain[...], normal, inverse)
        stream_grad[...] = grad
        part_grad[...] = (0.5 * grad).astype(LOW)
        total[...] = jnp.zeros_like(total)

    @pl.when(step >= 4)
    def _():
        before_grad = hidden_back(
            h, info[0], before[h], part_grad[...], down_value, send, keep, 64
        )
        store_halves(
            dot_tn(low[...], before_grad), send, keep, info[0], 16, pl.multiple_of(h * 16, 16)
        )
        total[...] += dot_nt(before_grad, up_value)

    @pl.when(step == 7)
    def _():
        normal, inverse = normalize(x_ref[...])
        gain_grad[...] = row_sum(total[...] * normal)
        stream[...] = stream_grad[...] + normalize_back(total[...], gain[...], normal, inverse)


def front_hidden_kernel(
    info, grad, heads_stream, gated_stream, before, down, down_two,
    stream_out, before_grad, send, keep, part_grad,
):
    h = pl.program_id(0)

    @pl.when(h == 0)
    def _():
        stream_sum = grad[...] + heads_stream[...] + gated_stream[...]
        stream_out[...] = stream_sum
        part_grad[...] = (0.5 * stream_sum).astype(LOW)

    down_value = pick_rows(down[...], down_two[...], h % 2 == info[0])
    before_grad[...] = hidden_back(
        h, info[0], before[...], part_grad[...], down_value, send, keep, 0
    )


def front_input_kernel(
    info, stream_grad, before_grad, x_ref, gain, up, up_two,
    x_grad, send, keep, low, total,
):
    h = pl.program_id(0)

    @pl.when(h == 0)
    def _():
        normal, _ = normalize(x_ref[...].astype(F32))
        low[...] = (normal * gain[...]).astype(LOW)
        total[...] = jnp.zeros_like(total)

    store_halves(
        dot_tn(low[...], before_grad[...]), send, keep, info[0], 16, pl.multiple_of(h * 16, 16)
    )
    total[...] += dot_nt(before_grad[...], join_rows(up[...], up_two[...], info[0]))

    @pl.when(h == 3)
    def _():
        normal, inverse = normalize(x_ref[...].astype(F32))
        gain_grad = row_sum(total[...] * normal).astype(LOW)
        gain_rows = jnp.broadcast_to(gain_grad.reshape(1, 1, 1, WIDTH), (2, 8, 16, WIDTH))
        send[:, :, 64:80, :] = gain_rows
        keep[:, :, 64:80, :] = gain_rows
        x_grad[...] = (
            stream_grad[...] + normalize_back(total[...], gain[...], normal, inverse)
        ).astype(LOW)


def whole(shape):
    return pl.BlockSpec(shape, lambda *_: (0,) * len(shape))


def call(kernel, grid, inputs, outputs, scratch, info, flops=0, after=()):
    in_specs = [
        whole(array.shape) if block is None else pl.BlockSpec(block, index)
        for array, block, index in inputs
    ]
    out_specs = [
        whole(shape) if block is None else pl.BlockSpec(block, index)
        for shape, _, block, index in outputs
    ]
    arrays = [array for array, _, _ in inputs]
    shapes = [jax.ShapeDtypeStruct(shape, kind) for shape, kind, _, _ in outputs]
    moved = sum(array.size * array.dtype.itemsize for array in arrays)
    moved = sum(shape.size * shape.dtype.itemsize for shape in shapes) + min(moved, 1 << 24)
    skipped = len(after)
    name = getattr(kernel, "func", kernel).__name__

    def body(info_ref, *refs):
        kernel(info_ref, *refs[skipped:])

    return pl.pallas_call(
        body,
        grid_spec=pltpu.PrefetchScalarGridSpec(
            num_scalar_prefetch=1,
            grid=grid,
            in_specs=[pl.BlockSpec(memory_space=pl.ANY)] * skipped + in_specs,
            out_specs=out_specs,
            scratch_shapes=scratch,
        ),
        out_shape=shapes,
        name=name,
        compiler_params=pltpu.CompilerParams(vmem_limit_bytes=56 * 1024 * 1024),
        cost_estimate=pl.CostEstimate(flops=flops, bytes_accessed=moved, transcendentals=0),
    )(info, *after, *arrays)


def segment_table(lengths, mine, row_count):
    ends = jnp.cumsum(lengths)
    position = jnp.arange(row_count, dtype=jnp.int32)
    segments = jnp.sum((position[None, :] >= ends[:, None]).astype(jnp.int32), axis=0)
    zero = jnp.zeros((1,), jnp.int32)
    last = jnp.full((1,), row_count, jnp.int32)
    info = jnp.concatenate([jnp.full((1,), mine, jnp.int32), zero, ends, ends, last])
    return segments, info.astype(jnp.int32)


def all_of(*arrays):
    return [(array, None, None) for array in arrays]


def plain(*shapes_and_types):
    return [(shape, kind, None, None) for shape, kind in shapes_and_types]


def halves(rows):
    return plain(((2, 8, rows, WIDTH), LOW)) * 2


def columns(pair, rows, start, index):
    block = (4, 4, rows, WIDTH), lambda *i: (0, 0, start // rows + index(*i), 0)
    return [(array, *block) for array in pair]


def lines(pair, index):
    block = (2, 4, 64, WIDTH), lambda *i: (index(*i) // 2, 0, 1, 0)
    return [(array, *block) for array in pair]


def first(*_):
    return 0


def step(h, _):
    return h


class Layer:
    def __init__(self, features, cotangent, lengths, mine, taps):
        self.features, self.cotangent, self.taps = features, cotangent, taps
        self.tokens = features.shape[0]
        self.count = lengths.shape[0]
        self.segments = self.count + 1
        seg_ids, self.info = segment_table(lengths, mine, self.tokens)
        self.segs_col, self.segs_row = seg_ids[:, None], seg_ids[None, :]
        self.valid = (self.segs_col < self.count).astype(F32)
        self.stream = ((self.tokens, WIDTH), F32)
        self.low = pltpu.VMEM((self.tokens, WIDTH), LOW)
        self.wide = pltpu.VMEM((self.tokens, WIDTH), F32)
        self.spread_rows = self.tokens + GAP * (self.segments + 1)
        self.conv = dict(
            segments=self.segments, row_block=(self.spread_rows - 2 * GAP) // 4, taps=taps
        )
        self.stat = ((8, WIDTH), F32)
        self.vector = ((1, WIDTH), F32)
        self.flop = 2 * self.tokens * WIDTH * WIDTH

    def set_small(self, smaller):
        (
            self.gate_taps, self.merge_taps, self.front_gain, self.heads_gain, self.gated_gain,
            self.gate_gain, self.rear_gain, self.final_gain,
        ) = smaller

    def padded(self, width):
        return pltpu.VMEM((width // CHAN, self.spread_rows, CHAN), F32)

    def tall(self, width, kind=F32):
        return ((self.tokens, width), kind)

    def by_column(self, array, start=0):
        return [(array, (self.tokens, WIDTH), lambda j, _: (0, j + start))]

    def front_forward(self, front, after=()):
        self.front = front
        self.after_front, self.front_before, self.front_stat = call(
            front_forward_kernel,
            (4,),
            all_of(self.features, self.front_gain, self.valid)
            + columns(front, 16, 0, step)
            + lines(front, step),
            plain(self.stream)
            + [(*self.tall(4 * WIDTH), (self.tokens, WIDTH), lambda h, _: (0, h))]
            + plain(self.stat),
            [self.low, self.wide],
            self.info,
            8 * self.flop,
            after,
        )
        return self.front_stat

    def heads_forward(self, heads, after=()):
        self.heads = columns(heads, 48, 144, first) + columns(heads, 16, 192, first)
        self.attended, self.packed, self.mixed = call(
            heads_forward_kernel,
            (1,),
            all_of(self.after_front, self.heads_gain, self.segs_col, self.segs_row) + self.heads,
            plain(self.stream, self.tall(3 * WIDTH, LOW), self.tall(WIDTH, LOW)),
            [],
            self.info,
            16 * self.flop,
            after,
        )
        return self.mixed

    def gated_forward(self, gated, after=()):
        self.gated_weights = gated
        (
            self.gated, self.gated_before, self.gate_normal, self.gate_inverse, self.gate_part,
            self.product,
        ) = call(
            functools.partial(gated_forward_kernel, **self.conv),
            (6,),
            all_of(self.after_front, self.gated_gain, self.gate_gain, self.gate_taps)
            + columns(gated, 16, 0, lambda j, _: (j + 3) % 6)
            + columns(gated, 48, 96, first),
            plain(self.stream)
            + [(*self.tall(6 * WIDTH), (self.tokens, WIDTH), lambda j, _: (0, (j + 3) % 6))]
            + plain(
                self.tall(3 * WIDTH), self.tall(1), self.tall(3 * WIDTH), self.tall(3 * WIDTH, LOW)
            ),
            [self.low, pltpu.VMEM((self.tokens, 3 * WIDTH), F32)] + [self.padded(3 * WIDTH)] * 2,
            self.info,
            36 * self.flop,
            after,
        )
        return self.gate_inverse

    def merge_forward(self, rear, after=()):
        self.rear = rear
        self.merge_weight = columns(rear, 32, 128, first)
        self.after_merge, self.merged_low, self.merge_stat = call(
            functools.partial(merge_forward_kernel, **self.conv),
            (1,),
            all_of(self.after_front, self.attended, self.gated, self.merge_taps, self.valid)
            + self.merge_weight,
            plain(self.stream, self.tall(2 * WIDTH, LOW), self.stat),
            [pltpu.VMEM((self.tokens, 2 * WIDTH), F32)] + [self.padded(2 * WIDTH)] * 2,
            self.info,
            18 * self.flop,
            after,
        )
        return self.merge_stat

    def rear_both(self, after=()):
        def bounce(i, _):
            return jnp.where(i < 4, i, 7 - i)

        (
            self.encoded, self.merge_grad, self.rear_gain_grad, self.final_gain_grad,
            self.rear_stat, *pair,
        ) = call(
            rear_kernel,
            (8,),
            all_of(self.after_merge, self.rear_gain, self.final_gain, self.valid, self.cotangent)
            + columns(self.rear, 16, 0, bounce)
            + lines(self.rear, bounce),
            plain(self.tall(WIDTH, LOW), self.stream, self.vector, self.vector, self.stat)
            + halves(128),
            [self.low, pltpu.VMEM((4, self.tokens, WIDTH), F32), self.low, self.wide, self.wide],
            self.info,
            32 * self.flop,
            after,
        )
        return pair

    def merge_backward(self, after=()):
        self.attended_grad, self.gated_grad, self.merge_taps_grad, *pair = call(
            functools.partial(merge_backward_kernel, **self.conv),
            (1,),
            all_of(
                self.merge_grad, self.attended, self.gated, self.merged_low, self.merge_taps
            )
            + self.merge_weight,
            plain(self.stream, self.stream, ((self.taps + 1, 2 * WIDTH), F32)) + halves(32),
            [pltpu.VMEM((self.tokens, 2 * WIDTH), F32)] + [self.padded(2 * WIDTH)] * 3,
            self.info,
            30 * self.flop,
            after,
        )
        return pair

    def heads_backward(self, after=()):
        self.heads_stream, self.heads_gain_grad, *pair = call(
            heads_backward_kernel,
            (1,),
            all_of(
                self.attended_grad, self.after_front, self.heads_gain, self.segs_col,
                self.segs_row, self.packed, self.mixed,
            )
            + self.heads,
            plain(self.stream, self.vector) + halves(64),
            [self.low, pltpu.VMEM((self.tokens, 3 * WIDTH), LOW), self.low],
            self.info,
            26 * self.flop,
            after,
        )
        return pair

    def gated_linear(self, after=()):
        self.part_grad, self.gated_total, *pair = call(
            gated_linear_kernel,
            (3,),
            all_of(self.gated_grad, self.after_front, self.gated_gain)
            + self.by_column(self.gated_before)
            + self.by_column(self.gate_part)
            + all_of(self.product)
            + columns(self.gated_weights, 16, 0, step)
            + columns(self.gated_weights, 48, 96, first),
            [(*self.tall(3 * WIDTH), (self.tokens, WIDTH), lambda j, _: (0, j))]
            + plain(self.stream)
            + halves(96),
            [self.low, pltpu.VMEM((self.tokens, 3 * WIDTH), F32), self.low],
            self.info,
            14 * self.flop,
            after,
        )
        return pair

    def gated_conv(self, after=()):
        self.gate_grad, self.gate_gain_grad, self.gate_taps_grad = call(
            functools.partial(gated_conv_kernel, **self.conv),
            (1,),
            all_of(
                self.part_grad, self.gate_normal, self.gate_inverse, self.gate_gain,
                self.gate_taps,
            ),
            plain(
                self.tall(3 * WIDTH), ((1, 3 * WIDTH), F32), ((self.taps + 1, 3 * WIDTH), F32)
            ),
            [self.padded(3 * WIDTH)] * 3 + [pltpu.VMEM((self.tokens, 3 * WIDTH), F32)],
            self.info,
            36 * self.flop,
            after,
        )
        return self.gate_gain_grad

    def gated_gate(self, after=()):
        self.gated_stream, self.gated_gain_grad, *pair = call(
            gated_gate_kernel,
            (3,),
            self.by_column(self.gate_grad)
            + all_of(self.after_front, self.gated_gain)
            + self.by_column(self.gated_before, 3)
            + all_of(self.gated_total)
            + columns(self.gated_weights, 16, 0, lambda j, _: j + 3),
            plain(self.stream, self.vector) + halves(48),
            [self.low, self.wide],
            self.info,
            12 * self.flop,
            after,
        )
        return pair

    def front_hidden(self, after=()):
        self.front_grad, self.front_before_grad, *pair = call(
            front_hidden_kernel,
            (4,),
            all_of(self.merge_grad, self.heads_stream, self.gated_stream)
            + self.by_column(self.front_before)
            + lines(self.front, step),
            plain(self.stream)
            + [(*self.tall(4 * WIDTH, LOW), (self.tokens, WIDTH), lambda h, _: (0, h))]
            + halves(64),
            [self.low],
            self.info,
            12 * self.flop,
            after,
        )
        return pair

    def front_input(self, after=()):
        self.features_grad, *pair = call(
            front_input_kernel,
            (4,),
            all_of(self.front_grad)
            + self.by_column(self.front_before_grad)
            + all_of(self.features, self.front_gain)
            + columns(self.front, 16, 0, step),
            plain(self.tall(WIDTH, LOW)) + halves(80),
            [self.low, self.wide],
            self.info,
            12 * self.flop,
            after,
        )
        return pair

    def small_grads(self):
        return (
            self.gate_taps_grad, self.merge_taps_grad, self.heads_gain_grad,
            self.gated_gain_grad, self.rear_gain_grad, self.final_gain_grad, self.gate_gain_grad,
        )

    def stats(self):
        return self.front_stat, self.merge_stat, self.rear_stat


SMALL = 16
STATS = 8


def ring(size, shift):
    return [(i, (i + shift) % size) for i in range(size)]


def pack_kernel(
    info, front_up, front_down, heads_in, heads_out, gated_in, gated_out, merge_out, rear_up,
    rear_down, gate_taps, merge_taps, front_gain, heads_gain, gated_gain, rear_gain, final_gain,
    gate_gain, front, middle, rear, small,
):
    def put(target, start, source):
        rows, width = source.shape
        for q in range(width // WIDTH):
            target[start + rows * q : start + rows * (q + 1), :] = source[
                :, WIDTH * q : WIDTH * (q + 1)
            ]

    put(front, 0, front_up)
    put(front, 64, front_down)
    put(middle, 0, gated_in)
    put(middle, 96, gated_out)
    put(middle, 144, heads_in)
    put(middle, 192, heads_out)
    put(rear, 0, rear_up)
    put(rear, 64, rear_down)
    put(rear, 128, merge_out)
    small[...] = jnp.zeros_like(small)
    for q, source in ((0, gate_taps), (2, merge_taps)):
        value = source[...].astype(F32)
        taps, width = value.shape
        small[0:SMALL, CHAN * q : CHAN * q + width] = value[:SMALL]
        small[0 : taps - SMALL, CHAN * (q + 1) : CHAN * (q + 1) + width] = value[SMALL:]
    start = CHAN
    for source in (front_gain, heads_gain, gated_gain, rear_gain, final_gain, gate_gain):
        width = source.shape[1]
        small[SMALL - 1 :, start : start + width] = source[...].astype(F32)
        start += width
    front[128 : 128 + SMALL, :] = small[...].astype(LOW)


def copy_all(copies):
    for copy in copies:
        copy.start()
    for copy in copies:
        copy.wait()


def place_line_kernel(info, *refs):
    pieces, out, sem = refs[:4], refs[4], refs[5]
    copy_all(
        [
            pltpu.make_async_copy(piece, out.at[chip, info[i]], sem.at[chip, i])
            for chip in range(4)
            for i, piece in enumerate(pieces)
        ]
    )


def place(kernel, pieces, rows, spots, after=()):
    skipped = len(after)

    def body(info, *refs):
        kernel(info, *refs[skipped:])

    anywhere = pl.BlockSpec(memory_space=pl.ANY)
    return pl.pallas_call(
        body,
        grid_spec=pltpu.PrefetchScalarGridSpec(
            num_scalar_prefetch=1,
            grid=(1,),
            in_specs=[anywhere] * skipped + [whole(piece.shape) for piece in pieces],
            out_specs=anywhere,
            scratch_shapes=[pltpu.SemaphoreType.DMA((4, 4))],
        ),
        out_shape=jax.ShapeDtypeStruct((4, 4, rows, WIDTH), LOW),
        name=kernel.__name__,
        cost_estimate=pl.CostEstimate(
            flops=0, bytes_accessed=32 * rows * WIDTH * 2, transcendentals=0
        ),
    )(spots, *after, *pieces)


def line_sends(array):
    return [lax.ppermute(array, "z", ring(4, d)) for d in (1, 2, 3)]


def plane_exchange(array):
    return lax.all_to_all(array, ("x", "y"), 0, 0, tiled=True)


def core_swap(array):
    return lax.ppermute(array, "k", ring(2, 1))


def tie(array, *others):
    return lax.optimization_barrier((array, others))[0]


def unpack_kernel(info, first, second, gate_taps, merge_taps, gains, gate_gain):
    mine = info[0]
    lane = lax.broadcasted_iota(jnp.int32, (SMALL, CHAN), 1)
    lane_row = lane[:1]
    gate_gain[...] = jnp.zeros_like(gate_gain)
    gains[...] = jnp.zeros_like(gains)

    def put(target, rows, value, start, size, lanes):
        block, offset = start // CHAN, start % CHAN
        inside = jnp.logical_and(lanes >= offset, lanes < offset + size)
        window = slice(CHAN * block, CHAN * (block + 1))
        target[rows, window] = jnp.where(inside, value, target[rows, window])
        spill = offset + size - CHAN
        if spill > 0:
            window = slice(CHAN * (block + 1), CHAN * (block + 2))
            target[rows, window] = jnp.where(lanes < spill, value, target[rows, window])

    for i in range(BLOCKS):
        x, core, rest = i // 16, (i // 8) % 2, i % 8
        chip, z = 2 * x + rest % 2, rest // 2
        value = jnp.where(mine == core, first[chip, z], second[chip, z]).astype(F32)
        quads = [value[:, CHAN * q : CHAN * (q + 1)] for q in range(4)]
        start = 48 * i
        for half in range(2):
            rows = slice(SMALL * half, SMALL * (half + 1))
            rolled = pltpu.roll(quads[half], start % CHAN, 1)
            put(gate_taps, rows, rolled, start, 48, lane)
            rolled = pltpu.roll(quads[2 + half], (32 * i) % CHAN, 1)
            put(merge_taps, rows, rolled, 32 * i, 32, lane)
        line = quads[1][SMALL - 1 :]
        for g in range(5):
            rolled = pltpu.roll(line, (16 * i - 16 * g) % CHAN, 1)
            put(gains, slice(g, g + 1), rolled, 16 * i, 16, lane_row)
        rolled = pltpu.roll(line, (48 * i - 80) % CHAN, 1)
        put(gate_gain, slice(0, 1), rolled, 48 * i, 48, lane_row)


def pack_small_kernel(
    info, gate_taps, merge_taps, heads_gain, gated_gain, rear_gain, final_gain, gate_gain,
    front_stat, merge_stat, rear_stat, send, keep, *, count_at,
):
    mine = info[0]
    lane = lax.broadcasted_iota(jnp.int32, (SMALL, CHAN), 1)
    lane_row = lane[:1]
    last = lax.broadcasted_iota(jnp.int32, (SMALL, CHAN), 0) == SMALL - 1
    stats = [
        front_stat[0:1, :], front_stat[1:2, :], merge_stat[0:1, :], rear_stat[0:1, :],
        front_stat[2:3, :], merge_stat[1:2, :], rear_stat[1:2, :],
    ]
    stat_line = jnp.where(lane_row == 7, info[count_at].astype(F32), 0.0)
    for i, stat in enumerate(stats):
        stat_line = jnp.where(lane_row == i, jnp.sum(stat, axis=1, keepdims=True), stat_line)
    rest = stat_line - stat_line.astype(LOW).astype(F32)
    stat_line += pltpu.roll(rest, STATS, 1)

    def take(source, rows, start, size, lanes):
        block, offset = start // CHAN, start % CHAN
        value = source[rows, CHAN * block : CHAN * (block + 1)]
        if offset:
            value = pltpu.roll(value, CHAN - offset, 1)
        if offset + size > CHAN:
            other = source[rows, CHAN * (block + 1) : CHAN * (block + 2)]
            value = jnp.where(lanes < CHAN - offset, value, pltpu.roll(other, CHAN - offset, 1))
        return value

    def quads_of(i):
        halves = [slice(0, SMALL), slice(SMALL, 2 * SMALL)]
        quads = [take(gate_taps, rows, 48 * i, 48, lane) for rows in halves]
        quads += [take(merge_taps, rows, 32 * i, 32, lane) for rows in halves]
        line = pltpu.roll(take(gate_gain, slice(0, 1), 48 * i, 48, lane_row), 80, 1)
        for g, gain in enumerate((heads_gain, gated_gain, rear_gain, final_gain)):
            start = 16 * (g + 1)
            block = gain[:, CHAN * (i // 8) : CHAN * (i // 8 + 1)]
            value = pltpu.roll(block, (start - 16 * i) % CHAN, 1)
            inside = jnp.logical_and(lane_row >= start, lane_row < start + 16)
            line = jnp.where(inside, value, line)
        quads[1] = jnp.where(last, line, quads[1])
        quads[3] = jnp.where(last, stat_line, quads[3])
        return quads

    for i in [*range(8), *range(16, 24)]:
        x, spot = i // 16, i % 8
        pairs = zip(quads_of(i), quads_of(i + 8))
        for q, (low, high) in enumerate(pairs):
            lanes = slice(CHAN * q, CHAN * (q + 1))
            keep[x, spot, :, lanes] = jnp.where(mine == 0, low, high).astype(LOW)
            send[x, spot, :, lanes] = jnp.where(mine == 0, high, low).astype(LOW)


def round_small(total):
    quad = total[:, 3 * CHAN :]
    lane = lax.broadcasted_iota(jnp.int32, quad.shape, 1)
    row = lax.broadcasted_iota(jnp.int32, quad.shape, 0)
    stat = jnp.logical_and(row == SMALL - 1, lane < STATS)
    rest = jnp.where(stat, quad - quad.astype(LOW).astype(F32), 0.0)
    quad = quad + pltpu.roll(rest, STATS, 1)
    return jnp.concatenate([total[:, : 3 * CHAN], quad], axis=1).astype(LOW)


def core_sum_kernel(info, *refs, sizes):
    inputs, out = refs[:-1], refs[-1]
    half = len(inputs) // 2
    keeps, gots = inputs[:half], inputs[half:]
    for chip in range(4):
        x, y = chip // 2, chip % 2
        start = 0
        for keep, got, (rows, small) in zip(keeps, gots, sizes):
            if small:
                total = keep[x, 0, y].astype(F32) + got[x, 0, y].astype(F32)
                out[chip, 0, start : start + rows, :] = round_small(total)
            else:
                out[chip, 0, start : start + rows, :] = keep[x, 0, y] + got[x, 0, y]
            start += rows


def plane_sum_kernel(info, pieces, *outs, sizes):
    for e in range(4):
        zi = lax.rem(info[0] + e, 4)
        start = 0
        for rows in sizes:
            small, rows = rows < 0, abs(rows)
            span = slice(start, start + rows)
            start += rows
            total = sum(pieces[chip, zi, span, :].astype(F32) for chip in range(4))
            if e == 0:
                outs[0][span, :] = total
            elif small:
                outs[e][span, :] = round_small(total)
            else:
                outs[e][span, :] = total.astype(LOW)


def line_sum_kernel(info, keep, one, two, three, *refs, pieces):
    refs = list(refs)
    start = 0
    for rows, what in pieces:
        span = slice(start, start + rows)
        start += rows
        total = keep[span, :]
        for piece in (one, two, three):
            total += piece[span, :].astype(F32)
        if what == "small":
            quads = [total[:, CHAN * q : CHAN * (q + 1)] for q in range(4)]
            gate_taps, merge_taps, heads_gain, gated_gain, rear_gain, final_gain, gate_gain, stats = refs
            gate_taps[0:SMALL, :] = quads[0][:, :48]
            gate_taps[SMALL : 2 * SMALL - 1, :] = quads[1][: SMALL - 1, :48]
            merge_taps[0:SMALL, :] = quads[2][:, :32]
            merge_taps[SMALL : 2 * SMALL - 1, :] = quads[3][: SMALL - 1, :32]
            line = quads[1][SMALL - 1 :, :]
            for g, target in enumerate((heads_gain, gated_gain, rear_gain, final_gain)):
                target[...] = pltpu.roll(line, CHAN - 16 * (g + 1), 1)[:, :16]
            gate_gain[...] = pltpu.roll(line, CHAN - 80, 1)[:, :48]
            line = quads[3][SMALL - 1 :, :]
            line += pltpu.roll(line, CHAN - STATS, 1)
            frames = jnp.sum(line[:, STATS - 1 : STATS])
            stats[...] = jnp.sqrt(line[:, : STATS - 1] / (frames * WIDTH))
        elif what == "gain":
            owner = info[4]
            line = jnp.zeros((1, CHAN), F32)
            for b in range(WIDTH // CHAN):
                block = total[0:1, CHAN * b : CHAN * (b + 1)]
                line = jnp.where(owner // 8 == b, block, line)
            line = pltpu.roll(line, lax.rem(CHAN - 16 * lax.rem(owner, 8), CHAN), 1)
            refs.pop(0)[...] = line[:, :16]
        elif what == "left":
            given, target = refs.pop(0), refs[0]
            target[:, : given.shape[1]] = given[...]
        else:
            shift = 0
            if what == "right":
                target = refs.pop(0)
                shift = target.shape[1] // 2
            else:
                target = refs.pop(0)
            height = target.shape[0]
            for q in range(rows // height):
                lanes = slice(shift + WIDTH * q, shift + WIDTH * (q + 1))
                target[:, lanes] = total[height * q : height * (q + 1), :]


def core_sum(pairs, spots, after=()):
    sizes = [(pair[0].shape[2], pair[0].shape[2] == SMALL) for pair in pairs]
    arrays = [pair[i] for i in (0, 1) for pair in pairs]
    arrays = [array.reshape(2, 4, 2, array.shape[2], WIDTH) for array in arrays]
    total = sum(array.shape[3] for array in arrays) // 2
    (out,) = call(
        functools.partial(core_sum_kernel, sizes=tuple(sizes)),
        (4,),
        [
            (array, (2, 1, 2, array.shape[3], WIDTH), lambda i, _: (0, i, 0, 0, 0))
            for array in arrays
        ],
        [((4, 4, total, WIDTH), LOW, (4, 1, total, WIDTH), lambda i, _: (0, i, 0, 0))],
        [],
        spots,
        after=after,
    )
    return out


def plane_sum(pieces, sizes, spots, after=()):
    total = pieces.shape[2]
    return call(
        functools.partial(plane_sum_kernel, sizes=sizes),
        (1,),
        all_of(pieces),
        plain(((total, WIDTH), F32), *[((total, WIDTH), LOW)] * 3),
        [],
        spots,
        after=after,
    )


def line_sum(sums, pieces, outputs, spots, given=(), after=()):
    own, rest = sums
    return call(
        functools.partial(line_sum_kernel, pieces=pieces),
        (1,),
        all_of(own, *rest, *given),
        plain(*[(shape, F32) for shape in outputs]),
        [],
        spots,
        after=after,
    )


def line_swap(sums):
    return sums[0], [lax.ppermute(array, "z", ring(4, d)) for d, array in zip((1, 2, 3), sums[1:])]


def pack_small(layer, mine_info, count, after=()):
    return call(
        functools.partial(pack_small_kernel, count_at=1 + 2 * count),
        (1,),
        all_of(*layer.small_grads(), *layer.stats()),
        plain(*[((2, 8, SMALL, WIDTH), LOW)] * 2),
        [],
        mine_info,
        after=after,
    )


def unpack_small(front, mine):
    block = (4, 4, SMALL, WIDTH), lambda *_: (0, 0, 8, 0)
    gate_taps, merge_taps, gains, gate_full = call(
        unpack_kernel,
        (1,),
        [(array, *block) for array in front],
        plain(
            ((32, 3 * WIDTH), F32), ((32, 2 * WIDTH), F32), ((8, WIDTH), F32), ((1, 3 * WIDTH), F32)
        ),
        [],
        mine.reshape(1),
    )
    lines = [gains[g : g + 1] for g in range(5)]
    return gate_taps, merge_taps, lines[0], lines[1], lines[2], gate_full, lines[3], lines[4]


def grid_device(
    features, cotangent, lengths, front_up, front_down, heads_input, heads_output, gated_input,
    gated_output, merge_output, rear_up, rear_down, gate_kernel, merge_kernel, front_gain,
    heads_gain, gated_gain, gate_gain, rear_gain, final_gain,
):
    x, k, z, y = (lax.axis_index(name) for name in ("x", "k", "z", "y"))
    places = [lax.rem(place, 4) for place in (z, z + 3, z + 2, z + 1)]
    places.append(((x * 2 + k) * 4 + z) * 2 + y)
    spots = jnp.stack([place.astype(jnp.int32) for place in places])
    mine = k.astype(jnp.int32)
    layer = Layer(features, cotangent, lengths[0], mine, gate_kernel.shape[0])

    front, middle, rear = call(
        pack_kernel,
        (1,),
        all_of(
            front_up, front_down, heads_input, heads_output, gated_input, gated_output,
            merge_output, rear_up, rear_down, gate_kernel, merge_kernel,
            *[
                gain.reshape(1, -1)
                for gain in (front_gain, heads_gain, gated_gain, rear_gain, final_gain, gate_gain)
            ],
        ),
        plain(((144, WIDTH), LOW), ((208, WIDTH), LOW), ((160, WIDTH), LOW)),
        [pltpu.VMEM((SMALL, WIDTH), F32)],
        spots,
    )
    front_four = place(place_line_kernel, [front] + line_sends(front), 144, spots)
    front = plane_exchange(front_four)
    middle = tie(middle, front_four)
    middle_four = place(place_line_kernel, [middle] + line_sends(middle), 208, spots)
    front = tie(front, middle_four)
    middle = plane_exchange(tie(middle_four, front))
    rear = tie(rear, front)
    rear_lines = line_sends(rear)
    front = front, core_swap(front)
    layer.set_small(unpack_small(front, mine))
    mark = layer.front_forward(front)
    rear_four = place(place_line_kernel, [rear] + rear_lines, 160, spots, after=(mark,))
    middle = tie(middle, rear_four)
    rear = plane_exchange(tie(rear_four, middle))
    middle = middle, core_swap(middle)
    mark = layer.heads_forward(middle)
    mark = layer.gated_forward(middle, after=(mark,))
    rear = tie(rear, mark)
    rear = rear, core_swap(rear)
    layer.merge_forward(rear)

    wide = ((32, None), (48, "half"), (48, None), (48, None), (16, None))
    last = ((48, "right"), (64, None), (16, "small"))
    send, rear_keep = layer.rear_both()
    rear_got = core_swap(send)
    merge_send, merge_keep = layer.merge_backward()
    rear_four = core_sum([(rear_keep, rear_got)], spots, after=(layer.attended_grad,))
    merge_got = core_swap(merge_send)
    rear_plane = plane_exchange(rear_four)
    send, heads_keep = layer.heads_backward(after=(rear_four,))
    heads_got = core_swap(send)
    send, gated_keep = layer.gated_linear(after=(layer.heads_stream,))
    gated_got = core_swap(send)
    rear_sums = plane_sum(rear_plane, (128,), spots, after=(layer.gated_total,))
    wide_four = core_sum(
        [(merge_keep, merge_got), (gated_keep, gated_got), (heads_keep, heads_got)], spots,
        after=(rear_sums[0],),
    )
    rear_sums = line_swap(rear_sums)
    wide_plane = plane_exchange(tie(wide_four, rear_plane))
    layer.gated_conv(after=(wide_four,))
    send, gate_keep = layer.gated_gate()
    gate_got = core_swap(send)
    small_send, small_keep = pack_small(layer, layer.info, lengths.shape[1])
    small_got = core_swap(small_send)
    rear_up_grad, rear_down_grad = line_sum(
        rear_sums, ((64, None), (64, None)), (rear_up.shape, rear_down.shape), spots,
        after=(small_send,),
    )
    send, down_keep = layer.front_hidden(after=(small_send, rear_up_grad))
    down_got = core_swap(send)
    wide_sums = plane_sum(wide_plane, (192,), spots, after=(layer.front_grad,))
    last_four = core_sum(
        [(gate_keep, gate_got), (down_keep, down_got), (small_keep, small_got)], spots,
        after=(wide_sums[0],),
    )
    wide_sums = line_swap(wide_sums)
    last_plane = plane_exchange(tie(last_four, wide_plane))
    send, up_keep = layer.front_input(after=(last_four,))
    up_got = core_swap(send)
    half_shape = (gated_input.shape[0], gated_input.shape[1] // 2)
    merge_output_grad, gated_left_grad, gated_output_grad, heads_input_grad, heads_output_grad = (
        line_sum(
            wide_sums,
            ((32, None), (48, None), (48, None), (48, None), (16, None)),
            (
                merge_output.shape, half_shape, gated_output.shape, heads_input.shape,
                heads_output.shape,
            ),
            spots,
            after=(layer.features_grad,),
        )
    )
    front_four = core_sum([(up_keep, up_got)], spots, after=(merge_output_grad,))
    last_sums = plane_sum(last_plane, (48, 64, -SMALL), spots, after=(front_four,))
    last_sums = line_swap(last_sums)
    front_plane = plane_exchange(tie(front_four, last_plane))
    vector = (1, front_gain.shape[0])
    (
        gated_input_grad, front_down_grad, gate_kernel_grad, merge_kernel_grad, heads_gain_grad,
        gated_gain_grad, rear_gain_grad, final_gain_grad, gate_gain_grad, statistics,
    ) = line_sum(
        last_sums,
        ((0, "left"), (48, "right"), (64, None), (16, "small")),
        (
            gated_input.shape, front_down.shape, gate_kernel.shape, merge_kernel.shape,
            vector, vector, vector, vector, (1, gate_gain.shape[0]), (1, STATS - 1),
        ),
        spots,
        given=(gated_left_grad,),
    )
    front_sums = plane_sum(front_plane, (80,), spots, after=(statistics,))
    front_up_grad, front_gain_grad = line_sum(
        line_swap(front_sums), ((64, None), (16, "gain")), (front_up.shape, vector), spots
    )
    return (
        layer.encoded, layer.features_grad, front_up_grad, front_down_grad, heads_input_grad,
        heads_output_grad, gated_input_grad, gated_output_grad, merge_output_grad, rear_up_grad,
        rear_down_grad, gate_kernel_grad, merge_kernel_grad, front_gain_grad[0],
        heads_gain_grad[0], gated_gain_grad[0], gate_gain_grad[0], rear_gain_grad[0],
        final_gain_grad[0], statistics[0],
    )


def pack_rows(shard):
    rows, columns = shard.shape
    pieces = shard.reshape(rows, columns // WIDTH, WIDTH).transpose(1, 0, 2)
    return pieces.reshape(rows * columns // WIDTH, WIDTH)


def pad_lines(flat):
    rows = -(-flat.shape[-1] // (WIDTH * 16)) * 16
    spare = [(0, 0)] * (flat.ndim - 1) + [(0, rows * WIDTH - flat.shape[-1])]
    return jnp.pad(flat, spare).reshape(flat.shape[:-1] + (rows, WIDTH))


def to_owners(weight):
    rows, columns = weight.shape
    pieces = weight.reshape(BLOCKS, rows // BLOCKS, columns // WIDTH, WIDTH)
    pieces = pieces.transpose(0, 2, 1, 3).reshape(2, 2, 4, 2, -1, WIDTH)
    pieces = pieces.transpose(1, 0, 3, 2, 4, 5)
    return pieces.reshape(2, 4, 4, -1, WIDTH)


def from_owners(halves, rows, columns):
    send, keep = halves
    pieces = jnp.stack([keep, send], axis=1)
    pieces = pieces.reshape(BLOCKS, columns // WIDTH, rows // BLOCKS, WIDTH)
    return pieces.transpose(0, 2, 1, 3).reshape(rows, columns)


def any_device(features, cotangent, lengths, *shards, axes):
    count = lax.axis_size(axes)
    matrices, smaller = shards[:9], shards[9:]
    packed = [pack_rows(element) for element in matrices]
    packed.append(pad_lines(jnp.concatenate([element.reshape(-1) for element in smaller])))
    gathered = lax.all_gather(jnp.concatenate(packed), axes, axis=0)
    weights = []
    start = 0
    for element, piece in zip(matrices, packed):
        rows, columns = element.shape
        window = gathered[:, start : start + piece.shape[0]]
        start += piece.shape[0]
        window = window.reshape(count, columns // WIDTH, rows, WIDTH).transpose(0, 2, 1, 3)
        weights.append(to_owners(window.reshape(count * rows, columns)))
    flat = gathered[:, start:].reshape(count, -1).astype(F32)
    lines = []
    start = 0
    for element in smaller:
        window = flat[:, start : start + element.size]
        start += element.size
        if element.ndim == 2:
            window = window.reshape((count,) + element.shape).transpose(1, 0, 2)
            window = window.reshape(element.shape[0], -1)
            lines.append(jnp.pad(window, ((0, 1), (0, 0))))
        else:
            lines.append(window.reshape(1, -1))
    up, down, h_in, h_out, g_in, g_out, m_out, r_up, r_down = weights

    def chunk(*members):
        return tuple(jnp.concatenate([member[i] for member in members], axis=2) for i in (0, 1))

    front = chunk(up, down)
    rear = chunk(r_up, r_down, m_out)
    layer = Layer(features, cotangent, lengths[0], jnp.int32(0), smaller[0].shape[0])
    layer.set_small(lines)
    layer.front_forward(front)
    middle = chunk(g_in, g_out, h_in, h_out)
    layer.heads_forward(middle)
    layer.gated_forward(middle)
    layer.merge_forward(rear)
    rear = layer.rear_both()
    merge = layer.merge_backward()
    left = layer.gated_linear()
    heads = layer.heads_backward()
    layer.gated_conv()
    right = layer.gated_gate()
    front_down_halves = layer.front_hidden()
    front_up_halves = layer.front_input()

    def part(pair, start, stop):
        return tuple(array[:, :, start:stop] for array in pair)

    gated_halves = tuple(
        jnp.concatenate([one[:, :, :48], two], axis=2) for one, two in zip(left, right)
    )
    ordered = (
        part(front_up_halves, 0, 64), front_down_halves, part(heads, 0, 48), part(heads, 48, 64),
        gated_halves, part(left, 48, 96), merge, part(rear, 0, 64), part(rear, 64, 128),
    )
    front_gain = front_up_halves[1][0, 0, 64].astype(F32)
    small_grads = layer.small_grads()
    pieces = []
    for element, halves in zip(matrices, ordered):
        rows, columns = element.shape
        full = from_owners(halves, rows * count, columns)
        full = full.reshape(count, rows, columns // WIDTH, WIDTH).transpose(0, 2, 1, 3)
        pieces.append(full.reshape(count, -1, WIDTH))
    gate_taps, merge_taps, heads_gain, gated_gain, rear_gain, final_gain, gate_gain = small_grads
    small_full = (gate_taps, merge_taps, front_gain, heads_gain, gated_gain, gate_gain, rear_gain, final_gain)
    flat = []
    for element, full in zip(smaller, small_full):
        if element.ndim == 2:
            full = full[: element.shape[0]].reshape(element.shape[0], count, -1).transpose(1, 0, 2)
        flat.append(full.reshape(count, -1))
    pieces.append(pad_lines(jnp.concatenate(flat, axis=1).astype(LOW)))
    summed = lax.psum_scatter(jnp.concatenate(pieces, axis=1), axes, scatter_dimension=0)
    outputs = []
    start = 0
    for element, piece in zip(matrices, pieces):
        rows, columns = element.shape
        window = summed[start : start + piece.shape[1]].astype(F32)
        start += piece.shape[1]
        window = window.reshape(columns // WIDTH, rows, WIDTH).transpose(1, 0, 2)
        outputs.append(window.reshape(rows, columns))
    flat = summed[start:].reshape(-1).astype(F32)
    start = 0
    for element in smaller:
        outputs.append(flat[start : start + element.size].reshape(element.shape))
        start += element.size
    front_stat, merge_stat, rear_stat = layer.stats()
    squares = jnp.stack(
        [
            front_stat[0], front_stat[1], merge_stat[0], rear_stat[0], front_stat[2],
            merge_stat[1], rear_stat[1],
        ]
    )
    totals = lax.psum(
        jnp.append(jnp.sum(squares, axis=1), jnp.sum(lengths).astype(F32)), axes
    )
    statistics = jnp.sqrt(totals[:7] / (totals[7] * features.shape[1]))
    return (layer.encoded, layer.features_grad) + tuple(outputs) + (statistics,)


def solution(mesh):
    body = grid_device
    axes = ("x", "k", "z", "y")
    if mesh.devices.shape == (4, 8):
        mesh = Mesh(mesh.devices.reshape(2, 2, 4, 2), axes)
    else:
        axes = tuple(mesh.axis_names)
        body = functools.partial(any_device, axes=axes)
    rows, columns, vector = P(axes, None), P(None, axes), P(axes)
    weights = (rows,) * 9 + (columns,) * 2 + (vector,) * 6
    return jax.shard_map(
        body,
        mesh=mesh,
        in_specs=(rows, rows, rows) + weights,
        out_specs=(rows, rows) + weights + (P(),),
        check_vma=False,
    )
```

```python
import functools

import jax
import jax.numpy as jnp
from jax import lax
from jax.experimental import pallas as pl
from jax.experimental.pallas import tpu as pltpu
from jax.sharding import Mesh, PartitionSpec as P

HEADS = 8
EPSILON = 1e-05
NEGATIVE = -1000000000.0
TILE = 8
GAP = 16
CHAN = 128
PLACE = 1
OWNER = 5
SEG = 6
WIDTH = 512
BLOCKS = 32
F32 = jnp.float32
LOW = jnp.bfloat16


def dot(left, right):
    return jnp.dot(left, right, preferred_element_type=F32)


def dot_tn(left, right):
    return lax.dot_general(left, right, (((0,), (0,)), ((), ())), preferred_element_type=F32)


def dot_nt(left, right):
    return lax.dot_general(left, right, (((1,), (1,)), ((), ())), preferred_element_type=F32)


def normalize(values):
    centred = values - jnp.mean(values, axis=-1, keepdims=True)
    variance = jnp.mean(centred * centred, axis=-1, keepdims=True)
    inverse = lax.rsqrt(variance + EPSILON)
    return centred * inverse, inverse


def normalize_back(upstream, gain, normal, inverse):
    scaled = upstream * gain
    mean_scaled = jnp.mean(scaled, axis=-1, keepdims=True)
    mean_cross = jnp.mean(scaled * normal, axis=-1, keepdims=True)
    return inverse * (scaled - mean_scaled - normal * mean_cross)


def part_of(index):
    return slice(None), pl.ds(pl.multiple_of(index * WIDTH, WIDTH), WIDTH)


def row_sum(values):
    return jnp.sum(values, axis=0, keepdims=True)


GELU_A = 0.7978845608028654
GELU_B = 0.044715


def gelu(v):
    return 0.5 * v * (1.0 + jnp.tanh(GELU_A * (v + GELU_B * v * v * v)))


def gelu_pair(v):
    square = v * v
    bend = jnp.tanh(GELU_A * (v + GELU_B * square * v))
    value = 0.5 * v * (1.0 + bend)
    slope = 0.5 * (1.0 + bend) + 0.5 * v * (1.0 - bend * bend) * (
        GELU_A * (1.0 + 3.0 * GELU_B * square)
    )
    return value, slope


def silu(v):
    return v * jax.nn.sigmoid(v)


def store_halves(value, send, keep, mine, rows, start):
    parts = value.astype(LOW).reshape(2, 2, 8, rows, WIDTH)

    @pl.when(mine == 0)
    def _():
        keep[:, :, pl.ds(start, rows), :] = parts[:, 0]
        send[:, :, pl.ds(start, rows), :] = parts[:, 1]

    @pl.when(mine == 1)
    def _():
        keep[:, :, pl.ds(start, rows), :] = parts[:, 1]
        send[:, :, pl.ds(start, rows), :] = parts[:, 0]


def join_rows(first, second, mine):
    cores = jnp.where(mine == 0, first, second), jnp.where(mine == 0, second, first)
    return jnp.concatenate(
        [core[2 * x + y, z] for x in (0, 1) for core in cores for z in range(4) for y in (0, 1)]
    )


def pick_rows(first, second, flag):
    chosen = jnp.where(flag, first, second)
    return jnp.concatenate([chosen[y, z] for z in range(4) for y in (0, 1)])


def visits(info, segments, body):
    for s in range(segments):
        begin, end = info[SEG + s], info[SEG + segments + s]

        def visit(i, _, s=s, begin=begin, end=end):
            row = i * TILE + lax.broadcasted_iota(jnp.int32, (TILE, CHAN), 0)
            inside = jnp.logical_and(row >= begin, row < end)
            body(s, pl.multiple_of(i * TILE, TILE), inside)
            return 0

        lax.fori_loop(begin // TILE, (end + TILE - 1) // TILE, visit, 0)


def spread(source, padded, info, segments, blocks):
    padded[...] = jnp.zeros_like(padded)

    def body(s, base, inside):
        for c in range(blocks):
            value = source[pl.ds(base, TILE), c * CHAN : (c + 1) * CHAN]
            padded[c, pl.ds(base + GAP * (s + 1), TILE), :] = jnp.where(inside, value, 0.0)

    visits(info, segments, body)


def unspread(padded, target, info, segments, blocks):
    def body(s, base, inside):
        for c in range(blocks):
            lanes = slice(c * CHAN, (c + 1) * CHAN)
            value = padded[c, pl.ds(base + GAP * (s + 1), TILE), :]
            target[pl.ds(base, TILE), lanes] = jnp.where(
                inside, value, target[pl.ds(base, TILE), lanes]
            )

    visits(info, segments, body)


def conv_rows(padded, kernel, out, blocks, row_block, taps, flip):
    half = (taps - 1) // 2
    steps = (padded.shape[1] - 2 * GAP) // row_block

    def body(step, _):
        c = step // steps
        base = (step % steps) * row_block + GAP
        lanes = pl.ds(pl.multiple_of(c * CHAN, CHAN), CHAN)
        total = jnp.zeros((row_block, CHAN), F32)
        for j in range(taps):
            shift = half - j if flip else j - half
            total += kernel[pl.ds(j, 1), lanes] * padded[c, pl.ds(base + shift, row_block), :]
        out[c, pl.ds(pl.multiple_of(base, TILE), row_block), :] = total
        return 0

    lax.fori_loop(0, blocks * steps, body, 0)


def conv_taps(padded_grad, padded, out, blocks, row_block, taps):
    half = (taps - 1) // 2
    steps = (padded.shape[1] - 2 * GAP) // row_block
    tiles = row_block // TILE

    def block(c, _):
        lanes = pl.ds(pl.multiple_of(c * CHAN, CHAN), CHAN)

        def body(step, sums):
            base = pl.multiple_of(step * row_block + GAP, TILE)
            grad = padded_grad[c, pl.ds(base, row_block), :]
            new = []
            for j in range(taps):
                term = grad * padded[c, pl.ds(base + j - half, row_block), :]
                new.append(sums[j] + jnp.sum(term.reshape(tiles, TILE, CHAN), axis=0))
            return tuple(new)

        zero = jnp.zeros((TILE, CHAN), F32)
        sums = lax.fori_loop(0, steps, body, (zero,) * taps)
        for j in range(taps):
            out[pl.ds(j, 1), lanes] = row_sum(sums[j])
        return 0

    lax.fori_loop(0, blocks, block, 0)


def front_forward_kernel(
    info, x_ref, gain, valid, up, up_two, down, down_two, out, before_out, stat, low, total
):
    h = pl.program_id(0)
    mine = info[0]
    up_value = join_rows(up[...], up_two[...], mine)
    down_value = pick_rows(down[...], down_two[...], h % 2 == mine)

    @pl.when(h == 0)
    def _():
        normal, _ = normalize(x_ref[...].astype(F32))
        low[...] = (normal * gain[...]).astype(LOW)
        total[...] = jnp.zeros_like(total)

    before = dot(low[...], up_value)
    before_out[...] = before
    total[...] += dot(silu(before).astype(LOW), down_value)

    @pl.when(h == pl.num_programs(0) - 1)
    def _():
        x = x_ref[...].astype(F32)
        part = 0.5 * total[...]
        after = x + part
        out[...] = after
        v = valid[...]
        stat[0:1, :] = row_sum(x * x * v)
        stat[1:2, :] = row_sum(after * after * v)
        stat[2:3, :] = row_sum(part * part * v)
        stat[3:, :] = jnp.zeros((5, WIDTH), F32)


def head_masks(segs_col, segs_row):
    allowed = segs_col == segs_row
    lane = lax.broadcasted_iota(jnp.int32, (1, CHAN), 1)
    return allowed, (lane < CHAN // 2, lane >= CHAN // 2)


def head_probs(query, key, allowed, scale):
    scores = jnp.where(allowed, dot_nt(query, key) * scale, NEGATIVE)
    exponent = jnp.exp(scores - jnp.max(scores, axis=-1, keepdims=True))
    return exponent / jnp.sum(exponent, axis=-1, keepdims=True)


def heads_forward(
    info, low, segs_col, segs_row, w_in, w_in_two, w_out, w_out_two, attended, packed, mixed,
):
    mine = info[0]
    scale = (WIDTH // HEADS) ** -0.5
    for q in range(3):
        rows = slice(16 * q, 16 * (q + 1))
        weight = join_rows(w_in[:, :, rows, :], w_in_two[:, :, rows, :], mine)
        packed[:, WIDTH * q : WIDTH * (q + 1)] = dot(low, weight).astype(LOW)
    allowed, halves = head_masks(segs_col[...], segs_row[...])

    def pair(p, _):
        lanes = [
            pl.ds(pl.multiple_of(WIDTH * q + CHAN * p, CHAN), CHAN) for q in range(3)
        ]
        query, key, value = (packed[:, lane] for lane in lanes)
        parts = []
        for half in halves:
            probs = head_probs(jnp.where(half, query, 0), key, allowed, scale)
            parts.append(dot(probs.astype(LOW), value))
        mixed[:, lanes[0]] = jnp.where(halves[0], parts[0], parts[1]).astype(LOW)
        return 0

    lax.fori_loop(0, HEADS // 2, pair, 0)
    attended[...] = dot(mixed[...], join_rows(w_out[...], w_out_two[...], mine))


def heads_backward(
    info, grad, x_ref, gain, segs_col, segs_row, packed, mixed, w_in, w_in_two, w_out, w_out_two,
    stream, gain_grad, send, keep, mixed_grad, packed_grad, low,
):
    scale = (WIDTH // HEADS) ** -0.5
    mine = info[0]
    attended_low = grad[...].astype(LOW)
    store_halves(dot_tn(mixed[...], attended_low), send, keep, mine, 16, 144)
    mixed_grad[...] = dot_nt(attended_low, join_rows(w_out[...], w_out_two[...], mine)).astype(LOW)
    normal, inverse = normalize(x_ref[...])
    low[...] = (normal * gain[...]).astype(LOW)
    allowed, halves = head_masks(segs_col[...], segs_row[...])

    def pair(p, _):
        lanes = [
            pl.ds(pl.multiple_of(WIDTH * q + CHAN * p, CHAN), CHAN) for q in range(3)
        ]
        query, key, value = (packed[:, lane] for lane in lanes)
        upstream = mixed_grad[:, lanes[0]]
        parts = []
        for half in halves:
            probs = head_probs(jnp.where(half, query, 0), key, allowed, scale)
            probs_grad = dot_nt(jnp.where(half, upstream, 0), value)
            value_grad = dot_tn(probs.astype(LOW), upstream)
            inner = jnp.sum(probs_grad * probs, axis=-1, keepdims=True)
            score_grad = (probs * (probs_grad - inner)).astype(LOW)
            query_grad = dot(score_grad, key) * scale
            key_grad = dot_tn(score_grad, query) * scale
            parts.append((query_grad, key_grad, value_grad))
        for q in range(3):
            packed_grad[:, lanes[q]] = jnp.where(halves[0], parts[0][q], parts[1][q]).astype(LOW)
        return 0

    lax.fori_loop(0, HEADS // 2, pair, 0)
    total = jnp.zeros(x_ref.shape, F32)
    for q in range(3):
        rows = slice(16 * q, 16 * (q + 1))
        weight = join_rows(w_in[:, :, rows, :], w_in_two[:, :, rows, :], mine)
        piece = packed_grad[:, WIDTH * q : WIDTH * (q + 1)]
        store_halves(dot_tn(low[...], piece), send, keep, mine, 16, 96 + 16 * q)
        total += dot_nt(piece, weight)
    gain_grad[...] = row_sum(total * normal)
    stream[...] = normalize_back(total, gain[...], normal, inverse)


def branches_forward_kernel(
    info, x_ref, heads_gain, segs_col, segs_row, w_heads, w_heads_two, w_mix, w_mix_two,
    gain, gate_gain, taps_ref, w_in, w_in_two, w_out, w_out_two, attended, packed, mixed,
    gated, before_out, normal_out, inverse_out, part_out, product,
    low, act, padded, conv, *, segments, row_block, taps,
):
    j = pl.program_id(0)
    thirds = WIDTH * 3

    @pl.when(j == 0)
    def _():
        normal, _ = normalize(x_ref[...])
        low[...] = (normal * gain[...]).astype(LOW)
        heads_forward(
            info, (normal * heads_gain[...]).astype(LOW), segs_col, segs_row, w_heads,
            w_heads_two, w_mix, w_mix_two, attended, packed, mixed,
        )

    before = dot(low[...], join_rows(w_in[...], w_in_two[...], info[0]))
    before_out[...] = before
    value = gelu(before)

    @pl.when(j < 3)
    def _():
        act[:, pl.ds(pl.multiple_of(j * WIDTH, WIDTH), WIDTH)] = value

    @pl.when(j == 2)
    def _():
        normal, inverse = normalize(act[...])
        normal_out[...] = normal
        inverse_out[...] = inverse
        act[...] = normal * gate_gain[...]
        blocks = thirds // CHAN
        spread(act, padded, info, segments, blocks)
        conv_rows(padded, taps_ref, conv, blocks, row_block, taps, False)
        unspread(conv, part_out, info, segments, blocks)

    @pl.when(j >= 3)
    def _():
        lanes = pl.ds(pl.multiple_of((j - 3) * WIDTH, WIDTH), WIDTH)
        product[:, lanes] = (value * part_out[:, lanes]).astype(LOW)

    @pl.when(j == 5)
    def _():
        gated[...] = dot(product[...], join_rows(w_out[...], w_out_two[...], info[0]))


def branches_backward_kernel(
    info, attended_grad, x_ref, heads_gain, segs_col, segs_row, packed, mixed, w_heads,
    w_heads_two, w_mix, w_mix_two, grad, gain, before, part, product, w_in, w_in_two, w_out,
    w_out_two,
    stream, heads_gain_grad, part_grad, total_out, send, keep, low, product_grad, gated_low,
    mixed_grad, packed_grad,
):
    j = pl.program_id(0)
    mine = info[0]

    @pl.when(j == 0)
    def _():
        heads_backward(
            info, attended_grad, x_ref, heads_gain, segs_col, segs_row, packed, mixed, w_heads,
            w_heads_two, w_mix, w_mix_two, stream, heads_gain_grad, send, keep, mixed_grad,
            packed_grad, low,
        )
        normal, _ = normalize(x_ref[...])
        low[...] = (normal * gain[...]).astype(LOW)
        total_out[...] = jnp.zeros_like(total_out)
        gated_low[...] = grad[...].astype(LOW)
        store_halves(dot_tn(product[...], gated_low[...]), send, keep, mine, 48, 48)
        product_grad[...] = dot_nt(gated_low[...], join_rows(w_out[...], w_out_two[...], mine))

    value, slope = gelu_pair(before[...])
    lanes = pl.ds(pl.multiple_of(j * WIDTH, WIDTH), WIDTH)
    upstream = product_grad[:, lanes]
    part_grad[...] = upstream * value
    before_grad = (upstream * part[...] * slope).astype(LOW)
    store_halves(
        dot_tn(low[...], before_grad), send, keep, mine, 16, pl.multiple_of(j * 16, 16)
    )
    total_out[...] += dot_nt(before_grad, join_rows(w_in[...], w_in_two[...], mine))


def gated_conv(
    info, part_grad, normal_ref, inverse_ref, gate_gain, taps_ref,
    gate_gain_grad, taps_grad, padded, padded_grad, conv, work, segments, row_block, taps,
):
    blocks = 3 * WIDTH // CHAN
    spread(part_grad, padded_grad, info, segments, blocks)
    work[...] = normal_ref[...] * gate_gain[...]
    spread(work, padded, info, segments, blocks)
    conv_taps(padded_grad, padded, taps_grad, blocks, row_block, taps)
    conv_rows(padded_grad, taps_ref, conv, blocks, row_block, taps, True)
    unspread(conv, work, info, segments, blocks)
    upstream = work[...]
    normal = normal_ref[...]
    gate_gain_grad[...] = row_sum(upstream * normal)
    work[...] = normalize_back(upstream, gate_gain[...], normal, inverse_ref[...])


def gated_gate_kernel(
    info, part_grad, normal_ref, inverse_ref, gate_gain, taps_ref, x_ref, gain, before, total_in,
    w_in, w_in_two,
    stream, gain_grad, gate_gain_grad, taps_grad, send, keep,
    low, total, padded, padded_grad, conv, work, *, segments, row_block, taps,
):
    j = pl.program_id(0)
    mine = info[0]

    @pl.when(j == 0)
    def _():
        gated_conv(
            info, part_grad, normal_ref, inverse_ref, gate_gain, taps_ref, gate_gain_grad,
            taps_grad, padded, padded_grad, conv, work, segments, row_block, taps,
        )
        normal, _ = normalize(x_ref[...])
        low[...] = (normal * gain[...]).astype(LOW)
        total[...] = total_in[...]

    _, slope = gelu_pair(before[...])
    before_grad = (work[part_of(j)] * slope).astype(LOW)
    store_halves(
        dot_tn(low[...], before_grad), send, keep, mine, 16, pl.multiple_of(j * 16, 16)
    )
    total[...] += dot_nt(before_grad, join_rows(w_in[...], w_in_two[...], mine))

    @pl.when(j == 2)
    def _():
        normal, inverse = normalize(x_ref[...])
        gain_grad[...] = row_sum(total[...] * normal)
        stream[...] = normalize_back(total[...], gain[...], normal, inverse)


def conv_add(padded, conv, taps_ref, blocks, row_block, taps, flip):
    conv_rows(padded, taps_ref, conv, blocks, row_block, taps, flip)
    for c in range(blocks):
        conv[c] += padded[c]


def hidden_back(h, mine, before, part_low, down, send, keep, start):
    gate = jax.nn.sigmoid(before)
    hidden = (before * gate).astype(LOW)
    hidden_grad = dot_nt(part_low, down)
    before_grad = (hidden_grad * (gate * (1.0 + before * (1.0 - gate)))).astype(LOW)
    down_grad = dot_tn(hidden, part_low).astype(LOW).reshape(8, 64, WIDTH)

    @pl.when(h % 2 == mine)
    def _():
        keep[h // 2, :, start : start + 64, :] = down_grad

    @pl.when(h % 2 != mine)
    def _():
        send[h // 2, :, start : start + 64, :] = down_grad

    return before_grad


def merge_rear_kernel(
    info, x_ref, attended, gated, taps_ref, weight, weight_two, gain, final_gain, valid, cotangent,
    up, up_two, down, down_two,
    encoded, stream, gain_grad, final_gain_grad, stat, attended_grad, gated_grad, taps_grad,
    send, keep, merge_send, merge_keep,
    low, before, part_grad, stream_grad, total, middle, joined, joined_low, padded, padded_grad,
    conv, *, segments, row_block, taps,
):
    step = pl.program_id(0)
    h = jnp.where(step < 4, step, 7 - step)
    up_value = join_rows(up[...], up_two[...], info[0])
    down_value = pick_rows(down[...], down_two[...], h % 2 == info[0])
    blocks = 2 * WIDTH // CHAN

    @pl.when(step == 0)
    def _():
        joined[:, :WIDTH] = attended[...]
        joined[:, WIDTH:] = gated[...]
        spread(joined, padded, info, segments, blocks)
        conv_add(padded, conv, taps_ref, blocks, row_block, taps, False)
        unspread(conv, joined, info, segments, blocks)
        joined_low[...] = joined[...].astype(LOW)
        part = dot(joined_low[...], join_rows(weight[...], weight_two[...], info[0]))
        after = x_ref[...] + part
        middle[...] = after
        v = valid[...]
        stat[0:1, :] = row_sum(after * after * v)
        stat[1:2, :] = row_sum(part * part * v)
        normal, _ = normalize(after)
        low[...] = (normal * gain[...]).astype(LOW)
        total[...] = jnp.zeros_like(total)

    @pl.when(step < 4)
    def _():
        value = dot(low[...], up_value)
        before[step] = value
        total[...] += dot(silu(value).astype(LOW), down_value)

    @pl.when(step == 3)
    def _():
        part = 0.5 * total[...]
        after = middle[...] + part
        v = valid[...]
        stat[2:3, :] = row_sum(after * after * v)
        stat[3:4, :] = row_sum(part * part * v)
        stat[4:, :] = jnp.zeros((4, WIDTH), F32)
        normal, inverse = normalize(after)
        encoded[...] = (normal * final_gain[...] * v).astype(LOW)
        upstream = cotangent[...].astype(F32) * v
        final_gain_grad[...] = row_sum(upstream * normal)
        grad = normalize_back(upstream, final_gain[...], normal, inverse)
        stream_grad[...] = grad
        part_grad[...] = (0.5 * grad).astype(LOW)
        total[...] = jnp.zeros_like(total)

    @pl.when(step >= 4)
    def _():
        before_grad = hidden_back(
            h, info[0], before[h], part_grad[...], down_value, send, keep, 64
        )
        store_halves(
            dot_tn(low[...], before_grad), send, keep, info[0], 16, pl.multiple_of(h * 16, 16)
        )
        total[...] += dot_nt(before_grad, up_value)

    @pl.when(step == 7)
    def _():
        normal, inverse = normalize(middle[...])
        gain_grad[...] = row_sum(total[...] * normal)
        grad = stream_grad[...] + normalize_back(total[...], gain[...], normal, inverse)
        stream[...] = grad
        grad_low = grad.astype(LOW)
        store_halves(dot_tn(joined_low[...], grad_low), merge_send, merge_keep, info[0], 32, 0)
        joined[...] = dot_nt(grad_low, join_rows(weight[...], weight_two[...], info[0]))
        spread(joined, padded_grad, info, segments, blocks)
        conv_taps(padded_grad, padded, taps_grad, blocks, row_block, taps)
        conv_add(padded_grad, conv, taps_ref, blocks, row_block, taps, True)
        unspread(conv, joined, info, segments, blocks)
        attended_grad[...] = joined[:, :WIDTH]
        gated_grad[...] = joined[:, WIDTH:]


def front_hidden_kernel(
    info, grad, heads_stream, gated_stream, before, down, down_two,
    stream_out, before_grad, send, keep, part_grad,
):
    h = pl.program_id(0)

    @pl.when(h == 0)
    def _():
        stream_sum = grad[...] + heads_stream[...] + gated_stream[...]
        stream_out[...] = stream_sum
        part_grad[...] = (0.5 * stream_sum).astype(LOW)

    down_value = pick_rows(down[...], down_two[...], h % 2 == info[0])
    before_grad[...] = hidden_back(
        h, info[0], before[...], part_grad[...], down_value, send, keep, 0
    )


def front_input_kernel(
    info, stream_grad, before_grad, x_ref, gain, up, up_two,
    x_grad, send, keep, low, total,
):
    h = pl.program_id(0)

    @pl.when(h == 0)
    def _():
        normal, _ = normalize(x_ref[...].astype(F32))
        low[...] = (normal * gain[...]).astype(LOW)
        total[...] = jnp.zeros_like(total)

    store_halves(
        dot_tn(low[...], before_grad[...]), send, keep, info[0], 16, pl.multiple_of(h * 16, 16)
    )
    total[...] += dot_nt(before_grad[...], join_rows(up[...], up_two[...], info[0]))

    @pl.when(h == 3)
    def _():
        normal, inverse = normalize(x_ref[...].astype(F32))
        gain_grad = row_sum(total[...] * normal).astype(LOW)
        gain_rows = jnp.broadcast_to(gain_grad.reshape(1, 1, 1, WIDTH), (2, 8, 16, WIDTH))
        send[:, :, 64:80, :] = gain_rows
        keep[:, :, 64:80, :] = gain_rows
        x_grad[...] = (
            stream_grad[...] + normalize_back(total[...], gain[...], normal, inverse)
        ).astype(LOW)


def whole(shape):
    return pl.BlockSpec(shape, lambda *_: (0,) * len(shape))


def call(kernel, grid, inputs, outputs, scratch, info, flops=0, after=()):
    in_specs = [
        whole(array.shape) if block is None else pl.BlockSpec(block, index)
        for array, block, index in inputs
    ]
    out_specs = [
        whole(shape) if block is None else pl.BlockSpec(block, index)
        for shape, _, block, index in outputs
    ]
    arrays = [array for array, _, _ in inputs]
    shapes = [jax.ShapeDtypeStruct(shape, kind) for shape, kind, _, _ in outputs]
    moved = sum(array.size * array.dtype.itemsize for array in arrays)
    moved = sum(shape.size * shape.dtype.itemsize for shape in shapes) + min(moved, 1 << 24)
    skipped = len(after)
    name = getattr(kernel, "func", kernel).__name__

    def body(info_ref, *refs):
        kernel(info_ref, *refs[skipped:])

    return pl.pallas_call(
        body,
        grid_spec=pltpu.PrefetchScalarGridSpec(
            num_scalar_prefetch=1,
            grid=grid,
            in_specs=[pl.BlockSpec(memory_space=pl.ANY)] * skipped + in_specs,
            out_specs=out_specs,
            scratch_shapes=scratch,
        ),
        out_shape=shapes,
        name=name,
        compiler_params=pltpu.CompilerParams(vmem_limit_bytes=56 * 1024 * 1024),
        cost_estimate=pl.CostEstimate(flops=flops, bytes_accessed=moved, transcendentals=0),
    )(info, *after, *arrays)


def segment_table(lengths, spots, row_count):
    ends = jnp.cumsum(lengths)
    position = jnp.arange(row_count, dtype=jnp.int32)
    segments = jnp.sum((position[None, :] >= ends[:, None]).astype(jnp.int32), axis=0)
    zero = jnp.zeros((1,), jnp.int32)
    last = jnp.full((1,), row_count, jnp.int32)
    return segments, jnp.concatenate([spots, zero, ends, ends, last]).astype(jnp.int32)


def all_of(*arrays):
    return [(array, None, None) for array in arrays]


def plain(*shapes_and_types):
    return [(shape, kind, None, None) for shape, kind in shapes_and_types]


def halves(rows):
    return plain(((2, 8, rows, WIDTH), LOW)) * 2


def columns(pair, rows, start, index):
    block = (4, 4, rows, WIDTH), lambda *i: (0, 0, start // rows + index(*i), 0)
    return [(array, *block) for array in pair]


def lines(pair, index):
    block = (2, 4, 64, WIDTH), lambda *i: (index(*i) // 2, 0, 1, 0)
    return [(array, *block) for array in pair]


def first(*_):
    return 0


def step(h, _):
    return h


class Layer:
    def __init__(self, features, cotangent, lengths, spots, taps):
        self.features, self.cotangent, self.taps = features, cotangent, taps
        self.tokens = features.shape[0]
        self.count = lengths.shape[0]
        self.segments = self.count + 1
        seg_ids, self.info = segment_table(lengths, spots, self.tokens)
        self.segs_col, self.segs_row = seg_ids[:, None], seg_ids[None, :]
        self.valid = (self.segs_col < self.count).astype(F32)
        self.stream = ((self.tokens, WIDTH), F32)
        self.low = pltpu.VMEM((self.tokens, WIDTH), LOW)
        self.wide = pltpu.VMEM((self.tokens, WIDTH), F32)
        self.spread_rows = self.tokens + GAP * (self.segments + 1)
        self.conv = dict(
            segments=self.segments, row_block=(self.spread_rows - 2 * GAP) // 4, taps=taps
        )
        self.stat = ((8, WIDTH), F32)
        self.vector = ((1, WIDTH), F32)
        self.flop = 2 * self.tokens * WIDTH * WIDTH

    def set_small(self, smaller):
        (
            self.gate_taps, self.merge_taps, self.front_gain, self.heads_gain, self.gated_gain,
            self.gate_gain, self.rear_gain, self.final_gain,
        ) = smaller

    def padded(self, width):
        return pltpu.VMEM((width // CHAN, self.spread_rows, CHAN), F32)

    def tall(self, width, kind=F32):
        return ((self.tokens, width), kind)

    def by_column(self, array, start=0):
        return [(array, (self.tokens, WIDTH), lambda j, _: (0, j + start))]

    def front_forward(self, front, after=()):
        self.front = front
        self.after_front, self.front_before, self.front_stat = call(
            front_forward_kernel,
            (4,),
            all_of(self.features, self.front_gain, self.valid)
            + columns(front, 16, 0, step)
            + lines(front, step),
            plain(self.stream)
            + [(*self.tall(4 * WIDTH), (self.tokens, WIDTH), lambda h, _: (0, h))]
            + plain(self.stat),
            [self.low, self.wide],
            self.info,
            8 * self.flop,
            after,
        )
        return self.front_stat

    def branches_forward(self, middle, after=()):
        self.middle = middle
        self.heads = columns(middle, 48, 144, first) + columns(middle, 16, 192, first)
        (
            self.attended, self.packed, self.mixed, self.gated, self.gated_before,
            self.gate_normal, self.gate_inverse, self.gate_part, self.product,
        ) = call(
            functools.partial(branches_forward_kernel, **self.conv),
            (6,),
            all_of(self.after_front, self.heads_gain, self.segs_col, self.segs_row)
            + self.heads
            + all_of(self.gated_gain, self.gate_gain, self.gate_taps)
            + columns(middle, 16, 0, lambda j, _: (j + 3) % 6)
            + columns(middle, 48, 96, first),
            plain(self.stream, self.tall(3 * WIDTH, LOW), self.tall(WIDTH, LOW), self.stream)
            + [(*self.tall(6 * WIDTH), (self.tokens, WIDTH), lambda j, _: (0, (j + 3) % 6))]
            + plain(
                self.tall(3 * WIDTH), self.tall(1), self.tall(3 * WIDTH), self.tall(3 * WIDTH, LOW)
            ),
            [self.low, pltpu.VMEM((self.tokens, 3 * WIDTH), F32)] + [self.padded(3 * WIDTH)] * 2,
            self.info,
            52 * self.flop,
            after,
        )
        return self.gate_inverse

    def merge_rear(self, rear, after=()):
        def bounce(i, _):
            return jnp.where(i < 4, i, 7 - i)

        padded = self.padded(2 * WIDTH)
        (
            self.encoded, self.merge_grad, self.rear_gain_grad, self.final_gain_grad,
            self.rear_stat, self.attended_grad, self.gated_grad, self.merge_taps_grad, *pair,
        ) = call(
            functools.partial(merge_rear_kernel, **self.conv),
            (8,),
            all_of(self.after_front, self.attended, self.gated, self.merge_taps)
            + columns(rear, 32, 128, first)
            + all_of(self.rear_gain, self.final_gain, self.valid, self.cotangent)
            + columns(rear, 16, 0, bounce)
            + lines(rear, bounce),
            plain(
                self.tall(WIDTH, LOW), self.stream, self.vector, self.vector, self.stat,
                self.stream, self.stream, ((self.taps + 1, 2 * WIDTH), F32),
            )
            + halves(128)
            + halves(32),
            [
                self.low, pltpu.VMEM((4, self.tokens, WIDTH), F32), self.low, self.wide, self.wide,
                self.wide, pltpu.VMEM((self.tokens, 2 * WIDTH), F32),
                pltpu.VMEM((self.tokens, 2 * WIDTH), LOW), padded, padded, padded,
            ],
            self.info,
            80 * self.flop,
            after,
        )
        return pair

    def branches_backward(self, after=()):
        self.heads_stream, self.heads_gain_grad, self.part_grad, self.gated_total, *pair = call(
            branches_backward_kernel,
            (3,),
            all_of(
                self.attended_grad, self.after_front, self.heads_gain, self.segs_col,
                self.segs_row, self.packed, self.mixed,
            )
            + self.heads
            + all_of(self.gated_grad, self.gated_gain)
            + self.by_column(self.gated_before)
            + self.by_column(self.gate_part)
            + all_of(self.product)
            + columns(self.middle, 16, 0, step)
            + columns(self.middle, 48, 96, first),
            plain(self.stream, self.vector)
            + [(*self.tall(3 * WIDTH), (self.tokens, WIDTH), lambda j, _: (0, j))]
            + plain(self.stream)
            + halves(160),
            [
                self.low, pltpu.VMEM((self.tokens, 3 * WIDTH), F32), self.low, self.low,
                pltpu.VMEM((self.tokens, 3 * WIDTH), LOW),
            ],
            self.info,
            40 * self.flop,
            after,
        )
        return pair

    def gated_gate(self, after=()):
        padded = self.padded(3 * WIDTH)
        (
            self.gated_stream, self.gated_gain_grad, self.gate_gain_grad, self.gate_taps_grad,
            *pair,
        ) = call(
            functools.partial(gated_gate_kernel, **self.conv),
            (3,),
            all_of(
                self.part_grad, self.gate_normal, self.gate_inverse, self.gate_gain,
                self.gate_taps, self.after_front, self.gated_gain,
            )
            + self.by_column(self.gated_before, 3)
            + all_of(self.gated_total)
            + columns(self.middle, 16, 0, lambda j, _: j + 3),
            plain(
                self.stream, self.vector, ((1, 3 * WIDTH), F32),
                ((self.taps + 1, 3 * WIDTH), F32),
            )
            + halves(48),
            [
                self.low, self.wide, padded, padded, padded,
                pltpu.VMEM((self.tokens, 3 * WIDTH), F32),
            ],
            self.info,
            48 * self.flop,
            after,
        )
        return pair

    def front_hidden(self, after=()):
        self.front_grad, self.front_before_grad, *pair = call(
            front_hidden_kernel,
            (4,),
            all_of(self.merge_grad, self.heads_stream, self.gated_stream)
            + self.by_column(self.front_before)
            + lines(self.front, step),
            plain(self.stream)
            + [(*self.tall(4 * WIDTH, LOW), (self.tokens, WIDTH), lambda h, _: (0, h))]
            + halves(64),
            [self.low],
            self.info,
            12 * self.flop,
            after,
        )
        return pair

    def front_input(self, after=()):
        self.features_grad, *pair = call(
            front_input_kernel,
            (4,),
            all_of(self.front_grad)
            + self.by_column(self.front_before_grad)
            + all_of(self.features, self.front_gain)
            + columns(self.front, 16, 0, step),
            plain(self.tall(WIDTH, LOW)) + halves(80),
            [self.low, self.wide],
            self.info,
            12 * self.flop,
            after,
        )
        return pair

    def small_grads(self):
        return (
            self.gate_taps_grad, self.merge_taps_grad, self.heads_gain_grad,
            self.gated_gain_grad, self.rear_gain_grad, self.final_gain_grad, self.gate_gain_grad,
        )

    def stats(self):
        return self.front_stat, self.rear_stat


SMALL = 16
STATS = 8


def ring(size, shift):
    return [(i, (i + shift) % size) for i in range(size)]


def pack_kernel(
    info, front_up, front_down, heads_in, heads_out, gated_in, gated_out, merge_out, rear_up,
    rear_down, gate_taps, merge_taps, front_gain, heads_gain, gated_gain, rear_gain, final_gain,
    gate_gain, front, middle, rear, small,
):
    def put(target, start, source):
        rows, width = source.shape
        for q in range(width // WIDTH):
            target[start + rows * q : start + rows * (q + 1), :] = source[
                :, WIDTH * q : WIDTH * (q + 1)
            ]

    put(front, 0, front_up)
    put(front, 64, front_down)
    put(middle, 0, gated_in)
    put(middle, 96, gated_out)
    put(middle, 144, heads_in)
    put(middle, 192, heads_out)
    put(rear, 0, rear_up)
    put(rear, 64, rear_down)
    put(rear, 128, merge_out)
    small[...] = jnp.zeros_like(small)
    for q, source in ((0, gate_taps), (2, merge_taps)):
        value = source[...].astype(F32)
        taps, width = value.shape
        small[0:SMALL, CHAN * q : CHAN * q + width] = value[:SMALL]
        small[0 : taps - SMALL, CHAN * (q + 1) : CHAN * (q + 1) + width] = value[SMALL:]
    start = CHAN
    for source in (front_gain, heads_gain, gated_gain, rear_gain, final_gain, gate_gain):
        width = source.shape[1]
        small[SMALL - 1 :, start : start + width] = source[...].astype(F32)
        start += width
    front[128 : 128 + SMALL, :] = small[...].astype(LOW)


def copy_all(copies):
    for copy in copies:
        copy.start()
    for copy in copies:
        copy.wait()


def place_line_kernel(info, *refs):
    pieces, out, sem = refs[:4], refs[4], refs[5]
    copy_all(
        [
            pltpu.make_async_copy(piece, out.at[chip, info[PLACE + i]], sem.at[chip, i])
            for chip in range(4)
            for i, piece in enumerate(pieces)
        ]
    )


def place(kernel, pieces, rows, spots, after=()):
    skipped = len(after)

    def body(info, *refs):
        kernel(info, *refs[skipped:])

    anywhere = pl.BlockSpec(memory_space=pl.ANY)
    return pl.pallas_call(
        body,
        grid_spec=pltpu.PrefetchScalarGridSpec(
            num_scalar_prefetch=1,
            grid=(1,),
            in_specs=[anywhere] * skipped + [whole(piece.shape) for piece in pieces],
            out_specs=anywhere,
            scratch_shapes=[pltpu.SemaphoreType.DMA((4, 4))],
        ),
        out_shape=jax.ShapeDtypeStruct((4, 4, rows, WIDTH), LOW),
        name=kernel.__name__,
        cost_estimate=pl.CostEstimate(
            flops=0, bytes_accessed=32 * rows * WIDTH * 2, transcendentals=0
        ),
    )(spots, *after, *pieces)


def line_sends(array):
    return [lax.ppermute(array, "z", ring(4, d)) for d in (1, 2, 3)]


def plane_exchange(array):
    return lax.all_to_all(array, ("x", "y"), 0, 0, tiled=True)


def core_swap(array):
    return lax.ppermute(array, "k", ring(2, 1))


def tie(array, *others):
    return lax.optimization_barrier((array, others))[0]


def unpack_kernel(info, first, second, gate_taps, merge_taps, gains, gate_gain):
    mine = info[0]
    lane = lax.broadcasted_iota(jnp.int32, (SMALL, CHAN), 1)
    lane_row = lane[:1]
    gate_gain[...] = jnp.zeros_like(gate_gain)
    gains[...] = jnp.zeros_like(gains)

    def put(target, rows, value, start, size, lanes):
        block, offset = start // CHAN, start % CHAN
        inside = jnp.logical_and(lanes >= offset, lanes < offset + size)
        window = slice(CHAN * block, CHAN * (block + 1))
        target[rows, window] = jnp.where(inside, value, target[rows, window])
        spill = offset + size - CHAN
        if spill > 0:
            window = slice(CHAN * (block + 1), CHAN * (block + 2))
            target[rows, window] = jnp.where(lanes < spill, value, target[rows, window])

    for i in range(BLOCKS):
        x, core, rest = i // 16, (i // 8) % 2, i % 8
        chip, z = 2 * x + rest % 2, rest // 2
        value = jnp.where(mine == core, first[chip, z], second[chip, z]).astype(F32)
        quads = [value[:, CHAN * q : CHAN * (q + 1)] for q in range(4)]
        start = 48 * i
        for half in range(2):
            rows = slice(SMALL * half, SMALL * (half + 1))
            rolled = pltpu.roll(quads[half], start % CHAN, 1)
            put(gate_taps, rows, rolled, start, 48, lane)
            rolled = pltpu.roll(quads[2 + half], (32 * i) % CHAN, 1)
            put(merge_taps, rows, rolled, 32 * i, 32, lane)
        line = quads[1][SMALL - 1 :]
        for g in range(5):
            rolled = pltpu.roll(line, (16 * i - 16 * g) % CHAN, 1)
            put(gains, slice(g, g + 1), rolled, 16 * i, 16, lane_row)
        rolled = pltpu.roll(line, (48 * i - 80) % CHAN, 1)
        put(gate_gain, slice(0, 1), rolled, 48 * i, 48, lane_row)


def pack_small_kernel(
    info, gate_taps, merge_taps, heads_gain, gated_gain, rear_gain, final_gain, gate_gain,
    front_stat, rear_stat, send, keep, *, count_at,
):
    mine = info[0]
    lane = lax.broadcasted_iota(jnp.int32, (SMALL, CHAN), 1)
    lane_row = lane[:1]
    last = lax.broadcasted_iota(jnp.int32, (SMALL, CHAN), 0) == SMALL - 1
    stats = [
        front_stat[0:1, :], front_stat[1:2, :], rear_stat[0:1, :], rear_stat[2:3, :],
        front_stat[2:3, :], rear_stat[1:2, :], rear_stat[3:4, :],
    ]
    stat_line = jnp.where(lane_row == 7, info[count_at].astype(F32), 0.0)
    for i, stat in enumerate(stats):
        stat_line = jnp.where(lane_row == i, jnp.sum(stat, axis=1, keepdims=True), stat_line)
    rest = stat_line - stat_line.astype(LOW).astype(F32)
    stat_line += pltpu.roll(rest, STATS, 1)

    def take(source, rows, start, size, lanes):
        block, offset = start // CHAN, start % CHAN
        value = source[rows, CHAN * block : CHAN * (block + 1)]
        if offset:
            value = pltpu.roll(value, CHAN - offset, 1)
        if offset + size > CHAN:
            other = source[rows, CHAN * (block + 1) : CHAN * (block + 2)]
            value = jnp.where(lanes < CHAN - offset, value, pltpu.roll(other, CHAN - offset, 1))
        return value

    def quads_of(i):
        halves = [slice(0, SMALL), slice(SMALL, 2 * SMALL)]
        quads = [take(gate_taps, rows, 48 * i, 48, lane) for rows in halves]
        quads += [take(merge_taps, rows, 32 * i, 32, lane) for rows in halves]
        line = pltpu.roll(take(gate_gain, slice(0, 1), 48 * i, 48, lane_row), 80, 1)
        for g, gain in enumerate((heads_gain, gated_gain, rear_gain, final_gain)):
            start = 16 * (g + 1)
            block = gain[:, CHAN * (i // 8) : CHAN * (i // 8 + 1)]
            value = pltpu.roll(block, (start - 16 * i) % CHAN, 1)
            inside = jnp.logical_and(lane_row >= start, lane_row < start + 16)
            line = jnp.where(inside, value, line)
        quads[1] = jnp.where(last, line, quads[1])
        quads[3] = jnp.where(last, stat_line, quads[3])
        return quads

    for i in [*range(8), *range(16, 24)]:
        x, spot = i // 16, i % 8
        pairs = zip(quads_of(i), quads_of(i + 8))
        for q, (low, high) in enumerate(pairs):
            lanes = slice(CHAN * q, CHAN * (q + 1))
            keep[x, spot, :, lanes] = jnp.where(mine == 0, low, high).astype(LOW)
            send[x, spot, :, lanes] = jnp.where(mine == 0, high, low).astype(LOW)


def round_small(total):
    quad = total[:, 3 * CHAN :]
    lane = lax.broadcasted_iota(jnp.int32, quad.shape, 1)
    row = lax.broadcasted_iota(jnp.int32, quad.shape, 0)
    stat = jnp.logical_and(row == SMALL - 1, lane < STATS)
    rest = jnp.where(stat, quad - quad.astype(LOW).astype(F32), 0.0)
    quad = quad + pltpu.roll(rest, STATS, 1)
    return jnp.concatenate([total[:, : 3 * CHAN], quad], axis=1).astype(LOW)


def core_sum_kernel(info, *refs, sizes):
    inputs, out = refs[:-1], refs[-1]
    half = len(inputs) // 2
    keeps, gots = inputs[:half], inputs[half:]

    def one(z, _):
        for chip in range(4):
            x, spot = chip // 2, 2 * z + chip % 2
            start = 0
            for keep, got, (rows, small) in zip(keeps, gots, sizes):
                span = slice(start, start + rows)
                start += rows
                if small:
                    total = keep[x, spot].astype(F32) + got[x, spot].astype(F32)
                    out[chip, z, span, :] = round_small(total)
                else:
                    out[chip, z, span, :] = keep[x, spot] + got[x, spot]
        return 0

    lax.fori_loop(0, 4, one, 0)


def plane_sum_kernel(info, pieces, *outs, sizes):
    for e in range(4):
        zi = lax.rem(info[PLACE] + e, 4)
        start = 0
        for rows in sizes:
            small, rows = rows < 0, abs(rows)
            span = slice(start, start + rows)
            start += rows
            total = sum(pieces[chip, zi, span, :].astype(F32) for chip in range(4))
            if e == 0:
                outs[0][span, :] = total
            elif small:
                outs[e][span, :] = round_small(total)
            else:
                outs[e][span, :] = total.astype(LOW)


def line_sum_kernel(info, keep, one, two, three, *refs, pieces):
    refs = list(refs)
    start = 0
    for rows, what in pieces:
        span = slice(start, start + rows)
        start += rows
        total = keep[span, :]
        for piece in (one, two, three):
            total += piece[span, :].astype(F32)
        if what == "small":
            quads = [total[:, CHAN * q : CHAN * (q + 1)] for q in range(4)]
            gate_taps, merge_taps, heads_gain, gated_gain, rear_gain, final_gain, gate_gain, stats = refs
            gate_taps[0:SMALL, :] = quads[0][:, :48]
            gate_taps[SMALL : 2 * SMALL - 1, :] = quads[1][: SMALL - 1, :48]
            merge_taps[0:SMALL, :] = quads[2][:, :32]
            merge_taps[SMALL : 2 * SMALL - 1, :] = quads[3][: SMALL - 1, :32]
            line = quads[1][SMALL - 1 :, :]
            for g, target in enumerate((heads_gain, gated_gain, rear_gain, final_gain)):
                target[...] = pltpu.roll(line, CHAN - 16 * (g + 1), 1)[:, :16]
            gate_gain[...] = pltpu.roll(line, CHAN - 80, 1)[:, :48]
            line = quads[3][SMALL - 1 :, :]
            line += pltpu.roll(line, CHAN - STATS, 1)
            frames = jnp.sum(line[:, STATS - 1 : STATS])
            stats[...] = jnp.sqrt(line[:, : STATS - 1] / (frames * WIDTH))
        elif what == "gain":
            owner = info[OWNER]
            line = jnp.zeros((1, CHAN), F32)
            for b in range(WIDTH // CHAN):
                block = total[0:1, CHAN * b : CHAN * (b + 1)]
                line = jnp.where(owner // 8 == b, block, line)
            line = pltpu.roll(line, lax.rem(CHAN - 16 * lax.rem(owner, 8), CHAN), 1)
            refs.pop(0)[...] = line[:, :16]
        elif what == "left":
            given, target = refs.pop(0), refs[0]
            target[:, : given.shape[1]] = given[...]
        else:
            shift = 0
            if what == "right":
                target = refs.pop(0)
                shift = target.shape[1] // 2
            else:
                target = refs.pop(0)
            height = target.shape[0]
            for q in range(rows // height):
                lanes = slice(shift + WIDTH * q, shift + WIDTH * (q + 1))
                target[:, lanes] = total[height * q : height * (q + 1), :]


def run(tasks, info, after=()):
    counts = [(len(inputs), len(outputs)) for _, inputs, outputs in tasks]

    def tasks_kernel(info_ref, *refs):
        total = sum(count for count, _ in counts)
        ins, outs = list(refs[:total]), list(refs[total:])
        for (kernel, _, _), (taken, given) in zip(tasks, counts):
            kernel(info_ref, *ins[:taken], *outs[:given])
            del ins[:taken], outs[:given]

    results = call(
        tasks_kernel,
        (1,),
        all_of(*[array for _, inputs, _ in tasks for array in inputs]),
        plain(*[output for _, _, outputs in tasks for output in outputs]),
        [],
        info,
        after=after,
    )
    grouped = []
    for _, given in counts:
        grouped.append(results[:given])
        results = results[given:]
    return grouped


def core_sum(pairs):
    sizes = tuple((pair[0].shape[2], pair[0].shape[2] == SMALL) for pair in pairs)
    total = sum(rows for rows, _ in sizes)
    return (
        functools.partial(core_sum_kernel, sizes=sizes),
        [pair[i] for i in (0, 1) for pair in pairs],
        [((4, 4, total, WIDTH), LOW)],
    )


def plane_sum(pieces, sizes):
    total = pieces.shape[2]
    return (
        functools.partial(plane_sum_kernel, sizes=sizes),
        [pieces],
        [((total, WIDTH), F32)] + [((total, WIDTH), LOW)] * 3,
    )


def line_sum(sums, pieces, outputs, given=()):
    own, rest = sums
    return (
        functools.partial(line_sum_kernel, pieces=pieces),
        [own, *rest, *given],
        [(shape, F32) for shape in outputs],
    )


def line_swap(sums):
    return sums[0], [lax.ppermute(array, "z", ring(4, d)) for d, array in zip((1, 2, 3), sums[1:])]


def pack_small(layer, count):
    return (
        functools.partial(pack_small_kernel, count_at=SEG + 2 * count),
        [*layer.small_grads(), *layer.stats()],
        [((2, 8, SMALL, WIDTH), LOW)] * 2,
    )


def unpack_small(front, info):
    block = (4, 4, SMALL, WIDTH), lambda *_: (0, 0, 8, 0)
    gate_taps, merge_taps, gains, gate_full = call(
        unpack_kernel,
        (1,),
        [(array, *block) for array in front],
        plain(
            ((32, 3 * WIDTH), F32), ((32, 2 * WIDTH), F32), ((8, WIDTH), F32), ((1, 3 * WIDTH), F32)
        ),
        [],
        info,
    )
    lines = [gains[g : g + 1] for g in range(5)]
    return gate_taps, merge_taps, lines[0], lines[1], lines[2], gate_full, lines[3], lines[4]


def grid_device(
    features, cotangent, lengths, front_up, front_down, heads_input, heads_output, gated_input,
    gated_output, merge_output, rear_up, rear_down, gate_kernel, merge_kernel, front_gain,
    heads_gain, gated_gain, gate_gain, rear_gain, final_gain,
):
    x, k, z, y = (lax.axis_index(name) for name in ("x", "k", "z", "y"))
    places = [k] + [lax.rem(place, 4) for place in (z, z + 3, z + 2, z + 1)]
    places.append(((x * 2 + k) * 4 + z) * 2 + y)
    spots = jnp.stack([place.astype(jnp.int32) for place in places])
    layer = Layer(features, cotangent, lengths[0], spots, gate_kernel.shape[0])
    info = layer.info

    front, middle, rear = call(
        pack_kernel,
        (1,),
        all_of(
            front_up, front_down, heads_input, heads_output, gated_input, gated_output,
            merge_output, rear_up, rear_down, gate_kernel, merge_kernel,
            *[
                gain.reshape(1, -1)
                for gain in (front_gain, heads_gain, gated_gain, rear_gain, final_gain, gate_gain)
            ],
        ),
        plain(((144, WIDTH), LOW), ((208, WIDTH), LOW), ((160, WIDTH), LOW)),
        [pltpu.VMEM((SMALL, WIDTH), F32)],
        spots,
    )
    front_four = place(place_line_kernel, [front] + line_sends(front), 144, info)
    front = plane_exchange(front_four)
    middle = tie(middle, front_four)
    middle_four = place(place_line_kernel, [middle] + line_sends(middle), 208, info)
    front = tie(front, middle_four)
    middle = plane_exchange(tie(middle_four, front))
    rear = tie(rear, front)
    rear_lines = line_sends(rear)
    front = front, core_swap(front)
    layer.set_small(unpack_small(front, info))
    mark = layer.front_forward(front)
    rear_four = place(place_line_kernel, [rear] + rear_lines, 160, info, after=(mark,))
    middle = tie(middle, rear_four)
    rear = plane_exchange(tie(rear_four, middle))
    middle = middle, core_swap(middle)
    mark = layer.branches_forward(middle)
    rear = tie(rear, mark)
    rear = rear, core_swap(rear)

    send, rear_keep, merge_send, merge_keep = layer.merge_rear(rear)
    rear_got = core_swap(send)
    ((rear_four,),) = run([core_sum([(rear_keep, rear_got)])], info)
    merge_got = core_swap(tie(merge_send, rear_got))
    rear_plane = plane_exchange(rear_four)
    send, wide_keep = layer.branches_backward(after=(rear_four,))
    wide_got = core_swap(tie(send, rear_plane))
    (rear_sums,) = run([plane_sum(rear_plane, (128,))], info, after=(layer.gated_total,))
    ((wide_four,),) = run(
        [core_sum([(merge_keep, merge_got), (wide_keep, wide_got)])], info,
        after=(rear_sums[0],),
    )
    rear_sums = line_swap(rear_sums)
    wide_plane = plane_exchange(tie(wide_four, rear_plane))
    send, gate_keep = layer.gated_gate(after=(wide_four,))
    gate_got = core_swap(send)
    ((small_send, small_keep),) = run(
        [pack_small(layer, lengths.shape[1])], info, after=rear_sums[1]
    )
    small_got = core_swap(small_send)
    send, down_keep = layer.front_hidden(after=(small_send,))
    down_got = core_swap(tie(send, wide_plane))
    (wide_sums,) = run([plane_sum(wide_plane, (192,))], info, after=(layer.front_grad,))
    ((last_four,),) = run(
        [
            core_sum([(gate_keep, gate_got), (down_keep, down_got), (small_keep, small_got)]),
        ],
        info,
        after=(wide_sums[0],),
    )
    wide_sums = line_swap(wide_sums)
    last_plane = plane_exchange(tie(last_four, wide_plane))
    send, up_keep = layer.front_input(after=(last_four, *wide_sums[1]))
    up_got = core_swap(send)
    ((front_four,),) = run([core_sum([(up_keep, up_got)])], info)
    half_shape = (gated_input.shape[0], gated_input.shape[1] // 2)
    front_plane = plane_exchange(tie(front_four, last_plane))
    (last_sums,) = run([plane_sum(last_plane, (48, 64, -SMALL))], info, after=(front_four,))
    last_sums = line_swap(last_sums)
    (
        (rear_up_grad, rear_down_grad),
        (
            merge_output_grad, gated_left_grad, gated_output_grad, heads_input_grad,
            heads_output_grad,
        ),
    ) = run(
        [
            line_sum(rear_sums, ((64, None), (64, None)), (rear_up.shape, rear_down.shape)),
            line_sum(
                wide_sums, ((32, None), (48, None), (48, None), (48, None), (16, None)),
                (
                    merge_output.shape, half_shape, gated_output.shape, heads_input.shape,
                    heads_output.shape,
                ),
            ),
        ],
        info,
        after=(last_sums[0],),
    )
    (front_sums,) = run(
        [plane_sum(front_plane, (80,))], info, after=(last_sums[0], merge_output_grad)
    )
    front_sums = line_swap(front_sums)
    vector = (1, front_gain.shape[0])
    (
        (
            gated_input_grad, front_down_grad, gate_kernel_grad, merge_kernel_grad,
            heads_gain_grad, gated_gain_grad, rear_gain_grad, final_gain_grad, gate_gain_grad,
            statistics,
        ),
    ) = run(
        [
            line_sum(
                last_sums,
                ((0, "left"), (48, "right"), (64, None), (16, "small")),
                (
                    gated_input.shape, front_down.shape, gate_kernel.shape, merge_kernel.shape,
                    vector, vector, vector, vector, (1, gate_gain.shape[0]), (1, STATS - 1),
                ),
                given=(gated_left_grad,),
            ),
        ],
        info,
        after=(front_sums[0],),
    )
    ((front_up_grad, front_gain_grad),) = run(
        [line_sum(front_sums, ((64, None), (16, "gain")), (front_up.shape, vector))], info,
        after=(statistics,),
    )
    return (
        layer.encoded, layer.features_grad, front_up_grad, front_down_grad, heads_input_grad,
        heads_output_grad, gated_input_grad, gated_output_grad, merge_output_grad, rear_up_grad,
        rear_down_grad, gate_kernel_grad, merge_kernel_grad, front_gain_grad[0],
        heads_gain_grad[0], gated_gain_grad[0], gate_gain_grad[0], rear_gain_grad[0],
        final_gain_grad[0], statistics[0],
    )


def pack_rows(shard):
    rows, columns = shard.shape
    pieces = shard.reshape(rows, columns // WIDTH, WIDTH).transpose(1, 0, 2)
    return pieces.reshape(rows * columns // WIDTH, WIDTH)


def pad_lines(flat):
    rows = -(-flat.shape[-1] // (WIDTH * 16)) * 16
    spare = [(0, 0)] * (flat.ndim - 1) + [(0, rows * WIDTH - flat.shape[-1])]
    return jnp.pad(flat, spare).reshape(flat.shape[:-1] + (rows, WIDTH))


def to_owners(weight):
    rows, columns = weight.shape
    pieces = weight.reshape(BLOCKS, rows // BLOCKS, columns // WIDTH, WIDTH)
    pieces = pieces.transpose(0, 2, 1, 3).reshape(2, 2, 4, 2, -1, WIDTH)
    pieces = pieces.transpose(1, 0, 3, 2, 4, 5)
    return pieces.reshape(2, 4, 4, -1, WIDTH)


def from_owners(halves, rows, columns):
    send, keep = halves
    pieces = jnp.stack([keep, send], axis=1)
    pieces = pieces.reshape(BLOCKS, columns // WIDTH, rows // BLOCKS, WIDTH)
    return pieces.transpose(0, 2, 1, 3).reshape(rows, columns)


def any_device(features, cotangent, lengths, *shards, axes):
    count = lax.axis_size(axes)
    matrices, smaller = shards[:9], shards[9:]
    packed = [pack_rows(element) for element in matrices]
    packed.append(pad_lines(jnp.concatenate([element.reshape(-1) for element in smaller])))
    gathered = lax.all_gather(jnp.concatenate(packed), axes, axis=0)
    weights = []
    start = 0
    for element, piece in zip(matrices, packed):
        rows, columns = element.shape
        window = gathered[:, start : start + piece.shape[0]]
        start += piece.shape[0]
        window = window.reshape(count, columns // WIDTH, rows, WIDTH).transpose(0, 2, 1, 3)
        weights.append(to_owners(window.reshape(count * rows, columns)))
    flat = gathered[:, start:].reshape(count, -1).astype(F32)
    lines = []
    start = 0
    for element in smaller:
        window = flat[:, start : start + element.size]
        start += element.size
        if element.ndim == 2:
            window = window.reshape((count,) + element.shape).transpose(1, 0, 2)
            window = window.reshape(element.shape[0], -1)
            lines.append(jnp.pad(window, ((0, 1), (0, 0))))
        else:
            lines.append(window.reshape(1, -1))
    up, down, h_in, h_out, g_in, g_out, m_out, r_up, r_down = weights

    def chunk(*members):
        return tuple(jnp.concatenate([member[i] for member in members], axis=2) for i in (0, 1))

    front = chunk(up, down)
    rear = chunk(r_up, r_down, m_out)
    layer = Layer(features, cotangent, lengths[0], jnp.zeros((SEG,), jnp.int32), smaller[0].shape[0])
    layer.set_small(lines)
    layer.front_forward(front)
    layer.branches_forward(chunk(g_in, g_out, h_in, h_out))
    rear = layer.merge_rear(rear)
    rear, merge = rear[:2], rear[2:]
    wide = layer.branches_backward()
    right = layer.gated_gate()
    front_down_halves = layer.front_hidden()
    front_up_halves = layer.front_input()

    def part(pair, start, stop):
        return tuple(array[:, :, start:stop] for array in pair)

    gated_halves = tuple(
        jnp.concatenate([one[:, :, :48], two], axis=2) for one, two in zip(wide, right)
    )
    ordered = (
        part(front_up_halves, 0, 64), front_down_halves, part(wide, 96, 144),
        part(wide, 144, 160), gated_halves, part(wide, 48, 96), merge,
        part(rear, 0, 64), part(rear, 64, 128),
    )
    front_gain = front_up_halves[1][0, 0, 64].astype(F32)
    small_grads = layer.small_grads()
    pieces = []
    for element, halves in zip(matrices, ordered):
        rows, columns = element.shape
        full = from_owners(halves, rows * count, columns)
        full = full.reshape(count, rows, columns // WIDTH, WIDTH).transpose(0, 2, 1, 3)
        pieces.append(full.reshape(count, -1, WIDTH))
    gate_taps, merge_taps, heads_gain, gated_gain, rear_gain, final_gain, gate_gain = small_grads
    small_full = (gate_taps, merge_taps, front_gain, heads_gain, gated_gain, gate_gain, rear_gain, final_gain)
    flat = []
    for element, full in zip(smaller, small_full):
        if element.ndim == 2:
            full = full[: element.shape[0]].reshape(element.shape[0], count, -1).transpose(1, 0, 2)
        flat.append(full.reshape(count, -1))
    pieces.append(pad_lines(jnp.concatenate(flat, axis=1).astype(LOW)))
    summed = lax.psum_scatter(jnp.concatenate(pieces, axis=1), axes, scatter_dimension=0)
    outputs = []
    start = 0
    for element, piece in zip(matrices, pieces):
        rows, columns = element.shape
        window = summed[start : start + piece.shape[1]].astype(F32)
        start += piece.shape[1]
        window = window.reshape(columns // WIDTH, rows, WIDTH).transpose(1, 0, 2)
        outputs.append(window.reshape(rows, columns))
    flat = summed[start:].reshape(-1).astype(F32)
    start = 0
    for element in smaller:
        outputs.append(flat[start : start + element.size].reshape(element.shape))
        start += element.size
    front_stat, rear_stat = layer.stats()
    squares = jnp.stack(
        [
            front_stat[0], front_stat[1], rear_stat[0], rear_stat[2], front_stat[2], rear_stat[1],
            rear_stat[3],
        ]
    )
    totals = lax.psum(
        jnp.append(jnp.sum(squares, axis=1), jnp.sum(lengths).astype(F32)), axes
    )
    statistics = jnp.sqrt(totals[:7] / (totals[7] * features.shape[1]))
    return (layer.encoded, layer.features_grad) + tuple(outputs) + (statistics,)


def solution(mesh):
    body = grid_device
    axes = ("x", "k", "z", "y")
    if mesh.devices.shape == (4, 8):
        mesh = Mesh(mesh.devices.reshape(2, 2, 4, 2), axes)
    else:
        axes = tuple(mesh.axis_names)
        body = functools.partial(any_device, axes=axes)
    rows, columns, vector = P(axes, None), P(None, axes), P(axes)
    weights = (rows,) * 9 + (columns,) * 2 + (vector,) * 6
    return jax.shard_map(
        body,
        mesh=mesh,
        in_specs=(rows, rows, rows) + weights,
        out_specs=(rows, rows) + weights + (P(),),
        check_vma=False,
    )
```

```python
import functools

import jax
import jax.numpy as jnp
from jax import lax
from jax.experimental import pallas as pl
from jax.experimental.pallas import tpu as pltpu
from jax.sharding import Mesh, PartitionSpec as P

HEADS = 8
EPSILON = 1e-05
NEGATIVE = -1000000000.0
TILE = 8
GAP = 16
CHAN = 128
PLACE = 1
OWNER = 5
SEG = 6
WIDTH = 512
BLOCKS = 32
F32 = jnp.float32
LOW = jnp.bfloat16


def dot(left, right):
    return jnp.dot(left, right, preferred_element_type=F32)


def dot_tn(left, right):
    return lax.dot_general(left, right, (((0,), (0,)), ((), ())), preferred_element_type=F32)


def dot_nt(left, right):
    return lax.dot_general(left, right, (((1,), (1,)), ((), ())), preferred_element_type=F32)


def normalize(values):
    centred = values - jnp.mean(values, axis=-1, keepdims=True)
    variance = jnp.mean(centred * centred, axis=-1, keepdims=True)
    inverse = lax.rsqrt(variance + EPSILON)
    return centred * inverse, inverse


def normalize_back(upstream, gain, normal, inverse):
    scaled = upstream * gain
    mean_scaled = jnp.mean(scaled, axis=-1, keepdims=True)
    mean_cross = jnp.mean(scaled * normal, axis=-1, keepdims=True)
    return inverse * (scaled - mean_scaled - normal * mean_cross)


def part_of(index):
    return slice(None), pl.ds(pl.multiple_of(index * WIDTH, WIDTH), WIDTH)


def row_sum(values):
    return jnp.sum(values, axis=0, keepdims=True)


GELU_A = 0.7978845608028654
GELU_B = 0.044715


def gelu(v):
    return 0.5 * v * (1.0 + jnp.tanh(GELU_A * (v + GELU_B * v * v * v)))


def gelu_pair(v):
    square = v * v
    bend = jnp.tanh(GELU_A * (v + GELU_B * square * v))
    value = 0.5 * v * (1.0 + bend)
    slope = 0.5 * (1.0 + bend) + 0.5 * v * (1.0 - bend * bend) * (
        GELU_A * (1.0 + 3.0 * GELU_B * square)
    )
    return value, slope


def silu(v):
    return v * jax.nn.sigmoid(v)


def store_halves(value, send, keep, mine, rows, start):
    parts = value.astype(LOW).reshape(2, 2, 8, rows, WIDTH)

    @pl.when(mine == 0)
    def _():
        keep[:, :, pl.ds(start, rows), :] = parts[:, 0]
        send[:, :, pl.ds(start, rows), :] = parts[:, 1]

    @pl.when(mine == 1)
    def _():
        keep[:, :, pl.ds(start, rows), :] = parts[:, 1]
        send[:, :, pl.ds(start, rows), :] = parts[:, 0]


def join_rows(first, second, mine):
    cores = jnp.where(mine == 0, first, second), jnp.where(mine == 0, second, first)
    return jnp.concatenate(
        [core[2 * x + y, z] for x in (0, 1) for core in cores for z in range(4) for y in (0, 1)]
    )


def pick_rows(first, second, flag):
    chosen = jnp.where(flag, first, second)
    return jnp.concatenate([chosen[y, z] for z in range(4) for y in (0, 1)])


def visits(info, segments, body):
    for s in range(segments):
        begin, end = info[SEG + s], info[SEG + segments + s]

        def visit(i, _, s=s, begin=begin, end=end):
            row = i * TILE + lax.broadcasted_iota(jnp.int32, (TILE, CHAN), 0)
            inside = jnp.logical_and(row >= begin, row < end)
            body(s, pl.multiple_of(i * TILE, TILE), inside)
            return 0

        lax.fori_loop(begin // TILE, (end + TILE - 1) // TILE, visit, 0)


def spread(source, padded, info, segments, blocks):
    padded[...] = jnp.zeros_like(padded)

    def body(s, base, inside):
        for c in range(blocks):
            value = source[pl.ds(base, TILE), c * CHAN : (c + 1) * CHAN]
            padded[c, pl.ds(base + GAP * (s + 1), TILE), :] = jnp.where(inside, value, 0.0)

    visits(info, segments, body)


def unspread(padded, target, info, segments, blocks):
    def body(s, base, inside):
        for c in range(blocks):
            lanes = slice(c * CHAN, (c + 1) * CHAN)
            value = padded[c, pl.ds(base + GAP * (s + 1), TILE), :]
            target[pl.ds(base, TILE), lanes] = jnp.where(
                inside, value, target[pl.ds(base, TILE), lanes]
            )

    visits(info, segments, body)


def conv_rows(padded, kernel, out, steps_ref, sums, blocks, taps, flip):
    half = (taps - 1) // 2
    rows = padded.shape[1]
    pairs = (rows - 2 * GAP) // (4 * GAP)
    order = [taps - 1 - j if flip else j for j in range(taps)]
    for c in range(blocks):
        steps_ref[c, 0 : rows - GAP, :] = padded[c, 0 : rows - GAP, :] - padded[c, GAP:rows, :]
    for j in range(GAP):
        total = kernel[order[j] : order[j] + 1, :]
        if j + GAP < taps:
            total = total + kernel[order[j + GAP] : order[j + GAP] + 1, :]
        sums[j : j + 1, :] = total

    def body(step, _):
        c = step // 2
        base = GAP + lax.rem(step, 2) * (pairs * 2 * GAP)
        lanes = pl.ds(pl.multiple_of(c * CHAN, CHAN), CHAN)
        for w in range(pairs):
            start = base + 2 * GAP * w
            first_part = second = third = jnp.zeros((GAP, CHAN), F32)
            for j in range(GAP):
                row = start + j - half
                first_part += kernel[pl.ds(order[j], 1), lanes] * steps_ref[c, pl.ds(row, GAP), :]
                second += sums[pl.ds(j, 1), lanes] * padded[c, pl.ds(row + GAP, GAP), :]
                if j + GAP < taps:
                    third += (
                        kernel[pl.ds(order[j + GAP], 1), lanes]
                        * steps_ref[c, pl.ds(row + GAP, GAP), :]
                    )
            start = pl.multiple_of(start, TILE)
            out[c, pl.ds(start, GAP), :] = first_part + second
            out[c, pl.ds(start + GAP, GAP), :] = second - third
        return 0

    lax.fori_loop(0, blocks * 2, body, 0)


def conv_taps(padded_grad, padded, steps_ref, out, blocks, taps):
    half = (taps - 1) // 2
    rows = padded.shape[1]
    pairs = (rows - 2 * GAP) // (2 * GAP)

    def fold(value):
        return value[:TILE] + value[TILE:]

    def block(c, _):
        lanes = pl.ds(pl.multiple_of(c * CHAN, CHAN), CHAN)
        zero = jnp.zeros((TILE, CHAN), F32)

        def body(step, sums):
            start = pl.multiple_of(step * 2 * GAP + GAP, TILE)
            lower = padded_grad[c, pl.ds(start, GAP), :]
            upper = padded_grad[c, pl.ds(start + GAP, GAP), :]
            both = lower + upper
            new = list(sums)
            for j in range(GAP):
                row = start + j - half
                shared = fold(both * padded[c, pl.ds(row + GAP, GAP), :])
                new[j] = new[j] + (fold(lower * steps_ref[c, pl.ds(row, GAP), :]) + shared)
                if j + GAP < taps:
                    rest = fold(upper * steps_ref[c, pl.ds(row + GAP, GAP), :])
                    new[j + GAP] = new[j + GAP] + (shared - rest)
            return tuple(new)

        sums = lax.fori_loop(0, pairs, body, (zero,) * taps)
        for j in range(taps):
            out[pl.ds(j, 1), lanes] = row_sum(sums[j])
        return 0

    lax.fori_loop(0, blocks, block, 0)


def front_forward_kernel(
    info, x_ref, gain, valid, up, up_two, down, down_two, out, before_out, stat, low, total
):
    h = pl.program_id(0)
    mine = info[0]
    up_value = join_rows(up[...], up_two[...], mine)
    down_value = pick_rows(down[...], down_two[...], h % 2 == mine)

    @pl.when(h == 0)
    def _():
        normal, _ = normalize(x_ref[...].astype(F32))
        low[...] = (normal * gain[...]).astype(LOW)
        total[...] = jnp.zeros_like(total)

    before = dot(low[...], up_value)
    before_out[...] = before
    total[...] += dot(silu(before).astype(LOW), down_value)

    @pl.when(h == pl.num_programs(0) - 1)
    def _():
        x = x_ref[...].astype(F32)
        part = 0.5 * total[...]
        after = x + part
        out[...] = after
        v = valid[...]
        stat[0:1, :] = row_sum(x * x * v)
        stat[1:2, :] = row_sum(after * after * v)
        stat[2:3, :] = row_sum(part * part * v)
        stat[3:, :] = jnp.zeros((5, WIDTH), F32)


def head_masks(segs_col, segs_row):
    allowed = segs_col == segs_row
    lane = lax.broadcasted_iota(jnp.int32, (1, CHAN), 1)
    return allowed, (lane < CHAN // 2, lane >= CHAN // 2)


def head_probs(query, key, allowed, scale):
    scores = jnp.where(allowed, dot_nt(query, key) * scale, NEGATIVE)
    exponent = jnp.exp(scores - jnp.max(scores, axis=-1, keepdims=True))
    return exponent / jnp.sum(exponent, axis=-1, keepdims=True)


def heads_forward(
    info, low, segs_col, segs_row, w_in, w_in_two, w_out, w_out_two, attended, packed, mixed,
):
    mine = info[0]
    scale = (WIDTH // HEADS) ** -0.5
    for q in range(3):
        rows = slice(16 * q, 16 * (q + 1))
        weight = join_rows(w_in[:, :, rows, :], w_in_two[:, :, rows, :], mine)
        packed[:, WIDTH * q : WIDTH * (q + 1)] = dot(low, weight).astype(LOW)
    allowed, halves = head_masks(segs_col[...], segs_row[...])

    def pair(p, _):
        lanes = [
            pl.ds(pl.multiple_of(WIDTH * q + CHAN * p, CHAN), CHAN) for q in range(3)
        ]
        query, key, value = (packed[:, lane] for lane in lanes)
        parts = []
        for half in halves:
            probs = head_probs(jnp.where(half, query, 0), key, allowed, scale)
            parts.append(dot(probs.astype(LOW), value))
        mixed[:, lanes[0]] = jnp.where(halves[0], parts[0], parts[1]).astype(LOW)
        return 0

    lax.fori_loop(0, HEADS // 2, pair, 0)
    attended[...] = dot(mixed[...], join_rows(w_out[...], w_out_two[...], mine))


def heads_backward(
    info, grad, x_ref, gain, segs_col, segs_row, packed, mixed, w_in, w_in_two, w_out, w_out_two,
    stream, gain_grad, send, keep, mixed_grad, packed_grad, low,
):
    scale = (WIDTH // HEADS) ** -0.5
    mine = info[0]
    attended_low = grad[...].astype(LOW)
    store_halves(dot_tn(mixed[...], attended_low), send, keep, mine, 16, 144)
    mixed_grad[...] = dot_nt(attended_low, join_rows(w_out[...], w_out_two[...], mine)).astype(LOW)
    normal, inverse = normalize(x_ref[...])
    low[...] = (normal * gain[...]).astype(LOW)
    allowed, halves = head_masks(segs_col[...], segs_row[...])

    def pair(p, _):
        lanes = [
            pl.ds(pl.multiple_of(WIDTH * q + CHAN * p, CHAN), CHAN) for q in range(3)
        ]
        query, key, value = (packed[:, lane] for lane in lanes)
        upstream = mixed_grad[:, lanes[0]]
        parts = []
        for half in halves:
            probs = head_probs(jnp.where(half, query, 0), key, allowed, scale)
            probs_grad = dot_nt(jnp.where(half, upstream, 0), value)
            value_grad = dot_tn(probs.astype(LOW), upstream)
            inner = jnp.sum(probs_grad * probs, axis=-1, keepdims=True)
            score_grad = (probs * (probs_grad - inner)).astype(LOW)
            query_grad = dot(score_grad, key) * scale
            key_grad = dot_tn(score_grad, query) * scale
            parts.append((query_grad, key_grad, value_grad))
        for q in range(3):
            packed_grad[:, lanes[q]] = jnp.where(halves[0], parts[0][q], parts[1][q]).astype(LOW)
        return 0

    lax.fori_loop(0, HEADS // 2, pair, 0)
    total = jnp.zeros(x_ref.shape, F32)
    for q in range(3):
        rows = slice(16 * q, 16 * (q + 1))
        weight = join_rows(w_in[:, :, rows, :], w_in_two[:, :, rows, :], mine)
        piece = packed_grad[:, WIDTH * q : WIDTH * (q + 1)]
        store_halves(dot_tn(low[...], piece), send, keep, mine, 16, 96 + 16 * q)
        total += dot_nt(piece, weight)
    gain_grad[...] = row_sum(total * normal)
    stream[...] = normalize_back(total, gain[...], normal, inverse)


def branches_forward_kernel(
    info, x_ref, heads_gain, segs_col, segs_row, w_heads, w_heads_two, w_mix, w_mix_two,
    gain, gate_gain, taps_ref, w_in, w_in_two, w_out, w_out_two, attended, packed, mixed,
    gated, before_out, normal_out, inverse_out, part_out, product,
    low, act, padded, conv, steps_ref, sums, *, segments, taps,
):
    j = pl.program_id(0)
    thirds = WIDTH * 3

    @pl.when(j == 0)
    def _():
        normal, _ = normalize(x_ref[...])
        low[...] = (normal * gain[...]).astype(LOW)
        heads_forward(
            info, (normal * heads_gain[...]).astype(LOW), segs_col, segs_row, w_heads,
            w_heads_two, w_mix, w_mix_two, attended, packed, mixed,
        )

    before = dot(low[...], join_rows(w_in[...], w_in_two[...], info[0]))
    before_out[...] = before
    value = gelu(before)

    @pl.when(j < 3)
    def _():
        act[:, pl.ds(pl.multiple_of(j * WIDTH, WIDTH), WIDTH)] = value

    @pl.when(j == 2)
    def _():
        normal, inverse = normalize(act[...])
        normal_out[...] = normal
        inverse_out[...] = inverse
        act[...] = normal * gate_gain[...]
        blocks = thirds // CHAN
        spread(act, padded, info, segments, blocks)
        conv_rows(padded, taps_ref, conv, steps_ref, sums, blocks, taps, False)
        unspread(conv, part_out, info, segments, blocks)

    @pl.when(j >= 3)
    def _():
        lanes = pl.ds(pl.multiple_of((j - 3) * WIDTH, WIDTH), WIDTH)
        product[:, lanes] = (value * part_out[:, lanes]).astype(LOW)

    @pl.when(j == 5)
    def _():
        gated[...] = dot(product[...], join_rows(w_out[...], w_out_two[...], info[0]))


def branches_backward_kernel(
    info, attended_grad, x_ref, heads_gain, segs_col, segs_row, packed, mixed, w_heads,
    w_heads_two, w_mix, w_mix_two, grad, gain, before, part, product, w_in, w_in_two, w_out,
    w_out_two,
    stream, heads_gain_grad, part_grad, total_out, send, keep, low, product_grad, gated_low,
    mixed_grad, packed_grad,
):
    j = pl.program_id(0)
    mine = info[0]

    @pl.when(j == 0)
    def _():
        heads_backward(
            info, attended_grad, x_ref, heads_gain, segs_col, segs_row, packed, mixed, w_heads,
            w_heads_two, w_mix, w_mix_two, stream, heads_gain_grad, send, keep, mixed_grad,
            packed_grad, low,
        )
        normal, _ = normalize(x_ref[...])
        low[...] = (normal * gain[...]).astype(LOW)
        total_out[...] = jnp.zeros_like(total_out)
        gated_low[...] = grad[...].astype(LOW)
        store_halves(dot_tn(product[...], gated_low[...]), send, keep, mine, 48, 48)
        product_grad[...] = dot_nt(gated_low[...], join_rows(w_out[...], w_out_two[...], mine))

    value, slope = gelu_pair(before[...])
    lanes = pl.ds(pl.multiple_of(j * WIDTH, WIDTH), WIDTH)
    upstream = product_grad[:, lanes]
    part_grad[...] = upstream * value
    before_grad = (upstream * part[...] * slope).astype(LOW)
    store_halves(
        dot_tn(low[...], before_grad), send, keep, mine, 16, pl.multiple_of(j * 16, 16)
    )
    total_out[...] += dot_nt(before_grad, join_rows(w_in[...], w_in_two[...], mine))


def gated_conv(
    info, part_grad, normal_ref, inverse_ref, gate_gain, taps_ref,
    gate_gain_grad, taps_grad, padded, padded_grad, conv, work, steps_ref, sums, segments, taps,
):
    blocks = 3 * WIDTH // CHAN
    spread(part_grad, padded_grad, info, segments, blocks)
    work[...] = normal_ref[...] * gate_gain[...]
    spread(work, padded, info, segments, blocks)
    rows = padded.shape[1]
    for c in range(blocks):
        steps_ref[c, 0 : rows - GAP, :] = padded[c, 0 : rows - GAP, :] - padded[c, GAP:rows, :]
    conv_taps(padded_grad, padded, steps_ref, taps_grad, blocks, taps)
    conv_rows(padded_grad, taps_ref, conv, steps_ref, sums, blocks, taps, True)
    unspread(conv, work, info, segments, blocks)
    upstream = work[...]
    normal = normal_ref[...]
    gate_gain_grad[...] = row_sum(upstream * normal)
    work[...] = normalize_back(upstream, gate_gain[...], normal, inverse_ref[...])


def gated_gate_kernel(
    info, part_grad, normal_ref, inverse_ref, gate_gain, taps_ref, x_ref, gain, before, total_in,
    w_in, w_in_two,
    stream, gain_grad, gate_gain_grad, taps_grad, send, keep,
    low, total, padded, padded_grad, conv, work, steps_ref, sums, *, segments, taps,
):
    j = pl.program_id(0)
    mine = info[0]

    @pl.when(j == 0)
    def _():
        gated_conv(
            info, part_grad, normal_ref, inverse_ref, gate_gain, taps_ref, gate_gain_grad,
            taps_grad, padded, padded_grad, conv, work, steps_ref, sums, segments, taps,
        )
        normal, _ = normalize(x_ref[...])
        low[...] = (normal * gain[...]).astype(LOW)
        total[...] = total_in[...]

    _, slope = gelu_pair(before[...])
    before_grad = (work[part_of(j)] * slope).astype(LOW)
    store_halves(
        dot_tn(low[...], before_grad), send, keep, mine, 16, pl.multiple_of(j * 16, 16)
    )
    total[...] += dot_nt(before_grad, join_rows(w_in[...], w_in_two[...], mine))

    @pl.when(j == 2)
    def _():
        normal, inverse = normalize(x_ref[...])
        gain_grad[...] = row_sum(total[...] * normal)
        stream[...] = normalize_back(total[...], gain[...], normal, inverse)


def conv_add(padded, conv, taps_ref, steps_ref, sums, blocks, taps, flip):
    conv_rows(padded, taps_ref, conv, steps_ref, sums, blocks, taps, flip)
    for c in range(blocks):
        conv[c] += padded[c]


def hidden_back(h, mine, before, part_low, down, send, keep, start):
    gate = jax.nn.sigmoid(before)
    hidden = (before * gate).astype(LOW)
    hidden_grad = dot_nt(part_low, down)
    before_grad = (hidden_grad * (gate * (1.0 + before * (1.0 - gate)))).astype(LOW)
    down_grad = dot_tn(hidden, part_low).astype(LOW).reshape(8, 64, WIDTH)

    @pl.when(h % 2 == mine)
    def _():
        keep[h // 2, :, start : start + 64, :] = down_grad

    @pl.when(h % 2 != mine)
    def _():
        send[h // 2, :, start : start + 64, :] = down_grad

    return before_grad


def merge_rear_kernel(
    info, x_ref, attended, gated, taps_ref, weight, weight_two, gain, final_gain, valid, cotangent,
    up, up_two, down, down_two,
    encoded, stream, gain_grad, final_gain_grad, stat, attended_grad, gated_grad, taps_grad,
    send, keep, merge_send, merge_keep,
    low, before, part_grad, stream_grad, total, middle, joined, joined_low, padded, padded_grad,
    conv, steps_ref, sums, *, segments, taps,
):
    step = pl.program_id(0)
    h = jnp.where(step < 4, step, 7 - step)
    up_value = join_rows(up[...], up_two[...], info[0])
    down_value = pick_rows(down[...], down_two[...], h % 2 == info[0])
    blocks = 2 * WIDTH // CHAN

    @pl.when(step == 0)
    def _():
        joined[:, :WIDTH] = attended[...]
        joined[:, WIDTH:] = gated[...]
        spread(joined, padded, info, segments, blocks)
        conv_add(padded, conv, taps_ref, steps_ref, sums, blocks, taps, False)
        unspread(conv, joined, info, segments, blocks)
        joined_low[...] = joined[...].astype(LOW)
        part = dot(joined_low[...], join_rows(weight[...], weight_two[...], info[0]))
        after = x_ref[...] + part
        middle[...] = after
        v = valid[...]
        stat[0:1, :] = row_sum(after * after * v)
        stat[1:2, :] = row_sum(part * part * v)
        normal, _ = normalize(after)
        low[...] = (normal * gain[...]).astype(LOW)
        total[...] = jnp.zeros_like(total)

    @pl.when(step < 4)
    def _():
        value = dot(low[...], up_value)
        before[step] = value
        total[...] += dot(silu(value).astype(LOW), down_value)

    @pl.when(step == 3)
    def _():
        part = 0.5 * total[...]
        after = middle[...] + part
        v = valid[...]
        stat[2:3, :] = row_sum(after * after * v)
        stat[3:4, :] = row_sum(part * part * v)
        stat[4:, :] = jnp.zeros((4, WIDTH), F32)
        normal, inverse = normalize(after)
        encoded[...] = (normal * final_gain[...] * v).astype(LOW)
        upstream = cotangent[...].astype(F32) * v
        final_gain_grad[...] = row_sum(upstream * normal)
        grad = normalize_back(upstream, final_gain[...], normal, inverse)
        stream_grad[...] = grad
        part_grad[...] = (0.5 * grad).astype(LOW)
        total[...] = jnp.zeros_like(total)

    @pl.when(step >= 4)
    def _():
        before_grad = hidden_back(
            h, info[0], before[h], part_grad[...], down_value, send, keep, 64
        )
        store_halves(
            dot_tn(low[...], before_grad), send, keep, info[0], 16, pl.multiple_of(h * 16, 16)
        )
        total[...] += dot_nt(before_grad, up_value)

    @pl.when(step == 7)
    def _():
        normal, inverse = normalize(middle[...])
        gain_grad[...] = row_sum(total[...] * normal)
        grad = stream_grad[...] + normalize_back(total[...], gain[...], normal, inverse)
        stream[...] = grad
        grad_low = grad.astype(LOW)
        store_halves(dot_tn(joined_low[...], grad_low), merge_send, merge_keep, info[0], 32, 0)
        joined[...] = dot_nt(grad_low, join_rows(weight[...], weight_two[...], info[0]))
        spread(joined, padded_grad, info, segments, blocks)
        conv_taps(padded_grad, padded, steps_ref, taps_grad, blocks, taps)
        conv_add(padded_grad, conv, taps_ref, steps_ref, sums, blocks, taps, True)
        unspread(conv, joined, info, segments, blocks)
        attended_grad[...] = joined[:, :WIDTH]
        gated_grad[...] = joined[:, WIDTH:]


def front_hidden_kernel(
    info, grad, heads_stream, gated_stream, before, down, down_two,
    stream_out, before_grad, send, keep, part_grad,
):
    h = pl.program_id(0)

    @pl.when(h == 0)
    def _():
        stream_sum = grad[...] + heads_stream[...] + gated_stream[...]
        stream_out[...] = stream_sum
        part_grad[...] = (0.5 * stream_sum).astype(LOW)

    down_value = pick_rows(down[...], down_two[...], h % 2 == info[0])
    before_grad[...] = hidden_back(
        h, info[0], before[...], part_grad[...], down_value, send, keep, 0
    )


def front_input_kernel(
    info, stream_grad, before_grad, x_ref, gain, up, up_two,
    x_grad, send, keep, low, total,
):
    h = pl.program_id(0)

    @pl.when(h == 0)
    def _():
        normal, _ = normalize(x_ref[...].astype(F32))
        low[...] = (normal * gain[...]).astype(LOW)
        total[...] = jnp.zeros_like(total)

    store_halves(
        dot_tn(low[...], before_grad[...]), send, keep, info[0], 16, pl.multiple_of(h * 16, 16)
    )
    total[...] += dot_nt(before_grad[...], join_rows(up[...], up_two[...], info[0]))

    @pl.when(h == 3)
    def _():
        normal, inverse = normalize(x_ref[...].astype(F32))
        gain_grad = row_sum(total[...] * normal).astype(LOW)
        gain_rows = jnp.broadcast_to(gain_grad.reshape(1, 1, 1, WIDTH), (2, 8, 16, WIDTH))
        send[:, :, 64:80, :] = gain_rows
        keep[:, :, 64:80, :] = gain_rows
        x_grad[...] = (
            stream_grad[...] + normalize_back(total[...], gain[...], normal, inverse)
        ).astype(LOW)


def whole(shape):
    return pl.BlockSpec(shape, lambda *_: (0,) * len(shape))


def call(kernel, grid, inputs, outputs, scratch, info, flops=0, after=(), room=56):
    in_specs = [
        whole(array.shape) if block is None else pl.BlockSpec(block, index)
        for array, block, index in inputs
    ]
    out_specs = [
        whole(shape) if block is None else pl.BlockSpec(block, index)
        for shape, _, block, index in outputs
    ]
    arrays = [array for array, _, _ in inputs]
    shapes = [jax.ShapeDtypeStruct(shape, kind) for shape, kind, _, _ in outputs]
    moved = sum(array.size * array.dtype.itemsize for array in arrays)
    moved = sum(shape.size * shape.dtype.itemsize for shape in shapes) + min(moved, 1 << 24)
    skipped = len(after)
    name = getattr(kernel, "func", kernel).__name__

    def body(info_ref, *refs):
        kernel(info_ref, *refs[skipped:])

    return pl.pallas_call(
        body,
        grid_spec=pltpu.PrefetchScalarGridSpec(
            num_scalar_prefetch=1,
            grid=grid,
            in_specs=[pl.BlockSpec(memory_space=pl.ANY)] * skipped + in_specs,
            out_specs=out_specs,
            scratch_shapes=scratch,
        ),
        out_shape=shapes,
        name=name,
        compiler_params=pltpu.CompilerParams(vmem_limit_bytes=room * 1024 * 1024),
        cost_estimate=pl.CostEstimate(flops=flops, bytes_accessed=moved, transcendentals=0),
    )(info, *after, *arrays)


def segment_table(lengths, spots, row_count):
    ends = jnp.cumsum(lengths)
    position = jnp.arange(row_count, dtype=jnp.int32)
    segments = jnp.sum((position[None, :] >= ends[:, None]).astype(jnp.int32), axis=0)
    zero = jnp.zeros((1,), jnp.int32)
    last = jnp.full((1,), row_count, jnp.int32)
    return segments, jnp.concatenate([spots, zero, ends, ends, last]).astype(jnp.int32)


def all_of(*arrays):
    return [(array, None, None) for array in arrays]


def plain(*shapes_and_types):
    return [(shape, kind, None, None) for shape, kind in shapes_and_types]


def halves(rows):
    return plain(((2, 8, rows, WIDTH), LOW)) * 2


def columns(pair, rows, start, index):
    block = (4, 4, rows, WIDTH), lambda *i: (0, 0, start // rows + index(*i), 0)
    return [(array, *block) for array in pair]


def lines(pair, index):
    block = (2, 4, 64, WIDTH), lambda *i: (index(*i) // 2, 0, 1, 0)
    return [(array, *block) for array in pair]


def first(*_):
    return 0


def step(h, _):
    return h


class Layer:
    def __init__(self, features, cotangent, lengths, spots, taps):
        self.features, self.cotangent, self.taps = features, cotangent, taps
        self.tokens = features.shape[0]
        self.count = lengths.shape[0]
        self.segments = self.count + 1
        seg_ids, self.info = segment_table(lengths, spots, self.tokens)
        self.segs_col, self.segs_row = seg_ids[:, None], seg_ids[None, :]
        self.valid = (self.segs_col < self.count).astype(F32)
        self.stream = ((self.tokens, WIDTH), F32)
        self.low = pltpu.VMEM((self.tokens, WIDTH), LOW)
        self.wide = pltpu.VMEM((self.tokens, WIDTH), F32)
        rows = self.tokens + GAP * (self.segments - 1)
        self.spread_rows = -(-rows // (4 * GAP)) * 4 * GAP + 2 * GAP
        self.conv = dict(segments=self.segments, taps=taps)
        self.stat = ((8, WIDTH), F32)
        self.vector = ((1, WIDTH), F32)
        self.flop = 2 * self.tokens * WIDTH * WIDTH

    def set_small(self, smaller):
        (
            self.gate_taps, self.merge_taps, self.front_gain, self.heads_gain, self.gated_gain,
            self.gate_gain, self.rear_gain, self.final_gain,
        ) = smaller

    def padded(self, width):
        return pltpu.VMEM((width // CHAN, self.spread_rows, CHAN), F32)

    def tall(self, width, kind=F32):
        return ((self.tokens, width), kind)

    def by_column(self, array, start=0):
        return [(array, (self.tokens, WIDTH), lambda j, _: (0, j + start))]

    def front_forward(self, front, after=()):
        self.front = front
        self.after_front, self.front_before, self.front_stat = call(
            front_forward_kernel,
            (4,),
            all_of(self.features, self.front_gain, self.valid)
            + columns(front, 16, 0, step)
            + lines(front, step),
            plain(self.stream)
            + [(*self.tall(4 * WIDTH), (self.tokens, WIDTH), lambda h, _: (0, h))]
            + plain(self.stat),
            [self.low, self.wide],
            self.info,
            8 * self.flop,
            after,
        )
        return self.front_stat

    def branches_forward(self, middle, after=()):
        self.middle = middle
        self.heads = columns(middle, 48, 144, first) + columns(middle, 16, 192, first)
        (
            self.attended, self.packed, self.mixed, self.gated, self.gated_before,
            self.gate_normal, self.gate_inverse, self.gate_part, self.product,
        ) = call(
            functools.partial(branches_forward_kernel, **self.conv),
            (6,),
            all_of(self.after_front, self.heads_gain, self.segs_col, self.segs_row)
            + self.heads
            + all_of(self.gated_gain, self.gate_gain, self.gate_taps)
            + columns(middle, 16, 0, lambda j, _: (j + 3) % 6)
            + columns(middle, 48, 96, first),
            plain(self.stream, self.tall(3 * WIDTH, LOW), self.tall(WIDTH, LOW), self.stream)
            + [(*self.tall(6 * WIDTH), (self.tokens, WIDTH), lambda j, _: (0, (j + 3) % 6))]
            + plain(
                self.tall(3 * WIDTH), self.tall(1), self.tall(3 * WIDTH), self.tall(3 * WIDTH, LOW)
            ),
            [self.low, pltpu.VMEM((self.tokens, 3 * WIDTH), F32)]
            + [self.padded(3 * WIDTH)] * 3
            + [pltpu.VMEM((GAP, 3 * WIDTH), F32)],
            self.info,
            52 * self.flop,
            after,
        )
        return self.gate_inverse

    def merge_rear(self, rear, after=()):
        def bounce(i, _):
            return jnp.where(i < 4, i, 7 - i)

        padded = self.padded(2 * WIDTH)
        (
            self.encoded, self.merge_grad, self.rear_gain_grad, self.final_gain_grad,
            self.rear_stat, self.attended_grad, self.gated_grad, self.merge_taps_grad, *pair,
        ) = call(
            functools.partial(merge_rear_kernel, **self.conv),
            (8,),
            all_of(self.after_front, self.attended, self.gated, self.merge_taps)
            + columns(rear, 32, 128, first)
            + all_of(self.rear_gain, self.final_gain, self.valid, self.cotangent)
            + columns(rear, 16, 0, bounce)
            + lines(rear, bounce),
            plain(
                self.tall(WIDTH, LOW), self.stream, self.vector, self.vector, self.stat,
                self.stream, self.stream, ((self.taps + 1, 2 * WIDTH), F32),
            )
            + halves(128)
            + halves(32),
            [
                self.low, pltpu.VMEM((4, self.tokens, WIDTH), F32), self.low, self.wide, self.wide,
                self.wide, pltpu.VMEM((self.tokens, 2 * WIDTH), F32),
                pltpu.VMEM((self.tokens, 2 * WIDTH), LOW), padded, padded, padded, padded,
                pltpu.VMEM((GAP, 2 * WIDTH), F32),
            ],
            self.info,
            80 * self.flop,
            after,
        )
        return pair

    def branches_backward(self, after=()):
        self.heads_stream, self.heads_gain_grad, self.part_grad, self.gated_total, *pair = call(
            branches_backward_kernel,
            (3,),
            all_of(
                self.attended_grad, self.after_front, self.heads_gain, self.segs_col,
                self.segs_row, self.packed, self.mixed,
            )
            + self.heads
            + all_of(self.gated_grad, self.gated_gain)
            + self.by_column(self.gated_before)
            + self.by_column(self.gate_part)
            + all_of(self.product)
            + columns(self.middle, 16, 0, step)
            + columns(self.middle, 48, 96, first),
            plain(self.stream, self.vector)
            + [(*self.tall(3 * WIDTH), (self.tokens, WIDTH), lambda j, _: (0, j))]
            + plain(self.stream)
            + halves(160),
            [
                self.low, pltpu.VMEM((self.tokens, 3 * WIDTH), F32), self.low, self.low,
                pltpu.VMEM((self.tokens, 3 * WIDTH), LOW),
            ],
            self.info,
            40 * self.flop,
            after,
        )
        return pair

    def gated_gate(self, after=()):
        padded = self.padded(3 * WIDTH)
        (
            self.gated_stream, self.gated_gain_grad, self.gate_gain_grad, self.gate_taps_grad,
            *pair,
        ) = call(
            functools.partial(gated_gate_kernel, **self.conv),
            (3,),
            all_of(
                self.part_grad, self.gate_normal, self.gate_inverse, self.gate_gain,
                self.gate_taps, self.after_front, self.gated_gain,
            )
            + self.by_column(self.gated_before, 3)
            + all_of(self.gated_total)
            + columns(self.middle, 16, 0, lambda j, _: j + 3),
            plain(
                self.stream, self.vector, ((1, 3 * WIDTH), F32),
                ((self.taps + 1, 3 * WIDTH), F32),
            )
            + halves(48),
            [
                self.low, self.wide, padded, padded, padded,
                pltpu.VMEM((self.tokens, 3 * WIDTH), F32), padded,
                pltpu.VMEM((GAP, 3 * WIDTH), F32),
            ],
            self.info,
            48 * self.flop,
            after,
        )
        return pair

    def front_hidden(self, after=()):
        self.front_grad, self.front_before_grad, *pair = call(
            front_hidden_kernel,
            (4,),
            all_of(self.merge_grad, self.heads_stream, self.gated_stream)
            + self.by_column(self.front_before)
            + lines(self.front, step),
            plain(self.stream)
            + [(*self.tall(4 * WIDTH, LOW), (self.tokens, WIDTH), lambda h, _: (0, h))]
            + halves(64),
            [self.low],
            self.info,
            12 * self.flop,
            after,
        )
        return pair

    def front_input(self, after=()):
        self.features_grad, *pair = call(
            front_input_kernel,
            (4,),
            all_of(self.front_grad)
            + self.by_column(self.front_before_grad)
            + all_of(self.features, self.front_gain)
            + columns(self.front, 16, 0, step),
            plain(self.tall(WIDTH, LOW)) + halves(80),
            [self.low, self.wide],
            self.info,
            12 * self.flop,
            after,
        )
        return pair

    def small_grads(self):
        return (
            self.gate_taps_grad, self.merge_taps_grad, self.heads_gain_grad,
            self.gated_gain_grad, self.rear_gain_grad, self.final_gain_grad, self.gate_gain_grad,
        )

    def stats(self):
        return self.front_stat, self.rear_stat


SMALL = 16
STATS = 8


def ring(size, shift):
    return [(i, (i + shift) % size) for i in range(size)]


def pack_kernel(
    info, front_up, front_down, heads_in, heads_out, gated_in, gated_out, merge_out, rear_up,
    rear_down, gate_taps, merge_taps, front_gain, heads_gain, gated_gain, rear_gain, final_gain,
    gate_gain, front, middle, rear, small,
):
    def put(target, start, source):
        rows, width = source.shape
        for q in range(width // WIDTH):
            target[start + rows * q : start + rows * (q + 1), :] = source[
                :, WIDTH * q : WIDTH * (q + 1)
            ]

    put(front, 0, front_up)
    put(front, 64, front_down)
    put(middle, 0, gated_in)
    put(middle, 96, gated_out)
    put(middle, 144, heads_in)
    put(middle, 192, heads_out)
    put(rear, 0, rear_up)
    put(rear, 64, rear_down)
    put(rear, 128, merge_out)
    small[...] = jnp.zeros_like(small)
    for q, source in ((0, gate_taps), (2, merge_taps)):
        value = source[...].astype(F32)
        taps, width = value.shape
        small[0:SMALL, CHAN * q : CHAN * q + width] = value[:SMALL]
        small[0 : taps - SMALL, CHAN * (q + 1) : CHAN * (q + 1) + width] = value[SMALL:]
    start = CHAN
    for source in (front_gain, heads_gain, gated_gain, rear_gain, final_gain, gate_gain):
        width = source.shape[1]
        small[SMALL - 1 :, start : start + width] = source[...].astype(F32)
        start += width
    front[128 : 128 + SMALL, :] = small[...].astype(LOW)


def copy_all(copies):
    for copy in copies:
        copy.start()
    for copy in copies:
        copy.wait()


def place_line_kernel(info, *refs):
    pieces, out, sem = refs[:4], refs[4], refs[5]
    copy_all(
        [
            pltpu.make_async_copy(piece, out.at[chip, info[PLACE + i]], sem.at[chip, i])
            for chip in range(4)
            for i, piece in enumerate(pieces)
        ]
    )


def place(kernel, pieces, rows, info, after=()):
    skipped = len(after)

    def body(info_ref, *refs):
        kernel(info_ref, *refs[skipped:])

    anywhere = pl.BlockSpec(memory_space=pl.ANY)
    return pl.pallas_call(
        body,
        grid_spec=pltpu.PrefetchScalarGridSpec(
            num_scalar_prefetch=1,
            grid=(1,),
            in_specs=[anywhere] * skipped + [pl.BlockSpec(memory_space=pltpu.VMEM)] * 4,
            out_specs=anywhere,
            scratch_shapes=[pltpu.SemaphoreType.DMA((4, 4))],
        ),
        out_shape=jax.ShapeDtypeStruct((4, 4, rows, WIDTH), LOW),
        name=kernel.__name__,
        compiler_params=pltpu.CompilerParams(vmem_limit_bytes=16 * 1024 * 1024),
        cost_estimate=pl.CostEstimate(
            flops=0, bytes_accessed=32 * rows * WIDTH * 2, transcendentals=0
        ),
    )(info, *after, *pieces)


def line_sends(array):
    return [lax.ppermute(array, "z", ring(4, d)) for d in (1, 2, 3)]


def plane_exchange(array):
    return lax.all_to_all(array, ("x", "y"), 0, 0, tiled=True)


def core_swap(array):
    return lax.ppermute(array, "k", ring(2, 1))


def tie(array, *others):
    return lax.optimization_barrier((array, others))[0]


def unpack_kernel(info, first, second, gate_taps, merge_taps, gains, gate_gain):
    mine = info[0]
    lane = lax.broadcasted_iota(jnp.int32, (SMALL, CHAN), 1)
    lane_row = lane[:1]
    gate_gain[...] = jnp.zeros_like(gate_gain)
    gains[...] = jnp.zeros_like(gains)

    def put(target, rows, value, start, size, lanes):
        block, offset = start // CHAN, start % CHAN
        inside = jnp.logical_and(lanes >= offset, lanes < offset + size)
        window = slice(CHAN * block, CHAN * (block + 1))
        target[rows, window] = jnp.where(inside, value, target[rows, window])
        spill = offset + size - CHAN
        if spill > 0:
            window = slice(CHAN * (block + 1), CHAN * (block + 2))
            target[rows, window] = jnp.where(lanes < spill, value, target[rows, window])

    for i in range(BLOCKS):
        x, core, rest = i // 16, (i // 8) % 2, i % 8
        chip, z = 2 * x + rest % 2, rest // 2
        value = jnp.where(mine == core, first[chip, z], second[chip, z]).astype(F32)
        quads = [value[:, CHAN * q : CHAN * (q + 1)] for q in range(4)]
        start = 48 * i
        for half in range(2):
            rows = slice(SMALL * half, SMALL * (half + 1))
            rolled = pltpu.roll(quads[half], start % CHAN, 1)
            put(gate_taps, rows, rolled, start, 48, lane)
            rolled = pltpu.roll(quads[2 + half], (32 * i) % CHAN, 1)
            put(merge_taps, rows, rolled, 32 * i, 32, lane)
        line = quads[1][SMALL - 1 :]
        for g in range(5):
            rolled = pltpu.roll(line, (16 * i - 16 * g) % CHAN, 1)
            put(gains, slice(g, g + 1), rolled, 16 * i, 16, lane_row)
        rolled = pltpu.roll(line, (48 * i - 80) % CHAN, 1)
        put(gate_gain, slice(0, 1), rolled, 48 * i, 48, lane_row)


def pack_small_kernel(
    info, gate_taps, merge_taps, heads_gain, gated_gain, rear_gain, final_gain, gate_gain,
    front_stat, rear_stat, send, keep, *, count_at,
):
    mine = info[0]
    lane = lax.broadcasted_iota(jnp.int32, (SMALL, CHAN), 1)
    lane_row = lane[:1]
    last = lax.broadcasted_iota(jnp.int32, (SMALL, CHAN), 0) == SMALL - 1
    stats = [
        front_stat[0:1, :], front_stat[1:2, :], rear_stat[0:1, :], rear_stat[2:3, :],
        front_stat[2:3, :], rear_stat[1:2, :], rear_stat[3:4, :],
    ]
    stat_line = jnp.where(lane_row == 7, info[count_at].astype(F32), 0.0)
    for i, stat in enumerate(stats):
        stat_line = jnp.where(lane_row == i, jnp.sum(stat, axis=1, keepdims=True), stat_line)
    rest = stat_line - stat_line.astype(LOW).astype(F32)
    stat_line += pltpu.roll(rest, STATS, 1)

    def take(source, rows, start, size, lanes):
        block, offset = start // CHAN, start % CHAN
        value = source[rows, CHAN * block : CHAN * (block + 1)]
        if offset:
            value = pltpu.roll(value, CHAN - offset, 1)
        if offset + size > CHAN:
            other = source[rows, CHAN * (block + 1) : CHAN * (block + 2)]
            value = jnp.where(lanes < CHAN - offset, value, pltpu.roll(other, CHAN - offset, 1))
        return value

    def quads_of(i):
        halves = [slice(0, SMALL), slice(SMALL, 2 * SMALL)]
        quads = [take(gate_taps, rows, 48 * i, 48, lane) for rows in halves]
        quads += [take(merge_taps, rows, 32 * i, 32, lane) for rows in halves]
        line = pltpu.roll(take(gate_gain, slice(0, 1), 48 * i, 48, lane_row), 80, 1)
        for g, gain in enumerate((heads_gain, gated_gain, rear_gain, final_gain)):
            start = 16 * (g + 1)
            block = gain[:, CHAN * (i // 8) : CHAN * (i // 8 + 1)]
            value = pltpu.roll(block, (start - 16 * i) % CHAN, 1)
            inside = jnp.logical_and(lane_row >= start, lane_row < start + 16)
            line = jnp.where(inside, value, line)
        quads[1] = jnp.where(last, line, quads[1])
        quads[3] = jnp.where(last, stat_line, quads[3])
        return quads

    for i in [*range(8), *range(16, 24)]:
        x, spot = i // 16, i % 8
        pairs = zip(quads_of(i), quads_of(i + 8))
        for q, (low, high) in enumerate(pairs):
            lanes = slice(CHAN * q, CHAN * (q + 1))
            keep[x, spot, :, lanes] = jnp.where(mine == 0, low, high).astype(LOW)
            send[x, spot, :, lanes] = jnp.where(mine == 0, high, low).astype(LOW)


def round_small(total):
    quad = total[:, 3 * CHAN :]
    lane = lax.broadcasted_iota(jnp.int32, quad.shape, 1)
    row = lax.broadcasted_iota(jnp.int32, quad.shape, 0)
    stat = jnp.logical_and(row == SMALL - 1, lane < STATS)
    rest = jnp.where(stat, quad - quad.astype(LOW).astype(F32), 0.0)
    quad = quad + pltpu.roll(rest, STATS, 1)
    return jnp.concatenate([total[:, : 3 * CHAN], quad], axis=1).astype(LOW)


def core_sum_kernel(info, *refs, sizes):
    inputs, out = refs[:-1], refs[-1]
    half = len(inputs) // 2
    keeps, gots = inputs[:half], inputs[half:]

    def one(z, _):
        for chip in range(4):
            x, spot = chip // 2, 2 * z + chip % 2
            start = 0
            for keep, got, (rows, small) in zip(keeps, gots, sizes):
                span = slice(start, start + rows)
                start += rows
                if small:
                    total = keep[x, spot].astype(F32) + got[x, spot].astype(F32)
                    out[chip, z, span, :] = round_small(total)
                else:
                    out[chip, z, span, :] = keep[x, spot] + got[x, spot]
        return 0

    lax.fori_loop(0, 4, one, 0)


def plane_sum_kernel(info, pieces, *outs, sizes):
    for e in range(4):
        zi = lax.rem(info[PLACE] + e, 4)
        start = 0
        for rows in sizes:
            small, rows = rows < 0, abs(rows)
            span = slice(start, start + rows)
            start += rows
            total = sum(pieces[chip, zi, span, :].astype(F32) for chip in range(4))
            if e == 0:
                outs[0][span, :] = total
            elif small:
                outs[e][span, :] = round_small(total)
            else:
                outs[e][span, :] = total.astype(LOW)


def line_sum_kernel(info, keep, one, two, three, *refs, pieces):
    refs = list(refs)
    start = 0
    for rows, what in pieces:
        span = slice(start, start + rows)
        start += rows
        total = keep[span, :]
        for piece in (one, two, three):
            total += piece[span, :].astype(F32)
        if what == "small":
            quads = [total[:, CHAN * q : CHAN * (q + 1)] for q in range(4)]
            gate_taps, merge_taps, heads_gain, gated_gain, rear_gain, final_gain, gate_gain, stats = refs
            gate_taps[0:SMALL, :] = quads[0][:, :48]
            gate_taps[SMALL : 2 * SMALL - 1, :] = quads[1][: SMALL - 1, :48]
            merge_taps[0:SMALL, :] = quads[2][:, :32]
            merge_taps[SMALL : 2 * SMALL - 1, :] = quads[3][: SMALL - 1, :32]
            line = quads[1][SMALL - 1 :, :]
            for g, target in enumerate((heads_gain, gated_gain, rear_gain, final_gain)):
                target[...] = pltpu.roll(line, CHAN - 16 * (g + 1), 1)[:, :16]
            gate_gain[...] = pltpu.roll(line, CHAN - 80, 1)[:, :48]
            line = quads[3][SMALL - 1 :, :]
            line += pltpu.roll(line, CHAN - STATS, 1)
            frames = jnp.sum(line[:, STATS - 1 : STATS])
            stats[...] = jnp.sqrt(line[:, : STATS - 1] / (frames * WIDTH))
        elif what == "gain":
            owner = info[OWNER]
            line = jnp.zeros((1, CHAN), F32)
            for b in range(WIDTH // CHAN):
                block = total[0:1, CHAN * b : CHAN * (b + 1)]
                line = jnp.where(owner // 8 == b, block, line)
            line = pltpu.roll(line, lax.rem(CHAN - 16 * lax.rem(owner, 8), CHAN), 1)
            refs.pop(0)[...] = line[:, :16]
        elif what == "left":
            given, target = refs.pop(0), refs[0]
            target[:, : given.shape[1]] = given[...]
        else:
            shift = 0
            if what == "right":
                target = refs.pop(0)
                shift = target.shape[1] // 2
            else:
                target = refs.pop(0)
            height = target.shape[0]
            for q in range(rows // height):
                lanes = slice(shift + WIDTH * q, shift + WIDTH * (q + 1))
                target[:, lanes] = total[height * q : height * (q + 1), :]


def run(tasks, info, after=()):
    counts = [(len(inputs), len(outputs)) for _, inputs, outputs in tasks]

    def tasks_kernel(info_ref, *refs):
        total = sum(count for count, _ in counts)
        ins, outs = list(refs[:total]), list(refs[total:])
        for (kernel, _, _), (taken, given) in zip(tasks, counts):
            kernel(info_ref, *ins[:taken], *outs[:given])
            del ins[:taken], outs[:given]

    results = call(
        tasks_kernel,
        (1,),
        all_of(*[array for _, inputs, _ in tasks for array in inputs]),
        plain(*[output for _, _, outputs in tasks for output in outputs]),
        [],
        info,
        after=after,
        room=24,
    )
    grouped = []
    for _, given in counts:
        grouped.append(results[:given])
        results = results[given:]
    return grouped


def core_sum(pairs):
    sizes = tuple((pair[0].shape[2], pair[0].shape[2] == SMALL) for pair in pairs)
    total = sum(rows for rows, _ in sizes)
    return (
        functools.partial(core_sum_kernel, sizes=sizes),
        [pair[i] for i in (0, 1) for pair in pairs],
        [((4, 4, total, WIDTH), LOW)],
    )


def plane_sum(pieces, sizes):
    total = pieces.shape[2]
    return (
        functools.partial(plane_sum_kernel, sizes=sizes),
        [pieces],
        [((total, WIDTH), F32)] + [((total, WIDTH), LOW)] * 3,
    )


def line_sum(sums, pieces, outputs, given=()):
    own, rest = sums
    return (
        functools.partial(line_sum_kernel, pieces=pieces),
        [own, *rest, *given],
        [(shape, F32) for shape in outputs],
    )


def line_swap(sums):
    return sums[0], [lax.ppermute(array, "z", ring(4, d)) for d, array in zip((1, 2, 3), sums[1:])]


def pack_small(layer, count):
    return (
        functools.partial(pack_small_kernel, count_at=SEG + 2 * count),
        [*layer.small_grads(), *layer.stats()],
        [((2, 8, SMALL, WIDTH), LOW)] * 2,
    )


def unpack_small(front, info):
    block = (4, 4, SMALL, WIDTH), lambda *_: (0, 0, 8, 0)
    gate_taps, merge_taps, gains, gate_full = call(
        unpack_kernel,
        (1,),
        [(array, *block) for array in front],
        plain(
            ((32, 3 * WIDTH), F32), ((32, 2 * WIDTH), F32), ((8, WIDTH), F32), ((1, 3 * WIDTH), F32)
        ),
        [],
        info,
    )
    lines = [gains[g : g + 1] for g in range(5)]
    return gate_taps, merge_taps, lines[0], lines[1], lines[2], gate_full, lines[3], lines[4]


def grid_device(
    features, cotangent, lengths, front_up, front_down, heads_input, heads_output, gated_input,
    gated_output, merge_output, rear_up, rear_down, gate_kernel, merge_kernel, front_gain,
    heads_gain, gated_gain, gate_gain, rear_gain, final_gain,
):
    x, k, z, y = (lax.axis_index(name) for name in ("x", "k", "z", "y"))
    places = [k] + [lax.rem(place, 4) for place in (z, z + 3, z + 2, z + 1)]
    places.append(((x * 2 + k) * 4 + z) * 2 + y)
    spots = jnp.stack([place.astype(jnp.int32) for place in places])
    layer = Layer(features, cotangent, lengths[0], spots, gate_kernel.shape[0])
    info = layer.info

    front, middle, rear = call(
        pack_kernel,
        (1,),
        all_of(
            front_up, front_down, heads_input, heads_output, gated_input, gated_output,
            merge_output, rear_up, rear_down, gate_kernel, merge_kernel,
            *[
                gain.reshape(1, -1)
                for gain in (front_gain, heads_gain, gated_gain, rear_gain, final_gain, gate_gain)
            ],
        ),
        plain(((144, WIDTH), LOW), ((208, WIDTH), LOW), ((160, WIDTH), LOW)),
        [pltpu.VMEM((SMALL, WIDTH), F32)],
        spots,
    )
    front_four = place(place_line_kernel, [front] + line_sends(front), 144, info)
    front = plane_exchange(front_four)
    middle = tie(middle, front_four)
    middle_four = place(place_line_kernel, [middle] + line_sends(middle), 208, info)
    front = tie(front, middle_four)
    middle = plane_exchange(tie(middle_four, front))
    rear = tie(rear, front)
    rear_lines = line_sends(rear)
    front = front, core_swap(front)
    layer.set_small(unpack_small(front, info))
    mark = layer.front_forward(front)
    rear_four = place(place_line_kernel, [rear] + rear_lines, 160, info, after=(mark,))
    middle = tie(middle, rear_four)
    rear = plane_exchange(tie(rear_four, middle))
    middle = middle, core_swap(middle)
    mark = layer.branches_forward(middle)
    rear = tie(rear, mark)
    rear = rear, core_swap(rear)

    send, rear_keep, merge_send, merge_keep = layer.merge_rear(rear)
    rear_got = core_swap(send)
    ((rear_four,),) = run([core_sum([(rear_keep, rear_got)])], info)
    merge_got = core_swap(tie(merge_send, rear_got))
    rear_plane = plane_exchange(rear_four)
    send, wide_keep = layer.branches_backward(after=(rear_four,))
    wide_got = core_swap(tie(send, rear_plane))
    (rear_sums,) = run([plane_sum(rear_plane, (128,))], info, after=(layer.gated_total,))
    ((wide_four,),) = run(
        [core_sum([(merge_keep, merge_got), (wide_keep, wide_got)])], info,
        after=(rear_sums[0],),
    )
    rear_sums = line_swap(rear_sums)
    wide_plane = plane_exchange(tie(wide_four, rear_plane))
    send, gate_keep = layer.gated_gate(after=(wide_four,))
    gate_got = core_swap(send)
    ((small_send, small_keep),) = run(
        [pack_small(layer, lengths.shape[1])], info, after=rear_sums[1]
    )
    small_got = core_swap(small_send)
    send, down_keep = layer.front_hidden(after=(small_send,))
    down_got = core_swap(tie(send, wide_plane))
    (wide_sums,) = run([plane_sum(wide_plane, (192,))], info, after=(layer.front_grad,))
    ((last_four,),) = run(
        [
            core_sum([(gate_keep, gate_got), (down_keep, down_got), (small_keep, small_got)]),
        ],
        info,
        after=(wide_sums[0],),
    )
    wide_sums = line_swap(wide_sums)
    last_plane = plane_exchange(tie(last_four, wide_plane))
    send, up_keep = layer.front_input(after=(last_four, *wide_sums[1]))
    up_got = core_swap(send)
    ((front_four,),) = run([core_sum([(up_keep, up_got)])], info)
    half_shape = (gated_input.shape[0], gated_input.shape[1] // 2)
    front_plane = plane_exchange(tie(front_four, last_plane))
    (last_sums,) = run([plane_sum(last_plane, (48, 64, -SMALL))], info, after=(front_four,))
    last_sums = line_swap(last_sums)
    (
        (rear_up_grad, rear_down_grad),
        (
            merge_output_grad, gated_left_grad, gated_output_grad, heads_input_grad,
            heads_output_grad,
        ),
    ) = run(
        [
            line_sum(rear_sums, ((64, None), (64, None)), (rear_up.shape, rear_down.shape)),
            line_sum(
                wide_sums, ((32, None), (48, None), (48, None), (48, None), (16, None)),
                (
                    merge_output.shape, half_shape, gated_output.shape, heads_input.shape,
                    heads_output.shape,
                ),
            ),
        ],
        info,
        after=(last_sums[0],),
    )
    (front_sums,) = run(
        [plane_sum(front_plane, (80,))], info, after=(last_sums[0], merge_output_grad)
    )
    front_sums = line_swap(front_sums)
    vector = (1, front_gain.shape[0])
    (
        (
            gated_input_grad, front_down_grad, gate_kernel_grad, merge_kernel_grad,
            heads_gain_grad, gated_gain_grad, rear_gain_grad, final_gain_grad, gate_gain_grad,
            statistics,
        ),
    ) = run(
        [
            line_sum(
                last_sums,
                ((0, "left"), (48, "right"), (64, None), (16, "small")),
                (
                    gated_input.shape, front_down.shape, gate_kernel.shape, merge_kernel.shape,
                    vector, vector, vector, vector, (1, gate_gain.shape[0]), (1, STATS - 1),
                ),
                given=(gated_left_grad,),
            ),
        ],
        info,
        after=(front_sums[0],),
    )
    ((front_up_grad, front_gain_grad),) = run(
        [line_sum(front_sums, ((64, None), (16, "gain")), (front_up.shape, vector))], info,
        after=(statistics,),
    )
    return (
        layer.encoded, layer.features_grad, front_up_grad, front_down_grad, heads_input_grad,
        heads_output_grad, gated_input_grad, gated_output_grad, merge_output_grad, rear_up_grad,
        rear_down_grad, gate_kernel_grad, merge_kernel_grad, front_gain_grad[0],
        heads_gain_grad[0], gated_gain_grad[0], gate_gain_grad[0], rear_gain_grad[0],
        final_gain_grad[0], statistics[0],
    )


def pack_rows(shard):
    rows, columns = shard.shape
    pieces = shard.reshape(rows, columns // WIDTH, WIDTH).transpose(1, 0, 2)
    return pieces.reshape(rows * columns // WIDTH, WIDTH)


def pad_lines(flat):
    rows = -(-flat.shape[-1] // (WIDTH * 16)) * 16
    spare = [(0, 0)] * (flat.ndim - 1) + [(0, rows * WIDTH - flat.shape[-1])]
    return jnp.pad(flat, spare).reshape(flat.shape[:-1] + (rows, WIDTH))


def to_owners(weight):
    rows, columns = weight.shape
    pieces = weight.reshape(BLOCKS, rows // BLOCKS, columns // WIDTH, WIDTH)
    pieces = pieces.transpose(0, 2, 1, 3).reshape(2, 2, 4, 2, -1, WIDTH)
    pieces = pieces.transpose(1, 0, 3, 2, 4, 5)
    return pieces.reshape(2, 4, 4, -1, WIDTH)


def from_owners(halves, rows, columns):
    send, keep = halves
    pieces = jnp.stack([keep, send], axis=1)
    pieces = pieces.reshape(BLOCKS, columns // WIDTH, rows // BLOCKS, WIDTH)
    return pieces.transpose(0, 2, 1, 3).reshape(rows, columns)


def any_device(features, cotangent, lengths, *shards, axes):
    count = lax.axis_size(axes)
    matrices, smaller = shards[:9], shards[9:]
    packed = [pack_rows(element) for element in matrices]
    packed.append(pad_lines(jnp.concatenate([element.reshape(-1) for element in smaller])))
    gathered = lax.all_gather(jnp.concatenate(packed), axes, axis=0)
    weights = []
    start = 0
    for element, piece in zip(matrices, packed):
        rows, columns = element.shape
        window = gathered[:, start : start + piece.shape[0]]
        start += piece.shape[0]
        window = window.reshape(count, columns // WIDTH, rows, WIDTH).transpose(0, 2, 1, 3)
        weights.append(to_owners(window.reshape(count * rows, columns)))
    flat = gathered[:, start:].reshape(count, -1).astype(F32)
    lines = []
    start = 0
    for element in smaller:
        window = flat[:, start : start + element.size]
        start += element.size
        if element.ndim == 2:
            window = window.reshape((count,) + element.shape).transpose(1, 0, 2)
            window = window.reshape(element.shape[0], -1)
            lines.append(jnp.pad(window, ((0, 1), (0, 0))))
        else:
            lines.append(window.reshape(1, -1))
    up, down, h_in, h_out, g_in, g_out, m_out, r_up, r_down = weights

    def chunk(*members):
        return tuple(jnp.concatenate([member[i] for member in members], axis=2) for i in (0, 1))

    front = chunk(up, down)
    rear = chunk(r_up, r_down, m_out)
    layer = Layer(features, cotangent, lengths[0], jnp.zeros((SEG,), jnp.int32), smaller[0].shape[0])
    layer.set_small(lines)
    layer.front_forward(front)
    layer.branches_forward(chunk(g_in, g_out, h_in, h_out))
    rear = layer.merge_rear(rear)
    rear, merge = rear[:2], rear[2:]
    wide = layer.branches_backward()
    right = layer.gated_gate()
    front_down_halves = layer.front_hidden()
    front_up_halves = layer.front_input()

    def part(pair, start, stop):
        return tuple(array[:, :, start:stop] for array in pair)

    gated_halves = tuple(
        jnp.concatenate([one[:, :, :48], two], axis=2) for one, two in zip(wide, right)
    )
    ordered = (
        part(front_up_halves, 0, 64), front_down_halves, part(wide, 96, 144),
        part(wide, 144, 160), gated_halves, part(wide, 48, 96), merge,
        part(rear, 0, 64), part(rear, 64, 128),
    )
    front_gain = front_up_halves[1][0, 0, 64].astype(F32)
    small_grads = layer.small_grads()
    pieces = []
    for element, halves in zip(matrices, ordered):
        rows, columns = element.shape
        full = from_owners(halves, rows * count, columns)
        full = full.reshape(count, rows, columns // WIDTH, WIDTH).transpose(0, 2, 1, 3)
        pieces.append(full.reshape(count, -1, WIDTH))
    gate_taps, merge_taps, heads_gain, gated_gain, rear_gain, final_gain, gate_gain = small_grads
    small_full = (gate_taps, merge_taps, front_gain, heads_gain, gated_gain, gate_gain, rear_gain, final_gain)
    flat = []
    for element, full in zip(smaller, small_full):
        if element.ndim == 2:
            full = full[: element.shape[0]].reshape(element.shape[0], count, -1).transpose(1, 0, 2)
        flat.append(full.reshape(count, -1))
    pieces.append(pad_lines(jnp.concatenate(flat, axis=1).astype(LOW)))
    summed = lax.psum_scatter(jnp.concatenate(pieces, axis=1), axes, scatter_dimension=0)
    outputs = []
    start = 0
    for element, piece in zip(matrices, pieces):
        rows, columns = element.shape
        window = summed[start : start + piece.shape[1]].astype(F32)
        start += piece.shape[1]
        window = window.reshape(columns // WIDTH, rows, WIDTH).transpose(1, 0, 2)
        outputs.append(window.reshape(rows, columns))
    flat = summed[start:].reshape(-1).astype(F32)
    start = 0
    for element in smaller:
        outputs.append(flat[start : start + element.size].reshape(element.shape))
        start += element.size
    front_stat, rear_stat = layer.stats()
    squares = jnp.stack(
        [
            front_stat[0], front_stat[1], rear_stat[0], rear_stat[2], front_stat[2], rear_stat[1],
            rear_stat[3],
        ]
    )
    totals = lax.psum(
        jnp.append(jnp.sum(squares, axis=1), jnp.sum(lengths).astype(F32)), axes
    )
    statistics = jnp.sqrt(totals[:7] / (totals[7] * features.shape[1]))
    return (layer.encoded, layer.features_grad) + tuple(outputs) + (statistics,)


def solution(mesh):
    body = grid_device
    axes = ("x", "k", "z", "y")
    if mesh.devices.shape == (4, 8):
        mesh = Mesh(mesh.devices.reshape(2, 2, 4, 2), axes)
    else:
        axes = tuple(mesh.axis_names)
        body = functools.partial(any_device, axes=axes)
    rows, columns, vector = P(axes, None), P(None, axes), P(axes)
    weights = (rows,) * 9 + (columns,) * 2 + (vector,) * 6
    return jax.shard_map(
        body,
        mesh=mesh,
        in_specs=(rows, rows, rows) + weights,
        out_specs=(rows, rows) + weights + (P(),),
        check_vma=False,
    )
```

```python
import functools

import jax
import jax.numpy as jnp
from jax import lax
from jax.experimental import pallas as pl
from jax.experimental.pallas import tpu as pltpu
from jax.sharding import Mesh, PartitionSpec as P

HEADS = 8
EPSILON = 1e-05
NEGATIVE = -1000000000.0
TILE = 8
GAP = 16
CHAN = 128
PLACE = 1
OWNER = 5
SEG = 6
WIDTH = 512
BLOCKS = 32
F32 = jnp.float32
LOW = jnp.bfloat16


def dot(left, right):
    return jnp.dot(left, right, preferred_element_type=F32)


def dot_tn(left, right):
    return lax.dot_general(left, right, (((0,), (0,)), ((), ())), preferred_element_type=F32)


def dot_nt(left, right):
    return lax.dot_general(left, right, (((1,), (1,)), ((), ())), preferred_element_type=F32)


def normalize(values):
    centred = values - jnp.mean(values, axis=-1, keepdims=True)
    variance = jnp.mean(centred * centred, axis=-1, keepdims=True)
    inverse = lax.rsqrt(variance + EPSILON)
    return centred * inverse, inverse


def normalize_back(upstream, gain, normal, inverse):
    scaled = upstream * gain
    mean_scaled = jnp.mean(scaled, axis=-1, keepdims=True)
    mean_cross = jnp.mean(scaled * normal, axis=-1, keepdims=True)
    return inverse * (scaled - mean_scaled - normal * mean_cross)


def row_sum(values):
    return jnp.sum(values, axis=0, keepdims=True)


GELU_A = 0.7978845608028654
GELU_B = 0.044715


def gelu(v):
    return 0.5 * v * (1.0 + jnp.tanh(GELU_A * (v + GELU_B * v * v * v)))


def gelu_pair(v):
    square = v * v
    bend = jnp.tanh(GELU_A * (v + GELU_B * square * v))
    value = 0.5 * v * (1.0 + bend)
    slope = 0.5 * (1.0 + bend) + 0.5 * v * (1.0 - bend * bend) * (
        GELU_A * (1.0 + 3.0 * GELU_B * square)
    )
    return value, slope


def silu(v):
    return v * jax.nn.sigmoid(v)


def store_halves(value, send, keep, mine, rows, start):
    parts = value.astype(LOW).reshape(2, 2, 8, rows, WIDTH)

    @pl.when(mine == 0)
    def _():
        keep[:, :, pl.ds(start, rows), :] = parts[:, 0]
        send[:, :, pl.ds(start, rows), :] = parts[:, 1]

    @pl.when(mine == 1)
    def _():
        keep[:, :, pl.ds(start, rows), :] = parts[:, 1]
        send[:, :, pl.ds(start, rows), :] = parts[:, 0]


def join_rows(first, second, mine):
    cores = jnp.where(mine == 0, first, second), jnp.where(mine == 0, second, first)
    return jnp.concatenate(
        [core[2 * x + y, z] for x in (0, 1) for core in cores for z in range(4) for y in (0, 1)]
    )


def join_columns(first, second, mine):
    blocks = range(0, first.shape[2], 16)
    return jnp.concatenate(
        [join_rows(first[:, :, i : i + 16, :], second[:, :, i : i + 16, :], mine) for i in blocks],
        axis=1,
    )


def join_lines(first, second, mine):
    cores = jnp.where(mine == 0, first, second), jnp.where(mine == 0, second, first)
    return jnp.concatenate([core[y, z] for core in cores for z in range(4) for y in (0, 1)])


def store_columns(value, send, keep, mine, start):
    for i in range(value.shape[1] // WIDTH):
        store_halves(value[:, WIDTH * i : WIDTH * (i + 1)], send, keep, mine, 16, start + 16 * i)


def visits(info, segments, body):
    for s in range(segments):
        begin, end = info[SEG + s], info[SEG + segments + s]

        def visit(i, _, s=s, begin=begin, end=end):
            row = i * TILE + lax.broadcasted_iota(jnp.int32, (TILE, CHAN), 0)
            inside = jnp.logical_and(row >= begin, row < end)
            body(s, pl.multiple_of(i * TILE, TILE), inside)
            return 0

        lax.fori_loop(begin // TILE, (end + TILE - 1) // TILE, visit, 0)


def spread(source, padded, info, segments, blocks):
    padded[...] = jnp.zeros_like(padded)

    def body(s, base, inside):
        for c in range(blocks):
            value = source[pl.ds(base, TILE), c * CHAN : (c + 1) * CHAN]
            padded[c, pl.ds(base + GAP * (s + 1), TILE), :] = jnp.where(inside, value, 0.0)

    visits(info, segments, body)


def unspread(padded, target, info, segments, blocks):
    def body(s, base, inside):
        for c in range(blocks):
            lanes = slice(c * CHAN, (c + 1) * CHAN)
            value = padded[c, pl.ds(base + GAP * (s + 1), TILE), :]
            target[pl.ds(base, TILE), lanes] = jnp.where(
                inside, value, target[pl.ds(base, TILE), lanes]
            )

    visits(info, segments, body)


def conv_rows(padded, kernel, out, steps_ref, sums, blocks, taps, flip):
    half = (taps - 1) // 2
    rows = padded.shape[1]
    pairs = (rows - 2 * GAP) // (4 * GAP)
    order = [taps - 1 - j if flip else j for j in range(taps)]
    for c in range(blocks):
        steps_ref[c, 0 : rows - GAP, :] = padded[c, 0 : rows - GAP, :] - padded[c, GAP:rows, :]
    for j in range(GAP):
        total = kernel[order[j] : order[j] + 1, :]
        if j + GAP < taps:
            total = total + kernel[order[j + GAP] : order[j + GAP] + 1, :]
        sums[j : j + 1, :] = total

    def body(step, _):
        c = step // 2
        base = GAP + lax.rem(step, 2) * (pairs * 2 * GAP)
        lanes = pl.ds(pl.multiple_of(c * CHAN, CHAN), CHAN)
        for w in range(pairs):
            start = base + 2 * GAP * w
            first_part = second = third = jnp.zeros((GAP, CHAN), F32)
            for j in range(GAP):
                row = start + j - half
                first_part += kernel[pl.ds(order[j], 1), lanes] * steps_ref[c, pl.ds(row, GAP), :]
                second += sums[pl.ds(j, 1), lanes] * padded[c, pl.ds(row + GAP, GAP), :]
                if j + GAP < taps:
                    third += (
                        kernel[pl.ds(order[j + GAP], 1), lanes]
                        * steps_ref[c, pl.ds(row + GAP, GAP), :]
                    )
            start = pl.multiple_of(start, TILE)
            out[c, pl.ds(start, GAP), :] = first_part + second
            out[c, pl.ds(start + GAP, GAP), :] = second - third
        return 0

    lax.fori_loop(0, blocks * 2, body, 0)


def conv_taps(padded_grad, padded, steps_ref, out, blocks, taps):
    half = (taps - 1) // 2
    rows = padded.shape[1]
    pairs = (rows - 2 * GAP) // (2 * GAP)

    def fold(value):
        return value[:TILE] + value[TILE:]

    def block(c, _):
        lanes = pl.ds(pl.multiple_of(c * CHAN, CHAN), CHAN)
        zero = jnp.zeros((TILE, CHAN), F32)

        def body(step, sums):
            start = pl.multiple_of(step * 2 * GAP + GAP, TILE)
            lower = padded_grad[c, pl.ds(start, GAP), :]
            upper = padded_grad[c, pl.ds(start + GAP, GAP), :]
            both = lower + upper
            new = list(sums)
            for j in range(GAP):
                row = start + j - half
                shared = fold(both * padded[c, pl.ds(row + GAP, GAP), :])
                new[j] = new[j] + (fold(lower * steps_ref[c, pl.ds(row, GAP), :]) + shared)
                if j + GAP < taps:
                    rest = fold(upper * steps_ref[c, pl.ds(row + GAP, GAP), :])
                    new[j + GAP] = new[j + GAP] + (shared - rest)
            return tuple(new)

        sums = lax.fori_loop(0, pairs, body, (zero,) * taps)
        for j in range(taps):
            out[pl.ds(j, 1), lanes] = row_sum(sums[j])
        return 0

    lax.fori_loop(0, blocks, block, 0)


def front_forward_kernel(
    info, x_ref, gain, valid, up, up_two, down, down_two, out, before_out, stat, low, total
):
    h = pl.program_id(0)
    mine = info[0]
    up_value = join_columns(up[...], up_two[...], mine)
    down_value = join_lines(down[...], down_two[...], mine)

    @pl.when(h == 0)
    def _():
        normal, _ = normalize(x_ref[...].astype(F32))
        low[...] = (normal * gain[...]).astype(LOW)
        total[...] = jnp.zeros_like(total)

    before = dot(low[...], up_value)
    before_out[...] = before
    total[...] += dot(silu(before).astype(LOW), down_value)

    @pl.when(h == pl.num_programs(0) - 1)
    def _():
        x = x_ref[...].astype(F32)
        part = 0.5 * total[...]
        after = x + part
        out[...] = after
        v = valid[...]
        stat[0:1, :] = row_sum(x * x * v)
        stat[1:2, :] = row_sum(after * after * v)
        stat[2:3, :] = row_sum(part * part * v)
        stat[3:, :] = jnp.zeros((5, WIDTH), F32)


def head_masks(segs_col, segs_row):
    allowed = segs_col == segs_row
    lane = lax.broadcasted_iota(jnp.int32, (1, CHAN), 1)
    return allowed, (lane < CHAN // 2, lane >= CHAN // 2)


def head_probs(query, key, allowed, scale):
    scores = jnp.where(allowed, dot_nt(query, key) * scale, NEGATIVE)
    exponent = jnp.exp(scores - jnp.max(scores, axis=-1, keepdims=True))
    return exponent / jnp.sum(exponent, axis=-1, keepdims=True)


def heads_forward(
    info, low, segs_col, segs_row, w_in, w_in_two, w_out, w_out_two, attended, packed, mixed,
):
    mine = info[0]
    scale = (WIDTH // HEADS) ** -0.5
    packed[...] = dot(low, join_columns(w_in[...], w_in_two[...], mine)).astype(LOW)
    allowed, halves = head_masks(segs_col[...], segs_row[...])

    def pair(p, _):
        lanes = [
            pl.ds(pl.multiple_of(WIDTH * q + CHAN * p, CHAN), CHAN) for q in range(3)
        ]
        query, key, value = (packed[:, lane] for lane in lanes)
        parts = []
        for half in halves:
            probs = head_probs(jnp.where(half, query, 0), key, allowed, scale)
            parts.append(dot(probs.astype(LOW), value))
        mixed[:, lanes[0]] = jnp.where(halves[0], parts[0], parts[1]).astype(LOW)
        return 0

    lax.fori_loop(0, HEADS // 2, pair, 0)
    attended[...] = dot(mixed[...], join_rows(w_out[...], w_out_two[...], mine))


def heads_backward(
    info, grad, x_ref, gain, segs_col, segs_row, packed, mixed, w_in, w_in_two, w_out, w_out_two,
    stream, gain_grad, send, keep, mixed_grad, packed_grad, low,
):
    scale = (WIDTH // HEADS) ** -0.5
    mine = info[0]
    attended_low = grad[...].astype(LOW)
    store_halves(dot_tn(mixed[...], attended_low), send, keep, mine, 16, 144)
    mixed_grad[...] = dot_nt(attended_low, join_rows(w_out[...], w_out_two[...], mine)).astype(LOW)
    normal, inverse = normalize(x_ref[...])
    low[...] = (normal * gain[...]).astype(LOW)
    allowed, halves = head_masks(segs_col[...], segs_row[...])

    def pair(p, _):
        lanes = [
            pl.ds(pl.multiple_of(WIDTH * q + CHAN * p, CHAN), CHAN) for q in range(3)
        ]
        query, key, value = (packed[:, lane] for lane in lanes)
        upstream = mixed_grad[:, lanes[0]]
        parts = []
        for half in halves:
            probs = head_probs(jnp.where(half, query, 0), key, allowed, scale)
            probs_grad = dot_nt(jnp.where(half, upstream, 0), value)
            value_grad = dot_tn(probs.astype(LOW), upstream)
            inner = jnp.sum(probs_grad * probs, axis=-1, keepdims=True)
            score_grad = (probs * (probs_grad - inner)).astype(LOW)
            query_grad = dot(score_grad, key) * scale
            key_grad = dot_tn(score_grad, query) * scale
            parts.append((query_grad, key_grad, value_grad))
        for q in range(3):
            packed_grad[:, lanes[q]] = jnp.where(halves[0], parts[0][q], parts[1][q]).astype(LOW)
        return 0

    lax.fori_loop(0, HEADS // 2, pair, 0)
    pieces = packed_grad[...]
    store_columns(dot_tn(low[...], pieces), send, keep, mine, 96)
    total = dot_nt(pieces, join_columns(w_in[...], w_in_two[...], mine))
    gain_grad[...] = row_sum(total * normal)
    stream[...] = normalize_back(total, gain[...], normal, inverse)


def branches_forward_kernel(
    info, x_ref, heads_gain, segs_col, segs_row, w_heads, w_heads_two, w_mix, w_mix_two,
    gain, gate_gain, taps_ref, w_in, w_in_two, w_out, w_out_two, attended, packed, mixed,
    gated, before_out, normal_out, inverse_out, part_out, product,
    low, act, padded, conv, steps_ref, sums, *, segments, taps,
):
    j = pl.program_id(0)
    thirds = WIDTH * 3

    @pl.when(j == 0)
    def _():
        normal, _ = normalize(x_ref[...])
        low[...] = (normal * gain[...]).astype(LOW)
        heads_forward(
            info, (normal * heads_gain[...]).astype(LOW), segs_col, segs_row, w_heads,
            w_heads_two, w_mix, w_mix_two, attended, packed, mixed,
        )

    before = dot(low[...], join_columns(w_in[...], w_in_two[...], info[0]))
    before_out[...] = before
    value = gelu(before)

    @pl.when(j == 0)
    def _():
        normal, inverse = normalize(value)
        normal_out[...] = normal
        inverse_out[...] = inverse
        act[...] = normal * gate_gain[...]
        blocks = thirds // CHAN
        spread(act, padded, info, segments, blocks)
        conv_rows(padded, taps_ref, conv, steps_ref, sums, blocks, taps, False)
        unspread(conv, part_out, info, segments, blocks)

    @pl.when(j == 1)
    def _():
        product[...] = (value * part_out[...]).astype(LOW)
        gated[...] = dot(product[...], join_rows(w_out[...], w_out_two[...], info[0]))


def branches_backward_kernel(
    info, attended_grad, x_ref, heads_gain, segs_col, segs_row, packed, mixed, w_heads,
    w_heads_two, w_mix, w_mix_two, grad, gain, before, part, product, w_in, w_in_two, w_out,
    w_out_two,
    stream, heads_gain_grad, part_grad, total_out, send, keep, low, mixed_grad, packed_grad,
):
    mine = info[0]
    heads_backward(
        info, attended_grad, x_ref, heads_gain, segs_col, segs_row, packed, mixed, w_heads,
        w_heads_two, w_mix, w_mix_two, stream, heads_gain_grad, send, keep, mixed_grad,
        packed_grad, low,
    )
    normal, _ = normalize(x_ref[...])
    low[...] = (normal * gain[...]).astype(LOW)
    gated_low = grad[...].astype(LOW)
    store_halves(dot_tn(product[...], gated_low), send, keep, mine, 48, 48)
    upstream = dot_nt(gated_low, join_rows(w_out[...], w_out_two[...], mine))
    value, slope = gelu_pair(before[...])
    part_grad[...] = upstream * value
    before_grad = (upstream * part[...] * slope).astype(LOW)
    store_columns(dot_tn(low[...], before_grad), send, keep, mine, 0)
    total_out[...] = dot_nt(before_grad, join_columns(w_in[...], w_in_two[...], mine))


def gated_conv(
    info, part_grad, normal_ref, inverse_ref, gate_gain, taps_ref,
    gate_gain_grad, taps_grad, padded, padded_grad, conv, work, steps_ref, sums, segments, taps,
):
    blocks = 3 * WIDTH // CHAN
    spread(part_grad, padded_grad, info, segments, blocks)
    work[...] = normal_ref[...] * gate_gain[...]
    spread(work, padded, info, segments, blocks)
    rows = padded.shape[1]
    for c in range(blocks):
        steps_ref[c, 0 : rows - GAP, :] = padded[c, 0 : rows - GAP, :] - padded[c, GAP:rows, :]
    conv_taps(padded_grad, padded, steps_ref, taps_grad, blocks, taps)
    conv_rows(padded_grad, taps_ref, conv, steps_ref, sums, blocks, taps, True)
    unspread(conv, work, info, segments, blocks)
    upstream = work[...]
    normal = normal_ref[...]
    gate_gain_grad[...] = row_sum(upstream * normal)
    work[...] = normalize_back(upstream, gate_gain[...], normal, inverse_ref[...])


def gated_gate_kernel(
    info, part_grad, normal_ref, inverse_ref, gate_gain, taps_ref, x_ref, gain, before, total_in,
    w_in, w_in_two,
    stream, gain_grad, gate_gain_grad, taps_grad, send, keep,
    padded, padded_grad, conv, work, steps_ref, sums, *, segments, taps,
):
    mine = info[0]
    gated_conv(
        info, part_grad, normal_ref, inverse_ref, gate_gain, taps_ref, gate_gain_grad,
        taps_grad, padded, padded_grad, conv, work, steps_ref, sums, segments, taps,
    )
    normal, inverse = normalize(x_ref[...])
    low = (normal * gain[...]).astype(LOW)
    _, slope = gelu_pair(before[...])
    before_grad = (work[...] * slope).astype(LOW)
    store_columns(dot_tn(low, before_grad), send, keep, mine, 0)
    total = total_in[...] + dot_nt(before_grad, join_columns(w_in[...], w_in_two[...], mine))
    gain_grad[...] = row_sum(total * normal)
    stream[...] = normalize_back(total, gain[...], normal, inverse)


def conv_add(padded, conv, taps_ref, steps_ref, sums, blocks, taps, flip):
    conv_rows(padded, taps_ref, conv, steps_ref, sums, blocks, taps, flip)
    for c in range(blocks):
        conv[c] += padded[c]


def hidden_back(x, mine, before, part_low, down, send, keep, start):
    gate = jax.nn.sigmoid(before)
    hidden = (before * gate).astype(LOW)
    hidden_grad = dot_nt(part_low, down)
    before_grad = (hidden_grad * (gate * (1.0 + before * (1.0 - gate)))).astype(LOW)
    down_grad = dot_tn(hidden, part_low).astype(LOW).reshape(2, 8, 64, WIDTH)

    @pl.when(mine == 0)
    def _():
        keep[x, :, start : start + 64, :] = down_grad[0]
        send[x, :, start : start + 64, :] = down_grad[1]

    @pl.when(mine == 1)
    def _():
        keep[x, :, start : start + 64, :] = down_grad[1]
        send[x, :, start : start + 64, :] = down_grad[0]

    return before_grad


def merge_rear_kernel(
    info, x_ref, attended, gated, taps_ref, weight, weight_two, gain, final_gain, valid, cotangent,
    up, up_two, down, down_two,
    encoded, stream, gain_grad, final_gain_grad, stat, attended_grad, gated_grad, taps_grad,
    send, keep, merge_send, merge_keep,
    low, before, part_grad, stream_grad, total, middle, joined, joined_low, padded, padded_grad,
    conv, steps_ref, sums, *, segments, taps,
):
    step = pl.program_id(0)
    h = jnp.where(step < 2, step, 3 - step)
    up_value = join_columns(up[...], up_two[...], info[0])
    down_value = join_lines(down[...], down_two[...], info[0])
    blocks = 2 * WIDTH // CHAN

    @pl.when(step == 0)
    def _():
        joined[:, :WIDTH] = attended[...]
        joined[:, WIDTH:] = gated[...]
        spread(joined, padded, info, segments, blocks)
        conv_add(padded, conv, taps_ref, steps_ref, sums, blocks, taps, False)
        unspread(conv, joined, info, segments, blocks)
        joined_low[...] = joined[...].astype(LOW)
        part = dot(joined_low[...], join_rows(weight[...], weight_two[...], info[0]))
        after = x_ref[...] + part
        middle[...] = after
        v = valid[...]
        stat[0:1, :] = row_sum(after * after * v)
        stat[1:2, :] = row_sum(part * part * v)
        normal, _ = normalize(after)
        low[...] = (normal * gain[...]).astype(LOW)
        total[...] = jnp.zeros_like(total)

    @pl.when(step < 2)
    def _():
        value = dot(low[...], up_value)
        before[step] = value
        total[...] += dot(silu(value).astype(LOW), down_value)

    @pl.when(step == 1)
    def _():
        part = 0.5 * total[...]
        after = middle[...] + part
        v = valid[...]
        stat[2:3, :] = row_sum(after * after * v)
        stat[3:4, :] = row_sum(part * part * v)
        stat[4:, :] = jnp.zeros((4, WIDTH), F32)
        normal, inverse = normalize(after)
        encoded[...] = (normal * final_gain[...] * v).astype(LOW)
        upstream = cotangent[...].astype(F32) * v
        final_gain_grad[...] = row_sum(upstream * normal)
        grad = normalize_back(upstream, final_gain[...], normal, inverse)
        stream_grad[...] = grad
        part_grad[...] = (0.5 * grad).astype(LOW)
        total[...] = jnp.zeros_like(total)

    @pl.when(step >= 2)
    def _():
        before_grad = hidden_back(
            h, info[0], before[h], part_grad[...], down_value, send, keep, 64
        )
        store_columns(
            dot_tn(low[...], before_grad), send, keep, info[0], pl.multiple_of(h * 32, 32)
        )
        total[...] += dot_nt(before_grad, up_value)

    @pl.when(step == 3)
    def _():
        normal, inverse = normalize(middle[...])
        gain_grad[...] = row_sum(total[...] * normal)
        grad = stream_grad[...] + normalize_back(total[...], gain[...], normal, inverse)
        stream[...] = grad
        grad_low = grad.astype(LOW)
        store_halves(dot_tn(joined_low[...], grad_low), merge_send, merge_keep, info[0], 32, 0)
        joined[...] = dot_nt(grad_low, join_rows(weight[...], weight_two[...], info[0]))
        spread(joined, padded_grad, info, segments, blocks)
        conv_taps(padded_grad, padded, steps_ref, taps_grad, blocks, taps)
        conv_add(padded_grad, conv, taps_ref, steps_ref, sums, blocks, taps, True)
        unspread(conv, joined, info, segments, blocks)
        attended_grad[...] = joined[:, :WIDTH]
        gated_grad[...] = joined[:, WIDTH:]


def front_hidden_kernel(
    info, grad, heads_stream, gated_stream, before, down, down_two,
    stream_out, before_grad, send, keep, part_grad,
):
    h = pl.program_id(0)

    @pl.when(h == 0)
    def _():
        stream_sum = grad[...] + heads_stream[...] + gated_stream[...]
        stream_out[...] = stream_sum
        part_grad[...] = (0.5 * stream_sum).astype(LOW)

    down_value = join_lines(down[...], down_two[...], info[0])
    before_grad[...] = hidden_back(
        h, info[0], before[...], part_grad[...], down_value, send, keep, 0
    )


def front_input_kernel(
    info, stream_grad, before_grad, x_ref, gain, up, up_two,
    x_grad, send, keep, low, total,
):
    h = pl.program_id(0)

    @pl.when(h == 0)
    def _():
        normal, _ = normalize(x_ref[...].astype(F32))
        low[...] = (normal * gain[...]).astype(LOW)
        total[...] = jnp.zeros_like(total)

    store_columns(
        dot_tn(low[...], before_grad[...]), send, keep, info[0], pl.multiple_of(h * 32, 32)
    )
    total[...] += dot_nt(before_grad[...], join_columns(up[...], up_two[...], info[0]))

    @pl.when(h == 1)
    def _():
        normal, inverse = normalize(x_ref[...].astype(F32))
        gain_grad = row_sum(total[...] * normal).astype(LOW)
        gain_rows = jnp.broadcast_to(gain_grad.reshape(1, 1, 1, WIDTH), (2, 8, 16, WIDTH))
        send[:, :, 64:80, :] = gain_rows
        keep[:, :, 64:80, :] = gain_rows
        x_grad[...] = (
            stream_grad[...] + normalize_back(total[...], gain[...], normal, inverse)
        ).astype(LOW)


def whole(shape):
    return pl.BlockSpec(shape, lambda *_: (0,) * len(shape))


def call(kernel, grid, inputs, outputs, scratch, info, flops=0, after=(), room=56):
    in_specs = [
        whole(array.shape) if block is None else pl.BlockSpec(block, index)
        for array, block, index in inputs
    ]
    out_specs = [
        whole(shape) if block is None else pl.BlockSpec(block, index)
        for shape, _, block, index in outputs
    ]
    arrays = [array for array, _, _ in inputs]
    shapes = [jax.ShapeDtypeStruct(shape, kind) for shape, kind, _, _ in outputs]
    moved = sum(array.size * array.dtype.itemsize for array in arrays)
    moved = sum(shape.size * shape.dtype.itemsize for shape in shapes) + min(moved, 1 << 24)
    skipped = len(after)
    name = getattr(kernel, "func", kernel).__name__

    def body(info_ref, *refs):
        kernel(info_ref, *refs[skipped:])

    return pl.pallas_call(
        body,
        grid_spec=pltpu.PrefetchScalarGridSpec(
            num_scalar_prefetch=1,
            grid=grid,
            in_specs=[pl.BlockSpec(memory_space=pl.ANY)] * skipped + in_specs,
            out_specs=out_specs,
            scratch_shapes=scratch,
        ),
        out_shape=shapes,
        name=name,
        compiler_params=pltpu.CompilerParams(vmem_limit_bytes=room * 1024 * 1024),
        cost_estimate=pl.CostEstimate(flops=flops, bytes_accessed=moved, transcendentals=0),
    )(info, *after, *arrays)


def segment_table(lengths, spots, row_count):
    ends = jnp.cumsum(lengths)
    position = jnp.arange(row_count, dtype=jnp.int32)
    segments = jnp.sum((position[None, :] >= ends[:, None]).astype(jnp.int32), axis=0)
    zero = jnp.zeros((1,), jnp.int32)
    last = jnp.full((1,), row_count, jnp.int32)
    return segments, jnp.concatenate([spots, zero, ends, ends, last]).astype(jnp.int32)


def all_of(*arrays):
    return [(array, None, None) for array in arrays]


def plain(*shapes_and_types):
    return [(shape, kind, None, None) for shape, kind in shapes_and_types]


def halves(rows):
    return plain(((2, 8, rows, WIDTH), LOW)) * 2


def columns(pair, rows, start, index):
    block = (4, 4, rows, WIDTH), lambda *i: (0, 0, start // rows + index(*i), 0)
    return [(array, *block) for array in pair]


def lines(pair, index):
    block = (2, 4, 64, WIDTH), lambda *i: (index(*i), 0, 1, 0)
    return [(array, *block) for array in pair]


def first(*_):
    return 0


def step(h, _):
    return h


class Layer:
    def __init__(self, features, cotangent, lengths, spots, taps):
        self.features, self.cotangent, self.taps = features, cotangent, taps
        self.tokens = features.shape[0]
        self.count = lengths.shape[0]
        self.segments = self.count + 1
        seg_ids, self.info = segment_table(lengths, spots, self.tokens)
        self.segs_col, self.segs_row = seg_ids[:, None], seg_ids[None, :]
        self.valid = (self.segs_col < self.count).astype(F32)
        self.stream = ((self.tokens, WIDTH), F32)
        self.low = pltpu.VMEM((self.tokens, WIDTH), LOW)
        self.wide = pltpu.VMEM((self.tokens, WIDTH), F32)
        rows = self.tokens + GAP * (self.segments - 1)
        self.spread_rows = -(-rows // (4 * GAP)) * 4 * GAP + 2 * GAP
        self.conv = dict(segments=self.segments, taps=taps)
        self.stat = ((8, WIDTH), F32)
        self.vector = ((1, WIDTH), F32)
        self.flop = 2 * self.tokens * WIDTH * WIDTH

    def set_small(self, smaller):
        (
            self.gate_taps, self.merge_taps, self.front_gain, self.heads_gain, self.gated_gain,
            self.gate_gain, self.rear_gain, self.final_gain,
        ) = smaller

    def padded(self, width):
        return pltpu.VMEM((width // CHAN, self.spread_rows, CHAN), F32)

    def tall(self, width, kind=F32):
        return ((self.tokens, width), kind)

    def by_column(self, array, start=0):
        return [(array, (self.tokens, 2 * WIDTH), lambda j, _: (0, j + start))]

    def front_forward(self, front, after=()):
        self.front = front
        self.after_front, self.front_before, self.front_stat = call(
            front_forward_kernel,
            (2,),
            all_of(self.features, self.front_gain, self.valid)
            + columns(front, 32, 0, step)
            + lines(front, step),
            plain(self.stream)
            + [(*self.tall(4 * WIDTH), (self.tokens, 2 * WIDTH), lambda h, _: (0, h))]
            + plain(self.stat),
            [self.low, self.wide],
            self.info,
            8 * self.flop,
            after,
        )
        return self.front_stat

    def branches_forward(self, middle, after=()):
        self.middle = middle
        self.heads = columns(middle, 48, 144, first) + columns(middle, 16, 192, first)
        (
            self.attended, self.packed, self.mixed, self.gated, self.gated_before,
            self.gate_normal, self.gate_inverse, self.gate_part, self.product,
        ) = call(
            functools.partial(branches_forward_kernel, **self.conv),
            (2,),
            all_of(self.after_front, self.heads_gain, self.segs_col, self.segs_row)
            + self.heads
            + all_of(self.gated_gain, self.gate_gain, self.gate_taps)
            + columns(middle, 48, 0, lambda j, _: 1 - j)
            + columns(middle, 48, 96, first),
            plain(self.stream, self.tall(3 * WIDTH, LOW), self.tall(WIDTH, LOW), self.stream)
            + [(*self.tall(6 * WIDTH), (self.tokens, 3 * WIDTH), lambda j, _: (0, 1 - j))]
            + plain(
                self.tall(3 * WIDTH), self.tall(1), self.tall(3 * WIDTH), self.tall(3 * WIDTH, LOW)
            ),
            [self.low, pltpu.VMEM((self.tokens, 3 * WIDTH), F32)]
            + [self.padded(3 * WIDTH)] * 3
            + [pltpu.VMEM((GAP, 3 * WIDTH), F32)],
            self.info,
            52 * self.flop,
            after,
        )
        return self.gate_inverse

    def merge_rear(self, rear, after=()):
        def bounce(i, _):
            return jnp.where(i < 2, i, 3 - i)

        padded = self.padded(2 * WIDTH)
        (
            self.encoded, self.merge_grad, self.rear_gain_grad, self.final_gain_grad,
            self.rear_stat, self.attended_grad, self.gated_grad, self.merge_taps_grad, *pair,
        ) = call(
            functools.partial(merge_rear_kernel, **self.conv),
            (4,),
            all_of(self.after_front, self.attended, self.gated, self.merge_taps)
            + columns(rear, 32, 128, first)
            + all_of(self.rear_gain, self.final_gain, self.valid, self.cotangent)
            + columns(rear, 32, 0, bounce)
            + lines(rear, bounce),
            plain(
                self.tall(WIDTH, LOW), self.stream, self.vector, self.vector, self.stat,
                self.stream, self.stream, ((self.taps + 1, 2 * WIDTH), F32),
            )
            + halves(128)
            + halves(32),
            [
                self.low, pltpu.VMEM((2, self.tokens, 2 * WIDTH), F32), self.low, self.wide, self.wide,
                self.wide, pltpu.VMEM((self.tokens, 2 * WIDTH), F32),
                pltpu.VMEM((self.tokens, 2 * WIDTH), LOW), padded, padded, padded, padded,
                pltpu.VMEM((GAP, 2 * WIDTH), F32),
            ],
            self.info,
            80 * self.flop,
            after,
        )
        return pair

    def branches_backward(self, after=()):
        third = (self.tokens, 3 * WIDTH), lambda *_: (0, 0)
        self.heads_stream, self.heads_gain_grad, self.part_grad, self.gated_total, *pair = call(
            branches_backward_kernel,
            (1,),
            all_of(
                self.attended_grad, self.after_front, self.heads_gain, self.segs_col,
                self.segs_row, self.packed, self.mixed,
            )
            + self.heads
            + all_of(self.gated_grad, self.gated_gain)
            + [(self.gated_before, *third)]
            + all_of(self.gate_part, self.product)
            + columns(self.middle, 48, 0, first)
            + columns(self.middle, 48, 96, first),
            plain(self.stream, self.vector, self.tall(3 * WIDTH), self.stream) + halves(160),
            [self.low, self.low, pltpu.VMEM((self.tokens, 3 * WIDTH), LOW)],
            self.info,
            40 * self.flop,
            after,
        )
        return pair

    def gated_gate(self, after=()):
        padded = self.padded(3 * WIDTH)
        (
            self.gated_stream, self.gated_gain_grad, self.gate_gain_grad, self.gate_taps_grad,
            *pair,
        ) = call(
            functools.partial(gated_gate_kernel, **self.conv),
            (1,),
            all_of(
                self.part_grad, self.gate_normal, self.gate_inverse, self.gate_gain,
                self.gate_taps, self.after_front, self.gated_gain,
            )
            + [(self.gated_before, (self.tokens, 3 * WIDTH), lambda *_: (0, 1))]
            + all_of(self.gated_total)
            + columns(self.middle, 48, 48, first),
            plain(
                self.stream, self.vector, ((1, 3 * WIDTH), F32),
                ((self.taps + 1, 3 * WIDTH), F32),
            )
            + halves(48),
            [
                padded, padded, padded, pltpu.VMEM((self.tokens, 3 * WIDTH), F32), padded,
                pltpu.VMEM((GAP, 3 * WIDTH), F32),
            ],
            self.info,
            48 * self.flop,
            after,
        )
        return pair

    def front_hidden(self, after=()):
        self.front_grad, self.front_before_grad, *pair = call(
            front_hidden_kernel,
            (2,),
            all_of(self.merge_grad, self.heads_stream, self.gated_stream)
            + self.by_column(self.front_before)
            + lines(self.front, step),
            plain(self.stream)
            + [(*self.tall(4 * WIDTH, LOW), (self.tokens, 2 * WIDTH), lambda h, _: (0, h))]
            + halves(64),
            [self.low],
            self.info,
            12 * self.flop,
            after,
        )
        return pair

    def front_input(self, after=()):
        self.features_grad, *pair = call(
            front_input_kernel,
            (2,),
            all_of(self.front_grad)
            + self.by_column(self.front_before_grad)
            + all_of(self.features, self.front_gain)
            + columns(self.front, 32, 0, step),
            plain(self.tall(WIDTH, LOW)) + halves(80),
            [self.low, self.wide],
            self.info,
            12 * self.flop,
            after,
        )
        return pair

    def small_grads(self):
        return (
            self.gate_taps_grad, self.merge_taps_grad, self.heads_gain_grad,
            self.gated_gain_grad, self.rear_gain_grad, self.final_gain_grad, self.gate_gain_grad,
        )

    def stats(self):
        return self.front_stat, self.rear_stat


SMALL = 16
STATS = 8


def ring(size, shift):
    return [(i, (i + shift) % size) for i in range(size)]


def pack_kernel(
    info, front_up, front_down, heads_in, heads_out, gated_in, gated_out, merge_out, rear_up,
    rear_down, gate_taps, merge_taps, front_gain, heads_gain, gated_gain, rear_gain, final_gain,
    gate_gain, front, middle, rear, small,
):
    def put(target, start, source):
        rows, width = source.shape
        for q in range(width // WIDTH):
            target[start + rows * q : start + rows * (q + 1), :] = source[
                :, WIDTH * q : WIDTH * (q + 1)
            ]

    put(front, 0, front_up)
    put(front, 64, front_down)
    put(middle, 0, gated_in)
    put(middle, 96, gated_out)
    put(middle, 144, heads_in)
    put(middle, 192, heads_out)
    put(rear, 0, rear_up)
    put(rear, 64, rear_down)
    put(rear, 128, merge_out)
    small[...] = jnp.zeros_like(small)
    for q, source in ((0, gate_taps), (2, merge_taps)):
        value = source[...].astype(F32)
        taps, width = value.shape
        small[0:SMALL, CHAN * q : CHAN * q + width] = value[:SMALL]
        small[0 : taps - SMALL, CHAN * (q + 1) : CHAN * (q + 1) + width] = value[SMALL:]
    start = CHAN
    for source in (front_gain, heads_gain, gated_gain, rear_gain, final_gain, gate_gain):
        width = source.shape[1]
        small[SMALL - 1 :, start : start + width] = source[...].astype(F32)
        start += width
    front[128 : 128 + SMALL, :] = small[...].astype(LOW)


def copy_all(copies):
    for copy in copies:
        copy.start()
    for copy in copies:
        copy.wait()


def place_line_kernel(info, *refs):
    pieces, out, sem = refs[:4], refs[4], refs[5]
    copy_all(
        [
            pltpu.make_async_copy(piece, out.at[chip, info[PLACE + i]], sem.at[chip, i])
            for chip in range(4)
            for i, piece in enumerate(pieces)
        ]
    )


def place(kernel, pieces, rows, info, after=()):
    skipped = len(after)

    def body(info_ref, *refs):
        kernel(info_ref, *refs[skipped:])

    anywhere = pl.BlockSpec(memory_space=pl.ANY)
    return pl.pallas_call(
        body,
        grid_spec=pltpu.PrefetchScalarGridSpec(
            num_scalar_prefetch=1,
            grid=(1,),
            in_specs=[anywhere] * skipped + [pl.BlockSpec(memory_space=pltpu.VMEM)] * 4,
            out_specs=anywhere,
            scratch_shapes=[pltpu.SemaphoreType.DMA((4, 4))],
        ),
        out_shape=jax.ShapeDtypeStruct((4, 4, rows, WIDTH), LOW),
        name=kernel.__name__,
        compiler_params=pltpu.CompilerParams(vmem_limit_bytes=16 * 1024 * 1024),
        cost_estimate=pl.CostEstimate(
            flops=0, bytes_accessed=32 * rows * WIDTH * 2, transcendentals=0
        ),
    )(info, *after, *pieces)


def line_sends(array):
    return [lax.ppermute(array, "z", ring(4, d)) for d in (1, 2, 3)]


def plane_exchange(array):
    return lax.all_to_all(array, ("x", "y"), 0, 0, tiled=True)


def core_swap(array):
    return lax.ppermute(array, "k", ring(2, 1))


def tie(array, *others):
    return lax.optimization_barrier((array, others))[0]


def unpack_kernel(info, first, second, gate_taps, merge_taps, gains, gate_gain):
    mine = info[0]
    lane = lax.broadcasted_iota(jnp.int32, (SMALL, CHAN), 1)
    lane_row = lane[:1]
    gate_gain[...] = jnp.zeros_like(gate_gain)
    gains[...] = jnp.zeros_like(gains)

    def put(target, rows, value, start, size, lanes):
        block, offset = start // CHAN, start % CHAN
        inside = jnp.logical_and(lanes >= offset, lanes < offset + size)
        window = slice(CHAN * block, CHAN * (block + 1))
        target[rows, window] = jnp.where(inside, value, target[rows, window])
        spill = offset + size - CHAN
        if spill > 0:
            window = slice(CHAN * (block + 1), CHAN * (block + 2))
            target[rows, window] = jnp.where(lanes < spill, value, target[rows, window])

    for i in range(BLOCKS):
        x, core, rest = i // 16, (i // 8) % 2, i % 8
        chip, z = 2 * x + rest % 2, rest // 2
        value = jnp.where(mine == core, first[chip, z], second[chip, z]).astype(F32)
        quads = [value[:, CHAN * q : CHAN * (q + 1)] for q in range(4)]
        start = 48 * i
        for half in range(2):
            rows = slice(SMALL * half, SMALL * (half + 1))
            rolled = pltpu.roll(quads[half], start % CHAN, 1)
            put(gate_taps, rows, rolled, start, 48, lane)
            rolled = pltpu.roll(quads[2 + half], (32 * i) % CHAN, 1)
            put(merge_taps, rows, rolled, 32 * i, 32, lane)
        line = quads[1][SMALL - 1 :]
        for g in range(5):
            rolled = pltpu.roll(line, (16 * i - 16 * g) % CHAN, 1)
            put(gains, slice(g, g + 1), rolled, 16 * i, 16, lane_row)
        rolled = pltpu.roll(line, (48 * i - 80) % CHAN, 1)
        put(gate_gain, slice(0, 1), rolled, 48 * i, 48, lane_row)


def pack_small_kernel(
    info, gate_taps, merge_taps, heads_gain, gated_gain, rear_gain, final_gain, gate_gain,
    front_stat, rear_stat, send, keep, *, count_at,
):
    mine = info[0]
    lane = lax.broadcasted_iota(jnp.int32, (SMALL, CHAN), 1)
    lane_row = lane[:1]
    last = lax.broadcasted_iota(jnp.int32, (SMALL, CHAN), 0) == SMALL - 1
    stats = [
        front_stat[0:1, :], front_stat[1:2, :], rear_stat[0:1, :], rear_stat[2:3, :],
        front_stat[2:3, :], rear_stat[1:2, :], rear_stat[3:4, :],
    ]
    stat_line = jnp.where(lane_row == 7, info[count_at].astype(F32), 0.0)
    for i, stat in enumerate(stats):
        stat_line = jnp.where(lane_row == i, jnp.sum(stat, axis=1, keepdims=True), stat_line)
    rest = stat_line - stat_line.astype(LOW).astype(F32)
    stat_line += pltpu.roll(rest, STATS, 1)

    def take(source, rows, start, size, lanes):
        block, offset = start // CHAN, start % CHAN
        value = source[rows, CHAN * block : CHAN * (block + 1)]
        if offset:
            value = pltpu.roll(value, CHAN - offset, 1)
        if offset + size > CHAN:
            other = source[rows, CHAN * (block + 1) : CHAN * (block + 2)]
            value = jnp.where(lanes < CHAN - offset, value, pltpu.roll(other, CHAN - offset, 1))
        return value

    def quads_of(i):
        halves = [slice(0, SMALL), slice(SMALL, 2 * SMALL)]
        quads = [take(gate_taps, rows, 48 * i, 48, lane) for rows in halves]
        quads += [take(merge_taps, rows, 32 * i, 32, lane) for rows in halves]
        line = pltpu.roll(take(gate_gain, slice(0, 1), 48 * i, 48, lane_row), 80, 1)
        for g, gain in enumerate((heads_gain, gated_gain, rear_gain, final_gain)):
            start = 16 * (g + 1)
            block = gain[:, CHAN * (i // 8) : CHAN * (i // 8 + 1)]
            value = pltpu.roll(block, (start - 16 * i) % CHAN, 1)
            inside = jnp.logical_and(lane_row >= start, lane_row < start + 16)
            line = jnp.where(inside, value, line)
        quads[1] = jnp.where(last, line, quads[1])
        quads[3] = jnp.where(last, stat_line, quads[3])
        return quads

    for i in [*range(8), *range(16, 24)]:
        x, spot = i // 16, i % 8
        pairs = zip(quads_of(i), quads_of(i + 8))
        for q, (low, high) in enumerate(pairs):
            lanes = slice(CHAN * q, CHAN * (q + 1))
            keep[x, spot, :, lanes] = jnp.where(mine == 0, low, high).astype(LOW)
            send[x, spot, :, lanes] = jnp.where(mine == 0, high, low).astype(LOW)


def round_small(total):
    quad = total[:, 3 * CHAN :]
    lane = lax.broadcasted_iota(jnp.int32, quad.shape, 1)
    row = lax.broadcasted_iota(jnp.int32, quad.shape, 0)
    stat = jnp.logical_and(row == SMALL - 1, lane < STATS)
    rest = jnp.where(stat, quad - quad.astype(LOW).astype(F32), 0.0)
    quad = quad + pltpu.roll(rest, STATS, 1)
    return jnp.concatenate([total[:, : 3 * CHAN], quad], axis=1).astype(LOW)


def core_sum_kernel(info, *refs, sizes):
    inputs, out = refs[:-1], refs[-1]
    half = len(inputs) // 2
    keeps, gots = inputs[:half], inputs[half:]

    def one(z, _):
        for chip in range(4):
            x, spot = chip // 2, 2 * z + chip % 2
            start = 0
            for keep, got, (rows, small) in zip(keeps, gots, sizes):
                span = slice(start, start + rows)
                start += rows
                if small:
                    total = keep[x, spot].astype(F32) + got[x, spot].astype(F32)
                    out[chip, z, span, :] = round_small(total)
                else:
                    out[chip, z, span, :] = keep[x, spot] + got[x, spot]
        return 0

    lax.fori_loop(0, 4, one, 0)


def plane_sum_kernel(info, pieces, *outs, sizes):
    for e in range(4):
        zi = lax.rem(info[PLACE] + e, 4)
        start = 0
        for rows in sizes:
            small, rows = rows < 0, abs(rows)
            span = slice(start, start + rows)
            start += rows
            total = sum(pieces[chip, zi, span, :].astype(F32) for chip in range(4))
            if e == 0:
                outs[0][span, :] = total
            elif small:
                outs[e][span, :] = round_small(total)
            else:
                outs[e][span, :] = total.astype(LOW)


def line_sum_kernel(info, keep, one, two, three, *refs, pieces):
    refs = list(refs)
    start = 0
    for rows, what in pieces:
        span = slice(start, start + rows)
        start += rows
        total = keep[span, :]
        for piece in (one, two, three):
            total += piece[span, :].astype(F32)
        if what == "small":
            quads = [total[:, CHAN * q : CHAN * (q + 1)] for q in range(4)]
            gate_taps, merge_taps, heads_gain, gated_gain, rear_gain, final_gain, gate_gain, stats = refs
            gate_taps[0:SMALL, :] = quads[0][:, :48]
            gate_taps[SMALL : 2 * SMALL - 1, :] = quads[1][: SMALL - 1, :48]
            merge_taps[0:SMALL, :] = quads[2][:, :32]
            merge_taps[SMALL : 2 * SMALL - 1, :] = quads[3][: SMALL - 1, :32]
            line = quads[1][SMALL - 1 :, :]
            for g, target in enumerate((heads_gain, gated_gain, rear_gain, final_gain)):
                target[...] = pltpu.roll(line, CHAN - 16 * (g + 1), 1)[:, :16]
            gate_gain[...] = pltpu.roll(line, CHAN - 80, 1)[:, :48]
            line = quads[3][SMALL - 1 :, :]
            line += pltpu.roll(line, CHAN - STATS, 1)
            frames = jnp.sum(line[:, STATS - 1 : STATS])
            stats[...] = jnp.sqrt(line[:, : STATS - 1] / (frames * WIDTH))
        elif what == "gain":
            owner = info[OWNER]
            line = jnp.zeros((1, CHAN), F32)
            for b in range(WIDTH // CHAN):
                block = total[0:1, CHAN * b : CHAN * (b + 1)]
                line = jnp.where(owner // 8 == b, block, line)
            line = pltpu.roll(line, lax.rem(CHAN - 16 * lax.rem(owner, 8), CHAN), 1)
            refs.pop(0)[...] = line[:, :16]
        elif what == "left":
            given, target = refs.pop(0), refs[0]
            target[:, : given.shape[1]] = given[...]
        else:
            shift = 0
            if what == "right":
                target = refs.pop(0)
                shift = target.shape[1] // 2
            else:
                target = refs.pop(0)
            height = target.shape[0]
            for q in range(rows // height):
                lanes = slice(shift + WIDTH * q, shift + WIDTH * (q + 1))
                target[:, lanes] = total[height * q : height * (q + 1), :]


def run(tasks, info, after=()):
    counts = [(len(inputs), len(outputs)) for _, inputs, outputs in tasks]

    def tasks_kernel(info_ref, *refs):
        total = sum(count for count, _ in counts)
        ins, outs = list(refs[:total]), list(refs[total:])
        for (kernel, _, _), (taken, given) in zip(tasks, counts):
            kernel(info_ref, *ins[:taken], *outs[:given])
            del ins[:taken], outs[:given]

    results = call(
        tasks_kernel,
        (1,),
        all_of(*[array for _, inputs, _ in tasks for array in inputs]),
        plain(*[output for _, _, outputs in tasks for output in outputs]),
        [],
        info,
        after=after,
        room=24,
    )
    grouped = []
    for _, given in counts:
        grouped.append(results[:given])
        results = results[given:]
    return grouped


def core_sum(pairs):
    sizes = tuple((pair[0].shape[2], pair[0].shape[2] == SMALL) for pair in pairs)
    total = sum(rows for rows, _ in sizes)
    return (
        functools.partial(core_sum_kernel, sizes=sizes),
        [pair[i] for i in (0, 1) for pair in pairs],
        [((4, 4, total, WIDTH), LOW)],
    )


def plane_sum(pieces, sizes):
    total = pieces.shape[2]
    return (
        functools.partial(plane_sum_kernel, sizes=sizes),
        [pieces],
        [((total, WIDTH), F32)] + [((total, WIDTH), LOW)] * 3,
    )


def line_sum(sums, pieces, outputs, given=()):
    own, rest = sums
    return (
        functools.partial(line_sum_kernel, pieces=pieces),
        [own, *rest, *given],
        [(shape, F32) for shape in outputs],
    )


def line_swap(sums):
    return sums[0], [lax.ppermute(array, "z", ring(4, d)) for d, array in zip((1, 2, 3), sums[1:])]


def pack_small(layer, count):
    return (
        functools.partial(pack_small_kernel, count_at=SEG + 2 * count),
        [*layer.small_grads(), *layer.stats()],
        [((2, 8, SMALL, WIDTH), LOW)] * 2,
    )


def unpack_small(front, info):
    block = (4, 4, SMALL, WIDTH), lambda *_: (0, 0, 8, 0)
    gate_taps, merge_taps, gains, gate_full = call(
        unpack_kernel,
        (1,),
        [(array, *block) for array in front],
        plain(
            ((32, 3 * WIDTH), F32), ((32, 2 * WIDTH), F32), ((8, WIDTH), F32), ((1, 3 * WIDTH), F32)
        ),
        [],
        info,
    )
    lines = [gains[g : g + 1] for g in range(5)]
    return gate_taps, merge_taps, lines[0], lines[1], lines[2], gate_full, lines[3], lines[4]


def grid_device(
    features, cotangent, lengths, front_up, front_down, heads_input, heads_output, gated_input,
    gated_output, merge_output, rear_up, rear_down, gate_kernel, merge_kernel, front_gain,
    heads_gain, gated_gain, gate_gain, rear_gain, final_gain,
):
    x, k, z, y = (lax.axis_index(name) for name in ("x", "k", "z", "y"))
    places = [k] + [lax.rem(place, 4) for place in (z, z + 3, z + 2, z + 1)]
    places.append(((x * 2 + k) * 4 + z) * 2 + y)
    spots = jnp.stack([place.astype(jnp.int32) for place in places])
    layer = Layer(features, cotangent, lengths[0], spots, gate_kernel.shape[0])
    info = layer.info

    front, middle, rear = call(
        pack_kernel,
        (1,),
        all_of(
            front_up, front_down, heads_input, heads_output, gated_input, gated_output,
            merge_output, rear_up, rear_down, gate_kernel, merge_kernel,
            *[
                gain.reshape(1, -1)
                for gain in (front_gain, heads_gain, gated_gain, rear_gain, final_gain, gate_gain)
            ],
        ),
        plain(((144, WIDTH), LOW), ((208, WIDTH), LOW), ((160, WIDTH), LOW)),
        [pltpu.VMEM((SMALL, WIDTH), F32)],
        spots,
    )
    front_four = place(place_line_kernel, [front] + line_sends(front), 144, info)
    front = plane_exchange(front_four)
    middle = tie(middle, front_four)
    middle_four = place(place_line_kernel, [middle] + line_sends(middle), 208, info)
    front = tie(front, middle_four)
    middle = plane_exchange(tie(middle_four, front))
    rear = tie(rear, front)
    rear_lines = line_sends(rear)
    front = front, core_swap(front)
    layer.set_small(unpack_small(front, info))
    mark = layer.front_forward(front)
    rear_four = place(place_line_kernel, [rear] + rear_lines, 160, info, after=(mark,))
    middle = tie(middle, rear_four)
    rear = plane_exchange(tie(rear_four, middle))
    middle = middle, core_swap(middle)
    mark = layer.branches_forward(middle)
    rear = tie(rear, mark)
    rear = rear, core_swap(rear)

    send, rear_keep, merge_send, merge_keep = layer.merge_rear(rear)
    rear_got = core_swap(send)
    ((rear_four,),) = run([core_sum([(rear_keep, rear_got)])], info)
    merge_got = core_swap(tie(merge_send, rear_got))
    rear_plane = plane_exchange(rear_four)
    send, wide_keep = layer.branches_backward(after=(rear_four,))
    wide_got = core_swap(tie(send, rear_plane))
    (rear_sums,) = run([plane_sum(rear_plane, (128,))], info, after=(layer.gated_total,))
    ((wide_four,),) = run(
        [core_sum([(merge_keep, merge_got), (wide_keep, wide_got)])], info,
        after=(rear_sums[0],),
    )
    rear_sums = line_swap(rear_sums)
    wide_plane = plane_exchange(tie(wide_four, rear_plane))
    send, gate_keep = layer.gated_gate(after=(wide_four,))
    gate_got = core_swap(send)
    ((small_send, small_keep),) = run(
        [pack_small(layer, lengths.shape[1])], info, after=rear_sums[1]
    )
    small_got = core_swap(small_send)
    send, down_keep = layer.front_hidden(after=(small_send,))
    down_got = core_swap(tie(send, wide_plane))
    (wide_sums,) = run([plane_sum(wide_plane, (192,))], info, after=(layer.front_grad,))
    ((last_four,),) = run(
        [
            core_sum([(gate_keep, gate_got), (down_keep, down_got), (small_keep, small_got)]),
        ],
        info,
        after=(wide_sums[0],),
    )
    wide_sums = line_swap(wide_sums)
    last_plane = plane_exchange(tie(last_four, wide_plane))
    send, up_keep = layer.front_input(after=(last_four, *wide_sums[1]))
    up_got = core_swap(send)
    ((front_four,),) = run([core_sum([(up_keep, up_got)])], info)
    half_shape = (gated_input.shape[0], gated_input.shape[1] // 2)
    front_plane = plane_exchange(tie(front_four, last_plane))
    (last_sums,) = run([plane_sum(last_plane, (48, 64, -SMALL))], info, after=(front_four,))
    last_sums = line_swap(last_sums)
    (
        (rear_up_grad, rear_down_grad),
        (
            merge_output_grad, gated_left_grad, gated_output_grad, heads_input_grad,
            heads_output_grad,
        ),
    ) = run(
        [
            line_sum(rear_sums, ((64, None), (64, None)), (rear_up.shape, rear_down.shape)),
            line_sum(
                wide_sums, ((32, None), (48, None), (48, None), (48, None), (16, None)),
                (
                    merge_output.shape, half_shape, gated_output.shape, heads_input.shape,
                    heads_output.shape,
                ),
            ),
        ],
        info,
        after=(last_sums[0],),
    )
    (front_sums,) = run(
        [plane_sum(front_plane, (80,))], info, after=(last_sums[0], merge_output_grad)
    )
    front_sums = line_swap(front_sums)
    vector = (1, front_gain.shape[0])
    (
        (
            gated_input_grad, front_down_grad, gate_kernel_grad, merge_kernel_grad,
            heads_gain_grad, gated_gain_grad, rear_gain_grad, final_gain_grad, gate_gain_grad,
            statistics,
        ),
    ) = run(
        [
            line_sum(
                last_sums,
                ((0, "left"), (48, "right"), (64, None), (16, "small")),
                (
                    gated_input.shape, front_down.shape, gate_kernel.shape, merge_kernel.shape,
                    vector, vector, vector, vector, (1, gate_gain.shape[0]), (1, STATS - 1),
                ),
                given=(gated_left_grad,),
            ),
        ],
        info,
        after=(front_sums[0],),
    )
    ((front_up_grad, front_gain_grad),) = run(
        [line_sum(front_sums, ((64, None), (16, "gain")), (front_up.shape, vector))], info,
        after=(statistics,),
    )
    return (
        layer.encoded, layer.features_grad, front_up_grad, front_down_grad, heads_input_grad,
        heads_output_grad, gated_input_grad, gated_output_grad, merge_output_grad, rear_up_grad,
        rear_down_grad, gate_kernel_grad, merge_kernel_grad, front_gain_grad[0],
        heads_gain_grad[0], gated_gain_grad[0], gate_gain_grad[0], rear_gain_grad[0],
        final_gain_grad[0], statistics[0],
    )


def pack_rows(shard):
    rows, columns = shard.shape
    pieces = shard.reshape(rows, columns // WIDTH, WIDTH).transpose(1, 0, 2)
    return pieces.reshape(rows * columns // WIDTH, WIDTH)


def pad_lines(flat):
    rows = -(-flat.shape[-1] // (WIDTH * 16)) * 16
    spare = [(0, 0)] * (flat.ndim - 1) + [(0, rows * WIDTH - flat.shape[-1])]
    return jnp.pad(flat, spare).reshape(flat.shape[:-1] + (rows, WIDTH))


def to_owners(weight):
    rows, columns = weight.shape
    pieces = weight.reshape(BLOCKS, rows // BLOCKS, columns // WIDTH, WIDTH)
    pieces = pieces.transpose(0, 2, 1, 3).reshape(2, 2, 4, 2, -1, WIDTH)
    pieces = pieces.transpose(1, 0, 3, 2, 4, 5)
    return pieces.reshape(2, 4, 4, -1, WIDTH)


def from_owners(halves, rows, columns):
    send, keep = halves
    pieces = jnp.stack([keep, send], axis=1)
    pieces = pieces.reshape(BLOCKS, columns // WIDTH, rows // BLOCKS, WIDTH)
    return pieces.transpose(0, 2, 1, 3).reshape(rows, columns)


def any_device(features, cotangent, lengths, *shards, axes):
    count = lax.axis_size(axes)
    matrices, smaller = shards[:9], shards[9:]
    packed = [pack_rows(element) for element in matrices]
    packed.append(pad_lines(jnp.concatenate([element.reshape(-1) for element in smaller])))
    gathered = lax.all_gather(jnp.concatenate(packed), axes, axis=0)
    weights = []
    start = 0
    for element, piece in zip(matrices, packed):
        rows, columns = element.shape
        window = gathered[:, start : start + piece.shape[0]]
        start += piece.shape[0]
        window = window.reshape(count, columns // WIDTH, rows, WIDTH).transpose(0, 2, 1, 3)
        weights.append(to_owners(window.reshape(count * rows, columns)))
    flat = gathered[:, start:].reshape(count, -1).astype(F32)
    lines = []
    start = 0
    for element in smaller:
        window = flat[:, start : start + element.size]
        start += element.size
        if element.ndim == 2:
            window = window.reshape((count,) + element.shape).transpose(1, 0, 2)
            window = window.reshape(element.shape[0], -1)
            lines.append(jnp.pad(window, ((0, 1), (0, 0))))
        else:
            lines.append(window.reshape(1, -1))
    up, down, h_in, h_out, g_in, g_out, m_out, r_up, r_down = weights

    def chunk(*members):
        return tuple(jnp.concatenate([member[i] for member in members], axis=2) for i in (0, 1))

    front = chunk(up, down)
    rear = chunk(r_up, r_down, m_out)
    layer = Layer(features, cotangent, lengths[0], jnp.zeros((SEG,), jnp.int32), smaller[0].shape[0])
    layer.set_small(lines)
    layer.front_forward(front)
    layer.branches_forward(chunk(g_in, g_out, h_in, h_out))
    rear = layer.merge_rear(rear)
    rear, merge = rear[:2], rear[2:]
    wide = layer.branches_backward()
    right = layer.gated_gate()
    front_down_halves = layer.front_hidden()
    front_up_halves = layer.front_input()

    def part(pair, start, stop):
        return tuple(array[:, :, start:stop] for array in pair)

    gated_halves = tuple(
        jnp.concatenate([one[:, :, :48], two], axis=2) for one, two in zip(wide, right)
    )
    ordered = (
        part(front_up_halves, 0, 64), front_down_halves, part(wide, 96, 144),
        part(wide, 144, 160), gated_halves, part(wide, 48, 96), merge,
        part(rear, 0, 64), part(rear, 64, 128),
    )
    front_gain = front_up_halves[1][0, 0, 64].astype(F32)
    small_grads = layer.small_grads()
    pieces = []
    for element, halves in zip(matrices, ordered):
        rows, columns = element.shape
        full = from_owners(halves, rows * count, columns)
        full = full.reshape(count, rows, columns // WIDTH, WIDTH).transpose(0, 2, 1, 3)
        pieces.append(full.reshape(count, -1, WIDTH))
    gate_taps, merge_taps, heads_gain, gated_gain, rear_gain, final_gain, gate_gain = small_grads
    small_full = (gate_taps, merge_taps, front_gain, heads_gain, gated_gain, gate_gain, rear_gain, final_gain)
    flat = []
    for element, full in zip(smaller, small_full):
        if element.ndim == 2:
            full = full[: element.shape[0]].reshape(element.shape[0], count, -1).transpose(1, 0, 2)
        flat.append(full.reshape(count, -1))
    pieces.append(pad_lines(jnp.concatenate(flat, axis=1).astype(LOW)))
    summed = lax.psum_scatter(jnp.concatenate(pieces, axis=1), axes, scatter_dimension=0)
    outputs = []
    start = 0
    for element, piece in zip(matrices, pieces):
        rows, columns = element.shape
        window = summed[start : start + piece.shape[1]].astype(F32)
        start += piece.shape[1]
        window = window.reshape(columns // WIDTH, rows, WIDTH).transpose(1, 0, 2)
        outputs.append(window.reshape(rows, columns))
    flat = summed[start:].reshape(-1).astype(F32)
    start = 0
    for element in smaller:
        outputs.append(flat[start : start + element.size].reshape(element.shape))
        start += element.size
    front_stat, rear_stat = layer.stats()
    squares = jnp.stack(
        [
            front_stat[0], front_stat[1], rear_stat[0], rear_stat[2], front_stat[2], rear_stat[1],
            rear_stat[3],
        ]
    )
    totals = lax.psum(
        jnp.append(jnp.sum(squares, axis=1), jnp.sum(lengths).astype(F32)), axes
    )
    statistics = jnp.sqrt(totals[:7] / (totals[7] * features.shape[1]))
    return (layer.encoded, layer.features_grad) + tuple(outputs) + (statistics,)


def solution(mesh):
    body = grid_device
    axes = ("x", "k", "z", "y")
    if mesh.devices.shape == (4, 8):
        mesh = Mesh(mesh.devices.reshape(2, 2, 4, 2), axes)
    else:
        axes = tuple(mesh.axis_names)
        body = functools.partial(any_device, axes=axes)
    rows, columns, vector = P(axes, None), P(None, axes), P(axes)
    weights = (rows,) * 9 + (columns,) * 2 + (vector,) * 6
    return jax.shard_map(
        body,
        mesh=mesh,
        in_specs=(rows, rows, rows) + weights,
        out_specs=(rows, rows) + weights + (P(),),
        check_vma=False,
    )
```

```python
import functools

import jax
import jax.numpy as jnp
from jax import lax
from jax.experimental import pallas as pl
from jax.experimental.pallas import tpu as pltpu
from jax.sharding import Mesh, PartitionSpec as P

HEADS = 8
EPSILON = 1e-05
NEGATIVE = -1000000000.0
TILE = 8
GAP = 16
CHAN = 128
PLACE = 1
OWNER = 5
SEG = 6
WIDTH = 512
BLOCKS = 32
F32 = jnp.float32
LOW = jnp.bfloat16


def dot(left, right):
    return jnp.dot(left, right, preferred_element_type=F32)


def dot_tn(left, right):
    return lax.dot_general(left, right, (((0,), (0,)), ((), ())), preferred_element_type=F32)


def dot_nt(left, right):
    return lax.dot_general(left, right, (((1,), (1,)), ((), ())), preferred_element_type=F32)


def normalize(values):
    centred = values - jnp.mean(values, axis=-1, keepdims=True)
    variance = jnp.mean(centred * centred, axis=-1, keepdims=True)
    inverse = lax.rsqrt(variance + EPSILON)
    return centred * inverse, inverse


def normalize_back(upstream, gain, normal, inverse):
    scaled = upstream * gain
    mean_scaled = jnp.mean(scaled, axis=-1, keepdims=True)
    mean_cross = jnp.mean(scaled * normal, axis=-1, keepdims=True)
    return inverse * (scaled - mean_scaled - normal * mean_cross)


def part_of(index):
    return slice(None), pl.ds(pl.multiple_of(index * WIDTH, WIDTH), WIDTH)


def row_sum(values):
    return jnp.sum(values, axis=0, keepdims=True)


GELU_A = 0.7978845608028654
GELU_B = 0.044715


def gelu(v):
    return 0.5 * v * (1.0 + jnp.tanh(GELU_A * (v + GELU_B * v * v * v)))


def gelu_pair(v):
    square = v * v
    bend = jnp.tanh(GELU_A * (v + GELU_B * square * v))
    value = 0.5 * v * (1.0 + bend)
    slope = 0.5 * (1.0 + bend) + 0.5 * v * (1.0 - bend * bend) * (
        GELU_A * (1.0 + 3.0 * GELU_B * square)
    )
    return value, slope


def silu(v):
    return v * jax.nn.sigmoid(v)


def store_halves(value, send, keep, mine, rows, start):
    parts = value.astype(LOW).reshape(2, 2, 8, rows, WIDTH)

    @pl.when(mine == 0)
    def _():
        keep[:, :, pl.ds(start, rows), :] = parts[:, 0]
        send[:, :, pl.ds(start, rows), :] = parts[:, 1]

    @pl.when(mine == 1)
    def _():
        keep[:, :, pl.ds(start, rows), :] = parts[:, 1]
        send[:, :, pl.ds(start, rows), :] = parts[:, 0]


def join_rows(first, second, mine):
    cores = jnp.where(mine == 0, first, second), jnp.where(mine == 0, second, first)
    return jnp.concatenate(
        [core[2 * x + y, z] for x in (0, 1) for core in cores for z in range(4) for y in (0, 1)]
    )


def pick_rows(first, second, flag):
    chosen = jnp.where(flag, first, second)
    return jnp.concatenate([chosen[y, z] for z in range(4) for y in (0, 1)])


def join_columns(first, second, mine):
    blocks = range(0, first.shape[2], 16)
    return jnp.concatenate(
        [join_rows(first[:, :, i : i + 16, :], second[:, :, i : i + 16, :], mine) for i in blocks],
        axis=1,
    )


def join_lines(first, second, mine):
    cores = jnp.where(mine == 0, first, second), jnp.where(mine == 0, second, first)
    return jnp.concatenate([core[y, z] for core in cores for z in range(4) for y in (0, 1)])


def store_columns(value, send, keep, mine, start):
    for i in range(value.shape[1] // WIDTH):
        store_halves(value[:, WIDTH * i : WIDTH * (i + 1)], send, keep, mine, 16, start + 16 * i)


def visits(info, segments, body):
    def segment(s, _):
        begin, end = info[SEG + s], info[SEG + segments + s]

        def visit(i, _):
            row = i * TILE + lax.broadcasted_iota(jnp.int32, (TILE, CHAN), 0)
            inside = jnp.logical_and(row >= begin, row < end)
            base = pl.multiple_of(i * TILE, TILE)
            body(base, pl.multiple_of(base + GAP * (s + 1), TILE), inside)
            return 0

        lax.fori_loop(begin // TILE, (end + TILE - 1) // TILE, visit, 0)
        return 0

    lax.fori_loop(0, segments, segment, 0)


def spread(source, padded, info, segments, blocks):
    padded[...] = jnp.zeros_like(padded)

    def body(base, apart, inside):
        for c in range(blocks):
            value = source[pl.ds(base, TILE), c * CHAN : (c + 1) * CHAN]
            padded[c, pl.ds(apart, TILE), :] = jnp.where(inside, value, 0.0)

    visits(info, segments, body)


def unspread(padded, target, info, segments, blocks):
    def body(base, apart, inside):
        for c in range(blocks):
            lanes = slice(c * CHAN, (c + 1) * CHAN)
            value = padded[c, pl.ds(apart, TILE), :]
            target[pl.ds(base, TILE), lanes] = jnp.where(
                inside, value, target[pl.ds(base, TILE), lanes]
            )

    visits(info, segments, body)


def conv_rows(padded, kernel, out, steps_ref, sums, blocks, taps, flip):
    half = (taps - 1) // 2
    rows = padded.shape[1]
    pairs = (rows - 2 * GAP) // (4 * GAP)
    order = [taps - 1 - j if flip else j for j in range(taps)]
    for c in range(blocks):
        steps_ref[c, 0 : rows - GAP, :] = padded[c, 0 : rows - GAP, :] - padded[c, GAP:rows, :]
    for j in range(GAP):
        total = kernel[order[j] : order[j] + 1, :]
        if j + GAP < taps:
            total = total + kernel[order[j + GAP] : order[j + GAP] + 1, :]
        sums[j : j + 1, :] = total

    def body(step, _):
        c = step // 2
        base = GAP + lax.rem(step, 2) * (pairs * 2 * GAP)
        lanes = pl.ds(pl.multiple_of(c * CHAN, CHAN), CHAN)
        for w in range(pairs):
            start = base + 2 * GAP * w
            first_part = second = third = jnp.zeros((GAP, CHAN), F32)
            for j in range(GAP):
                row = start + j - half
                first_part += kernel[pl.ds(order[j], 1), lanes] * steps_ref[c, pl.ds(row, GAP), :]
                second += sums[pl.ds(j, 1), lanes] * padded[c, pl.ds(row + GAP, GAP), :]
                if j + GAP < taps:
                    third += (
                        kernel[pl.ds(order[j + GAP], 1), lanes]
                        * steps_ref[c, pl.ds(row + GAP, GAP), :]
                    )
            start = pl.multiple_of(start, TILE)
            out[c, pl.ds(start, GAP), :] = first_part + second
            out[c, pl.ds(start + GAP, GAP), :] = second - third
        return 0

    lax.fori_loop(0, blocks * 2, body, 0)


def conv_taps(padded_grad, padded, steps_ref, out, blocks, taps):
    half = (taps - 1) // 2
    rows = padded.shape[1]
    pairs = (rows - 2 * GAP) // (2 * GAP)

    def fold(value):
        return value[:TILE] + value[TILE:]

    def block(c, _):
        lanes = pl.ds(pl.multiple_of(c * CHAN, CHAN), CHAN)
        zero = jnp.zeros((TILE, CHAN), F32)

        def body(step, sums):
            start = pl.multiple_of(step * 2 * GAP + GAP, TILE)
            lower = padded_grad[c, pl.ds(start, GAP), :]
            upper = padded_grad[c, pl.ds(start + GAP, GAP), :]
            both = lower + upper
            new = list(sums)
            for j in range(GAP):
                row = start + j - half
                shared = fold(both * padded[c, pl.ds(row + GAP, GAP), :])
                new[j] = new[j] + (fold(lower * steps_ref[c, pl.ds(row, GAP), :]) + shared)
                if j + GAP < taps:
                    rest = fold(upper * steps_ref[c, pl.ds(row + GAP, GAP), :])
                    new[j + GAP] = new[j + GAP] + (shared - rest)
            return tuple(new)

        sums = lax.fori_loop(0, pairs, body, (zero,) * taps)
        for j in range(taps):
            out[pl.ds(j, 1), lanes] = row_sum(sums[j])
        return 0

    lax.fori_loop(0, blocks, block, 0)


def front_forward_kernel(
    info, x_ref, gain, valid, up, up_two, down, down_two, out, before_out, stat, low, total
):
    h = pl.program_id(0)
    mine = info[0]
    up_value = join_rows(up[...], up_two[...], mine)
    down_value = pick_rows(down[...], down_two[...], h % 2 == mine)

    @pl.when(h == 0)
    def _():
        normal, _ = normalize(x_ref[...].astype(F32))
        low[...] = (normal * gain[...]).astype(LOW)
        total[...] = jnp.zeros_like(total)

    before = dot(low[...], up_value)
    before_out[...] = before
    total[...] += dot(silu(before).astype(LOW), down_value)

    @pl.when(h == pl.num_programs(0) - 1)
    def _():
        x = x_ref[...].astype(F32)
        part = 0.5 * total[...]
        after = x + part
        out[...] = after
        v = valid[...]
        stat[0:1, :] = row_sum(x * x * v)
        stat[1:2, :] = row_sum(after * after * v)
        stat[2:3, :] = row_sum(part * part * v)
        stat[3:, :] = jnp.zeros((5, WIDTH), F32)


def head_masks(segs_col, segs_row):
    return segs_col == segs_row


def head_half(head):
    lane = lax.broadcasted_iota(jnp.int32, (1, CHAN), 1)
    return lane // (CHAN // 2) == lax.rem(head, 2)


def head_probs(query, key, allowed, scale):
    scores = jnp.where(allowed, dot_nt(query, key) * scale, NEGATIVE)
    exponent = jnp.exp(scores - jnp.max(scores, axis=-1, keepdims=True))
    return exponent / jnp.sum(exponent, axis=-1, keepdims=True)


def heads_forward(
    info, low, segs_col, segs_row, w_in, w_in_two, w_out, w_out_two, attended, packed, mixed,
):
    mine = info[0]
    scale = (WIDTH // HEADS) ** -0.5
    for q in range(3):
        rows = slice(16 * q, 16 * (q + 1))
        weight = join_rows(w_in[:, :, rows, :], w_in_two[:, :, rows, :], mine)
        packed[:, WIDTH * q : WIDTH * (q + 1)] = dot(low, weight).astype(LOW)
    allowed = head_masks(segs_col[...], segs_row[...])

    def one(head, _):
        half = head_half(head)
        start = CHAN * (head // 2)
        lanes = [pl.ds(pl.multiple_of(WIDTH * q + start, CHAN), CHAN) for q in range(3)]
        query, key, value = (packed[:, lane] for lane in lanes)
        probs = head_probs(jnp.where(half, query, 0), key, allowed, scale)
        part = dot(probs.astype(LOW), value).astype(LOW)
        mixed[:, lanes[0]] = jnp.where(half, part, mixed[:, lanes[0]])
        return 0

    lax.fori_loop(0, HEADS, one, 0)
    attended[...] = dot(mixed[...], join_rows(w_out[...], w_out_two[...], mine))


def heads_backward(
    info, grad, x_ref, gain, segs_col, segs_row, packed, mixed, w_in, w_in_two, w_out, w_out_two,
    stream, gain_grad, send, keep, mixed_grad, packed_grad, low,
):
    scale = (WIDTH // HEADS) ** -0.5
    mine = info[0]
    attended_low = grad[...].astype(LOW)
    store_halves(dot_tn(mixed[...], attended_low), send, keep, mine, 16, 144)
    mixed_grad[...] = dot_nt(attended_low, join_rows(w_out[...], w_out_two[...], mine)).astype(LOW)
    normal, inverse = normalize(x_ref[...])
    low[...] = (normal * gain[...]).astype(LOW)
    allowed = head_masks(segs_col[...], segs_row[...])

    def one(head, _):
        half = head_half(head)
        start = CHAN * (head // 2)
        lanes = [pl.ds(pl.multiple_of(WIDTH * q + start, CHAN), CHAN) for q in range(3)]
        query, key, value = (packed[:, lane] for lane in lanes)
        upstream = mixed_grad[:, lanes[0]]
        probs = head_probs(jnp.where(half, query, 0), key, allowed, scale)
        probs_grad = dot_nt(jnp.where(half, upstream, 0), value)
        value_grad = dot_tn(probs.astype(LOW), upstream)
        inner = jnp.sum(probs_grad * probs, axis=-1, keepdims=True)
        score_grad = (probs * (probs_grad - inner)).astype(LOW)
        query_grad = dot(score_grad, key) * scale
        key_grad = dot_tn(score_grad, query) * scale
        for lane, part in zip(lanes, (query_grad, key_grad, value_grad)):
            packed_grad[:, lane] = jnp.where(half, part.astype(LOW), packed_grad[:, lane])
        return 0

    lax.fori_loop(0, HEADS, one, 0)
    total = jnp.zeros(x_ref.shape, F32)
    for q in range(3):
        rows = slice(16 * q, 16 * (q + 1))
        weight = join_rows(w_in[:, :, rows, :], w_in_two[:, :, rows, :], mine)
        piece = packed_grad[:, WIDTH * q : WIDTH * (q + 1)]
        store_halves(dot_tn(low[...], piece), send, keep, mine, 16, 96 + 16 * q)
        total += dot_nt(piece, weight)
    gain_grad[...] = row_sum(total * normal)
    stream[...] = normalize_back(total, gain[...], normal, inverse)


def branches_forward_kernel(
    info, x_ref, heads_gain, segs_col, segs_row, w_heads, w_heads_two, w_mix, w_mix_two,
    gain, gate_gain, taps_ref, w_in, w_in_two, w_out, w_out_two, attended, packed, mixed,
    gated, before_out, normal_out, inverse_out, part_out, product,
    low, act, padded, conv, steps_ref, sums, *, segments, taps,
):
    j = pl.program_id(0)
    thirds = WIDTH * 3

    @pl.when(j == 0)
    def _():
        normal, _ = normalize(x_ref[...])
        low[...] = (normal * gain[...]).astype(LOW)
        heads_forward(
            info, (normal * heads_gain[...]).astype(LOW), segs_col, segs_row, w_heads,
            w_heads_two, w_mix, w_mix_two, attended, packed, mixed,
        )

    before = dot(low[...], join_rows(w_in[...], w_in_two[...], info[0]))
    before_out[...] = before
    value = gelu(before)

    @pl.when(j < 3)
    def _():
        act[:, pl.ds(pl.multiple_of(j * WIDTH, WIDTH), WIDTH)] = value

    @pl.when(j == 2)
    def _():
        normal, inverse = normalize(act[...])
        normal_out[...] = normal
        inverse_out[...] = inverse
        act[...] = normal * gate_gain[...]
        blocks = thirds // CHAN
        spread(act, padded, info, segments, blocks)
        conv_rows(padded, taps_ref, conv, steps_ref, sums, blocks, taps, False)
        unspread(conv, part_out, info, segments, blocks)

    @pl.when(j >= 3)
    def _():
        lanes = pl.ds(pl.multiple_of((j - 3) * WIDTH, WIDTH), WIDTH)
        product[:, lanes] = (value * part_out[:, lanes]).astype(LOW)

    @pl.when(j == 5)
    def _():
        gated[...] = dot(product[...], join_rows(w_out[...], w_out_two[...], info[0]))


def branches_backward_kernel(
    info, attended_grad, x_ref, heads_gain, segs_col, segs_row, packed, mixed, w_heads,
    w_heads_two, w_mix, w_mix_two, grad, gain, before, part, product, w_in, w_in_two, w_out,
    w_out_two,
    stream, heads_gain_grad, part_grad, total_out, send, keep, low, product_grad, gated_low,
    mixed_grad, packed_grad,
):
    j = pl.program_id(0)
    mine = info[0]

    @pl.when(j == 0)
    def _():
        heads_backward(
            info, attended_grad, x_ref, heads_gain, segs_col, segs_row, packed, mixed, w_heads,
            w_heads_two, w_mix, w_mix_two, stream, heads_gain_grad, send, keep, mixed_grad,
            packed_grad, low,
        )
        normal, _ = normalize(x_ref[...])
        low[...] = (normal * gain[...]).astype(LOW)
        total_out[...] = jnp.zeros_like(total_out)
        gated_low[...] = grad[...].astype(LOW)
        store_halves(dot_tn(product[...], gated_low[...]), send, keep, mine, 48, 48)
        product_grad[...] = dot_nt(gated_low[...], join_rows(w_out[...], w_out_two[...], mine))

    value, slope = gelu_pair(before[...])
    lanes = pl.ds(pl.multiple_of(j * WIDTH, WIDTH), WIDTH)
    upstream = product_grad[:, lanes]
    part_grad[...] = upstream * value
    before_grad = (upstream * part[...] * slope).astype(LOW)
    store_halves(
        dot_tn(low[...], before_grad), send, keep, mine, 16, pl.multiple_of(j * 16, 16)
    )
    total_out[...] += dot_nt(before_grad, join_rows(w_in[...], w_in_two[...], mine))


def gated_conv(
    info, part_grad, normal_ref, inverse_ref, gate_gain, taps_ref,
    gate_gain_grad, taps_grad, padded, padded_grad, conv, work, steps_ref, sums, segments, taps,
):
    blocks = 3 * WIDTH // CHAN
    spread(part_grad, padded_grad, info, segments, blocks)
    work[...] = normal_ref[...] * gate_gain[...]
    spread(work, padded, info, segments, blocks)
    rows = padded.shape[1]
    for c in range(blocks):
        steps_ref[c, 0 : rows - GAP, :] = padded[c, 0 : rows - GAP, :] - padded[c, GAP:rows, :]
    conv_taps(padded_grad, padded, steps_ref, taps_grad, blocks, taps)
    conv_rows(padded_grad, taps_ref, conv, steps_ref, sums, blocks, taps, True)
    unspread(conv, work, info, segments, blocks)
    upstream = work[...]
    normal = normal_ref[...]
    gate_gain_grad[...] = row_sum(upstream * normal)
    work[...] = normalize_back(upstream, gate_gain[...], normal, inverse_ref[...])


def gated_gate_kernel(
    info, part_grad, normal_ref, inverse_ref, gate_gain, taps_ref, x_ref, gain, before, total_in,
    w_in, w_in_two,
    stream, gain_grad, gate_gain_grad, taps_grad, send, keep,
    low, total, padded, padded_grad, conv, work, steps_ref, sums, *, segments, taps,
):
    j = pl.program_id(0)
    mine = info[0]

    @pl.when(j == 0)
    def _():
        gated_conv(
            info, part_grad, normal_ref, inverse_ref, gate_gain, taps_ref, gate_gain_grad,
            taps_grad, padded, padded_grad, conv, work, steps_ref, sums, segments, taps,
        )
        normal, _ = normalize(x_ref[...])
        low[...] = (normal * gain[...]).astype(LOW)
        total[...] = total_in[...]

    _, slope = gelu_pair(before[...])
    before_grad = (work[part_of(j)] * slope).astype(LOW)
    store_halves(
        dot_tn(low[...], before_grad), send, keep, mine, 16, pl.multiple_of(j * 16, 16)
    )
    total[...] += dot_nt(before_grad, join_rows(w_in[...], w_in_two[...], mine))

    @pl.when(j == 2)
    def _():
        normal, inverse = normalize(x_ref[...])
        gain_grad[...] = row_sum(total[...] * normal)
        stream[...] = normalize_back(total[...], gain[...], normal, inverse)


def conv_add(padded, conv, taps_ref, steps_ref, sums, blocks, taps, flip):
    conv_rows(padded, taps_ref, conv, steps_ref, sums, blocks, taps, flip)
    for c in range(blocks):
        conv[c] += padded[c]


def hidden_back(x, mine, before, part_low, down, send, keep, start):
    gate = jax.nn.sigmoid(before)
    hidden = (before * gate).astype(LOW)
    hidden_grad = dot_nt(part_low, down)
    before_grad = (hidden_grad * (gate * (1.0 + before * (1.0 - gate)))).astype(LOW)
    down_grad = dot_tn(hidden, part_low).astype(LOW).reshape(2, 8, 64, WIDTH)

    @pl.when(mine == 0)
    def _():
        keep[x, :, start : start + 64, :] = down_grad[0]
        send[x, :, start : start + 64, :] = down_grad[1]

    @pl.when(mine == 1)
    def _():
        keep[x, :, start : start + 64, :] = down_grad[1]
        send[x, :, start : start + 64, :] = down_grad[0]

    return before_grad


def merge_rear_kernel(
    info, x_ref, attended, gated, taps_ref, weight, weight_two, gain, final_gain, valid, cotangent,
    up, up_two, down, down_two,
    encoded, stream, gain_grad, final_gain_grad, stat, attended_grad, gated_grad, taps_grad,
    send, keep, merge_send, merge_keep,
    low, before, part_grad, stream_grad, total, middle, joined, joined_low, padded, padded_grad,
    conv, steps_ref, sums, *, segments, taps,
):
    step = pl.program_id(0)
    h = jnp.where(step < 2, step, 3 - step)
    up_value = join_columns(up[...], up_two[...], info[0])
    down_value = join_lines(down[...], down_two[...], info[0])
    blocks = 2 * WIDTH // CHAN

    @pl.when(step == 0)
    def _():
        joined[:, :WIDTH] = attended[...]
        joined[:, WIDTH:] = gated[...]
        spread(joined, padded, info, segments, blocks)
        conv_add(padded, conv, taps_ref, steps_ref, sums, blocks, taps, False)
        unspread(conv, joined, info, segments, blocks)
        joined_low[...] = joined[...].astype(LOW)
        part = dot(joined_low[...], join_rows(weight[...], weight_two[...], info[0]))
        after = x_ref[...] + part
        middle[...] = after
        v = valid[...]
        stat[0:1, :] = row_sum(after * after * v)
        stat[1:2, :] = row_sum(part * part * v)
        normal, _ = normalize(after)
        low[...] = (normal * gain[...]).astype(LOW)
        total[...] = jnp.zeros_like(total)

    @pl.when(step < 2)
    def _():
        value = dot(low[...], up_value)
        before[step] = value
        total[...] += dot(silu(value).astype(LOW), down_value)

    @pl.when(step == 1)
    def _():
        part = 0.5 * total[...]
        after = middle[...] + part
        v = valid[...]
        stat[2:3, :] = row_sum(after * after * v)
        stat[3:4, :] = row_sum(part * part * v)
        stat[4:, :] = jnp.zeros((4, WIDTH), F32)
        normal, inverse = normalize(after)
        encoded[...] = (normal * final_gain[...] * v).astype(LOW)
        upstream = cotangent[...].astype(F32) * v
        final_gain_grad[...] = row_sum(upstream * normal)
        grad = normalize_back(upstream, final_gain[...], normal, inverse)
        stream_grad[...] = grad
        part_grad[...] = (0.5 * grad).astype(LOW)
        total[...] = jnp.zeros_like(total)

    @pl.when(step >= 2)
    def _():
        before_grad = hidden_back(
            h, info[0], before[h], part_grad[...], down_value, send, keep, 64
        )
        store_columns(
            dot_tn(low[...], before_grad), send, keep, info[0], pl.multiple_of(h * 32, 32)
        )
        total[...] += dot_nt(before_grad, up_value)

    @pl.when(step == 3)
    def _():
        normal, inverse = normalize(middle[...])
        gain_grad[...] = row_sum(total[...] * normal)
        grad = stream_grad[...] + normalize_back(total[...], gain[...], normal, inverse)
        stream[...] = grad
        grad_low = grad.astype(LOW)
        store_halves(dot_tn(joined_low[...], grad_low), merge_send, merge_keep, info[0], 32, 0)
        joined[...] = dot_nt(grad_low, join_rows(weight[...], weight_two[...], info[0]))
        spread(joined, padded_grad, info, segments, blocks)
        conv_taps(padded_grad, padded, steps_ref, taps_grad, blocks, taps)
        conv_add(padded_grad, conv, taps_ref, steps_ref, sums, blocks, taps, True)
        unspread(conv, joined, info, segments, blocks)
        attended_grad[...] = joined[:, :WIDTH]
        gated_grad[...] = joined[:, WIDTH:]


def front_hidden_kernel(
    info, grad, heads_stream, gated_stream, before, down, down_two,
    stream_out, before_grad, send, keep, part_grad,
):
    h = pl.program_id(0)

    @pl.when(h == 0)
    def _():
        stream_sum = grad[...] + heads_stream[...] + gated_stream[...]
        stream_out[...] = stream_sum
        part_grad[...] = (0.5 * stream_sum).astype(LOW)

    down_value = join_lines(down[...], down_two[...], info[0])
    before_grad[...] = hidden_back(
        h, info[0], before[...], part_grad[...], down_value, send, keep, 0
    )


def front_input_kernel(
    info, stream_grad, before_grad, x_ref, gain, up, up_two,
    x_grad, send, keep, low, total,
):
    h = pl.program_id(0)

    @pl.when(h == 0)
    def _():
        normal, _ = normalize(x_ref[...].astype(F32))
        low[...] = (normal * gain[...]).astype(LOW)
        total[...] = jnp.zeros_like(total)

    store_columns(
        dot_tn(low[...], before_grad[...]), send, keep, info[0], pl.multiple_of(h * 32, 32)
    )
    total[...] += dot_nt(before_grad[...], join_columns(up[...], up_two[...], info[0]))

    @pl.when(h == 1)
    def _():
        normal, inverse = normalize(x_ref[...].astype(F32))
        gain_grad = row_sum(total[...] * normal).astype(LOW)
        gain_rows = jnp.broadcast_to(gain_grad.reshape(1, 1, 1, WIDTH), (2, 8, 16, WIDTH))
        send[:, :, 64:80, :] = gain_rows
        keep[:, :, 64:80, :] = gain_rows
        x_grad[...] = (
            stream_grad[...] + normalize_back(total[...], gain[...], normal, inverse)
        ).astype(LOW)


def whole(shape):
    return pl.BlockSpec(shape, lambda *_: (0,) * len(shape))


def call(kernel, grid, inputs, outputs, scratch, info, flops=0, after=(), room=56):
    in_specs = [
        whole(array.shape) if block is None else pl.BlockSpec(block, index)
        for array, block, index in inputs
    ]
    out_specs = [
        whole(shape) if block is None else pl.BlockSpec(block, index)
        for shape, _, block, index in outputs
    ]
    arrays = [array for array, _, _ in inputs]
    shapes = [jax.ShapeDtypeStruct(shape, kind) for shape, kind, _, _ in outputs]
    moved = sum(array.size * array.dtype.itemsize for array in arrays)
    moved = sum(shape.size * shape.dtype.itemsize for shape in shapes) + min(moved, 1 << 24)
    skipped = len(after)
    name = getattr(kernel, "func", kernel).__name__

    def body(info_ref, *refs):
        kernel(info_ref, *refs[skipped:])

    return pl.pallas_call(
        body,
        grid_spec=pltpu.PrefetchScalarGridSpec(
            num_scalar_prefetch=1,
            grid=grid,
            in_specs=[pl.BlockSpec(memory_space=pl.ANY)] * skipped + in_specs,
            out_specs=out_specs,
            scratch_shapes=scratch,
        ),
        out_shape=shapes,
        name=name,
        compiler_params=pltpu.CompilerParams(vmem_limit_bytes=room * 1024 * 1024),
        cost_estimate=pl.CostEstimate(flops=flops, bytes_accessed=moved, transcendentals=0),
    )(info, *after, *arrays)


def segment_table(lengths, spots, row_count):
    ends = jnp.cumsum(lengths)
    position = jnp.arange(row_count, dtype=jnp.int32)
    segments = jnp.sum((position[None, :] >= ends[:, None]).astype(jnp.int32), axis=0)
    zero = jnp.zeros((1,), jnp.int32)
    last = jnp.full((1,), row_count, jnp.int32)
    return segments, jnp.concatenate([spots, zero, ends, ends, last]).astype(jnp.int32)


def all_of(*arrays):
    return [(array, None, None) for array in arrays]


def plain(*shapes_and_types):
    return [(shape, kind, None, None) for shape, kind in shapes_and_types]


def halves(rows):
    return plain(((2, 8, rows, WIDTH), LOW)) * 2


def columns(pair, rows, start, index):
    block = (4, 4, rows, WIDTH), lambda *i: (0, 0, start // rows + index(*i), 0)
    return [(array, *block) for array in pair]


def lines(pair, index, steps=2):
    block = (2, 4, 64, WIDTH), lambda *i: (index(*i) // steps, 0, 1, 0)
    return [(array, *block) for array in pair]


def first(*_):
    return 0


def step(h, _):
    return h


class Layer:
    def __init__(self, features, cotangent, lengths, spots, taps):
        self.features, self.cotangent, self.taps = features, cotangent, taps
        self.tokens = features.shape[0]
        self.count = lengths.shape[0]
        self.segments = self.count + 1
        seg_ids, self.info = segment_table(lengths, spots, self.tokens)
        self.segs_col, self.segs_row = seg_ids[:, None], seg_ids[None, :]
        self.valid = (self.segs_col < self.count).astype(F32)
        self.stream = ((self.tokens, WIDTH), F32)
        self.low = pltpu.VMEM((self.tokens, WIDTH), LOW)
        self.wide = pltpu.VMEM((self.tokens, WIDTH), F32)
        rows = self.tokens + GAP * (self.segments - 1)
        self.spread_rows = -(-rows // (4 * GAP)) * 4 * GAP + 2 * GAP
        self.conv = dict(segments=self.segments, taps=taps)
        self.stat = ((8, WIDTH), F32)
        self.vector = ((1, WIDTH), F32)
        self.flop = 2 * self.tokens * WIDTH * WIDTH

    def set_small(self, smaller):
        (
            self.gate_taps, self.merge_taps, self.front_gain, self.heads_gain, self.gated_gain,
            self.gate_gain, self.rear_gain, self.final_gain,
        ) = smaller

    def padded(self, width):
        return pltpu.VMEM((width // CHAN, self.spread_rows, CHAN), F32)

    def tall(self, width, kind=F32):
        return ((self.tokens, width), kind)

    def by_column(self, array, start=0):
        return [(array, (self.tokens, WIDTH), lambda j, _: (0, j + start))]

    def by_pair(self, array):
        return [(array, (self.tokens, 2 * WIDTH), lambda j, _: (0, j))]

    def front_forward(self, front, after=()):
        self.front = front
        self.after_front, self.front_before, self.front_stat = call(
            front_forward_kernel,
            (4,),
            all_of(self.features, self.front_gain, self.valid)
            + columns(front, 16, 0, step)
            + lines(front, step),
            plain(self.stream)
            + [(*self.tall(4 * WIDTH), (self.tokens, WIDTH), lambda h, _: (0, h))]
            + plain(self.stat),
            [self.low, self.wide],
            self.info,
            8 * self.flop,
            after,
        )
        return self.front_stat

    def branches_forward(self, middle, after=()):
        self.middle = middle
        self.heads = columns(middle, 48, 144, first) + columns(middle, 16, 192, first)
        (
            self.attended, self.packed, self.mixed, self.gated, self.gated_before,
            self.gate_normal, self.gate_inverse, self.gate_part, self.product,
        ) = call(
            functools.partial(branches_forward_kernel, **self.conv),
            (6,),
            all_of(self.after_front, self.heads_gain, self.segs_col, self.segs_row)
            + self.heads
            + all_of(self.gated_gain, self.gate_gain, self.gate_taps)
            + columns(middle, 16, 0, lambda j, _: (j + 3) % 6)
            + columns(middle, 48, 96, first),
            plain(self.stream, self.tall(3 * WIDTH, LOW), self.tall(WIDTH, LOW), self.stream)
            + [(*self.tall(6 * WIDTH), (self.tokens, WIDTH), lambda j, _: (0, (j + 3) % 6))]
            + plain(
                self.tall(3 * WIDTH), self.tall(1), self.tall(3 * WIDTH), self.tall(3 * WIDTH, LOW)
            ),
            [self.low, pltpu.VMEM((self.tokens, 3 * WIDTH), F32)]
            + [self.padded(3 * WIDTH)] * 3
            + [pltpu.VMEM((GAP, 3 * WIDTH), F32)],
            self.info,
            52 * self.flop,
            after,
        )
        return self.gate_inverse

    def merge_rear(self, rear, after=()):
        def bounce(i, _):
            return jnp.where(i < 2, i, 3 - i)

        padded = self.padded(2 * WIDTH)
        (
            self.encoded, self.merge_grad, self.rear_gain_grad, self.final_gain_grad,
            self.rear_stat, self.attended_grad, self.gated_grad, self.merge_taps_grad, *pair,
        ) = call(
            functools.partial(merge_rear_kernel, **self.conv),
            (4,),
            all_of(self.after_front, self.attended, self.gated, self.merge_taps)
            + columns(rear, 32, 128, first)
            + all_of(self.rear_gain, self.final_gain, self.valid, self.cotangent)
            + columns(rear, 32, 0, bounce)
            + lines(rear, bounce, 1),
            plain(
                self.tall(WIDTH, LOW), self.stream, self.vector, self.vector, self.stat,
                self.stream, self.stream, ((self.taps + 1, 2 * WIDTH), F32),
            )
            + halves(128)
            + halves(32),
            [
                self.low, pltpu.VMEM((2, self.tokens, 2 * WIDTH), F32), self.low, self.wide, self.wide,
                self.wide, pltpu.VMEM((self.tokens, 2 * WIDTH), F32),
                pltpu.VMEM((self.tokens, 2 * WIDTH), LOW), padded, padded, padded, padded,
                pltpu.VMEM((GAP, 2 * WIDTH), F32),
            ],
            self.info,
            80 * self.flop,
            after,
        )
        return pair

    def branches_backward(self, after=()):
        self.heads_stream, self.heads_gain_grad, self.part_grad, self.gated_total, *pair = call(
            branches_backward_kernel,
            (3,),
            all_of(
                self.attended_grad, self.after_front, self.heads_gain, self.segs_col,
                self.segs_row, self.packed, self.mixed,
            )
            + self.heads
            + all_of(self.gated_grad, self.gated_gain)
            + self.by_column(self.gated_before)
            + self.by_column(self.gate_part)
            + all_of(self.product)
            + columns(self.middle, 16, 0, step)
            + columns(self.middle, 48, 96, first),
            plain(self.stream, self.vector)
            + [(*self.tall(3 * WIDTH), (self.tokens, WIDTH), lambda j, _: (0, j))]
            + plain(self.stream)
            + halves(160),
            [
                self.low, pltpu.VMEM((self.tokens, 3 * WIDTH), F32), self.low, self.low,
                pltpu.VMEM((self.tokens, 3 * WIDTH), LOW),
            ],
            self.info,
            40 * self.flop,
            after,
        )
        return pair

    def gated_gate(self, after=()):
        padded = self.padded(3 * WIDTH)
        (
            self.gated_stream, self.gated_gain_grad, self.gate_gain_grad, self.gate_taps_grad,
            *pair,
        ) = call(
            functools.partial(gated_gate_kernel, **self.conv),
            (3,),
            all_of(
                self.part_grad, self.gate_normal, self.gate_inverse, self.gate_gain,
                self.gate_taps, self.after_front, self.gated_gain,
            )
            + self.by_column(self.gated_before, 3)
            + all_of(self.gated_total)
            + columns(self.middle, 16, 0, lambda j, _: j + 3),
            plain(
                self.stream, self.vector, ((1, 3 * WIDTH), F32),
                ((self.taps + 1, 3 * WIDTH), F32),
            )
            + halves(48),
            [
                self.low, self.wide, padded, padded, padded,
                pltpu.VMEM((self.tokens, 3 * WIDTH), F32), padded,
                pltpu.VMEM((GAP, 3 * WIDTH), F32),
            ],
            self.info,
            48 * self.flop,
            after,
        )
        return pair

    def front_hidden(self, after=()):
        self.front_grad, self.front_before_grad, *pair = call(
            front_hidden_kernel,
            (2,),
            all_of(self.merge_grad, self.heads_stream, self.gated_stream)
            + self.by_pair(self.front_before)
            + lines(self.front, step, 1),
            plain(self.stream)
            + [(*self.tall(4 * WIDTH, LOW), (self.tokens, 2 * WIDTH), lambda h, _: (0, h))]
            + halves(64),
            [self.low],
            self.info,
            12 * self.flop,
            after,
        )
        return pair

    def front_input(self, after=()):
        self.features_grad, *pair = call(
            front_input_kernel,
            (2,),
            all_of(self.front_grad)
            + self.by_pair(self.front_before_grad)
            + all_of(self.features, self.front_gain)
            + columns(self.front, 32, 0, step),
            plain(self.tall(WIDTH, LOW)) + halves(80),
            [self.low, self.wide],
            self.info,
            12 * self.flop,
            after,
        )
        return pair

    def small_grads(self):
        return (
            self.gate_taps_grad, self.merge_taps_grad, self.heads_gain_grad,
            self.gated_gain_grad, self.rear_gain_grad, self.final_gain_grad, self.gate_gain_grad,
        )

    def stats(self):
        return self.front_stat, self.rear_stat


SMALL = 16
STATS = 8


def ring(size, shift):
    return [(i, (i + shift) % size) for i in range(size)]


def pack_kernel(
    info, front_up, front_down, heads_in, heads_out, gated_in, gated_out, merge_out, rear_up,
    rear_down, gate_taps, merge_taps, front_gain, heads_gain, gated_gain, rear_gain, final_gain,
    gate_gain, front, middle, rear, small,
):
    def put(target, start, source):
        rows, width = source.shape
        for q in range(width // WIDTH):
            target[start + rows * q : start + rows * (q + 1), :] = source[
                :, WIDTH * q : WIDTH * (q + 1)
            ]

    put(front, 0, front_up)
    put(front, 64, front_down)
    put(middle, 0, gated_in)
    put(middle, 96, gated_out)
    put(middle, 144, heads_in)
    put(middle, 192, heads_out)
    put(rear, 0, rear_up)
    put(rear, 64, rear_down)
    put(rear, 128, merge_out)
    small[...] = jnp.zeros_like(small)
    for q, source in ((0, gate_taps), (2, merge_taps)):
        value = source[...].astype(F32)
        taps, width = value.shape
        small[0:SMALL, CHAN * q : CHAN * q + width] = value[:SMALL]
        small[0 : taps - SMALL, CHAN * (q + 1) : CHAN * (q + 1) + width] = value[SMALL:]
    start = CHAN
    for source in (front_gain, heads_gain, gated_gain, rear_gain, final_gain, gate_gain):
        width = source.shape[1]
        small[SMALL - 1 :, start : start + width] = source[...].astype(F32)
        start += width
    front[128 : 128 + SMALL, :] = small[...].astype(LOW)


def copy_all(copies):
    for copy in copies:
        copy.start()
    for copy in copies:
        copy.wait()


def place_line_kernel(info, *refs):
    pieces, out, sem = refs[:4], refs[4], refs[5]
    copy_all(
        [
            pltpu.make_async_copy(piece, out.at[chip, info[PLACE + i]], sem.at[chip, i])
            for chip in range(4)
            for i, piece in enumerate(pieces)
        ]
    )


def place(kernel, pieces, rows, info, after=()):
    skipped = len(after)

    def body(info_ref, *refs):
        kernel(info_ref, *refs[skipped:])

    anywhere = pl.BlockSpec(memory_space=pl.ANY)
    return pl.pallas_call(
        body,
        grid_spec=pltpu.PrefetchScalarGridSpec(
            num_scalar_prefetch=1,
            grid=(1,),
            in_specs=[anywhere] * skipped + [pl.BlockSpec(memory_space=pltpu.VMEM)] * 4,
            out_specs=anywhere,
            scratch_shapes=[pltpu.SemaphoreType.DMA((4, 4))],
        ),
        out_shape=jax.ShapeDtypeStruct((4, 4, rows, WIDTH), LOW),
        name=kernel.__name__,
        compiler_params=pltpu.CompilerParams(vmem_limit_bytes=16 * 1024 * 1024),
        cost_estimate=pl.CostEstimate(
            flops=0, bytes_accessed=32 * rows * WIDTH * 2, transcendentals=0
        ),
    )(info, *after, *pieces)


def line_sends(array):
    return [lax.ppermute(array, "z", ring(4, d)) for d in (1, 2, 3)]


def plane_exchange(array):
    return lax.all_to_all(array, ("x", "y"), 0, 0, tiled=True)


def core_swap(array):
    return lax.ppermute(array, "k", ring(2, 1))


def tie(array, *others):
    return lax.optimization_barrier((array, others))[0]


def unpack_kernel(info, first, second, gate_taps, merge_taps, gains, gate_gain):
    mine = info[0]
    lane = lax.broadcasted_iota(jnp.int32, (SMALL, CHAN), 1)
    lane_row = lane[:1]
    gate_gain[...] = jnp.zeros_like(gate_gain)
    gains[...] = jnp.zeros_like(gains)

    def put(target, rows, value, start, size, lanes):
        block, offset = start // CHAN, start % CHAN
        inside = jnp.logical_and(lanes >= offset, lanes < offset + size)
        window = slice(CHAN * block, CHAN * (block + 1))
        target[rows, window] = jnp.where(inside, value, target[rows, window])
        spill = offset + size - CHAN
        if spill > 0:
            window = slice(CHAN * (block + 1), CHAN * (block + 2))
            target[rows, window] = jnp.where(lanes < spill, value, target[rows, window])

    for i in range(BLOCKS):
        x, core, rest = i // 16, (i // 8) % 2, i % 8
        chip, z = 2 * x + rest % 2, rest // 2
        value = jnp.where(mine == core, first[chip, z], second[chip, z]).astype(F32)
        quads = [value[:, CHAN * q : CHAN * (q + 1)] for q in range(4)]
        start = 48 * i
        for half in range(2):
            rows = slice(SMALL * half, SMALL * (half + 1))
            rolled = pltpu.roll(quads[half], start % CHAN, 1)
            put(gate_taps, rows, rolled, start, 48, lane)
            rolled = pltpu.roll(quads[2 + half], (32 * i) % CHAN, 1)
            put(merge_taps, rows, rolled, 32 * i, 32, lane)
        line = quads[1][SMALL - 1 :]
        for g in range(5):
            rolled = pltpu.roll(line, (16 * i - 16 * g) % CHAN, 1)
            put(gains, slice(g, g + 1), rolled, 16 * i, 16, lane_row)
        rolled = pltpu.roll(line, (48 * i - 80) % CHAN, 1)
        put(gate_gain, slice(0, 1), rolled, 48 * i, 48, lane_row)


def pack_small_kernel(
    info, gate_taps, merge_taps, heads_gain, gated_gain, rear_gain, final_gain, gate_gain,
    front_stat, rear_stat, send, keep, *, count_at,
):
    mine = info[0]
    lane = lax.broadcasted_iota(jnp.int32, (SMALL, CHAN), 1)
    lane_row = lane[:1]
    last = lax.broadcasted_iota(jnp.int32, (SMALL, CHAN), 0) == SMALL - 1
    stats = [
        front_stat[0:1, :], front_stat[1:2, :], rear_stat[0:1, :], rear_stat[2:3, :],
        front_stat[2:3, :], rear_stat[1:2, :], rear_stat[3:4, :],
    ]
    stat_line = jnp.where(lane_row == 7, info[count_at].astype(F32), 0.0)
    for i, stat in enumerate(stats):
        stat_line = jnp.where(lane_row == i, jnp.sum(stat, axis=1, keepdims=True), stat_line)
    rest = stat_line - stat_line.astype(LOW).astype(F32)
    stat_line += pltpu.roll(rest, STATS, 1)

    def take(source, rows, start, size, lanes):
        block, offset = start // CHAN, start % CHAN
        value = source[rows, CHAN * block : CHAN * (block + 1)]
        if offset:
            value = pltpu.roll(value, CHAN - offset, 1)
        if offset + size > CHAN:
            other = source[rows, CHAN * (block + 1) : CHAN * (block + 2)]
            value = jnp.where(lanes < CHAN - offset, value, pltpu.roll(other, CHAN - offset, 1))
        return value

    def quads_of(i):
        halves = [slice(0, SMALL), slice(SMALL, 2 * SMALL)]
        quads = [take(gate_taps, rows, 48 * i, 48, lane) for rows in halves]
        quads += [take(merge_taps, rows, 32 * i, 32, lane) for rows in halves]
        line = pltpu.roll(take(gate_gain, slice(0, 1), 48 * i, 48, lane_row), 80, 1)
        for g, gain in enumerate((heads_gain, gated_gain, rear_gain, final_gain)):
            start = 16 * (g + 1)
            block = gain[:, CHAN * (i // 8) : CHAN * (i // 8 + 1)]
            value = pltpu.roll(block, (start - 16 * i) % CHAN, 1)
            inside = jnp.logical_and(lane_row >= start, lane_row < start + 16)
            line = jnp.where(inside, value, line)
        quads[1] = jnp.where(last, line, quads[1])
        quads[3] = jnp.where(last, stat_line, quads[3])
        return quads

    for i in [*range(8), *range(16, 24)]:
        x, spot = i // 16, i % 8
        pairs = zip(quads_of(i), quads_of(i + 8))
        for q, (low, high) in enumerate(pairs):
            lanes = slice(CHAN * q, CHAN * (q + 1))
            keep[x, spot, :, lanes] = jnp.where(mine == 0, low, high).astype(LOW)
            send[x, spot, :, lanes] = jnp.where(mine == 0, high, low).astype(LOW)


def round_small(total):
    quad = total[:, 3 * CHAN :]
    lane = lax.broadcasted_iota(jnp.int32, quad.shape, 1)
    row = lax.broadcasted_iota(jnp.int32, quad.shape, 0)
    stat = jnp.logical_and(row == SMALL - 1, lane < STATS)
    rest = jnp.where(stat, quad - quad.astype(LOW).astype(F32), 0.0)
    quad = quad + pltpu.roll(rest, STATS, 1)
    return jnp.concatenate([total[:, : 3 * CHAN], quad], axis=1).astype(LOW)


def core_sum_kernel(info, *refs, sizes):
    inputs, out = refs[:-1], refs[-1]
    half = len(inputs) // 2
    keeps, gots = inputs[:half], inputs[half:]

    def one(z, _):
        for chip in range(4):
            x, spot = chip // 2, 2 * z + chip % 2
            start = 0
            for keep, got, (rows, small) in zip(keeps, gots, sizes):
                span = slice(start, start + rows)
                start += rows
                if small:
                    total = keep[x, spot].astype(F32) + got[x, spot].astype(F32)
                    out[chip, z, span, :] = round_small(total)
                else:
                    out[chip, z, span, :] = keep[x, spot] + got[x, spot]
        return 0

    lax.fori_loop(0, 4, one, 0)


def plane_sum_kernel(info, pieces, *outs, sizes):
    for e in range(4):
        zi = lax.rem(info[PLACE] + e, 4)
        start = 0
        for rows in sizes:
            small, rows = rows < 0, abs(rows)
            span = slice(start, start + rows)
            start += rows
            total = sum(pieces[chip, zi, span, :].astype(F32) for chip in range(4))
            if e == 0:
                outs[0][span, :] = total
            elif small:
                outs[e][span, :] = round_small(total)
            else:
                outs[e][span, :] = total.astype(LOW)


def line_sum_kernel(info, keep, one, two, three, *refs, pieces):
    refs = list(refs)
    start = 0
    for rows, what in pieces:
        span = slice(start, start + rows)
        start += rows
        total = keep[span, :]
        for piece in (one, two, three):
            total += piece[span, :].astype(F32)
        if what == "small":
            quads = [total[:, CHAN * q : CHAN * (q + 1)] for q in range(4)]
            gate_taps, merge_taps, heads_gain, gated_gain, rear_gain, final_gain, gate_gain, stats = refs
            gate_taps[0:SMALL, :] = quads[0][:, :48]
            gate_taps[SMALL : 2 * SMALL - 1, :] = quads[1][: SMALL - 1, :48]
            merge_taps[0:SMALL, :] = quads[2][:, :32]
            merge_taps[SMALL : 2 * SMALL - 1, :] = quads[3][: SMALL - 1, :32]
            line = quads[1][SMALL - 1 :, :]
            for g, target in enumerate((heads_gain, gated_gain, rear_gain, final_gain)):
                target[...] = pltpu.roll(line, CHAN - 16 * (g + 1), 1)[:, :16]
            gate_gain[...] = pltpu.roll(line, CHAN - 80, 1)[:, :48]
            line = quads[3][SMALL - 1 :, :]
            line += pltpu.roll(line, CHAN - STATS, 1)
            frames = jnp.sum(line[:, STATS - 1 : STATS])
            stats[...] = jnp.sqrt(line[:, : STATS - 1] / (frames * WIDTH))
        elif what == "gain":
            owner = info[OWNER]
            line = jnp.zeros((1, CHAN), F32)
            for b in range(WIDTH // CHAN):
                block = total[0:1, CHAN * b : CHAN * (b + 1)]
                line = jnp.where(owner // 8 == b, block, line)
            line = pltpu.roll(line, lax.rem(CHAN - 16 * lax.rem(owner, 8), CHAN), 1)
            refs.pop(0)[...] = line[:, :16]
        elif what == "left":
            given, target = refs.pop(0), refs[0]
            target[:, : given.shape[1]] = given[...]
        else:
            shift = 0
            if what == "right":
                target = refs.pop(0)
                shift = target.shape[1] // 2
            else:
                target = refs.pop(0)
            height = target.shape[0]
            for q in range(rows // height):
                lanes = slice(shift + WIDTH * q, shift + WIDTH * (q + 1))
                target[:, lanes] = total[height * q : height * (q + 1), :]


def run(tasks, info, after=()):
    counts = [(len(inputs), len(outputs)) for _, inputs, outputs in tasks]

    def tasks_kernel(info_ref, *refs):
        total = sum(count for count, _ in counts)
        ins, outs = list(refs[:total]), list(refs[total:])
        for (kernel, _, _), (taken, given) in zip(tasks, counts):
            kernel(info_ref, *ins[:taken], *outs[:given])
            del ins[:taken], outs[:given]

    results = call(
        tasks_kernel,
        (1,),
        all_of(*[array for _, inputs, _ in tasks for array in inputs]),
        plain(*[output for _, _, outputs in tasks for output in outputs]),
        [],
        info,
        after=after,
        room=24,
    )
    grouped = []
    for _, given in counts:
        grouped.append(results[:given])
        results = results[given:]
    return grouped


def core_sum(pairs):
    sizes = tuple((pair[0].shape[2], pair[0].shape[2] == SMALL) for pair in pairs)
    total = sum(rows for rows, _ in sizes)
    return (
        functools.partial(core_sum_kernel, sizes=sizes),
        [pair[i] for i in (0, 1) for pair in pairs],
        [((4, 4, total, WIDTH), LOW)],
    )


def plane_sum(pieces, sizes):
    total = pieces.shape[2]
    return (
        functools.partial(plane_sum_kernel, sizes=sizes),
        [pieces],
        [((total, WIDTH), F32)] + [((total, WIDTH), LOW)] * 3,
    )


def line_sum(sums, pieces, outputs, given=()):
    own, rest = sums
    return (
        functools.partial(line_sum_kernel, pieces=pieces),
        [own, *rest, *given],
        [(shape, F32) for shape in outputs],
    )


def line_swap(sums):
    return sums[0], [lax.ppermute(array, "z", ring(4, d)) for d, array in zip((1, 2, 3), sums[1:])]


def pack_small(layer, count):
    return (
        functools.partial(pack_small_kernel, count_at=SEG + 2 * count),
        [*layer.small_grads(), *layer.stats()],
        [((2, 8, SMALL, WIDTH), LOW)] * 2,
    )


def unpack_small(front, info):
    block = (4, 4, SMALL, WIDTH), lambda *_: (0, 0, 8, 0)
    gate_taps, merge_taps, gains, gate_full = call(
        unpack_kernel,
        (1,),
        [(array, *block) for array in front],
        plain(
            ((32, 3 * WIDTH), F32), ((32, 2 * WIDTH), F32), ((8, WIDTH), F32), ((1, 3 * WIDTH), F32)
        ),
        [],
        info,
    )
    lines = [gains[g : g + 1] for g in range(5)]
    return gate_taps, merge_taps, lines[0], lines[1], lines[2], gate_full, lines[3], lines[4]


def grid_device(
    features, cotangent, lengths, front_up, front_down, heads_input, heads_output, gated_input,
    gated_output, merge_output, rear_up, rear_down, gate_kernel, merge_kernel, front_gain,
    heads_gain, gated_gain, gate_gain, rear_gain, final_gain,
):
    x, k, z, y = (lax.axis_index(name) for name in ("x", "k", "z", "y"))
    places = [k] + [lax.rem(place, 4) for place in (z, z + 3, z + 2, z + 1)]
    places.append(((x * 2 + k) * 4 + z) * 2 + y)
    spots = jnp.stack([place.astype(jnp.int32) for place in places])
    layer = Layer(features, cotangent, lengths[0], spots, gate_kernel.shape[0])
    info = layer.info

    front, middle, rear = call(
        pack_kernel,
        (1,),
        all_of(
            front_up, front_down, heads_input, heads_output, gated_input, gated_output,
            merge_output, rear_up, rear_down, gate_kernel, merge_kernel,
            *[
                gain.reshape(1, -1)
                for gain in (front_gain, heads_gain, gated_gain, rear_gain, final_gain, gate_gain)
            ],
        ),
        plain(((144, WIDTH), LOW), ((208, WIDTH), LOW), ((160, WIDTH), LOW)),
        [pltpu.VMEM((SMALL, WIDTH), F32)],
        spots,
    )
    front_four = place(place_line_kernel, [front] + line_sends(front), 144, info)
    front = plane_exchange(front_four)
    middle = tie(middle, front_four)
    middle_four = place(place_line_kernel, [middle] + line_sends(middle), 208, info)
    front = tie(front, middle_four)
    middle = plane_exchange(tie(middle_four, front))
    rear = tie(rear, front)
    rear_lines = line_sends(rear)
    front = front, core_swap(front)
    layer.set_small(unpack_small(front, info))
    mark = layer.front_forward(front)
    rear_four = place(place_line_kernel, [rear] + rear_lines, 160, info, after=(mark,))
    middle = tie(middle, rear_four)
    rear = plane_exchange(tie(rear_four, middle))
    middle = middle, core_swap(middle)
    mark = layer.branches_forward(middle)
    rear = tie(rear, mark)
    rear = rear, core_swap(rear)

    send, rear_keep, merge_send, merge_keep = layer.merge_rear(rear)
    rear_got = core_swap(send)
    ((rear_four,),) = run([core_sum([(rear_keep, rear_got)])], info)
    merge_got = core_swap(tie(merge_send, rear_got))
    rear_plane = plane_exchange(rear_four)
    send, wide_keep = layer.branches_backward(after=(rear_four,))
    wide_got = core_swap(tie(send, rear_plane))
    (rear_sums,) = run([plane_sum(rear_plane, (128,))], info, after=(layer.gated_total,))
    ((wide_four,),) = run(
        [core_sum([(merge_keep, merge_got), (wide_keep, wide_got)])], info,
        after=(rear_sums[0],),
    )
    rear_sums = line_swap(rear_sums)
    wide_plane = plane_exchange(tie(wide_four, rear_plane))
    send, gate_keep = layer.gated_gate(after=(wide_four,))
    gate_got = core_swap(send)
    send, down_keep = layer.front_hidden(after=rear_sums[1])
    down_got = core_swap(tie(send, wide_plane))
    (wide_sums,) = run([plane_sum(wide_plane, (192,))], info, after=(layer.front_grad,))
    ((last_four,),) = run(
        [
            core_sum([(gate_keep, gate_got), (down_keep, down_got)]),
        ],
        info,
        after=(wide_sums[0],),
    )
    wide_sums = line_swap(wide_sums)
    last_plane = plane_exchange(tie(last_four, wide_plane))
    ((small_send, small_keep),) = run(
        [pack_small(layer, lengths.shape[1])], info, after=(last_four,)
    )
    small_got = core_swap(small_send)
    send, up_keep = layer.front_input(after=(small_send, *wide_sums[1]))
    up_got = core_swap(send)
    ((front_four,),) = run(
        [core_sum([(up_keep, up_got), (small_keep, small_got)])], info
    )
    half_shape = (gated_input.shape[0], gated_input.shape[1] // 2)
    front_plane = plane_exchange(tie(front_four, last_plane))
    (last_sums,) = run([plane_sum(last_plane, (112,))], info, after=(front_four,))
    last_sums = line_swap(last_sums)
    (
        (rear_up_grad, rear_down_grad),
        (
            merge_output_grad, gated_left_grad, gated_output_grad, heads_input_grad,
            heads_output_grad,
        ),
    ) = run(
        [
            line_sum(rear_sums, ((64, None), (64, None)), (rear_up.shape, rear_down.shape)),
            line_sum(
                wide_sums, ((32, None), (48, None), (48, None), (48, None), (16, None)),
                (
                    merge_output.shape, half_shape, gated_output.shape, heads_input.shape,
                    heads_output.shape,
                ),
            ),
        ],
        info,
        after=(last_sums[0],),
    )
    (front_sums,) = run(
        [plane_sum(front_plane, (80, -SMALL))], info, after=(last_sums[0], merge_output_grad)
    )
    front_sums = line_swap(front_sums)
    vector = (1, front_gain.shape[0])
    ((gated_input_grad, front_down_grad),) = run(
        [
            line_sum(
                last_sums,
                ((0, "left"), (48, "right"), (64, None)),
                (gated_input.shape, front_down.shape),
                given=(gated_left_grad,),
            ),
        ],
        info,
        after=(front_sums[0],),
    )
    (
        (
            front_up_grad, front_gain_grad, gate_kernel_grad, merge_kernel_grad,
            heads_gain_grad, gated_gain_grad, rear_gain_grad, final_gain_grad, gate_gain_grad,
            statistics,
        ),
    ) = run(
        [
            line_sum(
                front_sums,
                ((64, None), (16, "gain"), (16, "small")),
                (
                    front_up.shape, vector, gate_kernel.shape, merge_kernel.shape, vector,
                    vector, vector, vector, (1, gate_gain.shape[0]), (1, STATS - 1),
                ),
            ),
        ],
        info,
        after=(front_down_grad,),
    )
    return (
        layer.encoded, layer.features_grad, front_up_grad, front_down_grad, heads_input_grad,
        heads_output_grad, gated_input_grad, gated_output_grad, merge_output_grad, rear_up_grad,
        rear_down_grad, gate_kernel_grad, merge_kernel_grad, front_gain_grad[0],
        heads_gain_grad[0], gated_gain_grad[0], gate_gain_grad[0], rear_gain_grad[0],
        final_gain_grad[0], statistics[0],
    )


def pack_rows(shard):
    rows, columns = shard.shape
    pieces = shard.reshape(rows, columns // WIDTH, WIDTH).transpose(1, 0, 2)
    return pieces.reshape(rows * columns // WIDTH, WIDTH)


def pad_lines(flat):
    rows = -(-flat.shape[-1] // (WIDTH * 16)) * 16
    spare = [(0, 0)] * (flat.ndim - 1) + [(0, rows * WIDTH - flat.shape[-1])]
    return jnp.pad(flat, spare).reshape(flat.shape[:-1] + (rows, WIDTH))


def to_owners(weight):
    rows, columns = weight.shape
    pieces = weight.reshape(BLOCKS, rows // BLOCKS, columns // WIDTH, WIDTH)
    pieces = pieces.transpose(0, 2, 1, 3).reshape(2, 2, 4, 2, -1, WIDTH)
    pieces = pieces.transpose(1, 0, 3, 2, 4, 5)
    return pieces.reshape(2, 4, 4, -1, WIDTH)


def from_owners(halves, rows, columns):
    send, keep = halves
    pieces = jnp.stack([keep, send], axis=1)
    pieces = pieces.reshape(BLOCKS, columns // WIDTH, rows // BLOCKS, WIDTH)
    return pieces.transpose(0, 2, 1, 3).reshape(rows, columns)


def any_device(features, cotangent, lengths, *shards, axes):
    count = lax.axis_size(axes)
    matrices, smaller = shards[:9], shards[9:]
    packed = [pack_rows(element) for element in matrices]
    packed.append(pad_lines(jnp.concatenate([element.reshape(-1) for element in smaller])))
    gathered = lax.all_gather(jnp.concatenate(packed), axes, axis=0)
    weights = []
    start = 0
    for element, piece in zip(matrices, packed):
        rows, columns = element.shape
        window = gathered[:, start : start + piece.shape[0]]
        start += piece.shape[0]
        window = window.reshape(count, columns // WIDTH, rows, WIDTH).transpose(0, 2, 1, 3)
        weights.append(to_owners(window.reshape(count * rows, columns)))
    flat = gathered[:, start:].reshape(count, -1).astype(F32)
    lines = []
    start = 0
    for element in smaller:
        window = flat[:, start : start + element.size]
        start += element.size
        if element.ndim == 2:
            window = window.reshape((count,) + element.shape).transpose(1, 0, 2)
            window = window.reshape(element.shape[0], -1)
            lines.append(jnp.pad(window, ((0, 1), (0, 0))))
        else:
            lines.append(window.reshape(1, -1))
    up, down, h_in, h_out, g_in, g_out, m_out, r_up, r_down = weights

    def chunk(*members):
        return tuple(jnp.concatenate([member[i] for member in members], axis=2) for i in (0, 1))

    front = chunk(up, down)
    rear = chunk(r_up, r_down, m_out)
    layer = Layer(features, cotangent, lengths[0], jnp.zeros((SEG,), jnp.int32), smaller[0].shape[0])
    layer.set_small(lines)
    layer.front_forward(front)
    layer.branches_forward(chunk(g_in, g_out, h_in, h_out))
    rear = layer.merge_rear(rear)
    rear, merge = rear[:2], rear[2:]
    wide = layer.branches_backward()
    right = layer.gated_gate()
    front_down_halves = layer.front_hidden()
    front_up_halves = layer.front_input()

    def part(pair, start, stop):
        return tuple(array[:, :, start:stop] for array in pair)

    gated_halves = tuple(
        jnp.concatenate([one[:, :, :48], two], axis=2) for one, two in zip(wide, right)
    )
    ordered = (
        part(front_up_halves, 0, 64), front_down_halves, part(wide, 96, 144),
        part(wide, 144, 160), gated_halves, part(wide, 48, 96), merge,
        part(rear, 0, 64), part(rear, 64, 128),
    )
    front_gain = front_up_halves[1][0, 0, 64].astype(F32)
    small_grads = layer.small_grads()
    pieces = []
    for element, halves in zip(matrices, ordered):
        rows, columns = element.shape
        full = from_owners(halves, rows * count, columns)
        full = full.reshape(count, rows, columns // WIDTH, WIDTH).transpose(0, 2, 1, 3)
        pieces.append(full.reshape(count, -1, WIDTH))
    gate_taps, merge_taps, heads_gain, gated_gain, rear_gain, final_gain, gate_gain = small_grads
    small_full = (gate_taps, merge_taps, front_gain, heads_gain, gated_gain, gate_gain, rear_gain, final_gain)
    flat = []
    for element, full in zip(smaller, small_full):
        if element.ndim == 2:
            full = full[: element.shape[0]].reshape(element.shape[0], count, -1).transpose(1, 0, 2)
        flat.append(full.reshape(count, -1))
    pieces.append(pad_lines(jnp.concatenate(flat, axis=1).astype(LOW)))
    summed = lax.psum_scatter(jnp.concatenate(pieces, axis=1), axes, scatter_dimension=0)
    outputs = []
    start = 0
    for element, piece in zip(matrices, pieces):
        rows, columns = element.shape
        window = summed[start : start + piece.shape[1]].astype(F32)
        start += piece.shape[1]
        window = window.reshape(columns // WIDTH, rows, WIDTH).transpose(1, 0, 2)
        outputs.append(window.reshape(rows, columns))
    flat = summed[start:].reshape(-1).astype(F32)
    start = 0
    for element in smaller:
        outputs.append(flat[start : start + element.size].reshape(element.shape))
        start += element.size
    front_stat, rear_stat = layer.stats()
    squares = jnp.stack(
        [
            front_stat[0], front_stat[1], rear_stat[0], rear_stat[2], front_stat[2], rear_stat[1],
            rear_stat[3],
        ]
    )
    totals = lax.psum(
        jnp.append(jnp.sum(squares, axis=1), jnp.sum(lengths).astype(F32)), axes
    )
    statistics = jnp.sqrt(totals[:7] / (totals[7] * features.shape[1]))
    return (layer.encoded, layer.features_grad) + tuple(outputs) + (statistics,)


def solution(mesh):
    body = grid_device
    axes = ("x", "k", "z", "y")
    if mesh.devices.shape == (4, 8):
        mesh = Mesh(mesh.devices.reshape(2, 2, 4, 2), axes)
    else:
        axes = tuple(mesh.axis_names)
        body = functools.partial(any_device, axes=axes)
    rows, columns, vector = P(axes, None), P(None, axes), P(axes)
    weights = (rows,) * 9 + (columns,) * 2 + (vector,) * 6
    return jax.shard_map(
        body,
        mesh=mesh,
        in_specs=(rows, rows, rows) + weights,
        out_specs=(rows, rows) + weights + (P(),),
        check_vma=False,
    )
```

```python
import functools

import jax
import jax.numpy as jnp
from jax import lax
from jax.experimental import pallas as pl
from jax.experimental.pallas import tpu as pltpu
from jax.sharding import Mesh, PartitionSpec as P

HEADS = 8
EPSILON = 1e-05
NEGATIVE = -1000000000.0
TILE = 8
GAP = 16
CHAN = 128
PLACE = 1
OWNER = 5
SEG = 6
WIDTH = 512
BLOCKS = 32
F32 = jnp.float32
LOW = jnp.bfloat16


def dot(left, right):
    return jnp.dot(left, right, preferred_element_type=F32)


def dot_tn(left, right):
    return lax.dot_general(left, right, (((0,), (0,)), ((), ())), preferred_element_type=F32)


def dot_nt(left, right):
    return lax.dot_general(left, right, (((1,), (1,)), ((), ())), preferred_element_type=F32)


def normalize(values):
    centred = values - jnp.mean(values, axis=-1, keepdims=True)
    variance = jnp.mean(centred * centred, axis=-1, keepdims=True)
    inverse = lax.rsqrt(variance + EPSILON)
    return centred * inverse, inverse


def normalize_back(upstream, gain, normal, inverse):
    scaled = upstream * gain
    mean_scaled = jnp.mean(scaled, axis=-1, keepdims=True)
    mean_cross = jnp.mean(scaled * normal, axis=-1, keepdims=True)
    return inverse * (scaled - mean_scaled - normal * mean_cross)


def part_of(index):
    return slice(None), pl.ds(pl.multiple_of(index * WIDTH, WIDTH), WIDTH)


def by_rows(rows, body):
    size = 48 if rows % 48 == 0 else TILE

    def one(i, _):
        body(pl.ds(pl.multiple_of(i * size, size), size))
        return 0

    lax.fori_loop(0, rows // size, one, 0)


def row_sum(values):
    return jnp.sum(values, axis=0, keepdims=True)


GELU_A = 0.7978845608028654
GELU_B = 0.044715


def gelu(v):
    return 0.5 * v * (1.0 + jnp.tanh(GELU_A * (v + GELU_B * v * v * v)))


def gelu_pair(v):
    square = v * v
    bend = jnp.tanh(GELU_A * (v + GELU_B * square * v))
    value = 0.5 * v * (1.0 + bend)
    slope = 0.5 * (1.0 + bend) + 0.5 * v * (1.0 - bend * bend) * (
        GELU_A * (1.0 + 3.0 * GELU_B * square)
    )
    return value, slope


def silu(v):
    return v * jax.nn.sigmoid(v)


def store_halves(value, send, keep, mine, rows, start):
    parts = value.astype(LOW).reshape(2, 2, 8, rows, WIDTH)

    @pl.when(mine == 0)
    def _():
        keep[:, :, pl.ds(start, rows), :] = parts[:, 0]
        send[:, :, pl.ds(start, rows), :] = parts[:, 1]

    @pl.when(mine == 1)
    def _():
        keep[:, :, pl.ds(start, rows), :] = parts[:, 1]
        send[:, :, pl.ds(start, rows), :] = parts[:, 0]


def join_rows(first, second, mine):
    cores = jnp.where(mine == 0, first, second), jnp.where(mine == 0, second, first)
    return jnp.concatenate(
        [core[2 * x + y, z] for x in (0, 1) for core in cores for z in range(4) for y in (0, 1)]
    )


def pick_rows(first, second, flag):
    chosen = jnp.where(flag, first, second)
    return jnp.concatenate([chosen[y, z] for z in range(4) for y in (0, 1)])


def join_columns(first, second, mine):
    blocks = range(0, first.shape[2], 16)
    return jnp.concatenate(
        [join_rows(first[:, :, i : i + 16, :], second[:, :, i : i + 16, :], mine) for i in blocks],
        axis=1,
    )


def join_lines(first, second, mine):
    cores = jnp.where(mine == 0, first, second), jnp.where(mine == 0, second, first)
    return jnp.concatenate([core[y, z] for core in cores for z in range(4) for y in (0, 1)])


def store_columns(value, send, keep, mine, start):
    for i in range(value.shape[1] // WIDTH):
        store_halves(value[:, WIDTH * i : WIDTH * (i + 1)], send, keep, mine, 16, start + 16 * i)


def visits(info, segments, body):
    def segment(s, _):
        begin, end = info[SEG + s], info[SEG + segments + s]

        def visit(i, _):
            row = i * TILE + lax.broadcasted_iota(jnp.int32, (TILE, CHAN), 0)
            inside = jnp.logical_and(row >= begin, row < end)
            base = pl.multiple_of(i * TILE, TILE)
            body(base, pl.multiple_of(base + GAP * (s + 1), TILE), inside)
            return 0

        lax.fori_loop(begin // TILE, (end + TILE - 1) // TILE, visit, 0)
        return 0

    lax.fori_loop(0, segments, segment, 0)


def spread(source, padded, info, segments, blocks):
    def clear(c, _):
        padded[c] = jnp.zeros(padded.shape[1:], F32)
        return 0

    lax.fori_loop(0, blocks, clear, 0)

    def body(base, apart, inside):
        for c in range(blocks):
            value = source[pl.ds(base, TILE), c * CHAN : (c + 1) * CHAN]
            padded[c, pl.ds(apart, TILE), :] = jnp.where(inside, value, 0.0)

    visits(info, segments, body)


def unspread(padded, target, info, segments, blocks):
    def body(base, apart, inside):
        for c in range(blocks):
            lanes = slice(c * CHAN, (c + 1) * CHAN)
            value = padded[c, pl.ds(apart, TILE), :]
            target[pl.ds(base, TILE), lanes] = jnp.where(
                inside, value, target[pl.ds(base, TILE), lanes]
            )

    visits(info, segments, body)


def conv_rows(padded, kernel, out, steps_ref, sums, blocks, taps, flip):
    half = (taps - 1) // 2
    rows = padded.shape[1]
    pairs = (rows - 2 * GAP) // (4 * GAP)
    order = [taps - 1 - j if flip else j for j in range(taps)]

    def differ(c, _):
        steps_ref[c, 0 : rows - GAP, :] = padded[c, 0 : rows - GAP, :] - padded[c, GAP:rows, :]
        return 0

    lax.fori_loop(0, blocks, differ, 0)
    for j in range(GAP):
        total = kernel[order[j] : order[j] + 1, :]
        if j + GAP < taps:
            total = total + kernel[order[j + GAP] : order[j + GAP] + 1, :]
        sums[j : j + 1, :] = total

    def body(step, _):
        c = step // 2
        base = GAP + lax.rem(step, 2) * (pairs * 2 * GAP)
        lanes = pl.ds(pl.multiple_of(c * CHAN, CHAN), CHAN)
        for w in range(pairs):
            start = base + 2 * GAP * w
            first_part = second = third = jnp.zeros((GAP, CHAN), F32)
            for j in range(GAP):
                row = start + j - half
                first_part += kernel[pl.ds(order[j], 1), lanes] * steps_ref[c, pl.ds(row, GAP), :]
                second += sums[pl.ds(j, 1), lanes] * padded[c, pl.ds(row + GAP, GAP), :]
                if j + GAP < taps:
                    third += (
                        kernel[pl.ds(order[j + GAP], 1), lanes]
                        * steps_ref[c, pl.ds(row + GAP, GAP), :]
                    )
            start = pl.multiple_of(start, TILE)
            out[c, pl.ds(start, GAP), :] = first_part + second
            out[c, pl.ds(start + GAP, GAP), :] = second - third
        return 0

    lax.fori_loop(0, blocks * 2, body, 0)


def conv_taps(padded_grad, padded, steps_ref, out, blocks, taps):
    half = (taps - 1) // 2
    rows = padded.shape[1]
    pairs = (rows - 2 * GAP) // (2 * GAP)

    def fold(value):
        return value[:TILE] + value[TILE:]

    def block(c, _):
        lanes = pl.ds(pl.multiple_of(c * CHAN, CHAN), CHAN)
        zero = jnp.zeros((TILE, CHAN), F32)

        def body(step, sums):
            start = pl.multiple_of(step * 2 * GAP + GAP, TILE)
            lower = padded_grad[c, pl.ds(start, GAP), :]
            upper = padded_grad[c, pl.ds(start + GAP, GAP), :]
            both = lower + upper
            new = list(sums)
            for j in range(GAP):
                row = start + j - half
                shared = fold(both * padded[c, pl.ds(row + GAP, GAP), :])
                new[j] = new[j] + (fold(lower * steps_ref[c, pl.ds(row, GAP), :]) + shared)
                if j + GAP < taps:
                    rest = fold(upper * steps_ref[c, pl.ds(row + GAP, GAP), :])
                    new[j + GAP] = new[j + GAP] + (shared - rest)
            return tuple(new)

        sums = lax.fori_loop(0, pairs, body, (zero,) * taps)
        for j in range(taps):
            out[pl.ds(j, 1), lanes] = row_sum(sums[j])
        return 0

    lax.fori_loop(0, blocks, block, 0)


def front_forward_kernel(
    info, x_ref, gain, valid, up, up_two, down, down_two, out, before_out, stat, low, total
):
    h = pl.program_id(0)
    mine = info[0]
    up_value = join_rows(up[...], up_two[...], mine)
    down_value = pick_rows(down[...], down_two[...], h % 2 == mine)

    @pl.when(h == 0)
    def _():
        normal, _ = normalize(x_ref[...].astype(F32))
        low[...] = (normal * gain[...]).astype(LOW)
        total[...] = jnp.zeros_like(total)

    before = dot(low[...], up_value)
    before_out[...] = before
    total[...] += dot(silu(before).astype(LOW), down_value)

    @pl.when(h == pl.num_programs(0) - 1)
    def _():
        x = x_ref[...].astype(F32)
        part = 0.5 * total[...]
        after = x + part
        out[...] = after
        v = valid[...]
        stat[0:1, :] = row_sum(x * x * v)
        stat[1:2, :] = row_sum(after * after * v)
        stat[2:3, :] = row_sum(part * part * v)
        stat[3:, :] = jnp.zeros((5, WIDTH), F32)


def head_masks(segs_col, segs_row):
    return segs_col == segs_row


def head_half(head):
    lane = lax.broadcasted_iota(jnp.int32, (1, CHAN), 1)
    return lane // (CHAN // 2) == lax.rem(head, 2)


def head_probs(query, key, allowed, scale):
    scores = jnp.where(allowed, dot_nt(query, key) * scale, NEGATIVE)
    exponent = jnp.exp(scores - jnp.max(scores, axis=-1, keepdims=True))
    return exponent / jnp.sum(exponent, axis=-1, keepdims=True)


def heads_forward(
    info, low, segs_col, segs_row, w_in, w_in_two, w_out, w_out_two, attended, packed, mixed,
):
    mine = info[0]
    scale = (WIDTH // HEADS) ** -0.5
    for q in range(3):
        rows = slice(16 * q, 16 * (q + 1))
        weight = join_rows(w_in[:, :, rows, :], w_in_two[:, :, rows, :], mine)
        packed[:, WIDTH * q : WIDTH * (q + 1)] = dot(low, weight).astype(LOW)
    allowed = head_masks(segs_col[...], segs_row[...])

    def one(head, _):
        half = head_half(head)
        start = CHAN * (head // 2)
        lanes = [pl.ds(pl.multiple_of(WIDTH * q + start, CHAN), CHAN) for q in range(3)]
        query, key, value = (packed[:, lane] for lane in lanes)
        probs = head_probs(jnp.where(half, query, 0), key, allowed, scale)
        part = dot(probs.astype(LOW), value).astype(LOW)
        mixed[:, lanes[0]] = jnp.where(half, part, mixed[:, lanes[0]])
        return 0

    lax.fori_loop(0, HEADS, one, 0)
    attended[...] = dot(mixed[...], join_rows(w_out[...], w_out_two[...], mine))


def heads_backward(
    info, grad, x_ref, gain, segs_col, segs_row, packed, mixed, w_in, w_in_two, w_out, w_out_two,
    stream, gain_grad, send, keep, mixed_grad, packed_grad, low,
):
    scale = (WIDTH // HEADS) ** -0.5
    mine = info[0]
    attended_low = grad[...].astype(LOW)
    store_halves(dot_tn(mixed[...], attended_low), send, keep, mine, 16, 144)
    mixed_grad[...] = dot_nt(attended_low, join_rows(w_out[...], w_out_two[...], mine)).astype(LOW)
    normal, inverse = normalize(x_ref[...])
    low[...] = (normal * gain[...]).astype(LOW)
    allowed = head_masks(segs_col[...], segs_row[...])

    def one(head, _):
        half = head_half(head)
        start = CHAN * (head // 2)
        lanes = [pl.ds(pl.multiple_of(WIDTH * q + start, CHAN), CHAN) for q in range(3)]
        query, key, value = (packed[:, lane] for lane in lanes)
        upstream = mixed_grad[:, lanes[0]]
        probs = head_probs(jnp.where(half, query, 0), key, allowed, scale)
        probs_grad = dot_nt(jnp.where(half, upstream, 0), value)
        value_grad = dot_tn(probs.astype(LOW), upstream)
        inner = jnp.sum(probs_grad * probs, axis=-1, keepdims=True)
        score_grad = (probs * (probs_grad - inner)).astype(LOW)
        query_grad = dot(score_grad, key) * scale
        key_grad = dot_tn(score_grad, query) * scale
        for lane, part in zip(lanes, (query_grad, key_grad, value_grad)):
            packed_grad[:, lane] = jnp.where(half, part.astype(LOW), packed_grad[:, lane])
        return 0

    lax.fori_loop(0, HEADS, one, 0)
    total = jnp.zeros(x_ref.shape, F32)
    for q in range(3):
        rows = slice(16 * q, 16 * (q + 1))
        weight = join_rows(w_in[:, :, rows, :], w_in_two[:, :, rows, :], mine)
        piece = packed_grad[:, WIDTH * q : WIDTH * (q + 1)]
        store_halves(dot_tn(low[...], piece), send, keep, mine, 16, 96 + 16 * q)
        total += dot_nt(piece, weight)
    gain_grad[...] = row_sum(total * normal)
    stream[...] = normalize_back(total, gain[...], normal, inverse)


def branches_forward_kernel(
    info, x_ref, heads_gain, segs_col, segs_row, w_heads, w_heads_two, w_mix, w_mix_two,
    gain, gate_gain, taps_ref, w_in, w_in_two, w_out, w_out_two, attended, packed, mixed,
    gated, before_out, normal_out, inverse_out, part_out, product,
    low, act, padded, conv, steps_ref, sums, *, segments, taps,
):
    j = pl.program_id(0)
    thirds = WIDTH * 3

    @pl.when(j == 0)
    def _():
        normal, _ = normalize(x_ref[...])
        low[...] = (normal * gain[...]).astype(LOW)
        heads_forward(
            info, (normal * heads_gain[...]).astype(LOW), segs_col, segs_row, w_heads,
            w_heads_two, w_mix, w_mix_two, attended, packed, mixed,
        )

    before = dot(low[...], join_rows(w_in[...], w_in_two[...], info[0]))
    before_out[...] = before
    value = gelu(before)

    @pl.when(j < 3)
    def _():
        act[:, pl.ds(pl.multiple_of(j * WIDTH, WIDTH), WIDTH)] = value

    @pl.when(j == 2)
    def _():
        def scale(span):
            normal, inverse = normalize(act[span, :])
            normal_out[span, :] = normal
            inverse_out[span, :] = inverse
            act[span, :] = normal * gate_gain[...]

        by_rows(act.shape[0], scale)
        blocks = thirds // CHAN
        spread(act, padded, info, segments, blocks)
        conv_rows(padded, taps_ref, conv, steps_ref, sums, blocks, taps, False)
        unspread(conv, part_out, info, segments, blocks)

    @pl.when(j >= 3)
    def _():
        lanes = pl.ds(pl.multiple_of((j - 3) * WIDTH, WIDTH), WIDTH)
        product[:, lanes] = (value * part_out[:, lanes]).astype(LOW)

    @pl.when(j == 5)
    def _():
        gated[...] = dot(product[...], join_rows(w_out[...], w_out_two[...], info[0]))


def branches_backward_kernel(
    info, attended_grad, x_ref, heads_gain, segs_col, segs_row, packed, mixed, w_heads,
    w_heads_two, w_mix, w_mix_two, grad, gain, before, part, product, w_in, w_in_two, w_out,
    w_out_two,
    stream, heads_gain_grad, part_grad, total_out, send, keep, low, product_grad, gated_low,
    mixed_grad, packed_grad,
):
    j = pl.program_id(0)
    mine = info[0]

    @pl.when(j == 0)
    def _():
        heads_backward(
            info, attended_grad, x_ref, heads_gain, segs_col, segs_row, packed, mixed, w_heads,
            w_heads_two, w_mix, w_mix_two, stream, heads_gain_grad, send, keep, mixed_grad,
            packed_grad, low,
        )
        normal, _ = normalize(x_ref[...])
        low[...] = (normal * gain[...]).astype(LOW)
        total_out[...] = jnp.zeros_like(total_out)
        gated_low[...] = grad[...].astype(LOW)
        store_halves(dot_tn(product[...], gated_low[...]), send, keep, mine, 48, 48)
        product_grad[...] = dot_nt(gated_low[...], join_rows(w_out[...], w_out_two[...], mine))

    value, slope = gelu_pair(before[...])
    lanes = pl.ds(pl.multiple_of(j * WIDTH, WIDTH), WIDTH)
    upstream = product_grad[:, lanes]
    part_grad[...] = upstream * value
    before_grad = (upstream * part[...] * slope).astype(LOW)
    store_halves(
        dot_tn(low[...], before_grad), send, keep, mine, 16, pl.multiple_of(j * 16, 16)
    )
    total_out[...] += dot_nt(before_grad, join_rows(w_in[...], w_in_two[...], mine))


def gated_conv(
    info, part_grad, normal_ref, inverse_ref, gate_gain, taps_ref,
    gate_gain_grad, taps_grad, padded, padded_grad, conv, work, steps_ref, sums, segments, taps,
):
    blocks = 3 * WIDTH // CHAN
    spread(part_grad, padded_grad, info, segments, blocks)
    work[...] = normal_ref[...] * gate_gain[...]
    spread(work, padded, info, segments, blocks)
    rows = padded.shape[1]

    def differ(c, _):
        steps_ref[c, 0 : rows - GAP, :] = padded[c, 0 : rows - GAP, :] - padded[c, GAP:rows, :]
        return 0

    lax.fori_loop(0, blocks, differ, 0)
    conv_taps(padded_grad, padded, steps_ref, taps_grad, blocks, taps)
    conv_rows(padded_grad, taps_ref, conv, steps_ref, sums, blocks, taps, True)
    unspread(conv, work, info, segments, blocks)
    upstream = work[...]
    normal = normal_ref[...]
    gate_gain_grad[...] = row_sum(upstream * normal)
    work[...] = normalize_back(upstream, gate_gain[...], normal, inverse_ref[...])


def gated_gate_kernel(
    info, part_grad, normal_ref, inverse_ref, gate_gain, taps_ref, x_ref, gain, before, total_in,
    w_in, w_in_two,
    stream, gain_grad, gate_gain_grad, taps_grad, send, keep,
    low, total, padded, padded_grad, conv, work, steps_ref, sums, *, segments, taps,
):
    j = pl.program_id(0)
    mine = info[0]

    @pl.when(j == 0)
    def _():
        gated_conv(
            info, part_grad, normal_ref, inverse_ref, gate_gain, taps_ref, gate_gain_grad,
            taps_grad, padded, padded_grad, conv, work, steps_ref, sums, segments, taps,
        )
        normal, _ = normalize(x_ref[...])
        low[...] = (normal * gain[...]).astype(LOW)
        total[...] = total_in[...]

    _, slope = gelu_pair(before[...])
    before_grad = (work[part_of(j)] * slope).astype(LOW)
    store_halves(
        dot_tn(low[...], before_grad), send, keep, mine, 16, pl.multiple_of(j * 16, 16)
    )
    total[...] += dot_nt(before_grad, join_rows(w_in[...], w_in_two[...], mine))

    @pl.when(j == 2)
    def _():
        normal, inverse = normalize(x_ref[...])
        gain_grad[...] = row_sum(total[...] * normal)
        stream[...] = normalize_back(total[...], gain[...], normal, inverse)


def conv_add(padded, conv, taps_ref, steps_ref, sums, blocks, taps, flip):
    conv_rows(padded, taps_ref, conv, steps_ref, sums, blocks, taps, flip)
    def one(c, _):
        conv[c] += padded[c]
        return 0

    lax.fori_loop(0, blocks, one, 0)


def hidden_back(x, mine, before, part_low, down, send, keep, start):
    gate = jax.nn.sigmoid(before)
    hidden = (before * gate).astype(LOW)
    hidden_grad = dot_nt(part_low, down)
    before_grad = (hidden_grad * (gate * (1.0 + before * (1.0 - gate)))).astype(LOW)
    down_grad = dot_tn(hidden, part_low).astype(LOW).reshape(2, 8, 64, WIDTH)

    @pl.when(mine == 0)
    def _():
        keep[x, :, start : start + 64, :] = down_grad[0]
        send[x, :, start : start + 64, :] = down_grad[1]

    @pl.when(mine == 1)
    def _():
        keep[x, :, start : start + 64, :] = down_grad[1]
        send[x, :, start : start + 64, :] = down_grad[0]

    return before_grad


def merge_rear_kernel(
    info, x_ref, attended, gated, taps_ref, weight, weight_two, gain, final_gain, valid, cotangent,
    up, up_two, down, down_two,
    encoded, stream, gain_grad, final_gain_grad, stat, attended_grad, gated_grad, taps_grad,
    send, keep, merge_send, merge_keep,
    low, before, part_grad, stream_grad, total, middle, joined, joined_low, padded, padded_grad,
    conv, steps_ref, sums, *, segments, taps,
):
    step = pl.program_id(0)
    h = jnp.where(step < 2, step, 3 - step)
    up_value = join_columns(up[...], up_two[...], info[0])
    down_value = join_lines(down[...], down_two[...], info[0])
    blocks = 2 * WIDTH // CHAN

    @pl.when(step == 0)
    def _():
        joined[:, :WIDTH] = attended[...]
        joined[:, WIDTH:] = gated[...]
        spread(joined, padded, info, segments, blocks)
        conv_add(padded, conv, taps_ref, steps_ref, sums, blocks, taps, False)
        unspread(conv, joined, info, segments, blocks)
        joined_low[...] = joined[...].astype(LOW)
        part = dot(joined_low[...], join_rows(weight[...], weight_two[...], info[0]))
        after = x_ref[...] + part
        middle[...] = after
        v = valid[...]
        stat[0:1, :] = row_sum(after * after * v)
        stat[1:2, :] = row_sum(part * part * v)
        normal, _ = normalize(after)
        low[...] = (normal * gain[...]).astype(LOW)
        total[...] = jnp.zeros_like(total)

    @pl.when(step < 2)
    def _():
        value = dot(low[...], up_value)
        before[step] = value
        total[...] += dot(silu(value).astype(LOW), down_value)

    @pl.when(step == 1)
    def _():
        part = 0.5 * total[...]
        after = middle[...] + part
        v = valid[...]
        stat[2:3, :] = row_sum(after * after * v)
        stat[3:4, :] = row_sum(part * part * v)
        stat[4:, :] = jnp.zeros((4, WIDTH), F32)
        normal, inverse = normalize(after)
        encoded[...] = (normal * final_gain[...] * v).astype(LOW)
        upstream = cotangent[...].astype(F32) * v
        final_gain_grad[...] = row_sum(upstream * normal)
        grad = normalize_back(upstream, final_gain[...], normal, inverse)
        stream_grad[...] = grad
        part_grad[...] = (0.5 * grad).astype(LOW)
        total[...] = jnp.zeros_like(total)

    @pl.when(step >= 2)
    def _():
        before_grad = hidden_back(
            h, info[0], before[h], part_grad[...], down_value, send, keep, 64
        )
        store_columns(
            dot_tn(low[...], before_grad), send, keep, info[0], pl.multiple_of(h * 32, 32)
        )
        total[...] += dot_nt(before_grad, up_value)

    @pl.when(step == 3)
    def _():
        normal, inverse = normalize(middle[...])
        gain_grad[...] = row_sum(total[...] * normal)
        grad = stream_grad[...] + normalize_back(total[...], gain[...], normal, inverse)
        stream[...] = grad
        grad_low = grad.astype(LOW)
        store_halves(dot_tn(joined_low[...], grad_low), merge_send, merge_keep, info[0], 32, 0)
        joined[...] = dot_nt(grad_low, join_rows(weight[...], weight_two[...], info[0]))
        spread(joined, padded_grad, info, segments, blocks)
        conv_taps(padded_grad, padded, steps_ref, taps_grad, blocks, taps)
        conv_add(padded_grad, conv, taps_ref, steps_ref, sums, blocks, taps, True)
        unspread(conv, joined, info, segments, blocks)
        attended_grad[...] = joined[:, :WIDTH]
        gated_grad[...] = joined[:, WIDTH:]


def front_hidden_kernel(
    info, grad, heads_stream, gated_stream, before, down, down_two,
    stream_out, before_grad, send, keep, part_grad,
):
    h = pl.program_id(0)

    @pl.when(h == 0)
    def _():
        stream_sum = grad[...] + heads_stream[...] + gated_stream[...]
        stream_out[...] = stream_sum
        part_grad[...] = (0.5 * stream_sum).astype(LOW)

    down_value = join_lines(down[...], down_two[...], info[0])
    before_grad[...] = hidden_back(
        h, info[0], before[...], part_grad[...], down_value, send, keep, 0
    )


def front_input_kernel(
    info, stream_grad, before_grad, x_ref, gain, up, up_two,
    x_grad, send, keep, low, total,
):
    h = pl.program_id(0)

    @pl.when(h == 0)
    def _():
        normal, _ = normalize(x_ref[...].astype(F32))
        low[...] = (normal * gain[...]).astype(LOW)
        total[...] = jnp.zeros_like(total)

    store_columns(
        dot_tn(low[...], before_grad[...]), send, keep, info[0], pl.multiple_of(h * 32, 32)
    )
    total[...] += dot_nt(before_grad[...], join_columns(up[...], up_two[...], info[0]))

    @pl.when(h == 1)
    def _():
        normal, inverse = normalize(x_ref[...].astype(F32))
        gain_grad = row_sum(total[...] * normal).astype(LOW)
        gain_rows = jnp.broadcast_to(gain_grad.reshape(1, 1, 1, WIDTH), (2, 8, 16, WIDTH))
        send[:, :, 64:80, :] = gain_rows
        keep[:, :, 64:80, :] = gain_rows
        x_grad[...] = (
            stream_grad[...] + normalize_back(total[...], gain[...], normal, inverse)
        ).astype(LOW)


def whole(shape):
    return pl.BlockSpec(shape, lambda *_: (0,) * len(shape))


def call(kernel, grid, inputs, outputs, scratch, info, flops=0, after=(), room=56):
    in_specs = [
        whole(array.shape) if block is None else pl.BlockSpec(block, index)
        for array, block, index in inputs
    ]
    out_specs = [
        whole(shape) if block is None else pl.BlockSpec(block, index)
        for shape, _, block, index in outputs
    ]
    arrays = [array for array, _, _ in inputs]
    shapes = [jax.ShapeDtypeStruct(shape, kind) for shape, kind, _, _ in outputs]
    moved = sum(array.size * array.dtype.itemsize for array in arrays)
    moved = sum(shape.size * shape.dtype.itemsize for shape in shapes) + min(moved, 1 << 24)
    skipped = len(after)
    name = getattr(kernel, "func", kernel).__name__

    def body(info_ref, *refs):
        kernel(info_ref, *refs[skipped:])

    return pl.pallas_call(
        body,
        grid_spec=pltpu.PrefetchScalarGridSpec(
            num_scalar_prefetch=1,
            grid=grid,
            in_specs=[pl.BlockSpec(memory_space=pl.ANY)] * skipped + in_specs,
            out_specs=out_specs,
            scratch_shapes=scratch,
        ),
        out_shape=shapes,
        name=name,
        compiler_params=pltpu.CompilerParams(vmem_limit_bytes=room * 1024 * 1024),
        cost_estimate=pl.CostEstimate(flops=flops, bytes_accessed=moved, transcendentals=0),
    )(info, *after, *arrays)


def segment_table(lengths, spots, row_count):
    ends = jnp.cumsum(lengths)
    position = jnp.arange(row_count, dtype=jnp.int32)
    segments = jnp.sum((position[None, :] >= ends[:, None]).astype(jnp.int32), axis=0)
    zero = jnp.zeros((1,), jnp.int32)
    last = jnp.full((1,), row_count, jnp.int32)
    return segments, jnp.concatenate([spots, zero, ends, ends, last]).astype(jnp.int32)


def all_of(*arrays):
    return [(array, None, None) for array in arrays]


def plain(*shapes_and_types):
    return [(shape, kind, None, None) for shape, kind in shapes_and_types]


def halves(rows):
    return plain(((2, 8, rows, WIDTH), LOW)) * 2


def columns(pair, rows, start, index):
    block = (4, 4, rows, WIDTH), lambda *i: (0, 0, start // rows + index(*i), 0)
    return [(array, *block) for array in pair]


def lines(pair, index, steps=2):
    block = (2, 4, 64, WIDTH), lambda *i: (index(*i) // steps, 0, 1, 0)
    return [(array, *block) for array in pair]


def first(*_):
    return 0


def step(h, _):
    return h


class Layer:
    def __init__(self, features, cotangent, lengths, spots, taps):
        self.features, self.cotangent, self.taps = features, cotangent, taps
        self.tokens = features.shape[0]
        self.count = lengths.shape[0]
        self.segments = self.count + 1
        seg_ids, self.info = segment_table(lengths, spots, self.tokens)
        self.segs_col, self.segs_row = seg_ids[:, None], seg_ids[None, :]
        self.valid = (self.segs_col < self.count).astype(F32)
        self.stream = ((self.tokens, WIDTH), F32)
        self.low = pltpu.VMEM((self.tokens, WIDTH), LOW)
        self.wide = pltpu.VMEM((self.tokens, WIDTH), F32)
        rows = self.tokens + GAP * (self.segments - 1)
        self.spread_rows = -(-rows // (4 * GAP)) * 4 * GAP + 2 * GAP
        self.conv = dict(segments=self.segments, taps=taps)
        self.stat = ((8, WIDTH), F32)
        self.vector = ((1, WIDTH), F32)
        self.flop = 2 * self.tokens * WIDTH * WIDTH

    def set_small(self, smaller):
        (
            self.gate_taps, self.merge_taps, self.front_gain, self.heads_gain, self.gated_gain,
            self.gate_gain, self.rear_gain, self.final_gain,
        ) = smaller

    def padded(self, width):
        return pltpu.VMEM((width // CHAN, self.spread_rows, CHAN), F32)

    def tall(self, width, kind=F32):
        return ((self.tokens, width), kind)

    def by_column(self, array, start=0):
        return [(array, (self.tokens, WIDTH), lambda j, _: (0, j + start))]

    def by_pair(self, array):
        return [(array, (self.tokens, 2 * WIDTH), lambda j, _: (0, j))]

    def front_forward(self, front, after=()):
        self.front = front
        self.after_front, self.front_before, self.front_stat = call(
            front_forward_kernel,
            (4,),
            all_of(self.features, self.front_gain, self.valid)
            + columns(front, 16, 0, step)
            + lines(front, step),
            plain(self.stream)
            + [(*self.tall(4 * WIDTH), (self.tokens, WIDTH), lambda h, _: (0, h))]
            + plain(self.stat),
            [self.low, self.wide],
            self.info,
            8 * self.flop,
            after,
        )
        return self.front_stat

    def branches_forward(self, middle, after=()):
        self.middle = middle
        self.heads = columns(middle, 48, 144, first) + columns(middle, 16, 192, first)
        (
            self.attended, self.packed, self.mixed, self.gated, self.gated_before,
            self.gate_normal, self.gate_inverse, self.gate_part, self.product,
        ) = call(
            functools.partial(branches_forward_kernel, **self.conv),
            (6,),
            all_of(self.after_front, self.heads_gain, self.segs_col, self.segs_row)
            + self.heads
            + all_of(self.gated_gain, self.gate_gain, self.gate_taps)
            + columns(middle, 16, 0, lambda j, _: (j + 3) % 6)
            + columns(middle, 48, 96, first),
            plain(self.stream, self.tall(3 * WIDTH, LOW), self.tall(WIDTH, LOW), self.stream)
            + [(*self.tall(6 * WIDTH), (self.tokens, WIDTH), lambda j, _: (0, (j + 3) % 6))]
            + plain(
                self.tall(3 * WIDTH), self.tall(1), self.tall(3 * WIDTH), self.tall(3 * WIDTH, LOW)
            ),
            [self.low, pltpu.VMEM((self.tokens, 3 * WIDTH), F32)]
            + [self.padded(3 * WIDTH)] * 3
            + [pltpu.VMEM((GAP, 3 * WIDTH), F32)],
            self.info,
            52 * self.flop,
            after,
        )
        return self.gate_inverse

    def merge_rear(self, rear, after=()):
        def bounce(i, _):
            return jnp.where(i < 2, i, 3 - i)

        padded = self.padded(2 * WIDTH)
        (
            self.encoded, self.merge_grad, self.rear_gain_grad, self.final_gain_grad,
            self.rear_stat, self.attended_grad, self.gated_grad, self.merge_taps_grad, *pair,
        ) = call(
            functools.partial(merge_rear_kernel, **self.conv),
            (4,),
            all_of(self.after_front, self.attended, self.gated, self.merge_taps)
            + columns(rear, 32, 128, first)
            + all_of(self.rear_gain, self.final_gain, self.valid, self.cotangent)
            + columns(rear, 32, 0, bounce)
            + lines(rear, bounce, 1),
            plain(
                self.tall(WIDTH, LOW), self.stream, self.vector, self.vector, self.stat,
                self.stream, self.stream, ((self.taps + 1, 2 * WIDTH), F32),
            )
            + halves(128)
            + halves(32),
            [
                self.low, pltpu.VMEM((2, self.tokens, 2 * WIDTH), F32), self.low, self.wide, self.wide,
                self.wide, pltpu.VMEM((self.tokens, 2 * WIDTH), F32),
                pltpu.VMEM((self.tokens, 2 * WIDTH), LOW), padded, padded, padded, padded,
                pltpu.VMEM((GAP, 2 * WIDTH), F32),
            ],
            self.info,
            80 * self.flop,
            after,
        )
        return pair

    def branches_backward(self, after=()):
        self.heads_stream, self.heads_gain_grad, self.part_grad, self.gated_total, *pair = call(
            branches_backward_kernel,
            (3,),
            all_of(
                self.attended_grad, self.after_front, self.heads_gain, self.segs_col,
                self.segs_row, self.packed, self.mixed,
            )
            + self.heads
            + all_of(self.gated_grad, self.gated_gain)
            + self.by_column(self.gated_before)
            + self.by_column(self.gate_part)
            + all_of(self.product)
            + columns(self.middle, 16, 0, step)
            + columns(self.middle, 48, 96, first),
            plain(self.stream, self.vector)
            + [(*self.tall(3 * WIDTH), (self.tokens, WIDTH), lambda j, _: (0, j))]
            + plain(self.stream)
            + halves(160),
            [
                self.low, pltpu.VMEM((self.tokens, 3 * WIDTH), F32), self.low, self.low,
                pltpu.VMEM((self.tokens, 3 * WIDTH), LOW),
            ],
            self.info,
            40 * self.flop,
            after,
        )
        return pair

    def gated_gate(self, after=()):
        padded = self.padded(3 * WIDTH)
        (
            self.gated_stream, self.gated_gain_grad, self.gate_gain_grad, self.gate_taps_grad,
            *pair,
        ) = call(
            functools.partial(gated_gate_kernel, **self.conv),
            (3,),
            all_of(
                self.part_grad, self.gate_normal, self.gate_inverse, self.gate_gain,
                self.gate_taps, self.after_front, self.gated_gain,
            )
            + self.by_column(self.gated_before, 3)
            + all_of(self.gated_total)
            + columns(self.middle, 16, 0, lambda j, _: j + 3),
            plain(
                self.stream, self.vector, ((1, 3 * WIDTH), F32),
                ((self.taps + 1, 3 * WIDTH), F32),
            )
            + halves(48),
            [
                self.low, self.wide, padded, padded, padded,
                pltpu.VMEM((self.tokens, 3 * WIDTH), F32), padded,
                pltpu.VMEM((GAP, 3 * WIDTH), F32),
            ],
            self.info,
            48 * self.flop,
            after,
        )
        return pair

    def front_hidden(self, after=()):
        self.front_grad, self.front_before_grad, *pair = call(
            front_hidden_kernel,
            (2,),
            all_of(self.merge_grad, self.heads_stream, self.gated_stream)
            + self.by_pair(self.front_before)
            + lines(self.front, step, 1),
            plain(self.stream)
            + [(*self.tall(4 * WIDTH, LOW), (self.tokens, 2 * WIDTH), lambda h, _: (0, h))]
            + halves(64),
            [self.low],
            self.info,
            12 * self.flop,
            after,
        )
        return pair

    def front_input(self, after=()):
        self.features_grad, *pair = call(
            front_input_kernel,
            (2,),
            all_of(self.front_grad)
            + self.by_pair(self.front_before_grad)
            + all_of(self.features, self.front_gain)
            + columns(self.front, 32, 0, step),
            plain(self.tall(WIDTH, LOW)) + halves(80),
            [self.low, self.wide],
            self.info,
            12 * self.flop,
            after,
        )
        return pair

    def small_grads(self):
        return (
            self.gate_taps_grad, self.merge_taps_grad, self.heads_gain_grad,
            self.gated_gain_grad, self.rear_gain_grad, self.final_gain_grad, self.gate_gain_grad,
        )

    def stats(self):
        return self.front_stat, self.rear_stat


SMALL = 16
STATS = 8


def ring(size, shift):
    return [(i, (i + shift) % size) for i in range(size)]


def pack_kernel(
    info, front_up, front_down, heads_in, heads_out, gated_in, gated_out, merge_out, rear_up,
    rear_down, gate_taps, merge_taps, front_gain, heads_gain, gated_gain, rear_gain, final_gain,
    gate_gain, front, middle, rear, small,
):
    def put(target, start, source):
        rows, width = source.shape
        for q in range(width // WIDTH):
            target[start + rows * q : start + rows * (q + 1), :] = source[
                :, WIDTH * q : WIDTH * (q + 1)
            ]

    put(front, 0, front_up)
    put(front, 64, front_down)
    put(middle, 0, gated_in)
    put(middle, 96, gated_out)
    put(middle, 144, heads_in)
    put(middle, 192, heads_out)
    put(rear, 0, rear_up)
    put(rear, 64, rear_down)
    put(rear, 128, merge_out)
    small[...] = jnp.zeros_like(small)
    for q, source in ((0, gate_taps), (2, merge_taps)):
        value = source[...].astype(F32)
        taps, width = value.shape
        small[0:SMALL, CHAN * q : CHAN * q + width] = value[:SMALL]
        small[0 : taps - SMALL, CHAN * (q + 1) : CHAN * (q + 1) + width] = value[SMALL:]
    start = CHAN
    for source in (front_gain, heads_gain, gated_gain, rear_gain, final_gain, gate_gain):
        width = source.shape[1]
        small[SMALL - 1 :, start : start + width] = source[...].astype(F32)
        start += width
    front[128 : 128 + SMALL, :] = small[...].astype(LOW)


def copy_all(copies):
    for copy in copies:
        copy.start()
    for copy in copies:
        copy.wait()


def place_line_kernel(info, *refs):
    pieces, out, sem = refs[:4], refs[4], refs[5]
    copy_all(
        [
            pltpu.make_async_copy(piece, out.at[chip, info[PLACE + i]], sem.at[chip, i])
            for chip in range(4)
            for i, piece in enumerate(pieces)
        ]
    )


def place(kernel, pieces, rows, info, after=()):
    skipped = len(after)

    def body(info_ref, *refs):
        kernel(info_ref, *refs[skipped:])

    anywhere = pl.BlockSpec(memory_space=pl.ANY)
    return pl.pallas_call(
        body,
        grid_spec=pltpu.PrefetchScalarGridSpec(
            num_scalar_prefetch=1,
            grid=(1,),
            in_specs=[anywhere] * skipped + [pl.BlockSpec(memory_space=pltpu.VMEM)] * 4,
            out_specs=anywhere,
            scratch_shapes=[pltpu.SemaphoreType.DMA((4, 4))],
        ),
        out_shape=jax.ShapeDtypeStruct((4, 4, rows, WIDTH), LOW),
        name=kernel.__name__,
        compiler_params=pltpu.CompilerParams(vmem_limit_bytes=16 * 1024 * 1024),
        cost_estimate=pl.CostEstimate(
            flops=0, bytes_accessed=32 * rows * WIDTH * 2, transcendentals=0
        ),
    )(info, *after, *pieces)


def line_sends(array):
    return [lax.ppermute(array, "z", ring(4, d)) for d in (1, 2, 3)]


def plane_exchange(array):
    return lax.all_to_all(array, ("x", "y"), 0, 0, tiled=True)


def core_swap(array):
    return lax.ppermute(array, "k", ring(2, 1))


def tie(array, *others):
    return lax.optimization_barrier((array, others))[0]


def unpack_kernel(info, first, second, gate_taps, merge_taps, gains, gate_gain):
    mine = info[0]
    lane = lax.broadcasted_iota(jnp.int32, (SMALL, CHAN), 1)
    lane_row = lane[:1]
    gate_gain[...] = jnp.zeros_like(gate_gain)
    gains[...] = jnp.zeros_like(gains)

    def put(target, rows, value, start, size, lanes):
        block, offset = start // CHAN, start % CHAN
        inside = jnp.logical_and(lanes >= offset, lanes < offset + size)
        window = slice(CHAN * block, CHAN * (block + 1))
        target[rows, window] = jnp.where(inside, value, target[rows, window])
        spill = offset + size - CHAN
        if spill > 0:
            window = slice(CHAN * (block + 1), CHAN * (block + 2))
            target[rows, window] = jnp.where(lanes < spill, value, target[rows, window])

    for i in range(BLOCKS):
        x, core, rest = i // 16, (i // 8) % 2, i % 8
        chip, z = 2 * x + rest % 2, rest // 2
        value = jnp.where(mine == core, first[chip, z], second[chip, z]).astype(F32)
        quads = [value[:, CHAN * q : CHAN * (q + 1)] for q in range(4)]
        start = 48 * i
        for half in range(2):
            rows = slice(SMALL * half, SMALL * (half + 1))
            rolled = pltpu.roll(quads[half], start % CHAN, 1)
            put(gate_taps, rows, rolled, start, 48, lane)
            rolled = pltpu.roll(quads[2 + half], (32 * i) % CHAN, 1)
            put(merge_taps, rows, rolled, 32 * i, 32, lane)
        line = quads[1][SMALL - 1 :]
        for g in range(5):
            rolled = pltpu.roll(line, (16 * i - 16 * g) % CHAN, 1)
            put(gains, slice(g, g + 1), rolled, 16 * i, 16, lane_row)
        rolled = pltpu.roll(line, (48 * i - 80) % CHAN, 1)
        put(gate_gain, slice(0, 1), rolled, 48 * i, 48, lane_row)


def pack_small_kernel(
    info, gate_taps, merge_taps, heads_gain, gated_gain, rear_gain, final_gain, gate_gain,
    front_stat, rear_stat, send, keep, *, count_at,
):
    mine = info[0]
    lane = lax.broadcasted_iota(jnp.int32, (SMALL, CHAN), 1)
    lane_row = lane[:1]
    last = lax.broadcasted_iota(jnp.int32, (SMALL, CHAN), 0) == SMALL - 1
    stats = [
        front_stat[0:1, :], front_stat[1:2, :], rear_stat[0:1, :], rear_stat[2:3, :],
        front_stat[2:3, :], rear_stat[1:2, :], rear_stat[3:4, :],
    ]
    stat_line = jnp.where(lane_row == 7, info[count_at].astype(F32), 0.0)
    for i, stat in enumerate(stats):
        stat_line = jnp.where(lane_row == i, jnp.sum(stat, axis=1, keepdims=True), stat_line)
    rest = stat_line - stat_line.astype(LOW).astype(F32)
    stat_line += pltpu.roll(rest, STATS, 1)

    def take(source, rows, start, size, lanes):
        block, offset = start // CHAN, start % CHAN
        value = source[rows, CHAN * block : CHAN * (block + 1)]
        if offset:
            value = pltpu.roll(value, CHAN - offset, 1)
        if offset + size > CHAN:
            other = source[rows, CHAN * (block + 1) : CHAN * (block + 2)]
            value = jnp.where(lanes < CHAN - offset, value, pltpu.roll(other, CHAN - offset, 1))
        return value

    def quads_of(i):
        halves = [slice(0, SMALL), slice(SMALL, 2 * SMALL)]
        quads = [take(gate_taps, rows, 48 * i, 48, lane) for rows in halves]
        quads += [take(merge_taps, rows, 32 * i, 32, lane) for rows in halves]
        line = pltpu.roll(take(gate_gain, slice(0, 1), 48 * i, 48, lane_row), 80, 1)
        for g, gain in enumerate((heads_gain, gated_gain, rear_gain, final_gain)):
            start = 16 * (g + 1)
            block = gain[:, CHAN * (i // 8) : CHAN * (i // 8 + 1)]
            value = pltpu.roll(block, (start - 16 * i) % CHAN, 1)
            inside = jnp.logical_and(lane_row >= start, lane_row < start + 16)
            line = jnp.where(inside, value, line)
        quads[1] = jnp.where(last, line, quads[1])
        quads[3] = jnp.where(last, stat_line, quads[3])
        return quads

    for i in [*range(8), *range(16, 24)]:
        x, spot = i // 16, i % 8
        pairs = zip(quads_of(i), quads_of(i + 8))
        for q, (low, high) in enumerate(pairs):
            lanes = slice(CHAN * q, CHAN * (q + 1))
            keep[x, spot, :, lanes] = jnp.where(mine == 0, low, high).astype(LOW)
            send[x, spot, :, lanes] = jnp.where(mine == 0, high, low).astype(LOW)


def round_small(total):
    quad = total[:, 3 * CHAN :]
    lane = lax.broadcasted_iota(jnp.int32, quad.shape, 1)
    row = lax.broadcasted_iota(jnp.int32, quad.shape, 0)
    stat = jnp.logical_and(row == SMALL - 1, lane < STATS)
    rest = jnp.where(stat, quad - quad.astype(LOW).astype(F32), 0.0)
    quad = quad + pltpu.roll(rest, STATS, 1)
    return jnp.concatenate([total[:, : 3 * CHAN], quad], axis=1).astype(LOW)


def core_sum_kernel(info, *refs, sizes):
    inputs, out = refs[:-1], refs[-1]
    half = len(inputs) // 2
    keeps, gots = inputs[:half], inputs[half:]

    def one(z, _):
        for chip in range(4):
            x, spot = chip // 2, 2 * z + chip % 2
            start = 0
            for keep, got, (rows, small) in zip(keeps, gots, sizes):
                span = slice(start, start + rows)
                start += rows
                if small:
                    total = keep[x, spot].astype(F32) + got[x, spot].astype(F32)
                    out[chip, z, span, :] = round_small(total)
                else:
                    out[chip, z, span, :] = keep[x, spot] + got[x, spot]
        return 0

    lax.fori_loop(0, 4, one, 0)


def plane_sum_kernel(info, pieces, *outs, sizes):
    for e in range(4):
        zi = lax.rem(info[PLACE] + e, 4)
        start = 0
        for rows in sizes:
            small, rows = rows < 0, abs(rows)
            span = slice(start, start + rows)
            start += rows
            total = sum(pieces[chip, zi, span, :].astype(F32) for chip in range(4))
            if e == 0:
                outs[0][span, :] = total
            elif small:
                outs[e][span, :] = round_small(total)
            else:
                outs[e][span, :] = total.astype(LOW)


def line_sum_kernel(info, keep, one, two, three, *refs, pieces):
    refs = list(refs)
    start = 0
    for rows, what in pieces:
        span = slice(start, start + rows)
        start += rows
        total = keep[span, :]
        for piece in (one, two, three):
            total += piece[span, :].astype(F32)
        if what == "small":
            quads = [total[:, CHAN * q : CHAN * (q + 1)] for q in range(4)]
            gate_taps, merge_taps, heads_gain, gated_gain, rear_gain, final_gain, gate_gain, stats = refs
            gate_taps[0:SMALL, :] = quads[0][:, :48]
            gate_taps[SMALL : 2 * SMALL - 1, :] = quads[1][: SMALL - 1, :48]
            merge_taps[0:SMALL, :] = quads[2][:, :32]
            merge_taps[SMALL : 2 * SMALL - 1, :] = quads[3][: SMALL - 1, :32]
            line = quads[1][SMALL - 1 :, :]
            for g, target in enumerate((heads_gain, gated_gain, rear_gain, final_gain)):
                target[...] = pltpu.roll(line, CHAN - 16 * (g + 1), 1)[:, :16]
            gate_gain[...] = pltpu.roll(line, CHAN - 80, 1)[:, :48]
            line = quads[3][SMALL - 1 :, :]
            line += pltpu.roll(line, CHAN - STATS, 1)
            frames = jnp.sum(line[:, STATS - 1 : STATS])
            stats[...] = jnp.sqrt(line[:, : STATS - 1] / (frames * WIDTH))
        elif what == "gain":
            owner = info[OWNER]
            line = jnp.zeros((1, CHAN), F32)
            for b in range(WIDTH // CHAN):
                block = total[0:1, CHAN * b : CHAN * (b + 1)]
                line = jnp.where(owner // 8 == b, block, line)
            line = pltpu.roll(line, lax.rem(CHAN - 16 * lax.rem(owner, 8), CHAN), 1)
            refs.pop(0)[...] = line[:, :16]
        elif what == "left":
            given, target = refs.pop(0), refs[0]
            target[:, : given.shape[1]] = given[...]
        else:
            shift = 0
            if what == "right":
                target = refs.pop(0)
                shift = target.shape[1] // 2
            else:
                target = refs.pop(0)
            height = target.shape[0]
            for q in range(rows // height):
                lanes = slice(shift + WIDTH * q, shift + WIDTH * (q + 1))
                target[:, lanes] = total[height * q : height * (q + 1), :]


def run(tasks, info, after=()):
    counts = [(len(inputs), len(outputs)) for _, inputs, outputs in tasks]

    def tasks_kernel(info_ref, *refs):
        total = sum(count for count, _ in counts)
        ins, outs = list(refs[:total]), list(refs[total:])
        for (kernel, _, _), (taken, given) in zip(tasks, counts):
            kernel(info_ref, *ins[:taken], *outs[:given])
            del ins[:taken], outs[:given]

    results = call(
        tasks_kernel,
        (1,),
        all_of(*[array for _, inputs, _ in tasks for array in inputs]),
        plain(*[output for _, _, outputs in tasks for output in outputs]),
        [],
        info,
        after=after,
        room=24,
    )
    grouped = []
    for _, given in counts:
        grouped.append(results[:given])
        results = results[given:]
    return grouped


def core_sum(pairs):
    sizes = tuple((pair[0].shape[2], pair[0].shape[2] == SMALL) for pair in pairs)
    total = sum(rows for rows, _ in sizes)
    return (
        functools.partial(core_sum_kernel, sizes=sizes),
        [pair[i] for i in (0, 1) for pair in pairs],
        [((4, 4, total, WIDTH), LOW)],
    )


def plane_sum(pieces, sizes):
    total = pieces.shape[2]
    return (
        functools.partial(plane_sum_kernel, sizes=sizes),
        [pieces],
        [((total, WIDTH), F32)] + [((total, WIDTH), LOW)] * 3,
    )


def line_sum(sums, pieces, outputs, given=()):
    own, rest = sums
    return (
        functools.partial(line_sum_kernel, pieces=pieces),
        [own, *rest, *given],
        [(shape, F32) for shape in outputs],
    )


def line_swap(sums):
    return sums[0], [lax.ppermute(array, "z", ring(4, d)) for d, array in zip((1, 2, 3), sums[1:])]


def pack_small(layer, count):
    return (
        functools.partial(pack_small_kernel, count_at=SEG + 2 * count),
        [*layer.small_grads(), *layer.stats()],
        [((2, 8, SMALL, WIDTH), LOW)] * 2,
    )


def unpack_small(front, info):
    block = (4, 4, SMALL, WIDTH), lambda *_: (0, 0, 8, 0)
    gate_taps, merge_taps, gains, gate_full = call(
        unpack_kernel,
        (1,),
        [(array, *block) for array in front],
        plain(
            ((32, 3 * WIDTH), F32), ((32, 2 * WIDTH), F32), ((8, WIDTH), F32), ((1, 3 * WIDTH), F32)
        ),
        [],
        info,
    )
    lines = [gains[g : g + 1] for g in range(5)]
    return gate_taps, merge_taps, lines[0], lines[1], lines[2], gate_full, lines[3], lines[4]


def grid_device(
    features, cotangent, lengths, front_up, front_down, heads_input, heads_output, gated_input,
    gated_output, merge_output, rear_up, rear_down, gate_kernel, merge_kernel, front_gain,
    heads_gain, gated_gain, gate_gain, rear_gain, final_gain,
):
    x, k, z, y = (lax.axis_index(name) for name in ("x", "k", "z", "y"))
    places = [k] + [lax.rem(place, 4) for place in (z, z + 3, z + 2, z + 1)]
    places.append(((x * 2 + k) * 4 + z) * 2 + y)
    spots = jnp.stack([place.astype(jnp.int32) for place in places])
    layer = Layer(features, cotangent, lengths[0], spots, gate_kernel.shape[0])
    info = layer.info

    front, middle, rear = call(
        pack_kernel,
        (1,),
        all_of(
            front_up, front_down, heads_input, heads_output, gated_input, gated_output,
            merge_output, rear_up, rear_down, gate_kernel, merge_kernel,
            *[
                gain.reshape(1, -1)
                for gain in (front_gain, heads_gain, gated_gain, rear_gain, final_gain, gate_gain)
            ],
        ),
        plain(((144, WIDTH), LOW), ((208, WIDTH), LOW), ((160, WIDTH), LOW)),
        [pltpu.VMEM((SMALL, WIDTH), F32)],
        spots,
    )
    front_four = place(place_line_kernel, [front] + line_sends(front), 144, info)
    front = plane_exchange(front_four)
    middle = tie(middle, front_four)
    middle_four = place(place_line_kernel, [middle] + line_sends(middle), 208, info)
    front = tie(front, middle_four)
    middle = plane_exchange(tie(middle_four, front))
    rear = tie(rear, front)
    rear_lines = line_sends(rear)
    front = front, core_swap(front)
    layer.set_small(unpack_small(front, info))
    mark = layer.front_forward(front)
    rear_four = place(place_line_kernel, [rear] + rear_lines, 160, info, after=(mark,))
    middle = tie(middle, rear_four)
    rear = plane_exchange(tie(rear_four, middle))
    middle = middle, core_swap(middle)
    mark = layer.branches_forward(middle)
    rear = tie(rear, mark)
    rear = rear, core_swap(rear)

    send, rear_keep, merge_send, merge_keep = layer.merge_rear(rear)
    rear_got = core_swap(send)
    ((rear_four,),) = run([core_sum([(rear_keep, rear_got)])], info)
    merge_got = core_swap(tie(merge_send, rear_got))
    rear_plane = plane_exchange(rear_four)
    send, wide_keep = layer.branches_backward(after=(rear_four,))
    wide_got = core_swap(tie(send, rear_plane))
    (rear_sums,) = run([plane_sum(rear_plane, (128,))], info, after=(layer.gated_total,))
    ((wide_four,),) = run(
        [core_sum([(merge_keep, merge_got), (wide_keep, wide_got)])], info,
        after=(rear_sums[0],),
    )
    rear_sums = line_swap(rear_sums)
    wide_plane = plane_exchange(tie(wide_four, rear_plane))
    send, gate_keep = layer.gated_gate(after=(wide_four,))
    gate_got = core_swap(send)
    send, down_keep = layer.front_hidden(after=rear_sums[1])
    down_got = core_swap(tie(send, wide_plane))
    (wide_sums,) = run([plane_sum(wide_plane, (192,))], info, after=(layer.front_grad,))
    ((last_four,),) = run(
        [
            core_sum([(gate_keep, gate_got), (down_keep, down_got)]),
        ],
        info,
        after=(wide_sums[0],),
    )
    wide_sums = line_swap(wide_sums)
    last_plane = plane_exchange(tie(last_four, wide_plane))
    ((small_send, small_keep),) = run(
        [pack_small(layer, lengths.shape[1])], info, after=(last_four,)
    )
    small_got = core_swap(small_send)
    send, up_keep = layer.front_input(after=(small_send, *wide_sums[1]))
    up_got = core_swap(send)
    ((front_four,),) = run(
        [core_sum([(up_keep, up_got), (small_keep, small_got)])], info
    )
    half_shape = (gated_input.shape[0], gated_input.shape[1] // 2)
    front_plane = plane_exchange(tie(front_four, last_plane))
    (last_sums,) = run([plane_sum(last_plane, (112,))], info, after=(front_four,))
    last_sums = line_swap(last_sums)
    (
        (rear_up_grad, rear_down_grad),
        (
            merge_output_grad, gated_left_grad, gated_output_grad, heads_input_grad,
            heads_output_grad,
        ),
    ) = run(
        [
            line_sum(rear_sums, ((64, None), (64, None)), (rear_up.shape, rear_down.shape)),
            line_sum(
                wide_sums, ((32, None), (48, None), (48, None), (48, None), (16, None)),
                (
                    merge_output.shape, half_shape, gated_output.shape, heads_input.shape,
                    heads_output.shape,
                ),
            ),
        ],
        info,
        after=(last_sums[0],),
    )
    (front_sums,) = run(
        [plane_sum(front_plane, (80, -SMALL))], info, after=(last_sums[0], merge_output_grad)
    )
    front_sums = line_swap(front_sums)
    vector = (1, front_gain.shape[0])
    ((gated_input_grad, front_down_grad),) = run(
        [
            line_sum(
                last_sums,
                ((0, "left"), (48, "right"), (64, None)),
                (gated_input.shape, front_down.shape),
                given=(gated_left_grad,),
            ),
        ],
        info,
        after=(front_sums[0],),
    )
    (
        (
            front_up_grad, front_gain_grad, gate_kernel_grad, merge_kernel_grad,
            heads_gain_grad, gated_gain_grad, rear_gain_grad, final_gain_grad, gate_gain_grad,
            statistics,
        ),
    ) = run(
        [
            line_sum(
                front_sums,
                ((64, None), (16, "gain"), (16, "small")),
                (
                    front_up.shape, vector, gate_kernel.shape, merge_kernel.shape, vector,
                    vector, vector, vector, (1, gate_gain.shape[0]), (1, STATS - 1),
                ),
            ),
        ],
        info,
        after=(front_down_grad,),
    )
    return (
        layer.encoded, layer.features_grad, front_up_grad, front_down_grad, heads_input_grad,
        heads_output_grad, gated_input_grad, gated_output_grad, merge_output_grad, rear_up_grad,
        rear_down_grad, gate_kernel_grad, merge_kernel_grad, front_gain_grad[0],
        heads_gain_grad[0], gated_gain_grad[0], gate_gain_grad[0], rear_gain_grad[0],
        final_gain_grad[0], statistics[0],
    )


def pack_rows(shard):
    rows, columns = shard.shape
    pieces = shard.reshape(rows, columns // WIDTH, WIDTH).transpose(1, 0, 2)
    return pieces.reshape(rows * columns // WIDTH, WIDTH)


def pad_lines(flat):
    rows = -(-flat.shape[-1] // (WIDTH * 16)) * 16
    spare = [(0, 0)] * (flat.ndim - 1) + [(0, rows * WIDTH - flat.shape[-1])]
    return jnp.pad(flat, spare).reshape(flat.shape[:-1] + (rows, WIDTH))


def to_owners(weight):
    rows, columns = weight.shape
    pieces = weight.reshape(BLOCKS, rows // BLOCKS, columns // WIDTH, WIDTH)
    pieces = pieces.transpose(0, 2, 1, 3).reshape(2, 2, 4, 2, -1, WIDTH)
    pieces = pieces.transpose(1, 0, 3, 2, 4, 5)
    return pieces.reshape(2, 4, 4, -1, WIDTH)


def from_owners(halves, rows, columns):
    send, keep = halves
    pieces = jnp.stack([keep, send], axis=1)
    pieces = pieces.reshape(BLOCKS, columns // WIDTH, rows // BLOCKS, WIDTH)
    return pieces.transpose(0, 2, 1, 3).reshape(rows, columns)


def any_device(features, cotangent, lengths, *shards, axes):
    count = lax.axis_size(axes)
    matrices, smaller = shards[:9], shards[9:]
    packed = [pack_rows(element) for element in matrices]
    packed.append(pad_lines(jnp.concatenate([element.reshape(-1) for element in smaller])))
    gathered = lax.all_gather(jnp.concatenate(packed), axes, axis=0)
    weights = []
    start = 0
    for element, piece in zip(matrices, packed):
        rows, columns = element.shape
        window = gathered[:, start : start + piece.shape[0]]
        start += piece.shape[0]
        window = window.reshape(count, columns // WIDTH, rows, WIDTH).transpose(0, 2, 1, 3)
        weights.append(to_owners(window.reshape(count * rows, columns)))
    flat = gathered[:, start:].reshape(count, -1).astype(F32)
    lines = []
    start = 0
    for element in smaller:
        window = flat[:, start : start + element.size]
        start += element.size
        if element.ndim == 2:
            window = window.reshape((count,) + element.shape).transpose(1, 0, 2)
            window = window.reshape(element.shape[0], -1)
            lines.append(jnp.pad(window, ((0, 1), (0, 0))))
        else:
            lines.append(window.reshape(1, -1))
    up, down, h_in, h_out, g_in, g_out, m_out, r_up, r_down = weights

    def chunk(*members):
        return tuple(jnp.concatenate([member[i] for member in members], axis=2) for i in (0, 1))

    front = chunk(up, down)
    rear = chunk(r_up, r_down, m_out)
    layer = Layer(features, cotangent, lengths[0], jnp.zeros((SEG,), jnp.int32), smaller[0].shape[0])
    layer.set_small(lines)
    layer.front_forward(front)
    layer.branches_forward(chunk(g_in, g_out, h_in, h_out))
    rear = layer.merge_rear(rear)
    rear, merge = rear[:2], rear[2:]
    wide = layer.branches_backward()
    right = layer.gated_gate()
    front_down_halves = layer.front_hidden()
    front_up_halves = layer.front_input()

    def part(pair, start, stop):
        return tuple(array[:, :, start:stop] for array in pair)

    gated_halves = tuple(
        jnp.concatenate([one[:, :, :48], two], axis=2) for one, two in zip(wide, right)
    )
    ordered = (
        part(front_up_halves, 0, 64), front_down_halves, part(wide, 96, 144),
        part(wide, 144, 160), gated_halves, part(wide, 48, 96), merge,
        part(rear, 0, 64), part(rear, 64, 128),
    )
    front_gain = front_up_halves[1][0, 0, 64].astype(F32)
    small_grads = layer.small_grads()
    pieces = []
    for element, halves in zip(matrices, ordered):
        rows, columns = element.shape
        full = from_owners(halves, rows * count, columns)
        full = full.reshape(count, rows, columns // WIDTH, WIDTH).transpose(0, 2, 1, 3)
        pieces.append(full.reshape(count, -1, WIDTH))
    gate_taps, merge_taps, heads_gain, gated_gain, rear_gain, final_gain, gate_gain = small_grads
    small_full = (gate_taps, merge_taps, front_gain, heads_gain, gated_gain, gate_gain, rear_gain, final_gain)
    flat = []
    for element, full in zip(smaller, small_full):
        if element.ndim == 2:
            full = full[: element.shape[0]].reshape(element.shape[0], count, -1).transpose(1, 0, 2)
        flat.append(full.reshape(count, -1))
    pieces.append(pad_lines(jnp.concatenate(flat, axis=1).astype(LOW)))
    summed = lax.psum_scatter(jnp.concatenate(pieces, axis=1), axes, scatter_dimension=0)
    outputs = []
    start = 0
    for element, piece in zip(matrices, pieces):
        rows, columns = element.shape
        window = summed[start : start + piece.shape[1]].astype(F32)
        start += piece.shape[1]
        window = window.reshape(columns // WIDTH, rows, WIDTH).transpose(1, 0, 2)
        outputs.append(window.reshape(rows, columns))
    flat = summed[start:].reshape(-1).astype(F32)
    start = 0
    for element in smaller:
        outputs.append(flat[start : start + element.size].reshape(element.shape))
        start += element.size
    front_stat, rear_stat = layer.stats()
    squares = jnp.stack(
        [
            front_stat[0], front_stat[1], rear_stat[0], rear_stat[2], front_stat[2], rear_stat[1],
            rear_stat[3],
        ]
    )
    totals = lax.psum(
        jnp.append(jnp.sum(squares, axis=1), jnp.sum(lengths).astype(F32)), axes
    )
    statistics = jnp.sqrt(totals[:7] / (totals[7] * features.shape[1]))
    return (layer.encoded, layer.features_grad) + tuple(outputs) + (statistics,)


def solution(mesh):
    body = grid_device
    axes = ("x", "k", "z", "y")
    if mesh.devices.shape == (4, 8):
        mesh = Mesh(mesh.devices.reshape(2, 2, 4, 2), axes)
    else:
        axes = tuple(mesh.axis_names)
        body = functools.partial(any_device, axes=axes)
    rows, columns, vector = P(axes, None), P(None, axes), P(axes)
    weights = (rows,) * 9 + (columns,) * 2 + (vector,) * 6
    return jax.shard_map(
        body,
        mesh=mesh,
        in_specs=(rows, rows, rows) + weights,
        out_specs=(rows, rows) + weights + (P(),),
        check_vma=False,
    )
```
